32 devices in a mesh: dp: 4 (over y, x), expert: 8 (over z, core).
Axes of the slice: x: 2, y: 2, z: 4, core: 2. Of those that a mesh axis runs over, the one named last changes fastest.
Arguments:
- tokens_in: bfloat16 [32768, 768], P(('dp', 'expert')), may hold values from -6 to 6
- cont_ids: int32 [32, 512], P(('dp', 'expert')), may hold values from 0 to 3, never falling along the last dimension, each value on 1 to 256 neighbouring positions
- expert_ids: int32 [32768, 2], P(('dp', 'expert')), may hold values from 0 to 7, all different within a row; in each aligned block of 1024 rows (0 to 1023, 1024 to 2047, ...) at most 512 rows name the same one
- priority: int32 [32768, 2], P(('dp', 'expert')), may hold values from 0 to 3
- gain_attn: float32 [768], replicated, may hold values from 0.5 to 1.5
- w_qkv: bfloat16 [768, 2304], P(('dp', 'expert')), may hold values from -0.21875 to 0.21875
- rel_table: float32 [31, 12], replicated, may hold values from -4 to 4
- w_out: bfloat16 [768, 768], P(('dp', 'expert')), may hold values from -0.875 to 0.875
- gain_ffn: float32 [768], replicated, may hold values from 0.5 to 1.5
- w_router: bfloat16 [768, 8], P(('dp', 'expert')), may hold values from -0.21875 to 0.21875
- w_in: bfloat16 [8, 768, 3072], P('expert'), may hold values from -0.21875 to 0.21875
- w_down: bfloat16 [8, 3072, 768], P('expert'), may hold values from -0.109375 to 0.109375
- cotangent: bfloat16 [32768, 768], P(('dp', 'expert')), may hold values from -6 to 6
Outputs:
- out: bfloat16 [32768, 768], P(('dp', 'expert'))
- d_tokens: float32 [32768, 768], P(('dp', 'expert'))
- d_gain_attn: float32 [768], replicated
- d_w_qkv: float32 [768, 2304], P(('dp', 'expert'))
- d_rel_table: float32 [31, 12], replicated
- d_w_out: float32 [768, 768], P(('dp', 'expert'))
- d_gain_ffn: float32 [768], replicated
- d_w_router: float32 [768, 8], P(('dp', 'expert'))
- d_w_in: float32 [8, 768, 3072], P('expert', 'dp')
- d_w_down: float32 [8, 3072, 768], P('expert', 'dp')
The draws below stay inside these ranges and needn't reach their ends.
Inputs may be any that keep to these rules, and one draw needn't show every extreme that they name: `expert_ids`: each token names 2 different experts. Within the rows of one device no expert is named more than 512 times, a bound that some block reaches. `cont_ids`: along each device's row the ids never fall; each run of one id is 1 to 256 tokens long, and some run is exactly 256.
All inputs are finite; a program needn't handle non-finite values.
Results may differ from the reference program's by a relative error of at most 0.015.
Values may be sent and summed in bfloat16 or wider, within the bound.
A program may use at most 320 MiB of HBM per device.

```python
import math
import jax
import jax.numpy as jnp
import numpy as np
from jax import lax

D = 768
HEADS = 12
HEAD = 64
FF = 3072
EXPERTS = 8
TOP = 2
PRIO = 4
NB = 31
BLOCK = 512
PROMPT = 2048
CONT_LEN = 256
CONT_DEV = 512
TOK_DEV = 1024
SEGS = 4
SEND = 512
CAP = 2048
TOKENS = 32768
N_DP = 4
N_EXPERT = 8
DEVICES = 32


def plant(values, rng, least, largest):
    longest = values.shape.index(max(values.shape))
    spots = []
    for shift in (0, 1):
        where = [jax.random.randint(jax.random.fold_in(rng, axis), (), 0, length) for axis, length in enumerate(values.shape)]
        where[longest] = (where[longest] + shift) % values.shape[longest]
        spots.append(tuple(where))
    return values.at[spots[0]].set(least).at[spots[1]].set(largest)


def block_levels(own_key, dims, split, low, high):
    level, own = 1.0, jax.random.fold_in(own_key, 6)
    for axis_at, shards_of in split:
        steps = jnp.exp(jax.random.uniform(jax.random.fold_in(own, axis_at), (shards_of,), jnp.float32, low / len(split), high / len(split)))
        level = level * jnp.repeat(steps, dims[axis_at] // shards_of).reshape([-1 if axis == axis_at else 1 for axis in range(len(dims))])
    return level


def split_up(amount, total, bound, skew):
    weights = [(1 << 20) // math.isqrt(rank ** skew) + 1 for rank in range(2, amount + 1)]
    rest, holding = total - bound - (amount - 1), [1] * (amount - 1)
    while rest > 0:
        movable = [i for i in range(amount - 1) if holding[i] < bound]
        whole, budget = sum([weights[i] for i in movable]), rest
        for i in movable:
            more = min(bound - holding[i], max(1, budget * weights[i] // whole), rest)
            holding[i] = holding[i] + more
            rest = rest - more
    return np.array([bound] + holding)


def ragged_sizes(rng, number_of, total, limit, slope):
    if number_of == 2:
        one = jax.random.randint(rng, (), max(1, total - limit), min(limit, total - 1) + 1)
        return jnp.stack([one, total - one])
    lengths = jnp.asarray(split_up(number_of, total, limit, slope), jnp.int32)
    twos = (number_of - 1) // 2
    giver, sink = lengths[1:1 + 2 * twos:2], lengths[2:2 + 2 * twos:2]
    room = jnp.minimum(giver - 1, limit - sink)
    moved = jax.random.randint(jax.random.fold_in(rng, 1), (twos,), 0, 1 << 20) % (room + 1)
    lengths = lengths.at[1:1 + 2 * twos:2].set(giver - moved).at[2:2 + 2 * twos:2].set(sink + moved)
    return lengths[jax.random.permutation(jax.random.fold_in(rng, 2), number_of)]


def routed_block(key, own, number, rows, amount, top, bound, lean):
    order = jax.random.permutation(key, amount)
    crowded, common = load_shares(amount, rows * top, bound, lean, True), load_shares(amount, rows * top, bound, lean, False)
    places = jnp.arange(amount)

    def named(sizes, turn):
        used = int((sizes > 0).sum())
        fixed = max(1, used // 4)
        shifted = fixed + (places - fixed + turn * (used - fixed)) % max(1, amount - fixed)
        return jnp.zeros((amount,), jnp.int32).at[order[jnp.where(places < fixed, places, shifted)]].set(jnp.asarray(sizes, jnp.int32))

    sizes = jnp.where(number % 4 == 0, named(crowded, number // 4), named(common, number - number // 4 - 1))
    mixed = jax.random.permutation(jax.random.fold_in(own, 3), amount)
    giver, receiver = mixed[0:amount // 2 * 2:2], mixed[1:amount // 2 * 2:2]
    margin = jnp.minimum(sizes[giver] - 1, bound - sizes[receiver]) // 2
    margin = jnp.where((giver == order[0]) | (receiver == order[0]) | (sizes[receiver] == 0), 0, jnp.maximum(margin, 0))
    shifted = jax.random.randint(jax.random.fold_in(own, 4), (amount // 2,), 0, 1 << 20) % (margin + 1)
    sizes = sizes.at[giver].add(-shifted).at[receiver].add(shifted)
    items = jnp.searchsorted(jnp.cumsum(sizes), jnp.arange(rows * top), side="right").astype(jnp.int32)
    table = items.reshape(top, rows).T
    table = table[jax.random.permutation(jax.random.fold_in(own, 1), rows)]
    turn = jax.random.randint(jax.random.fold_in(own, 2), (rows, 1), 0, top)
    return jnp.take_along_axis(table, (jnp.arange(top)[None, :] + turn) % top, axis=1)


def load_shares(count, total, most, skew, full):
    portions = [(1 << 20) // math.isqrt(rank ** skew) + 1 for rank in range(1, count + 1)]
    largest = most if full else min(most, max(-(-total // count), total * portions[0] // sum(portions)))
    least = 1 if total - largest >= count - 1 else 0
    given, spare = [largest] + [least] * (count - 1), total - largest - least * (count - 1)
    while spare > 0:
        free = [i for i in range(1, count) if given[i] < largest] or [i for i in range(1, count) if given[i] < most]
        pool, left = sum([portions[i] for i in free]), spare
        for i in free:
            addition = min(most - given[i], max(1, left * portions[i] // pool), spare)
            given[i] = given[i] + addition
            spare = spare - addition
    return np.array(given)


def bell_draw(rng, extent, width, reach, shards=(), held_as=jnp.bfloat16):
    factor_of = block_levels(rng, extent, shards, -0.22, 0.18) if shards else 1.0
    entries = jax.random.normal(rng, extent, jnp.float32) * width * factor_of
    return jnp.minimum(jnp.maximum(entries, -reach), reach).astype(held_as)


def setup_inputs(seed: int = 0) -> dict:
    key_of = jax.random.split(jax.random.key(seed), 14)
    tokens_in = bell_draw(key_of[0], (TOKENS, D), 1.0, 6.0, ((0, 32),))
    cont_ids = jax.vmap(lambda own: jnp.searchsorted(jnp.cumsum(ragged_sizes(own, SEGS, CONT_DEV, CONT_LEN, 0)), jnp.arange(CONT_DEV), side="right"))(jax.random.split(key_of[1], DEVICES)).reshape((DEVICES, CONT_DEV)).astype(jnp.int32)
    expert_ids_keys = jax.random.split(jax.random.fold_in(key_of[2], 1), TOKENS // TOK_DEV)
    expert_ids_turns = jax.random.permutation(jax.random.fold_in(key_of[2], 3), TOKENS // TOK_DEV)
    expert_ids = jax.vmap(lambda own, number: routed_block(jax.random.fold_in(key_of[2], 2), own, number, TOK_DEV, EXPERTS, TOP, SEND, 1))(expert_ids_keys, expert_ids_turns).reshape((TOKENS, TOP))
    priority = plant(jax.random.randint(key_of[3], (TOKENS, TOP), 0, PRIO), jax.random.fold_in(key_of[3], 1), 0, PRIO - 1).astype(jnp.int32)
    gain_attn = jnp.clip(1.0 + 0.1 * jax.random.normal(key_of[4], (D,), jnp.float32), 0.5, 1.5)
    w_qkv = bell_draw(key_of[5], (D, 3 * D), D ** -0.5, 0.21875, ((0, 32),))
    rel_table = bell_draw(key_of[6], (NB, HEADS), 1.0, 4.0, (), jnp.float32)
    w_out = bell_draw(key_of[7], (D, D), (D // 16) ** -0.5, 0.875, ((0, 32),))
    gain_ffn = jnp.clip(1.0 + 0.1 * jax.random.normal(key_of[8], (D,), jnp.float32), 0.5, 1.5)
    w_router = bell_draw(key_of[9], (D, EXPERTS), D ** -0.5, 0.21875, ((0, 32),))
    w_in = bell_draw(key_of[10], (EXPERTS, D, FF), D ** -0.5, 0.21875, ((0, 8),))
    w_down = bell_draw(key_of[11], (EXPERTS, FF, D), FF ** -0.5, 0.109375, ((0, 8),))
    cotangent = bell_draw(key_of[12], (TOKENS, D), 1.0, 6.0, ((0, 32),))
    return dict(tokens_in=tokens_in, cont_ids=cont_ids, expert_ids=expert_ids, priority=priority, gain_attn=gain_attn, w_qkv=w_qkv, rel_table=rel_table, w_out=w_out, gain_ffn=gain_ffn, w_router=w_router, w_in=w_in, w_down=w_down, cotangent=cotangent)


@jax.custom_vjp
def low(v):
    return lax.optimization_barrier(v.astype(jnp.bfloat16)).astype(jnp.float32)

@jax.custom_vjp
def low_back(v):
    return v

def low_keep(v):
    return (low(v), None)

def low_pass(kept, grad):
    return (grad,)

def back_keep(v):
    return (v, None)

def back_low(kept, grad):
    return (low(grad),)
low.defvjp(low_keep, low_pass)
low_back.defvjp(back_keep, back_low)
BORDERS = (16, 24, 32, 48, 64, 96, 128, 192, 256, 384, 512, 768, 1024, 1536, 2048)
EPSILON = 1e-06
MASKED = -1e+30

def bucket_of(distance):
    distance = jnp.maximum(distance, 0)
    counted = jnp.minimum(distance, 15)
    for border in BORDERS:
        counted = counted + (distance >= border).astype(jnp.int32)
    return counted.astype(jnp.int32)

def normed(values, gain):
    return values * lax.rsqrt(lax.optimization_barrier(jnp.mean(values * values, axis=-1, keepdims=True)) + EPSILON) * gain

def positions_of(cont_ids):
    devices = N_DP * N_EXPERT
    prompt_rows = PROMPT // N_DP
    same = cont_ids[:, :, None] == cont_ids[:, None, :]
    earlier = jnp.arange(CONT_DEV)[None, :] < jnp.arange(CONT_DEV)[:, None]
    offset = lax.optimization_barrier(jnp.sum((same & earlier[None]).astype(jnp.int32), axis=2)).astype(jnp.int32)
    dp_index = (jnp.arange(devices) // N_EXPERT).astype(jnp.int32)
    prompt_position = dp_index[:, None] * prompt_rows + jnp.arange(prompt_rows).astype(jnp.int32)[None, :]
    position = jnp.concatenate([prompt_position, PROMPT + offset], axis=1).astype(jnp.int32)
    sequence = jnp.concatenate([jnp.full((devices, prompt_rows), -1, jnp.int32), dp_index[:, None] * CONT_DEV + cont_ids], axis=1).astype(jnp.int32)
    return (position, sequence)

def grouped(array):
    tail = array.shape[1:]
    shaped = array.reshape((N_DP, N_EXPERT, TOK_DEV) + tail)
    return jnp.swapaxes(shaped, 0, 1).reshape((N_EXPERT, N_DP * TOK_DEV) + tail)

def ungrouped(array):
    tail = array.shape[2:]
    shaped = array.reshape((N_EXPERT, N_DP, TOK_DEV) + tail)
    return jnp.swapaxes(shaped, 0, 1).reshape((N_DP * N_EXPERT * TOK_DEV,) + tail)

def forward(tokens, gain_attn, w_qkv, rel_table, w_out, gain_ffn, w_router, w_in, w_down, position, sequence, expert_ids, priority):
    precise = lax.Precision.HIGHEST
    scale = HEAD ** (-0.5)
    normed_attn = low(normed(tokens, gain_attn))
    projected = low_back(low(jnp.dot(normed_attn, w_qkv, precision=precise)))
    query = projected[:, :D].reshape(-1, HEADS, HEAD)
    keys = projected[:, D:2 * D].reshape(-1, HEADS, HEAD)
    values = projected[:, 2 * D:].reshape(-1, HEADS, HEAD)
    table_heads = rel_table.T

    def attend_group(group_in):
        group_query, group_keys, group_values, group_position, group_sequence = group_in
        blocks = group_query.shape[0] // BLOCK

        def attend_block(block_in):
            query_block, position_block, sequence_block = block_in
            scores = jnp.einsum('qhd,khd->hqk', query_block, group_keys, precision=precise) * scale
            distance = position_block[:, None] - group_position[None, :]
            seen = (distance >= 0) & ((group_sequence[None, :] < 0) | (group_sequence[None, :] == sequence_block[:, None]))
            scores = low_back(scores + jnp.take(table_heads, bucket_of(distance), axis=1))
            weights = jax.nn.softmax(jnp.where(seen[None], scores, MASKED), axis=-1)
            return jnp.einsum('hqk,khd->qhd', low(weights), group_values, precision=precise)
        outputs = lax.map(jax.checkpoint(attend_block), (group_query.reshape(blocks, BLOCK, HEADS, HEAD), group_position.reshape(blocks, BLOCK), group_sequence.reshape(blocks, BLOCK)))
        return outputs.reshape(-1, HEADS, HEAD)
    group_position = jnp.swapaxes(position.reshape(N_DP, N_EXPERT, TOK_DEV), 0, 1).reshape(N_EXPERT, -1)
    group_sequence = jnp.swapaxes(sequence.reshape(N_DP, N_EXPERT, TOK_DEV), 0, 1).reshape(N_EXPERT, -1)
    attended = lax.map(jax.checkpoint(attend_group), (grouped(query), grouped(keys), grouped(values), group_position, group_sequence))
    attended = low_back(low(ungrouped(attended).reshape(-1, D)))
    middle = tokens + low_back(jnp.dot(attended, w_out, precision=precise))
    normed_ffn = low(normed(middle, gain_ffn))
    logits = low_back(jnp.dot(normed_ffn, w_router, precision=precise))
    chosen = jnp.take_along_axis(logits, expert_ids, axis=1)
    gates = jax.nn.softmax(chosen, axis=-1)

    def moe_row(row_in):
        row_inputs, row_gates, row_experts, row_levels = row_in
        flat_expert = row_experts.reshape(-1)
        flat_level = row_levels.reshape(-1)
        code = flat_level * EXPERTS + flat_expert
        onehot = (code[:, None] == jnp.arange(PRIO * EXPERTS)[None, :]).astype(jnp.int32)
        before = (jnp.cumsum(onehot, axis=0) - onehot).astype(jnp.int32)
        rank = lax.optimization_barrier(jnp.sum(before * onehot, axis=1)).astype(jnp.int32)
        totals = lax.optimization_barrier(jnp.sum(onehot, axis=0)).astype(jnp.int32).reshape(PRIO, EXPERTS)
        lower = (jnp.cumsum(totals, axis=0) - totals).astype(jnp.int32).reshape(-1)
        slot = (rank + lax.optimization_barrier(jnp.sum(onehot * lower[None, :], axis=1))).astype(jnp.int32)
        kept = slot < CAP
        target = jnp.where(kept, flat_expert * CAP + slot, EXPERTS * CAP).astype(jnp.int32)
        pair_inputs = jnp.repeat(row_inputs, TOP, axis=0)
        buffer = jnp.zeros((EXPERTS * CAP, D), jnp.float32).at[target].set(pair_inputs, mode='drop')
        buffer = low_back(buffer).reshape(EXPERTS, CAP, D)

        def expert_apply(expert_in):
            slots_in, first, second = expert_in
            hidden = low_back(jnp.dot(slots_in, first, precision=precise))
            activated = low(jax.nn.gelu(hidden))
            return jnp.dot(activated, second, precision=precise)
        outputs = lax.map(jax.checkpoint(expert_apply), (buffer, w_in, w_down))
        outputs = low_back(low(outputs)).reshape(EXPERTS * CAP, D)
        pair_out = jnp.take(outputs, jnp.minimum(target, EXPERTS * CAP - 1), axis=0)
        pair_out = jnp.where(kept[:, None], pair_out, 0.0).reshape(-1, TOP, D)
        return lax.optimization_barrier(jnp.sum(row_gates[:, :, None] * pair_out, axis=1))
    mixed = lax.map(moe_row, (normed_ffn.reshape(N_DP, -1, D), gates.reshape(N_DP, -1, TOP), expert_ids.reshape(N_DP, -1, TOP), priority.reshape(N_DP, -1, TOP)))
    return middle + mixed.reshape(-1, D)

def reference(tokens_in, cont_ids, expert_ids, priority, gain_attn, w_qkv, rel_table, w_out, gain_ffn, w_router, w_in, w_down, cotangent):
    position, sequence = positions_of(cont_ids)

    def layer(tokens, gain_one, qkv_weight, table, out_weight, gain_two, router_weight, in_weight, down_weight):
        return forward(tokens, gain_one, qkv_weight, table, out_weight, gain_two, router_weight, in_weight, down_weight, position, sequence, expert_ids, priority)
    primal = (tokens_in.astype(jnp.float32), gain_attn, w_qkv.astype(jnp.float32), rel_table, w_out.astype(jnp.float32), gain_ffn, w_router.astype(jnp.float32), w_in.astype(jnp.float32), w_down.astype(jnp.float32))
    output, pullback = jax.vjp(layer, *primal)
    grads = pullback(cotangent.astype(jnp.float32))
    return (output.astype(jnp.bfloat16), grads[0], grads[1], grads[2], grads[3], grads[4], grads[5], grads[6], grads[7], grads[8])
```

```python
import functools
import math
import jax
import jax.numpy as jnp
from jax import lax
from jax.experimental import pallas as pl
from jax.experimental.pallas import tpu as pltpu
from jax.sharding import PartitionSpec as P

PRIO = 4
PROMPT = 2048


BORDERS = (16, 24, 32, 48, 64, 96, 128, 192, 256, 384, 512, 768, 1024, 1536, 2048)
EPSILON = 1e-06
MASKED = -1e30


def bucket_of(distance):
    distance = jnp.maximum(distance, 0)
    counted = jnp.minimum(distance, 15)
    for border in BORDERS:
        counted = counted + (distance >= border).astype(jnp.int32)
    return counted


def normed(values, gain):
    return values * lax.rsqrt(jnp.mean(values * values, axis=-1, keepdims=True) + EPSILON) * gain


def dense_gather(w_qkv, w_out, w_router):
    return (
        lax.all_gather(w_qkv, ("dp", "expert"), axis=0, tiled=True),
        lax.all_gather(w_out, ("dp", "expert"), axis=0, tiled=True),
        lax.all_gather(w_router, ("dp", "expert"), axis=0, tiled=True),
    )


def dense_regather(w_qkv, w_out, w_router):
    return (
        lax.all_gather(w_qkv, ("dp", "expert"), axis=0, tiled=True),
        lax.all_gather(w_out, ("dp", "expert"), axis=0, tiled=True),
        lax.all_gather(w_router, ("dp", "expert"), axis=0, tiled=True),
    )


def prompt_gather(own_keys, own_values):
    return (
        lax.all_gather(own_keys, "dp", axis=0, tiled=True),
        lax.all_gather(own_values, "dp", axis=0, tiled=True),
    )


LOG2E = math.log2(math.e)
F32, BF16 = jnp.float32, jnp.bfloat16
QT = 256
KT = 512
RUN = 256
ROWS = 32
NT = (((1,), (1,)), ((), ()))
NN = (((1,), (0,)), ((), ()))

def dot(a, b, dims=NN):
    return lax.dot_general(a, b, dims, preferred_element_type=F32)

def bias_rows(rel_table):
    width = PROMPT + 512 + RUN
    distance = PROMPT + RUN - jnp.arange(width)[None, :] + jnp.arange(8)[:, None]
    bucket = bucket_of(distance)
    table = rel_table.T[:, None, None, :] * LOG2E
    hot = (bucket[..., None] == jnp.arange(rel_table.shape[0])).astype(F32)
    rows = jnp.sum(hot[None] * table, axis=-1)
    return jnp.where(distance[None] >= 0, rows, MASKED)

def build_bias(info, base, row_start, t_scr, b_scr):
    width = base.shape[-1]
    for a in range(16):
        t_scr[8 * a:8 * a + 8, :] = pltpu.roll(base, 8 * a, 1) if a else base
    lane = lax.broadcasted_iota(jnp.int32, (ROWS, 128), 1)
    sub = lax.broadcasted_iota(jnp.int32, (ROWS, 128), 0)
    for s in range(4):
        start, end = info[s], info[s + 1]
        turn = start % 128
        left = (128 - turn) % 128
        here = (lane < left) | (left == 0)
        def place(g, _):
            at = pl.ds(pl.multiple_of(ROWS * g, ROWS), ROWS)
            first = start - turn + RUN - 128 * (g // (128 // ROWS))
            of = pl.ds(pl.multiple_of(ROWS * (g % (128 // ROWS)), ROWS), ROWS)
            mine = sub + ROWS * g >= start
            turned = None
            for b in range(PROMPT // 128 + 1):
                after = pltpu.roll(t_scr[of, pl.ds(pl.multiple_of(first + 128 * b, 128), 128)], left, 1)
                if b:
                    cols = slice(128 * b - 128, 128 * b)
                    b_scr[at, cols] = jnp.where(mine, jnp.where(here, turned, after), b_scr[at, cols])
                turned = after
            return 0
        lax.fori_loop(start // ROWS, (end + ROWS - 1) // ROWS, place, 0)
    lane = lax.broadcasted_iota(jnp.int32, (128, 128), 1)
    for i in range(KT // 128):
        rows = slice(128 * i, 128 * i + 128)
        own = row_start[rows, :]
        for b in range(KT // 128):
            first = PROMPT + RUN - 128 * i + 128 * b
            b_scr[rows, PROMPT + 128 * b:PROMPT + 128 * b + 128] = jnp.where(
                lane + 128 * b >= own, t_scr[:, first:first + 128], MASKED)

def own_lanes(h, rows):
    lane = lax.broadcasted_iota(jnp.int32, (rows, 128), 1)
    return lane // 64 == h % 2

def fwd_kernel(scale2, info, q_ref, k_ref, v_ref, r_ref, st_ref, o_ref, lse_ref, t_scr, b_scr):
    h = pl.program_id(0)
    dp = info[5]
    build_bias(info, r_ref[0], st_ref, t_scr, b_scr)
    own = own_lanes(h, QT)
    head_lane = lax.broadcasted_iota(jnp.int32, (QT, 128), 1) == h

    def tile(first, key_tiles, bias_of, block):
        rows = pl.ds(first, QT)
        q = jnp.where(own, q_ref[rows, :], jnp.zeros((), BF16))
        def step(t, carry):
            m, l, acc = carry
            cols = pl.ds(pl.multiple_of(block(t) * KT, KT), KT)
            s = dot(q, k_ref[cols, :], NT) * scale2 + bias_of(t)
            new = jnp.maximum(m, jnp.max(s, axis=1, keepdims=True))
            keep = jnp.exp2(m - new)
            p = jnp.exp2(s - new[:, :1])
            part = p[:, :128]
            for c in range(1, KT // 128):
                part = part + p[:, 128 * c:128 * (c + 1)]
            return new, l * keep + part, acc * keep + dot(p.astype(BF16), v_ref[cols, :])
        zero = jnp.zeros((QT, 128), F32)
        m, l, acc = lax.fori_loop(0, key_tiles, step, (jnp.full((QT, 128), MASKED, F32), zero, zero))
        l = jnp.sum(l, axis=1, keepdims=True)
        o_ref[rows, :] = jnp.where(own, acc / l, o_ref[rows, :])
        lse_ref[rows, :] = jnp.where(head_lane, m + jnp.log2(l), lse_ref[rows, :])

    for j in range(2):
        shift = PROMPT - KT * dp - QT * j + RUN
        def bias(t, shift=shift):
            first = (dp - t) * KT + shift
            return jnp.concatenate([t_scr[:, pl.ds(pl.multiple_of(first - 128 * x, 128), KT)] for x in range(QT // 128)], axis=0)
        tile(QT * j, dp + 1, bias, lambda t: dp - t)
    for j in range(2):
        tile(KT + QT * j, PROMPT // KT + 1,
             lambda t: b_scr[pl.ds(QT * j, QT), pl.ds(pl.multiple_of(t * KT, KT), KT)], lambda t: t)

def attention_forward(info, q, k, v, rows_bias, row_start, heads):
    n, width = q.shape
    keys = k.shape[0]
    pair = lambda r: pl.BlockSpec((r, 128), lambda h, *_: (0, h // 2))
    whole = pl.BlockSpec((n, 128), lambda h, *_: (0, 0))
    scale2 = (width // heads) ** -0.5 * LOG2E
    return pl.pallas_call(
        functools.partial(fwd_kernel, scale2),
        grid_spec=pltpu.PrefetchScalarGridSpec(
            num_scalar_prefetch=1, grid=(heads,),
            in_specs=[pair(n), pair(keys), pair(keys),
                      pl.BlockSpec((1, 8, rows_bias.shape[2]), lambda h, *_: (h, 0, 0)),
                      pl.BlockSpec((KT, 128), lambda h, *_: (0, 0))],
            out_specs=[pair(n), whole],
            scratch_shapes=[pltpu.VMEM((128, rows_bias.shape[2]), F32), pltpu.VMEM((KT, PROMPT + KT), F32)]),
        out_shape=[jax.ShapeDtypeStruct((n, width), F32), jax.ShapeDtypeStruct((n, 128), F32)],
        compiler_params=pltpu.CompilerParams(vmem_limit_bytes=60 << 20),
        name="attention_forward",
    )(info, q, k, v, rows_bias, row_start)

def split3(x):
    hi = x.astype(BF16)
    rest = x - hi.astype(F32)
    mid = rest.astype(BF16)
    return hi, mid, (rest - mid.astype(F32)).astype(BF16)

def bwd_kernel(scale, info, q_ref, do_ref, o_ref, lse_ref, k_ref, v_ref, r_ref, st_ref,
               dq_ref, dk_ref, dv_ref, dd_ref,
               t_scr, b_scr, e_scr, db_scr, qa, da, ka, va, qt, dot_t, dkt, dvt):
    h = pl.program_id(0)
    dp = info[5]
    n, keys = q_ref.shape[0], k_ref.shape[0]
    half = h % 2
    build_bias(info, r_ref[0], st_ref, t_scr, b_scr)
    base = pl.multiple_of(64 * half, 64)
    other = 64 - 64 * half

    @pl.when(half == 0)
    def _():
        qt[...] = q_ref[...].T
        dot_t[...] = do_ref[...].T
        dq_ref[...] = jnp.zeros_like(dq_ref)

    lane_n = lax.broadcasted_iota(jnp.int32, (QT, 128), 1)
    own_n = lane_n // 64 == half
    def augment(i, _):
        rows = pl.ds(pl.multiple_of(i * QT, QT), QT)
        lse = jnp.sum(jnp.where(lane_n == h, lse_ref[rows, :], 0.0), axis=1, keepdims=True)
        parts = split3(-lse / (scale * LOG2E))
        aug = jnp.zeros((QT, 128), BF16)
        for x in range(3):
            aug = jnp.where(lane_n == other + x, jnp.broadcast_to(parts[x], (QT, 128)), aug)
        qa[rows, :] = jnp.where(own_n, q_ref[rows, :], aug)
        do = do_ref[rows, :]
        delta = jnp.sum(jnp.where(own_n, do.astype(F32) * o_ref[rows, :], 0.0), axis=1, keepdims=True)
        parts = split3(-delta)
        aug = jnp.zeros((QT, 128), BF16)
        for x in range(3):
            aug = jnp.where(lane_n == other + x, jnp.broadcast_to(parts[x], (QT, 128)), aug)
        da[rows, :] = jnp.where(own_n, do, aug)
        return 0
    lax.fori_loop(0, n // QT, augment, 0)
    lane_k = lax.broadcasted_iota(jnp.int32, (KT, 128), 1)
    ones = jnp.where((lane_k >= other) & (lane_k < other + 3), 1.0, 0.0).astype(BF16)
    own_k = lane_k // 64 == half
    def augment_keys(i, _):
        rows = pl.ds(pl.multiple_of(i * KT, KT), KT)
        ka[rows, :] = jnp.where(own_k, k_ref[rows, :], ones)
        va[rows, :] = jnp.where(own_k, v_ref[rows, :], ones)
        return 0
    lax.fori_loop(0, keys // KT, augment_keys, 0)
    head_rows = pl.ds(base, 64)
    dkt[head_rows, :] = jnp.zeros((64, keys), F32)
    dvt[head_rows, :] = jnp.zeros((64, keys), F32)
    e_scr[...] = jnp.zeros_like(e_scr)

    def tile(first, key_tiles, bias_of, grad_bias):
        rows = pl.ds(first, QT)
        q, do = qa[rows, :], da[rows, :]
        q_t, do_t = qt[head_rows, rows], dot_t[head_rows, rows]
        def step(t, dq):
            cols = pl.ds(pl.multiple_of(t * KT, KT), KT)
            kk = ka[cols, :]
            p = jnp.exp2(dot(q, kk, NT) * (scale * LOG2E) + bias_of(t))
            ds = p * dot(do, va[cols, :], NT)
            grad_bias(t, ds)
            low = ds.astype(BF16)
            dvt[head_rows, cols] += dot(do_t, p.astype(BF16))
            dkt[head_rows, cols] += dot(q_t, low)
            return dq + dot(low, kk)
        dq = lax.fori_loop(0, key_tiles, step, jnp.zeros((QT, 128), F32))
        dq_ref[rows, :] = jnp.where(own_n, dq * scale, dq_ref[rows, :].astype(F32)).astype(BF16)

    for j in range(2):
        shift = PROMPT - KT * dp - QT * j + RUN
        def part(t, x, shift=shift):
            return (slice(None), pl.ds(pl.multiple_of(t * KT + shift - 128 * x, 128), KT))
        def bias(t):
            return jnp.concatenate([t_scr[part(t, x)] for x in range(QT // 128)], axis=0)
        def add(t, ds):
            for x in range(QT // 128):
                e_scr[part(t, x)] += ds[128 * x:128 * x + 128, :]
        tile(QT * j, dp + 1, bias, add)
    for j in range(2):
        def where(t):
            return (pl.ds(QT * j, QT), pl.ds(pl.multiple_of(t * KT, KT), KT))
        def put(t, ds):
            db_scr[where(t)] = ds
        tile(KT + QT * j, PROMPT // KT + 1, lambda t: b_scr[where(t)], put)

    lane = lax.broadcasted_iota(jnp.int32, (ROWS, 128), 1)
    sub = lax.broadcasted_iota(jnp.int32, (ROWS, 128), 0)
    for s in range(4):
        start, end = info[s], info[s + 1]
        turn = start % 128
        def fold(g, _):
            at = pl.ds(pl.multiple_of(ROWS * g, ROWS), ROWS)
            first = start - turn + RUN - 128 * (g // (128 // ROWS))
            to = pl.ds(pl.multiple_of(ROWS * (g % (128 // ROWS)), ROWS), ROWS)
            mine = (sub + ROWS * g >= start) & (sub + ROWS * g < end)
            before = jnp.zeros((ROWS, 128), F32)
            for b in range(PROMPT // 128 + 1):
                if b < PROMPT // 128:
                    turned = pltpu.roll(jnp.where(mine, db_scr[at, 128 * b:128 * b + 128], 0.0), turn, 1)
                else:
                    turned = jnp.zeros((ROWS, 128), F32)
                e_scr[to, pl.ds(pl.multiple_of(first + 128 * b, 128), 128)] += jnp.where(lane >= turn, turned, before)
                before = turned
            return 0
        lax.fori_loop(start // ROWS, (end + ROWS - 1) // ROWS, fold, 0)
    for i in range(KT // 128):
        first = PROMPT + RUN - 128 * i
        e_scr[:, first:first + KT] += db_scr[128 * i:128 * i + 128, PROMPT:]
    width = r_ref.shape[2]
    acc = e_scr[0:8, :]
    for a in range(1, 16):
        acc = acc + pltpu.roll(e_scr[8 * a:8 * a + 8, :], width - 8 * a, 1)
    total = acc[0:1, :]
    for i in range(1, 8):
        total = total + pltpu.roll(acc, width - i, 1)[i:i + 1, :]
    dd_ref[0] = total

    @pl.when(half == 1)
    def _():
        dk_ref[...] = (dkt[...] * scale).T.astype(BF16)
        dv_ref[...] = dvt[...].T.astype(BF16)

def attention_backward(info, q, do, o32, lse, k, v, rows_bias, row_start, heads):
    n, width = q.shape
    keys = k.shape[0]
    wide = rows_bias.shape[2]
    pair = lambda r: pl.BlockSpec((r, 128), lambda h, *_: (0, h // 2))
    whole = pl.BlockSpec((n, 128), lambda h, *_: (0, 0))
    line = pl.BlockSpec((1, 1, wide), lambda h, *_: (h, 0, 0))
    scale = (width // heads) ** -0.5
    cols = PROMPT + KT
    return pl.pallas_call(
        functools.partial(bwd_kernel, scale),
        grid_spec=pltpu.PrefetchScalarGridSpec(
            num_scalar_prefetch=1, grid=(heads,),
            in_specs=[pair(n), pair(n), pair(n), whole, pair(keys), pair(keys),
                      pl.BlockSpec((1, 8, wide), lambda h, *_: (h, 0, 0)), pl.BlockSpec((KT, 128), lambda h, *_: (0, 0))],
            out_specs=[pair(n), pair(keys), pair(keys), line],
            scratch_shapes=[pltpu.VMEM((128, wide), F32), pltpu.VMEM((KT, cols), F32),
                            pltpu.VMEM((128, wide), F32), pltpu.VMEM((KT, cols), F32),
                            pltpu.VMEM((n, 128), BF16), pltpu.VMEM((n, 128), BF16),
                            pltpu.VMEM((keys, 128), BF16), pltpu.VMEM((keys, 128), BF16),
                            pltpu.VMEM((128, n), BF16), pltpu.VMEM((128, n), BF16),
                            pltpu.VMEM((128, keys), F32), pltpu.VMEM((128, keys), F32)]),
        out_shape=[jax.ShapeDtypeStruct((n, width), BF16), jax.ShapeDtypeStruct((keys, width), BF16),
                   jax.ShapeDtypeStruct((keys, width), BF16), jax.ShapeDtypeStruct((heads, 1, wide), F32)],
        compiler_params=pltpu.CompilerParams(vmem_limit_bytes=60 << 20),
        name="attention_backward",
    )(info, q, do, o32, lse, k, v, rows_bias, row_start)

def info_of(ids, dp):
    starts = jnp.sum((ids[None, :] < jnp.arange(5)[:, None]).astype(jnp.int32), axis=1)
    return jnp.concatenate([starts, jnp.reshape(dp, (1,)).astype(jnp.int32)])

def table_grad(dd, buckets):
    width = dd.shape[2]
    distance = PROMPT + RUN - jnp.arange(width)
    hot = ((bucket_of(distance)[:, None] == jnp.arange(buckets)[None, :]) & (distance >= 0)[:, None]).astype(F32)
    return jnp.dot(dd[:, 0, :], hot, precision=lax.Precision.HIGHEST)

def row_start_of(ids):
    starts = jnp.sum((ids[None, :] < ids[:, None]).astype(jnp.int32), axis=1)
    return jnp.broadcast_to(starts[:, None], (ids.shape[0], 128))


def per_device(
    tokens_in,
    cont_ids,
    expert_ids,
    priority,
    gain_attn,
    w_qkv,
    rel_table,
    w_out,
    gain_ffn,
    w_router,
    w_in,
    w_down,
    cotangent,
):
    rows, width = tokens_in.shape
    heads = rel_table.shape[1]
    dp_count = lax.axis_size("dp")
    dp_index = lax.axis_index("dp")
    prompt_rows = PROMPT // dp_count
    cont_rows = rows - prompt_rows
    local_ids = cont_ids[0]
    info = info_of(local_ids, dp_index)
    row_start = row_start_of(local_ids)
    rows_bias = bias_rows(rel_table)
    whole_qkv, whole_out, whole_router = dense_gather(w_qkv, w_out, w_router)
    inputs = tokens_in.astype(jnp.float32)
    normed_attn = normed(inputs, gain_attn).astype(jnp.bfloat16)
    projected = jnp.dot(normed_attn, whole_qkv, preferred_element_type=jnp.float32).astype(
        jnp.bfloat16
    )
    query = projected[:, :width]
    own_keys = projected[:, width : 2 * width]
    own_values = projected[:, 2 * width :]
    prompt_keys, prompt_values = prompt_gather(own_keys[:prompt_rows], own_values[:prompt_rows])
    all_keys = jnp.concatenate([prompt_keys, own_keys[prompt_rows:]], axis=0)
    all_values = jnp.concatenate([prompt_values, own_values[prompt_rows:]], axis=0)
    exact, log_total = attention_forward(
        info, query, all_keys, all_values, rows_bias, row_start, heads
    )
    attended = exact.astype(jnp.bfloat16)
    middle = inputs + jnp.dot(attended, whole_out, preferred_element_type=jnp.float32)
    normed_ffn = normed(middle, gain_ffn).astype(jnp.bfloat16)
    logits = jnp.dot(normed_ffn, whole_router, preferred_element_type=jnp.float32)
    experts_total = whole_router.shape[1]
    top = expert_ids.shape[1]
    picks = expert_ids[:, :, None] == jnp.arange(experts_total)[None, None, :]
    chosen = jnp.sum(jnp.where(picks, logits[:, None, :], 0.0), axis=2)
    gates = jax.nn.softmax(chosen, axis=-1)
    levels = PRIO
    local_experts = w_in.shape[0]
    capacity = rows * top // local_experts
    send = max(2, 2 * rows * top // experts_total)
    flat_expert = expert_ids.reshape(-1)
    code = priority.reshape(-1) * experts_total + flat_expert
    onehot = (code[:, None] == jnp.arange(levels * experts_total)[None, :]).astype(jnp.int32)
    rank = jnp.sum((jnp.cumsum(onehot, axis=0) - onehot) * onehot, axis=1)
    counts = jnp.sum(onehot, axis=0)
    every = lax.all_gather(counts[None, :], "expert", axis=0, tiled=True).reshape(
        -1, levels, experts_total
    )
    expert_index = lax.axis_index("expert")
    totals = jnp.sum(every, axis=0)
    lower = jnp.cumsum(totals, axis=0) - totals
    earlier_sources = jnp.cumsum(every, axis=0) - every
    mine_prefix = lax.dynamic_index_in_dim(earlier_sources, expert_index, 0, keepdims=False)
    base = (lower + mine_prefix).reshape(-1)
    slot = rank + jnp.sum(onehot * base[None, :], axis=1)
    kept = slot < capacity
    own_counts = counts.reshape(levels, experts_total)
    own_lower = (jnp.cumsum(own_counts, axis=0) - own_counts).reshape(-1)
    place = rank + jnp.sum(onehot * own_lower[None, :], axis=1)
    target = flat_expert * send + place
    first_mine = expert_index * local_experts
    counts_mine = lax.dynamic_slice_in_dim(every, first_mine, local_experts, 2)
    base_mine = lax.dynamic_slice_in_dim(
        lower[None] + earlier_sources, first_mine, local_experts, 2
    )
    band_end = jnp.cumsum(counts_mine, axis=1)
    band_start = band_end - counts_mine
    place_index = jnp.arange(send, dtype=jnp.int32)
    level = jnp.sum(
        (place_index[None, None, None, :] >= band_end[:, :, :, None]).astype(jnp.int32), axis=1
    )
    level_hot = level[:, None, :, :] == jnp.arange(levels)[None, :, None, None]
    start_of = jnp.sum(jnp.where(level_hot, band_start[:, :, :, None], 0), axis=1)
    base_of = jnp.sum(jnp.where(level_hot, base_mine[:, :, :, None], 0), axis=1)
    arrived_slot = base_of + place_index[None, None, :] - start_of
    usable = (level < levels) & (arrived_slot < capacity)
    landing = jnp.where(
        usable,
        jnp.arange(local_experts)[None, :, None] * capacity + arrived_slot,
        local_experts * capacity,
    ).reshape(-1)
    live = landing < local_experts * capacity
    safe = jnp.minimum(landing, local_experts * capacity - 1)
    pair_inputs = jnp.repeat(normed_ffn, top, axis=0)
    outgoing = (
        jnp.zeros((experts_total * send, width), jnp.bfloat16)
        .at[target]
        .set(pair_inputs)
        .reshape(experts_total, send, width)
    )
    arrived = lax.all_to_all(outgoing, "expert", split_axis=0, concat_axis=0, tiled=True)
    expert_inputs = (
        jnp.zeros((local_experts * capacity, width), jnp.bfloat16)
        .at[landing]
        .set(arrived.reshape(-1, width), mode="drop")
        .reshape(local_experts, capacity, width)
    )
    hidden = jnp.einsum("ecd,edf->ecf", expert_inputs, w_in, preferred_element_type=jnp.float32)
    activated = jax.nn.gelu(hidden).astype(jnp.bfloat16)
    expert_out = jnp.einsum(
        "ecf,efd->ecd", activated, w_down, preferred_element_type=jnp.float32
    ).astype(jnp.bfloat16)
    returning = jnp.where(
        live[:, None],
        jnp.take(expert_out.reshape(-1, width), safe, axis=0),
        jnp.zeros((), jnp.bfloat16),
    ).reshape(experts_total, send, width)
    returned = lax.all_to_all(returning, "expert", split_axis=0, concat_axis=0, tiled=True)
    pair_out = jnp.where(
        kept[:, None],
        jnp.take(returned.reshape(-1, width), target, axis=0).astype(jnp.float32),
        0.0,
    ).reshape(rows, top, width)
    mixed = jnp.sum(gates[:, :, None] * pair_out, axis=1)
    output = (middle + mixed).astype(jnp.bfloat16)
    grad_out = cotangent.astype(jnp.float32)
    grad_gates = jnp.sum(grad_out[:, None, :] * pair_out, axis=2)
    pair_grads = (gates[:, :, None] * grad_out[:, None, :]).astype(jnp.bfloat16).reshape(-1, width)
    outgoing_grads = (
        jnp.zeros((experts_total * send, width), jnp.bfloat16)
        .at[target]
        .set(pair_grads)
        .reshape(experts_total, send, width)
    )
    arrived_grads = lax.all_to_all(
        outgoing_grads, "expert", split_axis=0, concat_axis=0, tiled=True
    )
    grad_expert_out = (
        jnp.zeros((local_experts * capacity, width), jnp.bfloat16)
        .at[landing]
        .set(arrived_grads.reshape(-1, width), mode="drop")
        .reshape(local_experts, capacity, width)
    )
    hidden_again = jnp.einsum(
        "ecd,edf->ecf", expert_inputs, w_in, preferred_element_type=jnp.float32
    )
    activated_again, gelu_back = jax.vjp(jax.nn.gelu, hidden_again)
    grad_activated = jnp.einsum(
        "ecd,efd->ecf", grad_expert_out, w_down, preferred_element_type=jnp.float32
    )
    grad_hidden = gelu_back(grad_activated)[0].astype(jnp.bfloat16)
    grad_w_down = jnp.einsum(
        "ecf,ecd->efd",
        activated_again.astype(jnp.bfloat16),
        grad_expert_out,
        preferred_element_type=jnp.float32,
    )
    grad_w_in = jnp.einsum(
        "ecd,ecf->edf", expert_inputs, grad_hidden, preferred_element_type=jnp.float32
    )
    grad_inputs = jnp.einsum(
        "ecf,edf->ecd", grad_hidden, w_in, preferred_element_type=jnp.float32
    ).astype(jnp.bfloat16)
    back_rows = jnp.where(
        live[:, None],
        jnp.take(grad_inputs.reshape(-1, width), safe, axis=0),
        jnp.zeros((), jnp.bfloat16),
    ).reshape(experts_total, send, width)
    came_back = lax.all_to_all(back_rows, "expert", split_axis=0, concat_axis=0, tiled=True)
    pair_back = jnp.where(
        kept[:, None],
        jnp.take(came_back.reshape(-1, width), target, axis=0).astype(jnp.float32),
        0.0,
    )
    grad_normed_ffn = jnp.sum(pair_back.reshape(rows, top, width), axis=1)
    grad_chosen = gates * (grad_gates - jnp.sum(gates * grad_gates, axis=-1, keepdims=True))
    grad_logits = jnp.sum(jnp.where(picks, grad_chosen[:, :, None], 0.0), axis=1).astype(
        jnp.bfloat16
    )
    back_qkv, back_out, back_router = dense_regather(w_qkv, w_out, w_router)
    grad_normed_ffn = grad_normed_ffn + jnp.dot(
        grad_logits, back_router.T, preferred_element_type=jnp.float32
    )
    grad_router = jnp.dot(normed_ffn.T, grad_logits, preferred_element_type=jnp.float32)
    _, ffn_norm_back = jax.vjp(normed, middle, gain_ffn)
    grad_middle_part, grad_gain_ffn = ffn_norm_back(grad_normed_ffn)
    grad_middle = grad_out + grad_middle_part
    grad_branch = grad_middle.astype(jnp.bfloat16)
    grad_out_weight = jnp.dot(attended.T, grad_branch, preferred_element_type=jnp.float32)
    grad_attended = jnp.dot(
        grad_branch, back_out.T, preferred_element_type=jnp.float32
    ).astype(jnp.bfloat16)
    grad_query, grad_keys, grad_values, grad_lines = attention_backward(
        info, query, grad_attended, exact, log_total, all_keys, all_values, rows_bias, row_start, heads
    )
    grad_table = table_grad(grad_lines, rel_table.shape[0])
    prompt_grad_keys, prompt_grad_values = (
        lax.psum_scatter(
            grad_keys[:PROMPT], "dp", scatter_dimension=0, tiled=True
        ),
        lax.psum_scatter(
            grad_values[:PROMPT], "dp", scatter_dimension=0, tiled=True
        ),
    )
    grad_projected = jnp.concatenate(
        [
            grad_query,
            jnp.concatenate([prompt_grad_keys, grad_keys[PROMPT:]], axis=0),
            jnp.concatenate([prompt_grad_values, grad_values[PROMPT:]], axis=0),
        ],
        axis=1,
    ).astype(jnp.bfloat16)
    grad_normed_attn = jnp.dot(grad_projected, back_qkv.T, preferred_element_type=jnp.float32)
    grad_qkv = jnp.dot(normed_attn.T, grad_projected, preferred_element_type=jnp.float32)
    _, attn_norm_back = jax.vjp(normed, inputs, gain_attn)
    grad_inputs_part, grad_gain_attn = attn_norm_back(grad_normed_attn)
    grad_tokens = grad_middle + grad_inputs_part
    dense_parts = (
        lax.psum_scatter(grad_qkv, ("dp", "expert"), scatter_dimension=0, tiled=True),
        lax.psum_scatter(grad_out_weight, ("dp", "expert"), scatter_dimension=0, tiled=True),
        lax.psum_scatter(grad_router, ("dp", "expert"), scatter_dimension=0, tiled=True),
    )
    expert_parts = (
        lax.psum_scatter(
            grad_w_in.astype(jnp.bfloat16), "dp", scatter_dimension=1, tiled=True
        ).astype(jnp.float32),
        lax.psum_scatter(
            grad_w_down.astype(jnp.bfloat16), "dp", scatter_dimension=1, tiled=True
        ).astype(jnp.float32),
    )
    small_parts = lax.psum((grad_gain_attn, grad_gain_ffn, grad_table.T), ("dp", "expert"))
    return (
        output,
        grad_tokens,
        small_parts[0],
        dense_parts[0],
        small_parts[2],
        dense_parts[1],
        small_parts[1],
        dense_parts[2],
        expert_parts[0],
        expert_parts[1],
    )


def solution(mesh):
    return jax.shard_map(
        per_device,
        mesh=mesh,
        in_specs=(
            P(("dp", "expert"), None),
            P(("dp", "expert"), None),
            P(("dp", "expert"), None),
            P(("dp", "expert"), None),
            P(),
            P(("dp", "expert"), None),
            P(),
            P(("dp", "expert"), None),
            P(),
            P(("dp", "expert"), None),
            P("expert", None, None),
            P("expert", None, None),
            P(("dp", "expert"), None),
        ),
        out_specs=(
            P(("dp", "expert"), None),
            P(("dp", "expert"), None),
            P(),
            P(("dp", "expert"), None),
            P(),
            P(("dp", "expert"), None),
            P(),
            P(("dp", "expert"), None),
            P("expert", "dp", None),
            P("expert", "dp", None),
        ),
        check_vma=False,
    )
```

```python
import functools
import math
import jax
import jax.numpy as jnp
from jax import lax
from jax.experimental import pallas as pl
from jax.experimental.pallas import tpu as pltpu
from jax.sharding import PartitionSpec as P

PRIO = 4
PROMPT = 2048


BORDERS = (16, 24, 32, 48, 64, 96, 128, 192, 256, 384, 512, 768, 1024, 1536, 2048)
EPSILON = 1e-06
MASKED = -1e30


def bucket_of(distance):
    distance = jnp.maximum(distance, 0)
    counted = jnp.minimum(distance, 15)
    for border in BORDERS:
        counted = counted + (distance >= border).astype(jnp.int32)
    return counted


def normed(values, gain):
    return values * lax.rsqrt(jnp.mean(values * values, axis=-1, keepdims=True) + EPSILON) * gain


def prompt_gather(own_keys, own_values):
    return (
        lax.all_gather(own_keys, "dp", axis=0, tiled=True),
        lax.all_gather(own_values, "dp", axis=0, tiled=True),
    )


LOG2E = math.log2(math.e)
F32, BF16 = jnp.float32, jnp.bfloat16
QT = 256
KT = 512
RUN = 256
ROWS = 32
NT = (((1,), (1,)), ((), ()))
NN = (((1,), (0,)), ((), ()))

def dot(a, b, dims=NN):
    return lax.dot_general(a, b, dims, preferred_element_type=F32)

def bias_rows(rel_table):
    width = PROMPT + 512 + RUN
    distance = PROMPT + RUN - jnp.arange(width)[None, :] + jnp.arange(8)[:, None]
    bucket = bucket_of(distance)
    table = rel_table.T[:, None, None, :] * LOG2E
    hot = (bucket[..., None] == jnp.arange(rel_table.shape[0])).astype(F32)
    rows = jnp.sum(hot[None] * table, axis=-1)
    return jnp.where(distance[None] >= 0, rows, MASKED)

def build_bias(info, base, row_start, t_scr, b_scr):
    width = base.shape[-1]
    for a in range(16):
        t_scr[8 * a:8 * a + 8, :] = pltpu.roll(base, 8 * a, 1) if a else base
    lane = lax.broadcasted_iota(jnp.int32, (ROWS, 128), 1)
    sub = lax.broadcasted_iota(jnp.int32, (ROWS, 128), 0)
    for s in range(4):
        start, end = info[s], info[s + 1]
        turn = start % 128
        left = (128 - turn) % 128
        here = (lane < left) | (left == 0)
        def place(g, _):
            at = pl.ds(pl.multiple_of(ROWS * g, ROWS), ROWS)
            first = start - turn + RUN - 128 * (g // (128 // ROWS))
            of = pl.ds(pl.multiple_of(ROWS * (g % (128 // ROWS)), ROWS), ROWS)
            mine = sub + ROWS * g >= start
            turned = None
            for b in range(PROMPT // 128 + 1):
                after = pltpu.roll(t_scr[of, pl.ds(pl.multiple_of(first + 128 * b, 128), 128)], left, 1)
                if b:
                    cols = slice(128 * b - 128, 128 * b)
                    b_scr[at, cols] = jnp.where(mine, jnp.where(here, turned, after), b_scr[at, cols])
                turned = after
            return 0
        lax.fori_loop(start // ROWS, (end + ROWS - 1) // ROWS, place, 0)
    lane = lax.broadcasted_iota(jnp.int32, (128, 128), 1)
    for i in range(KT // 128):
        rows = slice(128 * i, 128 * i + 128)
        own = row_start[rows, :]
        for b in range(KT // 128):
            first = PROMPT + RUN - 128 * i + 128 * b
            b_scr[rows, PROMPT + 128 * b:PROMPT + 128 * b + 128] = jnp.where(
                lane + 128 * b >= own, t_scr[:, first:first + 128], MASKED)

def own_lanes(h, rows):
    lane = lax.broadcasted_iota(jnp.int32, (rows, 128), 1)
    return lane // 64 == h % 2

def fwd_kernel(scale2, info, q_ref, k_ref, v_ref, r_ref, st_ref, o_ref, lse_ref, t_scr, b_scr):
    h = pl.program_id(0)
    dp = info[5]
    build_bias(info, r_ref[0], st_ref, t_scr, b_scr)
    own = own_lanes(h, QT)
    head_lane = lax.broadcasted_iota(jnp.int32, (QT, 128), 1) == h

    def tile(first, key_tiles, bias_of, block):
        rows = pl.ds(first, QT)
        q = jnp.where(own, q_ref[rows, :], jnp.zeros((), BF16))
        def step(t, carry):
            m, l, acc = carry
            cols = pl.ds(pl.multiple_of(block(t) * KT, KT), KT)
            s = dot(q, k_ref[cols, :], NT) * scale2 + bias_of(t)
            new = jnp.maximum(m, jnp.max(s, axis=1, keepdims=True))
            keep = jnp.exp2(m - new)
            p = jnp.exp2(s - new[:, :1])
            part = p[:, :128]
            for c in range(1, KT // 128):
                part = part + p[:, 128 * c:128 * (c + 1)]
            return new, l * keep + part, acc * keep + dot(p.astype(BF16), v_ref[cols, :])
        zero = jnp.zeros((QT, 128), F32)
        m, l, acc = lax.fori_loop(0, key_tiles, step, (jnp.full((QT, 128), MASKED, F32), zero, zero))
        l = jnp.sum(l, axis=1, keepdims=True)
        o_ref[rows, :] = jnp.where(own, acc / l, o_ref[rows, :])
        lse_ref[rows, :] = jnp.where(head_lane, m + jnp.log2(l), lse_ref[rows, :])

    for j in range(2):
        shift = PROMPT - KT * dp - QT * j + RUN
        def bias(t, shift=shift):
            first = (dp - t) * KT + shift
            return jnp.concatenate([t_scr[:, pl.ds(pl.multiple_of(first - 128 * x, 128), KT)] for x in range(QT // 128)], axis=0)
        tile(QT * j, dp + 1, bias, lambda t: dp - t)
    for j in range(2):
        tile(KT + QT * j, PROMPT // KT + 1,
             lambda t: b_scr[pl.ds(QT * j, QT), pl.ds(pl.multiple_of(t * KT, KT), KT)], lambda t: t)

def attention_forward(info, q, k, v, rows_bias, row_start, heads):
    n, width = q.shape
    keys = k.shape[0]
    pair = lambda r: pl.BlockSpec((r, 128), lambda h, *_: (0, h // 2))
    whole = pl.BlockSpec((n, 128), lambda h, *_: (0, 0))
    scale2 = (width // heads) ** -0.5 * LOG2E
    return pl.pallas_call(
        functools.partial(fwd_kernel, scale2),
        grid_spec=pltpu.PrefetchScalarGridSpec(
            num_scalar_prefetch=1, grid=(heads,),
            in_specs=[pair(n), pair(keys), pair(keys),
                      pl.BlockSpec((1, 8, rows_bias.shape[2]), lambda h, *_: (h, 0, 0)),
                      pl.BlockSpec((KT, 128), lambda h, *_: (0, 0))],
            out_specs=[pair(n), whole],
            scratch_shapes=[pltpu.VMEM((128, rows_bias.shape[2]), F32), pltpu.VMEM((KT, PROMPT + KT), F32)]),
        out_shape=[jax.ShapeDtypeStruct((n, width), F32), jax.ShapeDtypeStruct((n, 128), F32)],
        compiler_params=pltpu.CompilerParams(vmem_limit_bytes=60 << 20),
        name="attention_forward",
    )(info, q, k, v, rows_bias, row_start)

def split3(x):
    hi = x.astype(BF16)
    rest = x - hi.astype(F32)
    mid = rest.astype(BF16)
    return hi, mid, (rest - mid.astype(F32)).astype(BF16)

def bwd_kernel(scale, info, q_ref, do_ref, o_ref, lse_ref, k_ref, v_ref, r_ref, st_ref,
               dq_ref, dk_ref, dv_ref, dd_ref,
               t_scr, b_scr, e_scr, db_scr, qa, da, ka, va, qt, dot_t, dkt, dvt):
    h = pl.program_id(0)
    dp = info[5]
    n, keys = q_ref.shape[0], k_ref.shape[0]
    half = h % 2
    build_bias(info, r_ref[0], st_ref, t_scr, b_scr)
    base = pl.multiple_of(64 * half, 64)
    other = 64 - 64 * half

    @pl.when(half == 0)
    def _():
        qt[...] = q_ref[...].T
        dot_t[...] = do_ref[...].T
        dq_ref[...] = jnp.zeros_like(dq_ref)

    lane_n = lax.broadcasted_iota(jnp.int32, (QT, 128), 1)
    own_n = lane_n // 64 == half
    def augment(i, _):
        rows = pl.ds(pl.multiple_of(i * QT, QT), QT)
        lse = jnp.sum(jnp.where(lane_n == h, lse_ref[rows, :], 0.0), axis=1, keepdims=True)
        parts = split3(-lse / (scale * LOG2E))
        aug = jnp.zeros((QT, 128), BF16)
        for x in range(3):
            aug = jnp.where(lane_n == other + x, jnp.broadcast_to(parts[x], (QT, 128)), aug)
        qa[rows, :] = jnp.where(own_n, q_ref[rows, :], aug)
        do = do_ref[rows, :]
        delta = jnp.sum(jnp.where(own_n, do.astype(F32) * o_ref[rows, :], 0.0), axis=1, keepdims=True)
        parts = split3(-delta)
        aug = jnp.zeros((QT, 128), BF16)
        for x in range(3):
            aug = jnp.where(lane_n == other + x, jnp.broadcast_to(parts[x], (QT, 128)), aug)
        da[rows, :] = jnp.where(own_n, do, aug)
        return 0
    lax.fori_loop(0, n // QT, augment, 0)
    lane_k = lax.broadcasted_iota(jnp.int32, (KT, 128), 1)
    ones = jnp.where((lane_k >= other) & (lane_k < other + 3), 1.0, 0.0).astype(BF16)
    own_k = lane_k // 64 == half
    def augment_keys(i, _):
        rows = pl.ds(pl.multiple_of(i * KT, KT), KT)
        ka[rows, :] = jnp.where(own_k, k_ref[rows, :], ones)
        va[rows, :] = jnp.where(own_k, v_ref[rows, :], ones)
        return 0
    lax.fori_loop(0, keys // KT, augment_keys, 0)
    head_rows = pl.ds(base, 64)
    dkt[head_rows, :] = jnp.zeros((64, keys), F32)
    dvt[head_rows, :] = jnp.zeros((64, keys), F32)
    e_scr[...] = jnp.zeros_like(e_scr)

    def tile(first, key_tiles, bias_of, grad_bias):
        rows = pl.ds(first, QT)
        q, do = qa[rows, :], da[rows, :]
        q_t, do_t = qt[head_rows, rows], dot_t[head_rows, rows]
        def step(t, dq):
            cols = pl.ds(pl.multiple_of(t * KT, KT), KT)
            kk = ka[cols, :]
            p = jnp.exp2(dot(q, kk, NT) * (scale * LOG2E) + bias_of(t))
            ds = p * dot(do, va[cols, :], NT)
            grad_bias(t, ds)
            low = ds.astype(BF16)
            dvt[head_rows, cols] += dot(do_t, p.astype(BF16))
            dkt[head_rows, cols] += dot(q_t, low)
            return dq + dot(low, kk)
        dq = lax.fori_loop(0, key_tiles, step, jnp.zeros((QT, 128), F32))
        dq_ref[rows, :] = jnp.where(own_n, dq * scale, dq_ref[rows, :].astype(F32)).astype(BF16)

    for j in range(2):
        shift = PROMPT - KT * dp - QT * j + RUN
        def part(t, x, shift=shift):
            return (slice(None), pl.ds(pl.multiple_of(t * KT + shift - 128 * x, 128), KT))
        def bias(t):
            return jnp.concatenate([t_scr[part(t, x)] for x in range(QT // 128)], axis=0)
        def add(t, ds):
            for x in range(QT // 128):
                e_scr[part(t, x)] += ds[128 * x:128 * x + 128, :]
        tile(QT * j, dp + 1, bias, add)
    for j in range(2):
        def where(t):
            return (pl.ds(QT * j, QT), pl.ds(pl.multiple_of(t * KT, KT), KT))
        def put(t, ds):
            db_scr[where(t)] = ds
        tile(KT + QT * j, PROMPT // KT + 1, lambda t: b_scr[where(t)], put)

    lane = lax.broadcasted_iota(jnp.int32, (ROWS, 128), 1)
    sub = lax.broadcasted_iota(jnp.int32, (ROWS, 128), 0)
    for s in range(4):
        start, end = info[s], info[s + 1]
        turn = start % 128
        def fold(g, _):
            at = pl.ds(pl.multiple_of(ROWS * g, ROWS), ROWS)
            first = start - turn + RUN - 128 * (g // (128 // ROWS))
            to = pl.ds(pl.multiple_of(ROWS * (g % (128 // ROWS)), ROWS), ROWS)
            mine = (sub + ROWS * g >= start) & (sub + ROWS * g < end)
            before = jnp.zeros((ROWS, 128), F32)
            for b in range(PROMPT // 128 + 1):
                if b < PROMPT // 128:
                    turned = pltpu.roll(jnp.where(mine, db_scr[at, 128 * b:128 * b + 128], 0.0), turn, 1)
                else:
                    turned = jnp.zeros((ROWS, 128), F32)
                e_scr[to, pl.ds(pl.multiple_of(first + 128 * b, 128), 128)] += jnp.where(lane >= turn, turned, before)
                before = turned
            return 0
        lax.fori_loop(start // ROWS, (end + ROWS - 1) // ROWS, fold, 0)
    for i in range(KT // 128):
        first = PROMPT + RUN - 128 * i
        e_scr[:, first:first + KT] += db_scr[128 * i:128 * i + 128, PROMPT:]
    width = r_ref.shape[2]
    acc = e_scr[0:8, :]
    for a in range(1, 16):
        acc = acc + pltpu.roll(e_scr[8 * a:8 * a + 8, :], width - 8 * a, 1)
    total = acc[0:1, :]
    for i in range(1, 8):
        total = total + pltpu.roll(acc, width - i, 1)[i:i + 1, :]
    dd_ref[0] = total

    @pl.when(half == 1)
    def _():
        dk_ref[...] = (dkt[...] * scale).T.astype(BF16)
        dv_ref[...] = dvt[...].T.astype(BF16)

def attention_backward(info, q, do, o32, lse, k, v, rows_bias, row_start, heads):
    n, width = q.shape
    keys = k.shape[0]
    wide = rows_bias.shape[2]
    pair = lambda r: pl.BlockSpec((r, 128), lambda h, *_: (0, h // 2))
    whole = pl.BlockSpec((n, 128), lambda h, *_: (0, 0))
    line = pl.BlockSpec((1, 1, wide), lambda h, *_: (h, 0, 0))
    scale = (width // heads) ** -0.5
    cols = PROMPT + KT
    return pl.pallas_call(
        functools.partial(bwd_kernel, scale),
        grid_spec=pltpu.PrefetchScalarGridSpec(
            num_scalar_prefetch=1, grid=(heads,),
            in_specs=[pair(n), pair(n), pair(n), whole, pair(keys), pair(keys),
                      pl.BlockSpec((1, 8, wide), lambda h, *_: (h, 0, 0)), pl.BlockSpec((KT, 128), lambda h, *_: (0, 0))],
            out_specs=[pair(n), pair(keys), pair(keys), line],
            scratch_shapes=[pltpu.VMEM((128, wide), F32), pltpu.VMEM((KT, cols), F32),
                            pltpu.VMEM((128, wide), F32), pltpu.VMEM((KT, cols), F32),
                            pltpu.VMEM((n, 128), BF16), pltpu.VMEM((n, 128), BF16),
                            pltpu.VMEM((keys, 128), BF16), pltpu.VMEM((keys, 128), BF16),
                            pltpu.VMEM((128, n), BF16), pltpu.VMEM((128, n), BF16),
                            pltpu.VMEM((128, keys), F32), pltpu.VMEM((128, keys), F32)]),
        out_shape=[jax.ShapeDtypeStruct((n, width), BF16), jax.ShapeDtypeStruct((keys, width), BF16),
                   jax.ShapeDtypeStruct((keys, width), BF16), jax.ShapeDtypeStruct((heads, 1, wide), F32)],
        compiler_params=pltpu.CompilerParams(vmem_limit_bytes=60 << 20),
        name="attention_backward",
    )(info, q, do, o32, lse, k, v, rows_bias, row_start)

def info_of(ids, dp):
    starts = jnp.sum((ids[None, :] < jnp.arange(5)[:, None]).astype(jnp.int32), axis=1)
    return jnp.concatenate([starts, jnp.reshape(dp, (1,)).astype(jnp.int32)])

def table_grad(dd, buckets):
    width = dd.shape[2]
    distance = PROMPT + RUN - jnp.arange(width)
    hot = ((bucket_of(distance)[:, None] == jnp.arange(buckets)[None, :]) & (distance >= 0)[:, None]).astype(F32)
    return jnp.dot(dd[:, 0, :], hot, precision=lax.Precision.HIGHEST)

def row_start_of(ids):
    starts = jnp.sum((ids[None, :] < ids[:, None]).astype(jnp.int32), axis=1)
    return jnp.broadcast_to(starts[:, None], (ids.shape[0], 128))


TN = (((0,), (0,)), ((), ()))
MOE_ROWS = 256
FF_TILE = 768


def expert_slots(ids, levels, expert, capacity):
    hits = ids == expert
    hit = jnp.any(hits, axis=2)
    level = jnp.sum(jnp.where(hits, levels, 0), axis=2)
    hot = hit[:, :, None] & (level[:, :, None] == jnp.arange(PRIO)[None, None, :])
    tokens = ids.shape[1]
    earlier = (jnp.arange(tokens)[:, None] > jnp.arange(tokens)[None, :]).astype(BF16)
    rank = jnp.einsum("ut,dtl->dul", earlier, hot.astype(BF16), preferred_element_type=F32).astype(jnp.int32)
    counts = jnp.sum(hot.astype(jnp.int32), axis=1)
    totals = jnp.sum(counts, axis=0)
    lower = jnp.cumsum(totals) - totals
    base = lower[None, :] + jnp.cumsum(counts, axis=0) - counts
    slot = jnp.sum(jnp.where(hot, base[:, None, :] + rank, 0), axis=2)
    kept = hit & (slot < capacity)
    rank = jnp.einsum("ut,dt->du", earlier, kept.astype(BF16), preferred_element_type=F32).astype(jnp.int32)
    place = jnp.where(kept, rank, -1)
    sizes = jnp.sum(kept.astype(jnp.int32), axis=1)
    padded = (sizes + 15) // 16 * 16
    ends = jnp.cumsum(padded)
    other = jnp.sum(jnp.where(hits, 0, ids), axis=2)
    return place, jnp.concatenate([ends - padded, sizes, ends[-1:]]).astype(jnp.int32), other


def pack_kernel(sources, info, place_ref, *refs):
    ins, outs = refs[:len(refs) // 2], refs[len(refs) // 2:]
    d = pl.program_id(0)

    @pl.when(d == 0)
    def _():
        for out in outs:
            out[...] = jnp.zeros_like(out)

    tokens = place_ref.shape[2]
    row = lax.broadcasted_iota(jnp.int32, (MOE_ROWS, tokens), 0)

    def chunk(j, _):
        pick = jnp.where(place_ref[0] == row + MOE_ROWS * j, 1.0, 0.0).astype(BF16)
        at = pl.ds(pl.multiple_of(info[d] + MOE_ROWS * j, 16), MOE_ROWS)
        for x, out in zip(ins, outs):
            out[at, :] = dot(pick, x[...]).astype(BF16)
        return 0
    lax.fori_loop(0, (info[sources + d] + MOE_ROWS - 1) // MOE_ROWS, chunk, 0)


def pack(info, place, arrays, room):
    sources, tokens = place.shape
    return pl.pallas_call(
        functools.partial(pack_kernel, sources),
        grid_spec=pltpu.PrefetchScalarGridSpec(
            num_scalar_prefetch=1, grid=(sources,),
            in_specs=[pl.BlockSpec((1, 1, tokens), lambda d, *_: (d, 0, 0))]
            + [pl.BlockSpec((tokens, x.shape[1]), lambda d, *_: (d, 0)) for x in arrays],
            out_specs=[pl.BlockSpec((room, x.shape[1]), lambda d, *_: (0, 0)) for x in arrays]),
        out_shape=[jax.ShapeDtypeStruct((room, x.shape[1]), BF16) for x in arrays],
        compiler_params=pltpu.CompilerParams(vmem_limit_bytes=40 << 20),
        name="pack_tokens",
    )(info, place[:, None, :], *arrays)


def unpack_kernel(sources, info, place_ref, *refs):
    ins, outs = refs[:len(refs) // 2], refs[len(refs) // 2:]
    d = pl.program_id(0)
    tokens = place_ref.shape[0]
    lane = lax.broadcasted_iota(jnp.int32, (tokens, 128), 1)
    for x, out in zip(ins, outs):
        def chunk(j, total):
            put = jnp.concatenate(
                [jnp.where(place_ref[...] == lane + (MOE_ROWS * j + 128 * b), 1.0, 0.0).astype(BF16)
                 for b in range(MOE_ROWS // 128)], axis=1)
            at = pl.ds(pl.multiple_of(info[d] + MOE_ROWS * j, 16), MOE_ROWS)
            return total + dot(put, x[at, :])
        total = lax.fori_loop(0, (info[sources + d] + MOE_ROWS - 1) // MOE_ROWS, chunk,
                              jnp.zeros((tokens, x.shape[1]), F32))
        out[...] = total.astype(out.dtype)


def unpack(info, place, arrays, dtypes):
    sources, tokens = place.shape
    spread = jnp.broadcast_to(place.reshape(-1, 1), (sources * tokens, 128))
    return pl.pallas_call(
        functools.partial(unpack_kernel, sources),
        grid_spec=pltpu.PrefetchScalarGridSpec(
            num_scalar_prefetch=1, grid=(sources,),
            in_specs=[pl.BlockSpec((tokens, 128), lambda d, *_: (d, 0))]
            + [pl.BlockSpec(x.shape, lambda d, *_: (0, 0)) for x in arrays],
            out_specs=[pl.BlockSpec((tokens, x.shape[1]), lambda d, *_: (d, 0)) for x in arrays]),
        out_shape=[jax.ShapeDtypeStruct((sources * tokens, x.shape[1]), t) for x, t in zip(arrays, dtypes)],
        compiler_params=pltpu.CompilerParams(vmem_limit_bytes=40 << 20),
        name="unpack_tokens",
    )(info, spread, *arrays)


def gelu_and_slope(v):
    c = math.sqrt(2.0 / math.pi)
    t = jnp.tanh(c * (v + 0.044715 * (v * v * v)))
    half = 0.5 * (1.0 + t)
    return v * half, half + 0.5 * v * (1.0 - t * t) * (c * (1.0 + 3 * 0.044715 * (v * v)))


def expert_kernel(sources, info, expert, x_ref, o_ref, c_ref, r_ref, wi_ref, wd_ref,
                  gi_ref, eo_ref, gg_ref, dwi_ref, dwd_ref, geo, gate, eo, gi, dwi, dwd):
    f = pl.program_id(0)
    last = pl.num_programs(0) - 1
    tiles = (info[2 * sources] + MOE_ROWS - 1) // MOE_ROWS
    lane = lax.broadcasted_iota(jnp.int32, (MOE_ROWS, 128), 1)

    def rows_of(i):
        return pl.ds(pl.multiple_of(i * MOE_ROWS, MOE_ROWS), MOE_ROWS)

    @pl.when(f == 0)
    def _():
        gi_ref[...] = jnp.zeros_like(gi_ref)
        eo_ref[...] = jnp.zeros_like(eo_ref)
        gg_ref[...] = jnp.zeros_like(gg_ref)

        def start(i, _):
            at = rows_of(i)
            logits = dot(x_ref[at, :], r_ref[...])
            mine = jnp.sum(jnp.where(lane == expert[0], logits, 0.0), axis=1, keepdims=True)
            other = jnp.sum(jnp.where(o_ref[at, :] > 0, logits, 0.0), axis=1, keepdims=True)
            top = jnp.maximum(mine, other)
            a, b = jnp.exp(mine - top), jnp.exp(other - top)
            g = a / (a + b)
            gate[at, :] = jnp.broadcast_to(g, (MOE_ROWS, 128))
            geo[at, :] = (c_ref[at, :].astype(F32) * g).astype(BF16)
            eo[at, :] = jnp.zeros((MOE_ROWS, eo.shape[1]), F32)
            gi[at, :] = jnp.zeros((MOE_ROWS, gi.shape[1]), F32)
            return 0
        lax.fori_loop(0, tiles, start, 0)

    dwi[...] = jnp.zeros_like(dwi)
    dwd[...] = jnp.zeros_like(dwd)

    def tile(i, _):
        at = rows_of(i)
        x, g = x_ref[at, :], geo[at, :]
        act, slope = gelu_and_slope(dot(x, wi_ref[...]))
        act = act.astype(BF16)
        eo[at, :] += dot(act, wd_ref[...])
        gh = (dot(g, wd_ref[...], NT) * slope).astype(BF16)
        gi[at, :] += dot(gh, wi_ref[...], NT)
        dwd[...] += dot(act, g, TN)
        dwi[...] += dot(x, gh, TN)
        return 0
    lax.fori_loop(0, tiles, tile, 0)
    dwi_ref[...] = dwi[...].astype(BF16)
    dwd_ref[...] = dwd[...].astype(BF16)

    @pl.when(f == last)
    def _():
        def finish(i, _):
            at = rows_of(i)
            out = eo[at, :].astype(BF16).astype(F32)
            gg = jnp.sum(out * c_ref[at, :].astype(F32), axis=1, keepdims=True)
            parts = split3(gg)
            spread = jnp.zeros((MOE_ROWS, 128), BF16)
            for n in range(3):
                spread = jnp.where(lane == n, jnp.broadcast_to(parts[n], (MOE_ROWS, 128)), spread)
            gg_ref[at, :] = spread
            eo_ref[at, :] = (out * gate[at, :1]).astype(BF16)
            gi_ref[at, :] = gi[at, :].astype(BF16)
            return 0
        lax.fori_loop(0, tiles, finish, 0)


def expert_layer(info, expert, x, other, cot, router, w_in, w_down, sources):
    room, width = x.shape
    hidden = w_in.shape[1]
    whole = lambda a: pl.BlockSpec(a.shape, lambda f, *_: (0, 0))
    fixed = lambda cols: pl.BlockSpec((room, cols), lambda f, *_: (0, 0))
    return pl.pallas_call(
        functools.partial(expert_kernel, sources),
        grid_spec=pltpu.PrefetchScalarGridSpec(
            num_scalar_prefetch=2, grid=(hidden // FF_TILE,),
            in_specs=[whole(x), whole(other), whole(cot), whole(router),
                      pl.BlockSpec((width, FF_TILE), lambda f, *_: (0, f)),
                      pl.BlockSpec((FF_TILE, width), lambda f, *_: (f, 0))],
            out_specs=[fixed(width), fixed(width), fixed(128),
                       pl.BlockSpec((width, FF_TILE), lambda f, *_: (0, f)),
                       pl.BlockSpec((FF_TILE, width), lambda f, *_: (f, 0))],
            scratch_shapes=[pltpu.VMEM((room, width), BF16), pltpu.VMEM((room, 128), F32),
                            pltpu.VMEM((room, width), F32), pltpu.VMEM((room, width), F32),
                            pltpu.VMEM((width, FF_TILE), F32), pltpu.VMEM((FF_TILE, width), F32)]),
        out_shape=[jax.ShapeDtypeStruct((room, width), BF16), jax.ShapeDtypeStruct((room, width), BF16),
                   jax.ShapeDtypeStruct((room, 128), BF16),
                   jax.ShapeDtypeStruct(w_in.shape, BF16), jax.ShapeDtypeStruct(w_down.shape, BF16)],
        compiler_params=pltpu.CompilerParams(vmem_limit_bytes=63 << 20),
        name="expert_layer",
    )(info, expert, x, other, cot, router, w_in, w_down)


def exchange_pairs(normed_ffn, middle, cotangent, expert_ids, priority, router, w_in, w_down):
    rows, width = normed_ffn.shape
    logits = jnp.dot(normed_ffn, router, preferred_element_type=jnp.float32)
    experts_total = router.shape[1]
    picks = expert_ids[:, :, None] == jnp.arange(experts_total)[None, None, :]
    chosen = jnp.sum(jnp.where(picks, logits[:, None, :], 0.0), axis=2)
    gates = jax.nn.softmax(chosen, axis=-1)
    top = expert_ids.shape[1]
    levels = PRIO
    local_experts = w_in.shape[0]
    capacity = rows * top // local_experts
    send = max(2, 2 * rows * top // experts_total)
    flat_expert = expert_ids.reshape(-1)
    code = priority.reshape(-1) * experts_total + flat_expert
    onehot = (code[:, None] == jnp.arange(levels * experts_total)[None, :]).astype(jnp.int32)
    rank = jnp.sum((jnp.cumsum(onehot, axis=0) - onehot) * onehot, axis=1)
    counts = jnp.sum(onehot, axis=0)
    every = lax.all_gather(counts[None, :], "expert", axis=0, tiled=True).reshape(
        -1, levels, experts_total
    )
    expert_index = lax.axis_index("expert")
    totals = jnp.sum(every, axis=0)
    lower = jnp.cumsum(totals, axis=0) - totals
    earlier_sources = jnp.cumsum(every, axis=0) - every
    mine_prefix = lax.dynamic_index_in_dim(earlier_sources, expert_index, 0, keepdims=False)
    base = (lower + mine_prefix).reshape(-1)
    slot = rank + jnp.sum(onehot * base[None, :], axis=1)
    kept = slot < capacity
    own_counts = counts.reshape(levels, experts_total)
    own_lower = (jnp.cumsum(own_counts, axis=0) - own_counts).reshape(-1)
    place = rank + jnp.sum(onehot * own_lower[None, :], axis=1)
    target = flat_expert * send + place
    first_mine = expert_index * local_experts
    counts_mine = lax.dynamic_slice_in_dim(every, first_mine, local_experts, 2)
    base_mine = lax.dynamic_slice_in_dim(
        lower[None] + earlier_sources, first_mine, local_experts, 2
    )
    band_end = jnp.cumsum(counts_mine, axis=1)
    band_start = band_end - counts_mine
    place_index = jnp.arange(send, dtype=jnp.int32)
    level = jnp.sum(
        (place_index[None, None, None, :] >= band_end[:, :, :, None]).astype(jnp.int32), axis=1
    )
    level_hot = level[:, None, :, :] == jnp.arange(levels)[None, :, None, None]
    start_of = jnp.sum(jnp.where(level_hot, band_start[:, :, :, None], 0), axis=1)
    base_of = jnp.sum(jnp.where(level_hot, base_mine[:, :, :, None], 0), axis=1)
    arrived_slot = base_of + place_index[None, None, :] - start_of
    usable = (level < levels) & (arrived_slot < capacity)
    landing = jnp.where(
        usable,
        jnp.arange(local_experts)[None, :, None] * capacity + arrived_slot,
        local_experts * capacity,
    ).reshape(-1)
    live = landing < local_experts * capacity
    safe = jnp.minimum(landing, local_experts * capacity - 1)
    pair_inputs = jnp.repeat(normed_ffn, top, axis=0)
    outgoing = (
        jnp.zeros((experts_total * send, width), jnp.bfloat16)
        .at[target]
        .set(pair_inputs)
        .reshape(experts_total, send, width)
    )
    arrived = lax.all_to_all(outgoing, "expert", split_axis=0, concat_axis=0, tiled=True)
    expert_inputs = (
        jnp.zeros((local_experts * capacity, width), jnp.bfloat16)
        .at[landing]
        .set(arrived.reshape(-1, width), mode="drop")
        .reshape(local_experts, capacity, width)
    )
    hidden = jnp.einsum("ecd,edf->ecf", expert_inputs, w_in, preferred_element_type=jnp.float32)
    activated = jax.nn.gelu(hidden).astype(jnp.bfloat16)
    expert_out = jnp.einsum(
        "ecf,efd->ecd", activated, w_down, preferred_element_type=jnp.float32
    ).astype(jnp.bfloat16)
    returning = jnp.where(
        live[:, None],
        jnp.take(expert_out.reshape(-1, width), safe, axis=0),
        jnp.zeros((), jnp.bfloat16),
    ).reshape(experts_total, send, width)
    returned = lax.all_to_all(returning, "expert", split_axis=0, concat_axis=0, tiled=True)
    pair_out = jnp.where(
        kept[:, None],
        jnp.take(returned.reshape(-1, width), target, axis=0).astype(jnp.float32),
        0.0,
    ).reshape(rows, top, width)
    mixed = jnp.sum(gates[:, :, None] * pair_out, axis=1)
    grad_out = cotangent.astype(jnp.float32)
    grad_gates = jnp.sum(grad_out[:, None, :] * pair_out, axis=2)
    pair_grads = (gates[:, :, None] * grad_out[:, None, :]).astype(jnp.bfloat16).reshape(-1, width)
    outgoing_grads = (
        jnp.zeros((experts_total * send, width), jnp.bfloat16)
        .at[target]
        .set(pair_grads)
        .reshape(experts_total, send, width)
    )
    arrived_grads = lax.all_to_all(
        outgoing_grads, "expert", split_axis=0, concat_axis=0, tiled=True
    )
    grad_expert_out = (
        jnp.zeros((local_experts * capacity, width), jnp.bfloat16)
        .at[landing]
        .set(arrived_grads.reshape(-1, width), mode="drop")
        .reshape(local_experts, capacity, width)
    )
    hidden_again = jnp.einsum(
        "ecd,edf->ecf", expert_inputs, w_in, preferred_element_type=jnp.float32
    )
    activated_again, gelu_back = jax.vjp(jax.nn.gelu, hidden_again)
    grad_activated = jnp.einsum(
        "ecd,efd->ecf", grad_expert_out, w_down, preferred_element_type=jnp.float32
    )
    grad_hidden = gelu_back(grad_activated)[0].astype(jnp.bfloat16)
    grad_w_down = jnp.einsum(
        "ecf,ecd->efd",
        activated_again.astype(jnp.bfloat16),
        grad_expert_out,
        preferred_element_type=jnp.float32,
    )
    grad_w_in = jnp.einsum(
        "ecd,ecf->edf", expert_inputs, grad_hidden, preferred_element_type=jnp.float32
    )
    grad_inputs = jnp.einsum(
        "ecf,edf->ecd", grad_hidden, w_in, preferred_element_type=jnp.float32
    ).astype(jnp.bfloat16)
    back_rows = jnp.where(
        live[:, None],
        jnp.take(grad_inputs.reshape(-1, width), safe, axis=0),
        jnp.zeros((), jnp.bfloat16),
    ).reshape(experts_total, send, width)
    came_back = lax.all_to_all(back_rows, "expert", split_axis=0, concat_axis=0, tiled=True)
    pair_back = jnp.where(
        kept[:, None],
        jnp.take(came_back.reshape(-1, width), target, axis=0).astype(jnp.float32),
        0.0,
    )
    grad_normed_ffn = jnp.sum(pair_back.reshape(rows, top, width), axis=1)
    grad_chosen = gates * (grad_gates - jnp.sum(gates * grad_gates, axis=-1, keepdims=True))
    grad_logits = jnp.sum(jnp.where(picks, grad_chosen[:, :, None], 0.0), axis=1).astype(
        jnp.bfloat16
    )
    grad_normed_ffn = grad_normed_ffn + jnp.dot(
        grad_logits, router.T, preferred_element_type=jnp.float32
    )
    expert_parts = (
        lax.psum_scatter(
            grad_w_in.astype(jnp.bfloat16), "dp", scatter_dimension=1, tiled=True
        ).astype(jnp.float32),
        lax.psum_scatter(
            grad_w_down.astype(jnp.bfloat16), "dp", scatter_dimension=1, tiled=True
        ).astype(jnp.float32),
    )
    return mixed, grad_logits, grad_normed_ffn, expert_parts


def gather_codes(expert_ids, priority):
    return lax.all_gather(expert_ids * PRIO + priority, "expert", axis=0)


def plan_tokens(codes, rows, top):
    expert = lax.axis_index("expert").astype(jnp.int32)
    place, info, other = expert_slots(codes // PRIO, codes % PRIO, expert, rows * top)
    other_hot = (other.reshape(-1, 1) == jnp.arange(128)[None, :]).astype(jnp.bfloat16)
    return place, info, other_hot


def exchange_tokens(normed_ffn, all_cotangents, plan, expert_ids, router, w_in, w_down):
    rows, width = normed_ffn.shape
    experts_total = router.shape[1]
    top = expert_ids.shape[1]
    expert = lax.axis_index("expert").astype(jnp.int32)
    place, info, other_hot = plan
    sources = place.shape[0]
    room = (rows * top + 16 * sources + 2 * MOE_ROWS - 1) // MOE_ROWS * MOE_ROWS
    sent, all_cotangents = lax.optimization_barrier((normed_ffn, all_cotangents))
    all_tokens = lax.all_gather(sent, "expert", axis=0, tiled=True)
    packed_cot, packed_other = pack(info, place, [all_cotangents, other_hot], room)
    (packed,) = pack(info, place, [all_tokens], room)
    wide_router = jnp.pad(router, ((0, 0), (0, 128 - experts_total)))
    grad_rows, mixed_rows, grad_gate, grad_w_in, grad_w_down = expert_layer(
        info, expert[None], packed, packed_other, packed_cot, wide_router, w_in[0], w_down[0], sources
    )
    grad_all, gate_all = unpack(info, place, [grad_rows, grad_gate], [jnp.bfloat16, jnp.float32])
    gate_all = jnp.sum(gate_all[:, :3], axis=1).reshape(sources, rows)
    gate_own = lax.all_to_all(gate_all, "expert", split_axis=0, concat_axis=0, tiled=True)
    grad_own = lax.psum_scatter(grad_all, "expert", scatter_dimension=0, tiled=True)
    (mixed_all,) = unpack(info, place, [mixed_rows], [jnp.bfloat16])
    mixed_all, grad_own = lax.optimization_barrier((mixed_all, grad_own))
    mixed = lax.psum_scatter(mixed_all, "expert", scatter_dimension=0, tiled=True)
    grad_w_in, grad_w_down, mixed = lax.optimization_barrier((grad_w_in, grad_w_down, mixed))
    expert_parts = (
        lax.psum_scatter(grad_w_in[None], "dp", scatter_dimension=1, tiled=True).astype(jnp.float32),
        lax.psum_scatter(grad_w_down[None], "dp", scatter_dimension=1, tiled=True).astype(jnp.float32),
    )
    mixed = mixed.astype(jnp.float32)
    logits = jnp.dot(normed_ffn, router, preferred_element_type=jnp.float32)
    picks = expert_ids[:, :, None] == jnp.arange(experts_total)[None, None, :]
    chosen = jnp.sum(jnp.where(picks, logits[:, None, :], 0.0), axis=2)
    gates = jax.nn.softmax(chosen, axis=-1)
    grad_gates = jnp.sum(jnp.where(picks, gate_own.T[:, None, :], 0.0), axis=2)
    grad_chosen = gates * (grad_gates - jnp.sum(gates * grad_gates, axis=-1, keepdims=True))
    grad_logits = jnp.sum(jnp.where(picks, grad_chosen[:, :, None], 0.0), axis=1).astype(
        jnp.bfloat16
    )
    grad_normed_ffn = grad_own.astype(jnp.float32) + jnp.dot(
        grad_logits, router.T, preferred_element_type=jnp.float32
    )
    return mixed, grad_logits, grad_normed_ffn, expert_parts


def per_device(
    tokens_in,
    cont_ids,
    expert_ids,
    priority,
    gain_attn,
    w_qkv,
    rel_table,
    w_out,
    gain_ffn,
    w_router,
    w_in,
    w_down,
    cotangent,
):
    rows, width = tokens_in.shape
    heads = rel_table.shape[1]
    dp_count = lax.axis_size("dp")
    dp_index = lax.axis_index("dp")
    prompt_rows = PROMPT // dp_count
    few_experts = lax.axis_size("expert") <= 16 and w_in.shape[0] == 1
    local_ids = cont_ids[0]
    info = info_of(local_ids, dp_index)
    row_start = row_start_of(local_ids)
    rows_bias = bias_rows(rel_table)
    if few_experts:
        codes = gather_codes(expert_ids, priority)
    whole_qkv = lax.all_gather(w_qkv, ("dp", "expert"), axis=0, tiled=True)
    if few_experts:
        plan = plan_tokens(codes, rows, expert_ids.shape[1])
        whole_qkv, rows_bias, plan = lax.optimization_barrier((whole_qkv, rows_bias, plan))
    inputs = tokens_in.astype(jnp.float32)
    normed_attn = normed(inputs, gain_attn).astype(jnp.bfloat16)
    projected = jnp.dot(normed_attn, whole_qkv, preferred_element_type=jnp.float32).astype(
        jnp.bfloat16
    )
    query = projected[:, :width]
    own_keys = projected[:, width : 2 * width]
    own_values = projected[:, 2 * width :]
    prompt_keys, prompt_values = prompt_gather(own_keys[:prompt_rows], own_values[:prompt_rows])
    experts_total = w_router.shape[1]
    late = jnp.concatenate([w_out, jnp.pad(w_router, ((0, 0), (0, 128 - experts_total)))], axis=1)
    late, late_cotangent, prompt_keys, prompt_values = lax.optimization_barrier(
        (late, cotangent, prompt_keys, prompt_values)
    )
    late = lax.all_gather(late, ("dp", "expert"), axis=0, tiled=True)
    whole_out, whole_router = late[:, :width], late[:, width : width + experts_total]
    if few_experts:
        late_cotangent, _ = lax.optimization_barrier((late_cotangent, late))
        all_cotangents = lax.all_gather(late_cotangent, "expert", axis=0, tiled=True)
    all_keys = jnp.concatenate([prompt_keys, own_keys[prompt_rows:]], axis=0)
    all_values = jnp.concatenate([prompt_values, own_values[prompt_rows:]], axis=0)
    exact, log_total = attention_forward(
        info, query, all_keys, all_values, rows_bias, row_start, heads
    )
    attended = exact.astype(jnp.bfloat16)
    middle = inputs + jnp.dot(attended, whole_out, preferred_element_type=jnp.float32)
    normed_ffn = normed(middle, gain_ffn).astype(jnp.bfloat16)
    if few_experts:
        mixed, grad_logits, grad_normed_ffn, expert_parts = exchange_tokens(
            normed_ffn, all_cotangents, plan, expert_ids, whole_router, w_in, w_down
        )
    else:
        mixed, grad_logits, grad_normed_ffn, expert_parts = exchange_pairs(
            normed_ffn, middle, cotangent, expert_ids, priority, whole_router, w_in, w_down
        )
    output = (middle + mixed).astype(jnp.bfloat16)
    grad_out = cotangent.astype(jnp.float32)
    grad_router = jnp.dot(normed_ffn.T, grad_logits, preferred_element_type=jnp.float32)
    _, ffn_norm_back = jax.vjp(normed, middle, gain_ffn)
    grad_middle_part, grad_gain_ffn = ffn_norm_back(grad_normed_ffn)
    grad_middle = grad_out + grad_middle_part
    grad_branch = grad_middle.astype(jnp.bfloat16)
    grad_out_weight = jnp.dot(attended.T, grad_branch, preferred_element_type=jnp.float32)
    grad_attended = jnp.dot(
        grad_branch, whole_out.T, preferred_element_type=jnp.float32
    ).astype(jnp.bfloat16)
    grad_query, grad_keys, grad_values, grad_lines = attention_backward(
        info, query, grad_attended, exact, log_total, all_keys, all_values, rows_bias, row_start, heads
    )
    grad_table = table_grad(grad_lines, rel_table.shape[0])
    prompt_grads = lax.psum_scatter(
        jnp.concatenate([grad_keys[:PROMPT], grad_values[:PROMPT]], axis=1),
        "dp", scatter_dimension=0, tiled=True,
    )
    grad_projected = jnp.concatenate(
        [
            grad_query,
            jnp.concatenate(
                [prompt_grads, jnp.concatenate([grad_keys[PROMPT:], grad_values[PROMPT:]], axis=1)], axis=0
            ),
        ],
        axis=1,
    )
    grad_normed_attn = jnp.dot(grad_projected, whole_qkv.T, preferred_element_type=jnp.float32)
    grad_qkv = jnp.dot(normed_attn.T, grad_projected, preferred_element_type=jnp.float32)
    _, attn_norm_back = jax.vjp(normed, inputs, gain_attn)
    grad_inputs_part, grad_gain_attn = attn_norm_back(grad_normed_attn)
    grad_tokens = grad_middle + grad_inputs_part
    dense = lax.psum_scatter(
        jnp.concatenate([grad_qkv, grad_out_weight], axis=1), ("dp", "expert"), scatter_dimension=0, tiled=True
    )
    own_router = lax.psum_scatter(grad_router, ("dp", "expert"), scatter_dimension=0, tiled=True)
    small_parts = lax.psum((grad_gain_attn, grad_gain_ffn, grad_table.T), ("dp", "expert"))
    return (
        output,
        grad_tokens,
        small_parts[0],
        dense[:, : 3 * width],
        small_parts[2],
        dense[:, 3 * width :],
        small_parts[1],
        own_router,
        expert_parts[0],
        expert_parts[1],
    )


def solution(mesh):
    return jax.shard_map(
        per_device,
        mesh=mesh,
        in_specs=(
            P(("dp", "expert"), None),
            P(("dp", "expert"), None),
            P(("dp", "expert"), None),
            P(("dp", "expert"), None),
            P(),
            P(("dp", "expert"), None),
            P(),
            P(("dp", "expert"), None),
            P(),
            P(("dp", "expert"), None),
            P("expert", None, None),
            P("expert", None, None),
            P(("dp", "expert"), None),
        ),
        out_specs=(
            P(("dp", "expert"), None),
            P(("dp", "expert"), None),
            P(),
            P(("dp", "expert"), None),
            P(),
            P(("dp", "expert"), None),
            P(),
            P(("dp", "expert"), None),
            P("expert", "dp", None),
            P("expert", "dp", None),
        ),
        check_vma=False,
    )
```

```python
import functools
import math
import jax
import jax.numpy as jnp
from jax import lax
from jax.experimental import pallas as pl
from jax.experimental.pallas import tpu as pltpu
from jax.sharding import PartitionSpec as P

PRIO = 4
PROMPT = 2048


BORDERS = (16, 24, 32, 48, 64, 96, 128, 192, 256, 384, 512, 768, 1024, 1536, 2048)
EPSILON = 1e-06
MASKED = -1e30


def bucket_of(distance):
    distance = jnp.maximum(distance, 0)
    counted = jnp.minimum(distance, 15)
    for border in BORDERS:
        counted = counted + (distance >= border).astype(jnp.int32)
    return counted


def normed(values, gain):
    return values * lax.rsqrt(jnp.mean(values * values, axis=-1, keepdims=True) + EPSILON) * gain


def pairs_together(w_qkv):
    width = w_qkv.shape[1] // 3
    rows = w_qkv.shape[0]
    keys_values = w_qkv[:, width:].reshape(rows, 2, width // 128, 128).swapaxes(1, 2)
    return jnp.concatenate([w_qkv[:, :width], keys_values.reshape(rows, 2 * width)], axis=1)


def pairs_apart(grad):
    width = grad.shape[1] // 3
    rows = grad.shape[0]
    keys_values = grad[:, width:].reshape(rows, width // 128, 2, 128).swapaxes(1, 2)
    return jnp.concatenate([grad[:, :width], keys_values.reshape(rows, 2 * width)], axis=1)


LOG2E = math.log2(math.e)
F32, BF16 = jnp.float32, jnp.bfloat16
QT = 256
KT = 512
RUN = 256
PARTS = 2
ROWS = 32
NT = (((1,), (1,)), ((), ()))
NN = (((1,), (0,)), ((), ()))

def dot(a, b, dims=NN):
    return lax.dot_general(a, b, dims, preferred_element_type=F32)

def bias_rows(rel_table):
    width = PROMPT + 512 + RUN
    distance = PROMPT + RUN - jnp.arange(width)[None, :] + jnp.arange(8)[:, None]
    bucket = bucket_of(distance)
    table = rel_table.T[:, None, None, :] * LOG2E
    hot = (bucket[..., None] == jnp.arange(rel_table.shape[0])).astype(F32)
    rows = jnp.sum(hot[None] * table, axis=-1)
    return jnp.where(distance[None] >= 0, rows, MASKED)

def build_bias(info, base, row_start, t_scr, b_scr):
    width = base.shape[-1]
    for a in range(16):
        t_scr[8 * a:8 * a + 8, :] = pltpu.roll(base, 8 * a, 1) if a else base
    lane = lax.broadcasted_iota(jnp.int32, (ROWS, 128), 1)
    sub = lax.broadcasted_iota(jnp.int32, (ROWS, 128), 0)
    for s in range(4):
        start, end = info[s], info[s + 1]
        turn = start % 128
        left = (128 - turn) % 128
        here = (lane < left) | (left == 0)
        def place(g, _):
            at = pl.ds(pl.multiple_of(ROWS * g, ROWS), ROWS)
            first = start - turn + RUN - 128 * (g // (128 // ROWS))
            of = pl.ds(pl.multiple_of(ROWS * (g % (128 // ROWS)), ROWS), ROWS)
            mine = sub + ROWS * g >= start
            turned = None
            for b in range(PROMPT // 128 + 1):
                after = pltpu.roll(t_scr[of, pl.ds(pl.multiple_of(first + 128 * b, 128), 128)], left, 1)
                if b:
                    cols = slice(128 * b - 128, 128 * b)
                    b_scr[at, cols] = jnp.where(mine, jnp.where(here, turned, after), b_scr[at, cols])
                turned = after
            return 0
        lax.fori_loop(start // ROWS, (end + ROWS - 1) // ROWS, place, 0)
    lane = lax.broadcasted_iota(jnp.int32, (128, 128), 1)
    for i in range(KT // 128):
        rows = slice(128 * i, 128 * i + 128)
        own = row_start[rows, :]
        for b in range(KT // 128):
            first = PROMPT + RUN - 128 * i + 128 * b
            b_scr[rows, PROMPT + 128 * b:PROMPT + 128 * b + 128] = jnp.where(
                lane + 128 * b >= own, t_scr[:, first:first + 128], MASKED)

def own_lanes(h, rows):
    lane = lax.broadcasted_iota(jnp.int32, (rows, 128), 1)
    return lane // 64 == h % 2

def fwd_kernel(scale2, info, q_ref, k_ref, v_ref, r_ref, st_ref, o_ref, lse_ref, t_scr, b_scr):
    h = pl.program_id(0)
    dp = info[5]
    build_bias(info, r_ref[0], st_ref, t_scr, b_scr)
    own = own_lanes(h, QT)
    head_lane = lax.broadcasted_iota(jnp.int32, (QT, 128), 1) == h

    def tile(first, key_tiles, bias_of, block):
        rows = pl.ds(first, QT)
        q = jnp.where(own, q_ref[rows, :], jnp.zeros((), BF16))
        def step(t, carry):
            m, l, acc = carry
            cols = pl.ds(pl.multiple_of(block(t) * KT, KT), KT)
            s = dot(q, k_ref[cols, :], NT) * scale2 + bias_of(t)
            new = jnp.maximum(m, jnp.max(s, axis=1, keepdims=True))
            keep = jnp.exp2(m - new)
            p = jnp.exp2(s - new[:, :1])
            part = p[:, :128]
            for c in range(1, KT // 128):
                part = part + p[:, 128 * c:128 * (c + 1)]
            return new, l * keep + part, acc * keep + dot(p.astype(BF16), v_ref[cols, :])
        zero = jnp.zeros((QT, 128), F32)
        m, l, acc = lax.fori_loop(0, key_tiles, step, (jnp.full((QT, 128), MASKED, F32), zero, zero))
        l = jnp.sum(l, axis=1, keepdims=True)
        o_ref[rows, :] = jnp.where(own, acc / l, o_ref[rows, :])
        lse_ref[rows, :] = jnp.where(head_lane, m + jnp.log2(l), lse_ref[rows, :])

    for j in range(2):
        shift = PROMPT - KT * dp - QT * j + RUN
        def bias(t, shift=shift):
            first = (dp - t) * KT + shift
            return jnp.concatenate([t_scr[:, pl.ds(pl.multiple_of(first - 128 * x, 128), KT)] for x in range(QT // 128)], axis=0)
        tile(QT * j, dp + 1, bias, lambda t: dp - t)
    for j in range(2):
        tile(KT + QT * j, PROMPT // KT + 1,
             lambda t: b_scr[pl.ds(QT * j, QT), pl.ds(pl.multiple_of(t * KT, KT), KT)], lambda t: t)

def attention_forward(info, projected, keys_values, rows_bias, row_start, part):
    n = projected.shape[0]
    keys, columns = keys_values.shape
    heads = columns // 128
    head_size = 64
    scale2 = head_size ** -0.5 * LOG2E
    first = part * heads // 2
    return pl.pallas_call(
        functools.partial(fwd_kernel, scale2),
        grid_spec=pltpu.PrefetchScalarGridSpec(
            num_scalar_prefetch=1, grid=(heads,),
            in_specs=[pl.BlockSpec((n, 128), lambda h, *_: (0, first + h // 2)),
                      pl.BlockSpec((keys, 128), lambda h, *_: (0, h // 2 * 2)),
                      pl.BlockSpec((keys, 128), lambda h, *_: (0, h // 2 * 2 + 1)),
                      pl.BlockSpec((1, 8, rows_bias.shape[2]), lambda h, *_: (2 * first + h, 0, 0)),
                      pl.BlockSpec((KT, 128), lambda h, *_: (0, 0))],
            out_specs=[pl.BlockSpec((n, 128), lambda h, *_: (0, h // 2)),
                       pl.BlockSpec((n, 128), lambda h, *_: (0, 0))],
            scratch_shapes=[pltpu.VMEM((128, rows_bias.shape[2]), F32), pltpu.VMEM((KT, PROMPT + KT), F32)]),
        out_shape=[jax.ShapeDtypeStruct((n, heads * 64), F32), jax.ShapeDtypeStruct((n, 128), F32)],
        compiler_params=pltpu.CompilerParams(vmem_limit_bytes=60 << 20),
        cost_estimate=pl.CostEstimate(flops=heads * n * keys * 128 * 4, bytes_accessed=n * keys * 4, transcendentals=heads * n * keys),
        name="attention_forward",
    )(info, projected, keys_values, keys_values, rows_bias, row_start)

def split3(x):
    hi = x.astype(BF16)
    rest = x - hi.astype(F32)
    mid = rest.astype(BF16)
    return hi, mid, (rest - mid.astype(F32)).astype(BF16)

def bwd_kernel(scale, info, q_ref, do_ref, o_ref, lse_ref, k_ref, v_ref, r_ref, st_ref,
               dq_ref, dkv_ref, dd_ref,
               t_scr, b_scr, e_scr, db_scr, qa, da, ka, va, qt, dot_t, dkt, dvt):
    h = pl.program_id(0)
    dp = info[5]
    n, keys = q_ref.shape[0], k_ref.shape[0]
    half = h % 2
    build_bias(info, r_ref[0], st_ref, t_scr, b_scr)
    base = pl.multiple_of(64 * half, 64)
    other = 64 - 64 * half

    @pl.when(half == 0)
    def _():
        qt[...] = q_ref[...].T
        dot_t[...] = do_ref[...].T
        dq_ref[...] = jnp.zeros_like(dq_ref)

    lane_n = lax.broadcasted_iota(jnp.int32, (QT, 128), 1)
    own_n = lane_n // 64 == half
    def augment(i, _):
        rows = pl.ds(pl.multiple_of(i * QT, QT), QT)
        lse = jnp.sum(jnp.where(lane_n == h, lse_ref[rows, :], 0.0), axis=1, keepdims=True)
        parts = split3(-lse / (scale * LOG2E))
        aug = jnp.zeros((QT, 128), BF16)
        for x in range(3):
            aug = jnp.where(lane_n == other + x, jnp.broadcast_to(parts[x], (QT, 128)), aug)
        qa[rows, :] = jnp.where(own_n, q_ref[rows, :], aug)
        do = do_ref[rows, :]
        delta = jnp.sum(jnp.where(own_n, do.astype(F32) * o_ref[rows, :], 0.0), axis=1, keepdims=True)
        parts = split3(-delta)
        aug = jnp.zeros((QT, 128), BF16)
        for x in range(3):
            aug = jnp.where(lane_n == other + x, jnp.broadcast_to(parts[x], (QT, 128)), aug)
        da[rows, :] = jnp.where(own_n, do, aug)
        return 0
    lax.fori_loop(0, n // QT, augment, 0)
    lane_k = lax.broadcasted_iota(jnp.int32, (KT, 128), 1)
    ones = jnp.where((lane_k >= other) & (lane_k < other + 3), 1.0, 0.0).astype(BF16)
    own_k = lane_k // 64 == half
    def augment_keys(i, _):
        rows = pl.ds(pl.multiple_of(i * KT, KT), KT)
        ka[rows, :] = jnp.where(own_k, k_ref[rows, :], ones)
        va[rows, :] = jnp.where(own_k, v_ref[rows, :], ones)
        return 0
    lax.fori_loop(0, keys // KT, augment_keys, 0)
    head_rows = pl.ds(base, 64)
    dkt[head_rows, :] = jnp.zeros((64, keys), F32)
    dvt[head_rows, :] = jnp.zeros((64, keys), F32)
    e_scr[...] = jnp.zeros_like(e_scr)

    def tile(first, key_tiles, bias_of, grad_bias):
        rows = pl.ds(first, QT)
        q, do = qa[rows, :], da[rows, :]
        q_t, do_t = qt[head_rows, rows], dot_t[head_rows, rows]
        def step(t, dq):
            cols = pl.ds(pl.multiple_of(t * KT, KT), KT)
            kk = ka[cols, :]
            p = jnp.exp2(dot(q, kk, NT) * (scale * LOG2E) + bias_of(t))
            ds = p * dot(do, va[cols, :], NT)
            grad_bias(t, ds)
            low = ds.astype(BF16)
            dvt[head_rows, cols] += dot(do_t, p.astype(BF16))
            dkt[head_rows, cols] += dot(q_t, low)
            return dq + dot(low, kk)
        dq = lax.fori_loop(0, key_tiles, step, jnp.zeros((QT, 128), F32))
        dq_ref[rows, :] = jnp.where(own_n, dq * scale, dq_ref[rows, :].astype(F32)).astype(BF16)

    for j in range(2):
        shift = PROMPT - KT * dp - QT * j + RUN
        def part(t, x, shift=shift):
            return (slice(None), pl.ds(pl.multiple_of(t * KT + shift - 128 * x, 128), KT))
        def bias(t):
            return jnp.concatenate([t_scr[part(t, x)] for x in range(QT // 128)], axis=0)
        def add(t, ds):
            for x in range(QT // 128):
                e_scr[part(t, x)] += ds[128 * x:128 * x + 128, :]
        tile(QT * j, dp + 1, bias, add)
    for j in range(2):
        def where(t):
            return (pl.ds(QT * j, QT), pl.ds(pl.multiple_of(t * KT, KT), KT))
        def put(t, ds):
            db_scr[where(t)] = ds
        tile(KT + QT * j, PROMPT // KT + 1, lambda t: b_scr[where(t)], put)

    lane = lax.broadcasted_iota(jnp.int32, (ROWS, 128), 1)
    sub = lax.broadcasted_iota(jnp.int32, (ROWS, 128), 0)
    for s in range(4):
        start, end = info[s], info[s + 1]
        turn = start % 128
        def fold(g, _):
            at = pl.ds(pl.multiple_of(ROWS * g, ROWS), ROWS)
            first = start - turn + RUN - 128 * (g // (128 // ROWS))
            to = pl.ds(pl.multiple_of(ROWS * (g % (128 // ROWS)), ROWS), ROWS)
            mine = (sub + ROWS * g >= start) & (sub + ROWS * g < end)
            before = jnp.zeros((ROWS, 128), F32)
            for b in range(PROMPT // 128 + 1):
                if b < PROMPT // 128:
                    turned = pltpu.roll(jnp.where(mine, db_scr[at, 128 * b:128 * b + 128], 0.0), turn, 1)
                else:
                    turned = jnp.zeros((ROWS, 128), F32)
                e_scr[to, pl.ds(pl.multiple_of(first + 128 * b, 128), 128)] += jnp.where(lane >= turn, turned, before)
                before = turned
            return 0
        lax.fori_loop(start // ROWS, (end + ROWS - 1) // ROWS, fold, 0)
    for i in range(KT // 128):
        first = PROMPT + RUN - 128 * i
        e_scr[:, first:first + KT] += db_scr[128 * i:128 * i + 128, PROMPT:]
    width = r_ref.shape[2]
    acc = e_scr[0:8, :]
    for a in range(1, 16):
        acc = acc + pltpu.roll(e_scr[8 * a:8 * a + 8, :], width - 8 * a, 1)
    total = acc[0:1, :]
    for i in range(1, 8):
        total = total + pltpu.roll(acc, width - i, 1)[i:i + 1, :]
    dd_ref[0] = total

    @pl.when(half == 1)
    def _():
        dkv_ref[:, :128] = (dkt[...] * scale).T.astype(BF16)
        dkv_ref[:, 128:] = dvt[...].T.astype(BF16)

def attention_backward(info, projected, do, o32, lse, keys_values, rows_bias, row_start, part):
    n = projected.shape[0]
    keys, columns = keys_values.shape
    heads = columns // 128
    wide = rows_bias.shape[2]
    first = part * heads // 2
    own = pl.BlockSpec((n, 128), lambda h, *_: (0, h // 2))
    shifted = pl.BlockSpec((n, 128), lambda h, *_: (0, first + h // 2))
    cols = PROMPT + KT
    return pl.pallas_call(
        functools.partial(bwd_kernel, 64 ** -0.5),
        grid_spec=pltpu.PrefetchScalarGridSpec(
            num_scalar_prefetch=1, grid=(heads,),
            in_specs=[shifted, shifted, own, pl.BlockSpec((n, 128), lambda h, *_: (0, 0)),
                      pl.BlockSpec((keys, 128), lambda h, *_: (0, h // 2 * 2)),
                      pl.BlockSpec((keys, 128), lambda h, *_: (0, h // 2 * 2 + 1)),
                      pl.BlockSpec((1, 8, wide), lambda h, *_: (2 * first + h, 0, 0)),
                      pl.BlockSpec((KT, 128), lambda h, *_: (0, 0))],
            out_specs=[own, pl.BlockSpec((keys, 256), lambda h, *_: (0, h // 2)),
                       pl.BlockSpec((1, 1, wide), lambda h, *_: (h, 0, 0))],
            scratch_shapes=[pltpu.VMEM((128, wide), F32), pltpu.VMEM((KT, cols), F32),
                            pltpu.VMEM((128, wide), F32), pltpu.VMEM((KT, cols), F32),
                            pltpu.VMEM((n, 128), BF16), pltpu.VMEM((n, 128), BF16),
                            pltpu.VMEM((keys, 128), BF16), pltpu.VMEM((keys, 128), BF16),
                            pltpu.VMEM((128, n), BF16), pltpu.VMEM((128, n), BF16),
                            pltpu.VMEM((128, keys), F32), pltpu.VMEM((128, keys), F32)]),
        out_shape=[jax.ShapeDtypeStruct((n, heads * 64), BF16), jax.ShapeDtypeStruct((keys, columns), BF16),
                   jax.ShapeDtypeStruct((heads, 1, wide), F32)],
        compiler_params=pltpu.CompilerParams(vmem_limit_bytes=60 << 20),
        cost_estimate=pl.CostEstimate(flops=heads * n * keys * 128 * 10, bytes_accessed=n * keys * 4, transcendentals=heads * n * keys),
        name="attention_backward",
    )(info, projected, do, o32, lse, keys_values, keys_values, rows_bias, row_start)

def info_of(ids, dp):
    starts = jnp.sum((ids[None, :] < jnp.arange(5)[:, None]).astype(jnp.int32), axis=1)
    return jnp.concatenate([starts, jnp.reshape(dp, (1,)).astype(jnp.int32)])

def table_grad(dd, buckets):
    width = dd.shape[2]
    distance = PROMPT + RUN - jnp.arange(width)
    hot = ((bucket_of(distance)[:, None] == jnp.arange(buckets)[None, :]) & (distance >= 0)[:, None]).astype(F32)
    return jnp.dot(dd[:, 0, :], hot, precision=lax.Precision.HIGHEST)

def row_start_of(ids):
    starts = jnp.sum((ids[None, :] < ids[:, None]).astype(jnp.int32), axis=1)
    return jnp.broadcast_to(starts[:, None], (ids.shape[0], 128))


TN = (((0,), (0,)), ((), ()))
MOE_ROWS = 256
FF_TILE = 768


def expert_slots(ids, levels, expert, capacity):
    hits = ids == expert
    hit = jnp.any(hits, axis=2)
    level = jnp.sum(jnp.where(hits, levels, 0), axis=2)
    hot = hit[:, :, None] & (level[:, :, None] == jnp.arange(PRIO)[None, None, :])
    tokens = ids.shape[1]
    earlier = (jnp.arange(tokens)[:, None] > jnp.arange(tokens)[None, :]).astype(BF16)
    rank = jnp.einsum("ut,dtl->dul", earlier, hot.astype(BF16), preferred_element_type=F32).astype(jnp.int32)
    counts = jnp.sum(hot.astype(jnp.int32), axis=1)
    totals = jnp.sum(counts, axis=0)
    lower = jnp.cumsum(totals) - totals
    base = lower[None, :] + jnp.cumsum(counts, axis=0) - counts
    slot = jnp.sum(jnp.where(hot, base[:, None, :] + rank, 0), axis=2)
    kept = hit & (slot < capacity)
    rank = jnp.einsum("ut,dt->du", earlier, kept.astype(BF16), preferred_element_type=F32).astype(jnp.int32)
    place = jnp.where(kept, rank, -1)
    sizes = jnp.sum(kept.astype(jnp.int32), axis=1)
    padded = (sizes + 15) // 16 * 16
    ends = jnp.cumsum(padded)
    other = jnp.sum(jnp.where(hits, 0, ids), axis=2)
    return place, jnp.concatenate([ends - padded, sizes, ends[-1:]]).astype(jnp.int32), other


def pack_kernel(sources, info, place_ref, *refs):
    ins, outs = refs[:len(refs) // 2], refs[len(refs) // 2:]
    d = pl.program_id(0)

    @pl.when(d == 0)
    def _():
        for out in outs:
            out[...] = jnp.zeros_like(out)

    tokens = place_ref.shape[2]
    row = lax.broadcasted_iota(jnp.int32, (MOE_ROWS, tokens), 0)

    def chunk(j, _):
        pick = jnp.where(place_ref[0] == row + MOE_ROWS * j, 1.0, 0.0).astype(BF16)
        at = pl.ds(pl.multiple_of(info[d] + MOE_ROWS * j, 16), MOE_ROWS)
        for x, out in zip(ins, outs):
            out[at, :] = dot(pick, x[...]).astype(BF16)
        return 0
    lax.fori_loop(0, (info[sources + d] + MOE_ROWS - 1) // MOE_ROWS, chunk, 0)


def pack(info, place, arrays, room):
    sources, tokens = place.shape
    return pl.pallas_call(
        functools.partial(pack_kernel, sources),
        grid_spec=pltpu.PrefetchScalarGridSpec(
            num_scalar_prefetch=1, grid=(sources,),
            in_specs=[pl.BlockSpec((1, 1, tokens), lambda d, *_: (d, 0, 0))]
            + [pl.BlockSpec((tokens, x.shape[1]), lambda d, *_: (d, 0)) for x in arrays],
            out_specs=[pl.BlockSpec((room, x.shape[1]), lambda d, *_: (0, 0)) for x in arrays]),
        out_shape=[jax.ShapeDtypeStruct((room, x.shape[1]), BF16) for x in arrays],
        compiler_params=pltpu.CompilerParams(vmem_limit_bytes=40 << 20),
        name="pack_tokens",
    )(info, place[:, None, :], *arrays)


def unpack_kernel(sources, info, place_ref, *refs):
    ins, outs = refs[:len(refs) // 2], refs[len(refs) // 2:]
    d = pl.program_id(0)
    tokens = place_ref.shape[0]
    lane = lax.broadcasted_iota(jnp.int32, (tokens, 128), 1)
    for x, out in zip(ins, outs):
        def chunk(j, total):
            put = jnp.concatenate(
                [jnp.where(place_ref[...] == lane + (MOE_ROWS * j + 128 * b), 1.0, 0.0).astype(BF16)
                 for b in range(MOE_ROWS // 128)], axis=1)
            at = pl.ds(pl.multiple_of(info[d] + MOE_ROWS * j, 16), MOE_ROWS)
            return total + dot(put, x[at, :])
        total = lax.fori_loop(0, (info[sources + d] + MOE_ROWS - 1) // MOE_ROWS, chunk,
                              jnp.zeros((tokens, x.shape[1]), F32))
        out[...] = total.astype(out.dtype)


def unpack(info, place, arrays, dtypes):
    sources, tokens = place.shape
    spread = jnp.broadcast_to(place.reshape(-1, 1), (sources * tokens, 128))
    return pl.pallas_call(
        functools.partial(unpack_kernel, sources),
        grid_spec=pltpu.PrefetchScalarGridSpec(
            num_scalar_prefetch=1, grid=(sources,),
            in_specs=[pl.BlockSpec((tokens, 128), lambda d, *_: (d, 0))]
            + [pl.BlockSpec(x.shape, lambda d, *_: (0, 0)) for x in arrays],
            out_specs=[pl.BlockSpec((tokens, x.shape[1]), lambda d, *_: (d, 0)) for x in arrays]),
        out_shape=[jax.ShapeDtypeStruct((sources * tokens, x.shape[1]), t) for x, t in zip(arrays, dtypes)],
        compiler_params=pltpu.CompilerParams(vmem_limit_bytes=40 << 20),
        name="unpack_tokens",
    )(info, spread, *arrays)


def collect_kernel(place_ref, x_ref, out_ref):
    tokens = place_ref.shape[0]
    lane = lax.broadcasted_iota(jnp.int32, (tokens, 128), 1)
    put = jnp.concatenate(
        [jnp.where(place_ref[...] == lane + 128 * b, 1.0, 0.0).astype(BF16) for b in range(x_ref.shape[0] // 128)],
        axis=1)
    total = dot(put, x_ref[...])

    @pl.when(pl.program_id(0) == 0)
    def _():
        out_ref[...] = total

    @pl.when(pl.program_id(0) > 0)
    def _():
        out_ref[...] += total


def collect(place, returned, send):
    experts, tokens = place.shape
    width = returned.shape[1]
    spread = jnp.broadcast_to(place.reshape(-1, 1), (experts * tokens, 128))
    return pl.pallas_call(
        collect_kernel,
        grid=(experts,),
        in_specs=[pl.BlockSpec((tokens, 128), lambda e: (e, 0)), pl.BlockSpec((send, width), lambda e: (e, 0))],
        out_specs=pl.BlockSpec((tokens, width), lambda e: (0, 0)),
        out_shape=jax.ShapeDtypeStruct((tokens, width), F32),
        compiler_params=pltpu.CompilerParams(vmem_limit_bytes=40 << 20),
        name="collect_rows",
    )(spread, returned)


def gelu_and_slope(v):
    c = math.sqrt(2.0 / math.pi)
    t = jnp.tanh(c * (v + 0.044715 * (v * v * v)))
    half = 0.5 * (1.0 + t)
    return v * half, half + 0.5 * v * (1.0 - t * t) * (c * (1.0 + 3 * 0.044715 * (v * v)))


def expert_kernel(sources, info, expert, x_ref, o_ref, c_ref, r_ref, wi_ref, wd_ref,
                  gi_ref, eo_ref, gg_ref, dwi_ref, dwd_ref, geo, gate, eo, gi, dwi, dwd):
    f = pl.program_id(0)
    last = pl.num_programs(0) - 1
    tiles = (info[2 * sources] + MOE_ROWS - 1) // MOE_ROWS
    lane = lax.broadcasted_iota(jnp.int32, (MOE_ROWS, 128), 1)

    def rows_of(i):
        return pl.ds(pl.multiple_of(i * MOE_ROWS, MOE_ROWS), MOE_ROWS)

    @pl.when(f == 0)
    def _():
        gi_ref[...] = jnp.zeros_like(gi_ref)
        eo_ref[...] = jnp.zeros_like(eo_ref)
        gg_ref[...] = jnp.zeros_like(gg_ref)

        def start(i, _):
            at = rows_of(i)
            logits = dot(x_ref[at, :], r_ref[...])
            mine = jnp.sum(jnp.where(lane == expert[0], logits, 0.0), axis=1, keepdims=True)
            other = jnp.sum(jnp.where(o_ref[at, :] > 0, logits, 0.0), axis=1, keepdims=True)
            top = jnp.maximum(mine, other)
            a, b = jnp.exp(mine - top), jnp.exp(other - top)
            g = a / (a + b)
            gate[at, :] = jnp.broadcast_to(g, (MOE_ROWS, 128))
            geo[at, :] = (c_ref[at, :].astype(F32) * g).astype(BF16)
            eo[at, :] = jnp.zeros((MOE_ROWS, eo.shape[1]), F32)
            gi[at, :] = jnp.zeros((MOE_ROWS, gi.shape[1]), F32)
            return 0
        lax.fori_loop(0, tiles, start, 0)

    dwi[...] = jnp.zeros_like(dwi)
    dwd[...] = jnp.zeros_like(dwd)

    def tile(i, _):
        at = rows_of(i)
        x, g = x_ref[at, :], geo[at, :]
        act, slope = gelu_and_slope(dot(x, wi_ref[...]))
        act = act.astype(BF16)
        eo[at, :] += dot(act, wd_ref[...])
        gh = (dot(g, wd_ref[...], NT) * slope).astype(BF16)
        gi[at, :] += dot(gh, wi_ref[...], NT)
        dwd[...] += dot(act, g, TN)
        dwi[...] += dot(x, gh, TN)
        return 0
    lax.fori_loop(0, tiles, tile, 0)
    dwi_ref[...] = dwi[...].astype(BF16)
    dwd_ref[...] = dwd[...].astype(BF16)

    @pl.when(f == last)
    def _():
        def finish(i, _):
            at = rows_of(i)
            out = eo[at, :].astype(BF16).astype(F32)
            gg = jnp.sum(out * c_ref[at, :].astype(F32), axis=1, keepdims=True)
            parts = split3(gg)
            spread = jnp.zeros((MOE_ROWS, 128), BF16)
            for n in range(3):
                spread = jnp.where(lane == n, jnp.broadcast_to(parts[n], (MOE_ROWS, 128)), spread)
            gg_ref[at, :] = spread
            eo_ref[at, :] = (out * gate[at, :1]).astype(BF16)
            gi_ref[at, :] = gi[at, :].astype(BF16)
            return 0
        lax.fori_loop(0, tiles, finish, 0)


def expert_layer(info, expert, x, other, cot, router, w_in, w_down, sources):
    room, width = x.shape
    hidden = w_in.shape[1]
    whole = lambda a: pl.BlockSpec(a.shape, lambda f, *_: (0, 0))
    fixed = lambda cols: pl.BlockSpec((room, cols), lambda f, *_: (0, 0))
    return pl.pallas_call(
        functools.partial(expert_kernel, sources),
        grid_spec=pltpu.PrefetchScalarGridSpec(
            num_scalar_prefetch=2, grid=(hidden // FF_TILE,),
            in_specs=[whole(x), whole(other), whole(cot), whole(router),
                      pl.BlockSpec((width, FF_TILE), lambda f, *_: (0, f)),
                      pl.BlockSpec((FF_TILE, width), lambda f, *_: (f, 0))],
            out_specs=[fixed(width), fixed(width), fixed(128),
                       pl.BlockSpec((width, FF_TILE), lambda f, *_: (0, f)),
                       pl.BlockSpec((FF_TILE, width), lambda f, *_: (f, 0))],
            scratch_shapes=[pltpu.VMEM((room, width), BF16), pltpu.VMEM((room, 128), F32),
                            pltpu.VMEM((room, width), F32), pltpu.VMEM((room, width), F32),
                            pltpu.VMEM((width, FF_TILE), F32), pltpu.VMEM((FF_TILE, width), F32)]),
        out_shape=[jax.ShapeDtypeStruct((room, width), BF16), jax.ShapeDtypeStruct((room, width), BF16),
                   jax.ShapeDtypeStruct((room, 128), BF16),
                   jax.ShapeDtypeStruct(w_in.shape, BF16), jax.ShapeDtypeStruct(w_down.shape, BF16)],
        compiler_params=pltpu.CompilerParams(vmem_limit_bytes=63 << 20),
        name="expert_layer",
    )(info, expert, x, other, cot, router, w_in, w_down)


def exchange_pairs(normed_ffn, middle, cotangent, expert_ids, priority, router, w_in, w_down):
    rows, width = normed_ffn.shape
    logits = jnp.dot(normed_ffn, router, preferred_element_type=jnp.float32)
    experts_total = router.shape[1]
    picks = expert_ids[:, :, None] == jnp.arange(experts_total)[None, None, :]
    chosen = jnp.sum(jnp.where(picks, logits[:, None, :], 0.0), axis=2)
    gates = jax.nn.softmax(chosen, axis=-1)
    top = expert_ids.shape[1]
    levels = PRIO
    local_experts = w_in.shape[0]
    capacity = rows * top // local_experts
    send = max(2, 2 * rows * top // experts_total)
    flat_expert = expert_ids.reshape(-1)
    code = priority.reshape(-1) * experts_total + flat_expert
    onehot = (code[:, None] == jnp.arange(levels * experts_total)[None, :]).astype(jnp.int32)
    rank = jnp.sum((jnp.cumsum(onehot, axis=0) - onehot) * onehot, axis=1)
    counts = jnp.sum(onehot, axis=0)
    every = lax.all_gather(counts[None, :], "expert", axis=0, tiled=True).reshape(
        -1, levels, experts_total
    )
    expert_index = lax.axis_index("expert")
    totals = jnp.sum(every, axis=0)
    lower = jnp.cumsum(totals, axis=0) - totals
    earlier_sources = jnp.cumsum(every, axis=0) - every
    mine_prefix = lax.dynamic_index_in_dim(earlier_sources, expert_index, 0, keepdims=False)
    base = (lower + mine_prefix).reshape(-1)
    slot = rank + jnp.sum(onehot * base[None, :], axis=1)
    kept = slot < capacity
    own_counts = counts.reshape(levels, experts_total)
    own_lower = (jnp.cumsum(own_counts, axis=0) - own_counts).reshape(-1)
    place = rank + jnp.sum(onehot * own_lower[None, :], axis=1)
    target = flat_expert * send + place
    first_mine = expert_index * local_experts
    counts_mine = lax.dynamic_slice_in_dim(every, first_mine, local_experts, 2)
    base_mine = lax.dynamic_slice_in_dim(
        lower[None] + earlier_sources, first_mine, local_experts, 2
    )
    band_end = jnp.cumsum(counts_mine, axis=1)
    band_start = band_end - counts_mine
    place_index = jnp.arange(send, dtype=jnp.int32)
    level = jnp.sum(
        (place_index[None, None, None, :] >= band_end[:, :, :, None]).astype(jnp.int32), axis=1
    )
    level_hot = level[:, None, :, :] == jnp.arange(levels)[None, :, None, None]
    start_of = jnp.sum(jnp.where(level_hot, band_start[:, :, :, None], 0), axis=1)
    base_of = jnp.sum(jnp.where(level_hot, base_mine[:, :, :, None], 0), axis=1)
    arrived_slot = base_of + place_index[None, None, :] - start_of
    usable = (level < levels) & (arrived_slot < capacity)
    landing = jnp.where(
        usable,
        jnp.arange(local_experts)[None, :, None] * capacity + arrived_slot,
        local_experts * capacity,
    ).reshape(-1)
    live = landing < local_experts * capacity
    safe = jnp.minimum(landing, local_experts * capacity - 1)
    pair_inputs = jnp.repeat(normed_ffn, top, axis=0)
    outgoing = (
        jnp.zeros((experts_total * send, width), jnp.bfloat16)
        .at[target]
        .set(pair_inputs)
        .reshape(experts_total, send, width)
    )
    arrived = lax.all_to_all(outgoing, "expert", split_axis=0, concat_axis=0, tiled=True)
    expert_inputs = (
        jnp.zeros((local_experts * capacity, width), jnp.bfloat16)
        .at[landing]
        .set(arrived.reshape(-1, width), mode="drop")
        .reshape(local_experts, capacity, width)
    )
    hidden = jnp.einsum("ecd,edf->ecf", expert_inputs, w_in, preferred_element_type=jnp.float32)
    activated = jax.nn.gelu(hidden).astype(jnp.bfloat16)
    expert_out = jnp.einsum(
        "ecf,efd->ecd", activated, w_down, preferred_element_type=jnp.float32
    ).astype(jnp.bfloat16)
    returning = jnp.where(
        live[:, None],
        jnp.take(expert_out.reshape(-1, width), safe, axis=0),
        jnp.zeros((), jnp.bfloat16),
    ).reshape(experts_total, send, width)
    returned = lax.all_to_all(returning, "expert", split_axis=0, concat_axis=0, tiled=True)
    pair_out = jnp.where(
        kept[:, None],
        jnp.take(returned.reshape(-1, width), target, axis=0).astype(jnp.float32),
        0.0,
    ).reshape(rows, top, width)
    mixed = jnp.sum(gates[:, :, None] * pair_out, axis=1)
    grad_out = cotangent.astype(jnp.float32)
    grad_gates = jnp.sum(grad_out[:, None, :] * pair_out, axis=2)
    pair_grads = (gates[:, :, None] * grad_out[:, None, :]).astype(jnp.bfloat16).reshape(-1, width)
    outgoing_grads = (
        jnp.zeros((experts_total * send, width), jnp.bfloat16)
        .at[target]
        .set(pair_grads)
        .reshape(experts_total, send, width)
    )
    arrived_grads = lax.all_to_all(
        outgoing_grads, "expert", split_axis=0, concat_axis=0, tiled=True
    )
    grad_expert_out = (
        jnp.zeros((local_experts * capacity, width), jnp.bfloat16)
        .at[landing]
        .set(arrived_grads.reshape(-1, width), mode="drop")
        .reshape(local_experts, capacity, width)
    )
    hidden_again = jnp.einsum(
        "ecd,edf->ecf", expert_inputs, w_in, preferred_element_type=jnp.float32
    )
    activated_again, gelu_back = jax.vjp(jax.nn.gelu, hidden_again)
    grad_activated = jnp.einsum(
        "ecd,efd->ecf", grad_expert_out, w_down, preferred_element_type=jnp.float32
    )
    grad_hidden = gelu_back(grad_activated)[0].astype(jnp.bfloat16)
    grad_w_down = jnp.einsum(
        "ecf,ecd->efd",
        activated_again.astype(jnp.bfloat16),
        grad_expert_out,
        preferred_element_type=jnp.float32,
    )
    grad_w_in = jnp.einsum(
        "ecd,ecf->edf", expert_inputs, grad_hidden, preferred_element_type=jnp.float32
    )
    grad_inputs = jnp.einsum(
        "ecf,edf->ecd", grad_hidden, w_in, preferred_element_type=jnp.float32
    ).astype(jnp.bfloat16)
    back_rows = jnp.where(
        live[:, None],
        jnp.take(grad_inputs.reshape(-1, width), safe, axis=0),
        jnp.zeros((), jnp.bfloat16),
    ).reshape(experts_total, send, width)
    came_back = lax.all_to_all(back_rows, "expert", split_axis=0, concat_axis=0, tiled=True)
    pair_back = jnp.where(
        kept[:, None],
        jnp.take(came_back.reshape(-1, width), target, axis=0).astype(jnp.float32),
        0.0,
    )
    grad_normed_ffn = jnp.sum(pair_back.reshape(rows, top, width), axis=1)
    grad_chosen = gates * (grad_gates - jnp.sum(gates * grad_gates, axis=-1, keepdims=True))
    grad_logits = jnp.sum(jnp.where(picks, grad_chosen[:, :, None], 0.0), axis=1).astype(
        jnp.bfloat16
    )
    grad_normed_ffn = grad_normed_ffn + jnp.dot(
        grad_logits, router.T, preferred_element_type=jnp.float32
    )
    expert_parts = (
        lax.psum_scatter(grad_w_in.astype(jnp.bfloat16), "dp", scatter_dimension=1, tiled=True),
        lax.psum_scatter(grad_w_down.astype(jnp.bfloat16), "dp", scatter_dimension=1, tiled=True),
    )
    return mixed, grad_logits, grad_normed_ffn, expert_parts


def gather_codes(expert_ids, priority):
    return lax.all_gather(expert_ids * PRIO + priority, "expert", axis=0)


def plan_tokens(codes, rows, top):
    expert = lax.axis_index("expert").astype(jnp.int32)
    place, info, other = expert_slots(codes // PRIO, codes % PRIO, expert, rows * top)
    other_hot = (other.reshape(-1, 1) == jnp.arange(128)[None, :]).astype(jnp.bfloat16)
    own_place = lax.all_to_all(place, "expert", split_axis=0, concat_axis=0, tiled=True)
    return place, info, other_hot, own_place


def exchange_tokens(normed_ffn, all_cotangents, plan, expert_ids, router, w_in, w_down):
    rows, width = normed_ffn.shape
    experts_total = router.shape[1]
    top = expert_ids.shape[1]
    expert = lax.axis_index("expert").astype(jnp.int32)
    place, info, other_hot, own_place = plan
    sources = place.shape[0]
    room = (rows * top + 16 * sources + 2 * MOE_ROWS - 1) // MOE_ROWS * MOE_ROWS
    sent, all_cotangents = lax.optimization_barrier((normed_ffn, all_cotangents))
    all_tokens = lax.all_gather(sent, "expert", axis=0, tiled=True)
    packed_cot, packed_other = pack(info, place, [all_cotangents, other_hot], room)
    (packed,) = pack(info, place, [all_tokens], room)
    wide_router = jnp.pad(router, ((0, 0), (0, 128 - experts_total)))
    grad_rows, mixed_rows, grad_gate, grad_w_in, grad_w_down = expert_layer(
        info, expert[None], packed, packed_other, packed_cot, wide_router, w_in[0], w_down[0], sources
    )
    grad_all, gate_all = unpack(info, place, [grad_rows, grad_gate], [jnp.bfloat16, jnp.float32])
    gate_all = jnp.sum(gate_all[:, :3], axis=1).reshape(sources, rows)
    gate_own = lax.all_to_all(gate_all, "expert", split_axis=0, concat_axis=0, tiled=True)
    grad_own = lax.psum_scatter(grad_all, "expert", scatter_dimension=0, tiled=True)
    send = 2 * rows * top // experts_total
    windows = jnp.concatenate([lax.dynamic_slice_in_dim(mixed_rows, info[d], send, 0) for d in range(sources)], axis=0)
    windows, grad_w_in, grad_w_down, grad_own = lax.optimization_barrier(
        (windows, grad_w_in, grad_w_down, grad_own)
    )
    mixed = (lax.all_to_all(windows, "expert", split_axis=0, concat_axis=0, tiled=True), own_place)
    expert_parts = (
        lax.psum_scatter(grad_w_in[None], "dp", scatter_dimension=1, tiled=True),
        lax.psum_scatter(grad_w_down[None], "dp", scatter_dimension=1, tiled=True),
    )
    logits = jnp.dot(normed_ffn, router, preferred_element_type=jnp.float32)
    picks = expert_ids[:, :, None] == jnp.arange(experts_total)[None, None, :]
    chosen = jnp.sum(jnp.where(picks, logits[:, None, :], 0.0), axis=2)
    gates = jax.nn.softmax(chosen, axis=-1)
    grad_gates = jnp.sum(jnp.where(picks, gate_own.T[:, None, :], 0.0), axis=2)
    grad_chosen = gates * (grad_gates - jnp.sum(gates * grad_gates, axis=-1, keepdims=True))
    grad_logits = jnp.sum(jnp.where(picks, grad_chosen[:, :, None], 0.0), axis=1).astype(
        jnp.bfloat16
    )
    grad_normed_ffn = grad_own.astype(jnp.float32) + jnp.dot(
        grad_logits, router.T, preferred_element_type=jnp.float32
    )
    return mixed, grad_logits, grad_normed_ffn, expert_parts


def per_device(
    tokens_in,
    cont_ids,
    expert_ids,
    priority,
    gain_attn,
    w_qkv,
    rel_table,
    w_out,
    gain_ffn,
    w_router,
    w_in,
    w_down,
    cotangent,
):
    rows, width = tokens_in.shape
    heads = rel_table.shape[1]
    dp_count = lax.axis_size("dp")
    dp_index = lax.axis_index("dp")
    prompt_rows = PROMPT // dp_count
    few_experts = lax.axis_size("expert") <= 16 and w_in.shape[0] == 1
    local_ids = cont_ids[0]
    info = info_of(local_ids, dp_index)
    row_start = row_start_of(local_ids)
    rows_bias = bias_rows(rel_table)
    if few_experts:
        codes = gather_codes(expert_ids, priority)
    experts_total = w_router.shape[1]
    dense = jnp.concatenate(
        [pairs_together(w_qkv), w_out, jnp.pad(w_router, ((0, 0), (0, 128 - experts_total)))], axis=1
    )
    dense = lax.all_gather(dense, ("dp", "expert"), axis=0, tiled=True)
    if few_experts:
        plan = plan_tokens(codes, rows, expert_ids.shape[1])
        dense, rows_bias, plan = lax.optimization_barrier((dense, rows_bias, plan))
    whole_qkv, whole_out = dense[:, : 3 * width], dense[:, 3 * width : 4 * width]
    whole_router = dense[:, 4 * width : 4 * width + experts_total]
    inputs = tokens_in.astype(jnp.float32)
    normed_attn = normed(inputs, gain_attn).astype(jnp.bfloat16)
    projected = jnp.dot(normed_attn, whole_qkv, preferred_element_type=jnp.float32).astype(
        jnp.bfloat16
    )
    parts = PARTS
    columns = 2 * width // parts
    kept = [projected[:, width + columns * g : width + columns * (g + 1)] for g in range(parts)]
    gathered = [lax.all_gather(kv[:prompt_rows], "dp", axis=0, tiled=True) for kv in kept]
    if few_experts:
        late_cotangent, gathered[0] = lax.optimization_barrier((cotangent, gathered[0]))
        all_cotangents = lax.all_gather(late_cotangent, "expert", axis=0, tiled=True)
    keys_values = []
    exact, log_total = [], []
    for g in range(parts):
        if g:
            gathered[g], exact[-1] = lax.optimization_barrier((gathered[g], exact[-1]))
        keys_values.append(jnp.concatenate([gathered[g], kept[g][prompt_rows:]], axis=0))
        out, total = attention_forward(info, projected, keys_values[g], rows_bias, row_start, g)
        exact.append(out)
        log_total.append(total)
    attended = jnp.concatenate(exact, axis=1).astype(jnp.bfloat16)
    middle = inputs + jnp.dot(attended, whole_out, preferred_element_type=jnp.float32)
    normed_ffn = normed(middle, gain_ffn).astype(jnp.bfloat16)
    if few_experts:
        mixed, grad_logits, grad_normed_ffn, expert_parts = exchange_tokens(
            normed_ffn, all_cotangents, plan, expert_ids, whole_router, w_in, w_down
        )
    else:
        mixed, grad_logits, grad_normed_ffn, expert_parts = exchange_pairs(
            normed_ffn, middle, cotangent, expert_ids, priority, whole_router, w_in, w_down
        )
    grad_out = cotangent.astype(jnp.float32)
    grad_router = jnp.dot(normed_ffn.T, grad_logits, preferred_element_type=jnp.float32)
    _, ffn_norm_back = jax.vjp(normed, middle, gain_ffn)
    grad_middle_part, grad_gain_ffn = ffn_norm_back(grad_normed_ffn)
    grad_middle = grad_out + grad_middle_part
    grad_branch = grad_middle.astype(jnp.bfloat16)
    grad_out_weight = jnp.dot(attended.T, grad_branch, preferred_element_type=jnp.float32)
    grad_attended = jnp.dot(
        grad_branch, whole_out.T, preferred_element_type=jnp.float32
    ).astype(jnp.bfloat16)
    grad_queries, grad_prompts, grad_conts, grad_lines = [], [], [], []
    for g in range(parts):
        if g:
            grad_attended, expert_parts, grad_queries[-1] = lax.optimization_barrier(
                (grad_attended, expert_parts, grad_queries[-1])
            )
        grad_query, grad_kv, lines = attention_backward(
            info, projected, grad_attended, exact[g], log_total[g], keys_values[g], rows_bias, row_start, g
        )
        grad_queries.append(grad_query)
        grad_prompts.append(lax.psum_scatter(grad_kv[:PROMPT], "dp", scatter_dimension=0, tiled=True))
        grad_conts.append(grad_kv[PROMPT:])
        grad_lines.append(lines)
    mixed, middle, grad_queries[-1] = lax.optimization_barrier((mixed, middle, grad_queries[-1]))
    if few_experts:
        returned, own_place = mixed
        mixed = collect(own_place, returned, returned.shape[0] // own_place.shape[0])
    output = (middle + mixed).astype(jnp.bfloat16)
    grad_table = table_grad(jnp.concatenate(grad_lines, axis=0), rel_table.shape[0])
    grad_projected = jnp.concatenate(
        grad_queries + [jnp.concatenate([a, b], axis=0) for a, b in zip(grad_prompts, grad_conts)], axis=1
    )
    grad_normed_attn = jnp.dot(grad_projected, whole_qkv.T, preferred_element_type=jnp.float32)
    grad_qkv = jnp.dot(normed_attn.T, grad_projected, preferred_element_type=jnp.float32)
    _, attn_norm_back = jax.vjp(normed, inputs, gain_attn)
    grad_inputs_part, grad_gain_attn = attn_norm_back(grad_normed_attn)
    grad_tokens = grad_middle + grad_inputs_part
    dense_grad = lax.psum_scatter(
        jnp.concatenate([grad_qkv, grad_out_weight], axis=1), ("dp", "expert"), scatter_dimension=0, tiled=True
    )
    own_router = lax.psum_scatter(grad_router, ("dp", "expert"), scatter_dimension=0, tiled=True)
    small_parts = lax.psum((grad_gain_attn, grad_gain_ffn, grad_table.T), ("dp", "expert"))
    return (
        output,
        grad_tokens,
        small_parts[0],
        pairs_apart(dense_grad[:, : 3 * width]),
        small_parts[2],
        dense_grad[:, 3 * width :],
        small_parts[1],
        own_router,
        expert_parts[0].astype(jnp.float32),
        expert_parts[1].astype(jnp.float32),
    )


def solution(mesh):
    return jax.shard_map(
        per_device,
        mesh=mesh,
        in_specs=(
            P(("dp", "expert"), None),
            P(("dp", "expert"), None),
            P(("dp", "expert"), None),
            P(("dp", "expert"), None),
            P(),
            P(("dp", "expert"), None),
            P(),
            P(("dp", "expert"), None),
            P(),
            P(("dp", "expert"), None),
            P("expert", None, None),
            P("expert", None, None),
            P(("dp", "expert"), None),
        ),
        out_specs=(
            P(("dp", "expert"), None),
            P(("dp", "expert"), None),
            P(),
            P(("dp", "expert"), None),
            P(),
            P(("dp", "expert"), None),
            P(),
            P(("dp", "expert"), None),
            P("expert", "dp", None),
            P("expert", "dp", None),
        ),
        check_vma=False,
    )
```

```python
import functools
import math
import jax
import jax.numpy as jnp
from jax import lax
from jax.experimental import pallas as pl
from jax.experimental.pallas import tpu as pltpu
from jax.sharding import PartitionSpec as P

PRIO = 4
PROMPT = 2048


BORDERS = (16, 24, 32, 48, 64, 96, 128, 192, 256, 384, 512, 768, 1024, 1536, 2048)
EPSILON = 1e-06
MASKED = -1e30


def bucket_of(distance):
    distance = jnp.maximum(distance, 0)
    counted = jnp.minimum(distance, 15)
    for border in BORDERS:
        counted = counted + (distance >= border).astype(jnp.int32)
    return counted


def normed(values, gain):
    return values * lax.rsqrt(jnp.mean(values * values, axis=-1, keepdims=True) + EPSILON) * gain


def pairs_together(w_qkv):
    width = w_qkv.shape[1] // 3
    rows = w_qkv.shape[0]
    keys_values = w_qkv[:, width:].reshape(rows, 2, width // 128, 128).swapaxes(1, 2)
    return jnp.concatenate([w_qkv[:, :width], keys_values.reshape(rows, 2 * width)], axis=1)


def pairs_apart(grad):
    width = grad.shape[1] // 3
    rows = grad.shape[0]
    keys_values = grad[:, width:].reshape(rows, width // 128, 2, 128).swapaxes(1, 2)
    return jnp.concatenate([grad[:, :width], keys_values.reshape(rows, 2 * width)], axis=1)


LOG2E = math.log2(math.e)
F32, BF16 = jnp.float32, jnp.bfloat16
QT = 256
KT = 512
RUN = 256
PARTS = 2
ROWS = 32
NT = (((1,), (1,)), ((), ()))
NN = (((1,), (0,)), ((), ()))

def dot(a, b, dims=NN):
    return lax.dot_general(a, b, dims, preferred_element_type=F32)

def bias_rows(rel_table):
    width = PROMPT + 512 + RUN
    distance = PROMPT + RUN - jnp.arange(width)[None, :] + jnp.arange(8)[:, None]
    bucket = bucket_of(distance)
    table = rel_table.T[:, None, None, :] * LOG2E
    hot = (bucket[..., None] == jnp.arange(rel_table.shape[0])).astype(F32)
    rows = jnp.sum(hot[None] * table, axis=-1)
    return jnp.where(distance[None] >= 0, rows, MASKED)

def bias_kernel(info, base_ref, row_start, t_ref, b_ref):
    base, t_scr, b_scr = base_ref[0], t_ref.at[0], b_ref.at[0]
    width = base.shape[-1]
    for a in range(16):
        t_scr[8 * a:8 * a + 8, :] = pltpu.roll(base, 8 * a, 1) if a else base
    lane = lax.broadcasted_iota(jnp.int32, (ROWS, 128), 1)
    sub = lax.broadcasted_iota(jnp.int32, (ROWS, 128), 0)
    for s in range(4):
        start, end = info[s], info[s + 1]
        turn = start % 128
        left = (128 - turn) % 128
        here = (lane < left) | (left == 0)
        def place(g, _):
            at = pl.ds(pl.multiple_of(ROWS * g, ROWS), ROWS)
            first = start - turn + RUN - 128 * (g // (128 // ROWS))
            of = pl.ds(pl.multiple_of(ROWS * (g % (128 // ROWS)), ROWS), ROWS)
            mine = sub + ROWS * g >= start
            turned = None
            for b in range(PROMPT // 128 + 1):
                after = pltpu.roll(t_scr[of, pl.ds(pl.multiple_of(first + 128 * b, 128), 128)], left, 1)
                if b:
                    cols = slice(128 * b - 128, 128 * b)
                    b_scr[at, cols] = jnp.where(mine, jnp.where(here, turned, after), b_scr[at, cols])
                turned = after
            return 0
        lax.fori_loop(start // ROWS, (end + ROWS - 1) // ROWS, place, 0)
    lane = lax.broadcasted_iota(jnp.int32, (128, 128), 1)
    for i in range(KT // 128):
        rows = slice(128 * i, 128 * i + 128)
        own = row_start[rows, :]
        for b in range(KT // 128):
            first = PROMPT + RUN - 128 * i + 128 * b
            b_scr[rows, PROMPT + 128 * b:PROMPT + 128 * b + 128] = jnp.where(
                lane + 128 * b >= own, t_scr[:, first:first + 128], MASKED)

def bias_tables(info, rows_bias, row_start, first, heads):
    wide = rows_bias.shape[2]
    block = lambda rows, cols: pl.BlockSpec((1, rows, cols), lambda h, *_: (h, 0, 0))
    return pl.pallas_call(
        bias_kernel,
        grid_spec=pltpu.PrefetchScalarGridSpec(
            num_scalar_prefetch=1, grid=(heads,),
            in_specs=[pl.BlockSpec((1, 8, wide), lambda h, *_: (first + h, 0, 0)),
                      pl.BlockSpec((KT, 128), lambda h, *_: (0, 0))],
            out_specs=[block(128, wide), block(KT, PROMPT + KT)]),
        out_shape=[jax.ShapeDtypeStruct((heads, 128, wide), F32),
                   jax.ShapeDtypeStruct((heads, KT, PROMPT + KT), F32)],
        compiler_params=pltpu.CompilerParams(vmem_limit_bytes=32 << 20),
        cost_estimate=pl.CostEstimate(flops=0, bytes_accessed=heads * KT * (PROMPT + KT) * 8, transcendentals=0),
        name="bias_tables",
    )(info, rows_bias, row_start)

def own_lanes(h, rows):
    lane = lax.broadcasted_iota(jnp.int32, (rows, 128), 1)
    return lane // 64 == h % 2

def fwd_kernel(scale2, info, q_ref, k_ref, v_ref, t_ref, b_ref, o_ref, lse_ref):
    h = pl.program_id(0)
    dp = info[5]
    t_scr, b_scr = t_ref.at[0], b_ref.at[0]
    own = own_lanes(h, QT)
    head_lane = lax.broadcasted_iota(jnp.int32, (QT, 128), 1) == h

    def tile(first, key_tiles, bias_of, block):
        rows = pl.ds(first, QT)
        q = jnp.where(own, q_ref[rows, :], jnp.zeros((), BF16))
        def step(t, carry):
            m, l, acc = carry
            cols = pl.ds(pl.multiple_of(block(t) * KT, KT), KT)
            s = dot(q, k_ref[cols, :], NT) * scale2 + bias_of(t)
            new = jnp.maximum(m, jnp.max(s, axis=1, keepdims=True))
            keep = jnp.exp2(m - new)
            p = jnp.exp2(s - jnp.concatenate([new] * (KT // 128), axis=1))
            part = p[:, :128]
            for c in range(1, KT // 128):
                part = part + p[:, 128 * c:128 * (c + 1)]
            return new, l * keep + part, acc * keep + dot(p.astype(BF16), v_ref[cols, :])
        zero = jnp.zeros((QT, 128), F32)
        m, l, acc = lax.fori_loop(0, key_tiles, step, (jnp.full((QT, 128), MASKED, F32), zero, zero))
        l = jnp.sum(l, axis=1, keepdims=True)
        o_ref[rows, :] = jnp.where(own, acc / l, o_ref[rows, :])
        lse_ref[rows, :] = jnp.where(head_lane, m + jnp.log2(l), lse_ref[rows, :])

    for j in range(2):
        shift = PROMPT - KT * dp - QT * j + RUN
        def bias(t, shift=shift):
            first = (dp - t) * KT + shift
            return jnp.concatenate([t_scr[:, pl.ds(pl.multiple_of(first - 128 * x, 128), KT)] for x in range(QT // 128)], axis=0)
        tile(QT * j, dp + 1, bias, lambda t: dp - t)
    for j in range(2):
        tile(KT + QT * j, PROMPT // KT + 1,
             lambda t: b_scr[pl.ds(QT * j, QT), pl.ds(pl.multiple_of(t * KT, KT), KT)], lambda t: t)

def attention_forward(info, projected, keys_values, tables, part):
    n = projected.shape[0]
    keys, columns = keys_values.shape
    heads = columns // 128
    head_size = 64
    scale2 = head_size ** -0.5 * LOG2E
    first = part * heads // 2
    return pl.pallas_call(
        functools.partial(fwd_kernel, scale2),
        grid_spec=pltpu.PrefetchScalarGridSpec(
            num_scalar_prefetch=1, grid=(heads,),
            in_specs=[pl.BlockSpec((n, 128), lambda h, *_: (0, first + h // 2)),
                      pl.BlockSpec((keys, 128), lambda h, *_: (0, h // 2 * 2)),
                      pl.BlockSpec((keys, 128), lambda h, *_: (0, h // 2 * 2 + 1)),
                      *[pl.BlockSpec((1,) + t.shape[1:], lambda h, *_: (h, 0, 0)) for t in tables]],
            out_specs=[pl.BlockSpec((n, 128), lambda h, *_: (0, h // 2)),
                       pl.BlockSpec((n, 128), lambda h, *_: (0, 0))]),
        out_shape=[jax.ShapeDtypeStruct((n, heads * 64), F32), jax.ShapeDtypeStruct((n, 128), F32)],
        compiler_params=pltpu.CompilerParams(vmem_limit_bytes=60 << 20),
        cost_estimate=pl.CostEstimate(flops=heads * n * keys * 128 * 4, bytes_accessed=n * keys * 4, transcendentals=heads * n * keys),
        name="attention_forward",
    )(info, projected, keys_values, keys_values, *tables)

def split3(x):
    hi = x.astype(BF16)
    rest = x - hi.astype(F32)
    mid = rest.astype(BF16)
    return hi, mid, (rest - mid.astype(F32)).astype(BF16)

def bwd_kernel(scale, info, q_ref, do_ref, o_ref, lse_ref, k_ref, v_ref, t_ref, b_ref,
               dq_ref, dkv_ref, dd_ref,
               e_scr, db_scr, qa, da, ka, va, qt, dot_t, dkt, dvt):
    h = pl.program_id(0)
    dp = info[5]
    n, keys = q_ref.shape[0], k_ref.shape[0]
    half = h % 2
    t_scr, b_scr = t_ref.at[0], b_ref.at[0]
    base = pl.multiple_of(64 * half, 64)
    other = 64 - 64 * half

    @pl.when(half == 0)
    def _():
        qt[...] = q_ref[...].T
        dot_t[...] = do_ref[...].T
        dq_ref[...] = jnp.zeros_like(dq_ref)

    lane_n = lax.broadcasted_iota(jnp.int32, (QT, 128), 1)
    own_n = lane_n // 64 == half
    def augment(i, _):
        rows = pl.ds(pl.multiple_of(i * QT, QT), QT)
        lse = jnp.sum(jnp.where(lane_n == h, lse_ref[rows, :], 0.0), axis=1, keepdims=True)
        parts = split3(-lse / (scale * LOG2E))
        aug = jnp.zeros((QT, 128), BF16)
        for x in range(3):
            aug = jnp.where(lane_n == other + x, jnp.broadcast_to(parts[x], (QT, 128)), aug)
        qa[rows, :] = jnp.where(own_n, q_ref[rows, :], aug)
        do = do_ref[rows, :]
        delta = jnp.sum(jnp.where(own_n, do.astype(F32) * o_ref[rows, :], 0.0), axis=1, keepdims=True)
        parts = split3(-delta)
        aug = jnp.zeros((QT, 128), BF16)
        for x in range(3):
            aug = jnp.where(lane_n == other + x, jnp.broadcast_to(parts[x], (QT, 128)), aug)
        da[rows, :] = jnp.where(own_n, do, aug)
        return 0
    lax.fori_loop(0, n // QT, augment, 0)
    lane_k = lax.broadcasted_iota(jnp.int32, (KT, 128), 1)
    ones = jnp.where((lane_k >= other) & (lane_k < other + 3), 1.0, 0.0).astype(BF16)
    own_k = lane_k // 64 == half
    def augment_keys(i, _):
        rows = pl.ds(pl.multiple_of(i * KT, KT), KT)
        ka[rows, :] = jnp.where(own_k, k_ref[rows, :], ones)
        va[rows, :] = jnp.where(own_k, v_ref[rows, :], ones)
        return 0
    lax.fori_loop(0, keys // KT, augment_keys, 0)
    head_rows = pl.ds(base, 64)
    dkt[head_rows, :] = jnp.zeros((64, keys), F32)
    dvt[head_rows, :] = jnp.zeros((64, keys), F32)
    e_scr[...] = jnp.zeros_like(e_scr)

    def tile(first, key_tiles, bias_of, grad_bias):
        rows = pl.ds(first, QT)
        q, do = qa[rows, :], da[rows, :]
        q_t, do_t = qt[head_rows, rows], dot_t[head_rows, rows]
        def step(t, dq):
            cols = pl.ds(pl.multiple_of(t * KT, KT), KT)
            kk = ka[cols, :]
            p = jnp.exp2(dot(q, kk, NT) * (scale * LOG2E) + bias_of(t))
            ds = p * dot(do, va[cols, :], NT)
            grad_bias(t, ds)
            low = ds.astype(BF16)
            dvt[head_rows, cols] += dot(do_t, p.astype(BF16))
            dkt[head_rows, cols] += dot(q_t, low)
            return dq + dot(low, kk)
        dq = lax.fori_loop(0, key_tiles, step, jnp.zeros((QT, 128), F32))
        dq_ref[rows, :] = jnp.where(own_n, dq * scale, dq_ref[rows, :].astype(F32)).astype(BF16)

    for j in range(2):
        shift = PROMPT - KT * dp - QT * j + RUN
        def part(t, x, shift=shift):
            return (slice(None), pl.ds(pl.multiple_of(t * KT + shift - 128 * x, 128), KT))
        def bias(t):
            return jnp.concatenate([t_scr[part(t, x)] for x in range(QT // 128)], axis=0)
        def add(t, ds):
            for x in range(QT // 128):
                e_scr[part(t, x)] += ds[128 * x:128 * x + 128, :]
        tile(QT * j, dp + 1, bias, add)
    for j in range(2):
        def where(t):
            return (pl.ds(QT * j, QT), pl.ds(pl.multiple_of(t * KT, KT), KT))
        def put(t, ds):
            db_scr[where(t)] = ds
        tile(KT + QT * j, PROMPT // KT + 1, lambda t: b_scr[where(t)], put)

    lane = lax.broadcasted_iota(jnp.int32, (ROWS, 128), 1)
    sub = lax.broadcasted_iota(jnp.int32, (ROWS, 128), 0)
    for s in range(4):
        start, end = info[s], info[s + 1]
        turn = start % 128
        def fold(g, _):
            at = pl.ds(pl.multiple_of(ROWS * g, ROWS), ROWS)
            first = start - turn + RUN - 128 * (g // (128 // ROWS))
            to = pl.ds(pl.multiple_of(ROWS * (g % (128 // ROWS)), ROWS), ROWS)
            mine = (sub + ROWS * g >= start) & (sub + ROWS * g < end)
            before = jnp.zeros((ROWS, 128), F32)
            for b in range(PROMPT // 128 + 1):
                if b < PROMPT // 128:
                    turned = pltpu.roll(jnp.where(mine, db_scr[at, 128 * b:128 * b + 128], 0.0), turn, 1)
                else:
                    turned = jnp.zeros((ROWS, 128), F32)
                e_scr[to, pl.ds(pl.multiple_of(first + 128 * b, 128), 128)] += jnp.where(lane >= turn, turned, before)
                before = turned
            return 0
        lax.fori_loop(start // ROWS, (end + ROWS - 1) // ROWS, fold, 0)
    for i in range(KT // 128):
        first = PROMPT + RUN - 128 * i
        e_scr[:, first:first + KT] += db_scr[128 * i:128 * i + 128, PROMPT:]
    width = t_ref.shape[2]
    acc = e_scr[0:8, :]
    for a in range(1, 16):
        acc = acc + pltpu.roll(e_scr[8 * a:8 * a + 8, :], width - 8 * a, 1)
    total = acc[0:1, :]
    for i in range(1, 8):
        total = total + pltpu.roll(acc, width - i, 1)[i:i + 1, :]
    dd_ref[0] = total

    @pl.when(half == 1)
    def _():
        dkv_ref[:, :128] = (dkt[...] * scale).T.astype(BF16)
        dkv_ref[:, 128:] = dvt[...].T.astype(BF16)

def attention_backward(info, projected, do, o32, lse, keys_values, tables, part):
    n = projected.shape[0]
    keys, columns = keys_values.shape
    heads = columns // 128
    wide = tables[0].shape[2]
    first = part * heads // 2
    own = pl.BlockSpec((n, 128), lambda h, *_: (0, h // 2))
    shifted = pl.BlockSpec((n, 128), lambda h, *_: (0, first + h // 2))
    cols = PROMPT + KT
    return pl.pallas_call(
        functools.partial(bwd_kernel, 64 ** -0.5),
        grid_spec=pltpu.PrefetchScalarGridSpec(
            num_scalar_prefetch=1, grid=(heads,),
            in_specs=[shifted, shifted, own, pl.BlockSpec((n, 128), lambda h, *_: (0, 0)),
                      pl.BlockSpec((keys, 128), lambda h, *_: (0, h // 2 * 2)),
                      pl.BlockSpec((keys, 128), lambda h, *_: (0, h // 2 * 2 + 1)),
                      *[pl.BlockSpec((1,) + t.shape[1:], lambda h, *_: (h, 0, 0)) for t in tables]],
            out_specs=[own, pl.BlockSpec((keys, 256), lambda h, *_: (0, h // 2)),
                       pl.BlockSpec((1, 1, wide), lambda h, *_: (h, 0, 0))],
            scratch_shapes=[pltpu.VMEM((128, wide), F32), pltpu.VMEM((KT, cols), F32),
                            pltpu.VMEM((n, 128), BF16), pltpu.VMEM((n, 128), BF16),
                            pltpu.VMEM((keys, 128), BF16), pltpu.VMEM((keys, 128), BF16),
                            pltpu.VMEM((128, n), BF16), pltpu.VMEM((128, n), BF16),
                            pltpu.VMEM((128, keys), F32), pltpu.VMEM((128, keys), F32)]),
        out_shape=[jax.ShapeDtypeStruct((n, heads * 64), BF16), jax.ShapeDtypeStruct((keys, columns), BF16),
                   jax.ShapeDtypeStruct((heads, 1, wide), F32)],
        compiler_params=pltpu.CompilerParams(vmem_limit_bytes=60 << 20),
        cost_estimate=pl.CostEstimate(flops=heads * n * keys * 128 * 10, bytes_accessed=n * keys * 4, transcendentals=heads * n * keys),
        name="attention_backward",
    )(info, projected, do, o32, lse, keys_values, keys_values, *tables)

def info_of(ids, dp):
    starts = jnp.sum((ids[None, :] < jnp.arange(5)[:, None]).astype(jnp.int32), axis=1)
    return jnp.concatenate([starts, jnp.reshape(dp, (1,)).astype(jnp.int32)])

def table_grad(dd, buckets):
    width = dd.shape[2]
    distance = PROMPT + RUN - jnp.arange(width)
    hot = ((bucket_of(distance)[:, None] == jnp.arange(buckets)[None, :]) & (distance >= 0)[:, None]).astype(F32)
    return jnp.dot(dd[:, 0, :], hot, precision=lax.Precision.HIGHEST)

def row_start_of(ids):
    starts = jnp.sum((ids[None, :] < ids[:, None]).astype(jnp.int32), axis=1)
    return jnp.broadcast_to(starts[:, None], (ids.shape[0], 128))


TN = (((0,), (0,)), ((), ()))
MOE_ROWS = 256
FF_TILE = 768


def expert_slots(ids, levels, expert, capacity):
    hits = ids == expert
    hit = jnp.any(hits, axis=2)
    level = jnp.sum(jnp.where(hits, levels, 0), axis=2)
    hot = hit[:, :, None] & (level[:, :, None] == jnp.arange(PRIO)[None, None, :])
    tokens = ids.shape[1]
    earlier = (jnp.arange(tokens)[:, None] > jnp.arange(tokens)[None, :]).astype(BF16)
    rank = jnp.einsum("ut,dtl->dul", earlier, hot.astype(BF16), preferred_element_type=F32).astype(jnp.int32)
    counts = jnp.sum(hot.astype(jnp.int32), axis=1)
    totals = jnp.sum(counts, axis=0)
    lower = jnp.cumsum(totals) - totals
    base = lower[None, :] + jnp.cumsum(counts, axis=0) - counts
    slot = jnp.sum(jnp.where(hot, base[:, None, :] + rank, 0), axis=2)
    kept = hit & (slot < capacity)
    rank = jnp.einsum("ut,dt->du", earlier, kept.astype(BF16), preferred_element_type=F32).astype(jnp.int32)
    place = jnp.where(kept, rank, -1)
    sizes = jnp.sum(kept.astype(jnp.int32), axis=1)
    padded = (sizes + 15) // 16 * 16
    ends = jnp.cumsum(padded)
    other = jnp.sum(jnp.where(hits, 0, ids), axis=2)
    return place, jnp.concatenate([ends - padded, sizes, ends[-1:]]).astype(jnp.int32), other


def pack_kernel(sources, info, place_ref, *refs):
    ins, outs = refs[:len(refs) // 2], refs[len(refs) // 2:]
    d = pl.program_id(0)

    @pl.when(d == 0)
    def _():
        for out in outs:
            out[...] = jnp.zeros_like(out)

    tokens = place_ref.shape[2]
    row = lax.broadcasted_iota(jnp.int32, (MOE_ROWS, tokens), 0)

    def chunk(j, _):
        pick = jnp.where(place_ref[0] == row + MOE_ROWS * j, 1.0, 0.0).astype(BF16)
        at = pl.ds(pl.multiple_of(info[d] + MOE_ROWS * j, 16), MOE_ROWS)
        for x, out in zip(ins, outs):
            out[at, :] = dot(pick, x[...]).astype(BF16)
        return 0
    lax.fori_loop(0, (info[sources + d] + MOE_ROWS - 1) // MOE_ROWS, chunk, 0)


def pack(info, place, arrays, room):
    sources, tokens = place.shape
    return pl.pallas_call(
        functools.partial(pack_kernel, sources),
        grid_spec=pltpu.PrefetchScalarGridSpec(
            num_scalar_prefetch=1, grid=(sources,),
            in_specs=[pl.BlockSpec((1, 1, tokens), lambda d, *_: (d, 0, 0))]
            + [pl.BlockSpec((tokens, x.shape[1]), lambda d, *_: (d, 0)) for x in arrays],
            out_specs=[pl.BlockSpec((room, x.shape[1]), lambda d, *_: (0, 0)) for x in arrays]),
        out_shape=[jax.ShapeDtypeStruct((room, x.shape[1]), BF16) for x in arrays],
        compiler_params=pltpu.CompilerParams(vmem_limit_bytes=40 << 20),
        name="pack_tokens",
    )(info, place[:, None, :], *arrays)


def unpack_kernel(sources, info, place_ref, *refs):
    ins, outs = refs[:len(refs) // 2], refs[len(refs) // 2:]
    d = pl.program_id(0)
    tokens = place_ref.shape[0]
    lane = lax.broadcasted_iota(jnp.int32, (tokens, 128), 1)
    for x, out in zip(ins, outs):
        def chunk(j, total):
            put = jnp.concatenate(
                [jnp.where(place_ref[...] == lane + (MOE_ROWS * j + 128 * b), 1.0, 0.0).astype(BF16)
                 for b in range(MOE_ROWS // 128)], axis=1)
            at = pl.ds(pl.multiple_of(info[d] + MOE_ROWS * j, 16), MOE_ROWS)
            return total + dot(put, x[at, :])
        total = lax.fori_loop(0, (info[sources + d] + MOE_ROWS - 1) // MOE_ROWS, chunk,
                              jnp.zeros((tokens, x.shape[1]), F32))
        out[...] = total.astype(out.dtype)


def unpack(info, place, arrays, dtypes):
    sources, tokens = place.shape
    spread = jnp.broadcast_to(place.reshape(-1, 1), (sources * tokens, 128))
    return pl.pallas_call(
        functools.partial(unpack_kernel, sources),
        grid_spec=pltpu.PrefetchScalarGridSpec(
            num_scalar_prefetch=1, grid=(sources,),
            in_specs=[pl.BlockSpec((tokens, 128), lambda d, *_: (d, 0))]
            + [pl.BlockSpec(x.shape, lambda d, *_: (0, 0)) for x in arrays],
            out_specs=[pl.BlockSpec((tokens, x.shape[1]), lambda d, *_: (d, 0)) for x in arrays]),
        out_shape=[jax.ShapeDtypeStruct((sources * tokens, x.shape[1]), t) for x, t in zip(arrays, dtypes)],
        compiler_params=pltpu.CompilerParams(vmem_limit_bytes=40 << 20),
        name="unpack_tokens",
    )(info, spread, *arrays)


def collect_kernel(place_ref, x_ref, out_ref):
    tokens = place_ref.shape[0]
    lane = lax.broadcasted_iota(jnp.int32, (tokens, 128), 1)
    put = jnp.concatenate(
        [jnp.where(place_ref[...] == lane + 128 * b, 1.0, 0.0).astype(BF16) for b in range(x_ref.shape[0] // 128)],
        axis=1)
    total = dot(put, x_ref[...])

    @pl.when(pl.program_id(0) == 0)
    def _():
        out_ref[...] = total

    @pl.when(pl.program_id(0) > 0)
    def _():
        out_ref[...] += total


def collect(place, returned, send):
    experts, tokens = place.shape
    width = returned.shape[1]
    spread = jnp.broadcast_to(place.reshape(-1, 1), (experts * tokens, 128))
    return pl.pallas_call(
        collect_kernel,
        grid=(experts,),
        in_specs=[pl.BlockSpec((tokens, 128), lambda e: (e, 0)), pl.BlockSpec((send, width), lambda e: (e, 0))],
        out_specs=pl.BlockSpec((tokens, width), lambda e: (0, 0)),
        out_shape=jax.ShapeDtypeStruct((tokens, width), F32),
        compiler_params=pltpu.CompilerParams(vmem_limit_bytes=40 << 20),
        name="collect_rows",
    )(spread, returned)


def gelu_and_slope(v):
    c = math.sqrt(2.0 / math.pi)
    t = jnp.tanh(c * (v + 0.044715 * (v * v * v)))
    half = 0.5 * (1.0 + t)
    return v * half, half + 0.5 * v * (1.0 - t * t) * (c * (1.0 + 3 * 0.044715 * (v * v)))


def expert_kernel(sources, info, expert, x_ref, o_ref, c_ref, r_ref, wi_ref, wd_ref,
                  gi_ref, eo_ref, gg_ref, dwi_ref, dwd_ref, geo, gate, eo, gi, dwi, dwd):
    f = pl.program_id(0)
    last = pl.num_programs(0) - 1
    tiles = (info[2 * sources] + MOE_ROWS - 1) // MOE_ROWS
    lane = lax.broadcasted_iota(jnp.int32, (MOE_ROWS, 128), 1)

    def rows_of(i):
        return pl.ds(pl.multiple_of(i * MOE_ROWS, MOE_ROWS), MOE_ROWS)

    @pl.when(f == 0)
    def _():
        gi_ref[...] = jnp.zeros_like(gi_ref)
        eo_ref[...] = jnp.zeros_like(eo_ref)
        gg_ref[...] = jnp.zeros_like(gg_ref)

        def start(i, _):
            at = rows_of(i)
            logits = dot(x_ref[at, :], r_ref[...])
            mine = jnp.sum(jnp.where(lane == expert[0], logits, 0.0), axis=1, keepdims=True)
            other = jnp.sum(jnp.where(o_ref[at, :] > 0, logits, 0.0), axis=1, keepdims=True)
            top = jnp.maximum(mine, other)
            a, b = jnp.exp(mine - top), jnp.exp(other - top)
            g = a / (a + b)
            gate[at, :] = jnp.broadcast_to(g, (MOE_ROWS, 128))
            geo[at, :] = (c_ref[at, :].astype(F32) * g).astype(BF16)
            eo[at, :] = jnp.zeros((MOE_ROWS, eo.shape[1]), F32)
            gi[at, :] = jnp.zeros((MOE_ROWS, gi.shape[1]), F32)
            return 0
        lax.fori_loop(0, tiles, start, 0)

    dwi[...] = jnp.zeros_like(dwi)
    dwd[...] = jnp.zeros_like(dwd)

    def tile(i, _):
        at = rows_of(i)
        x, g = x_ref[at, :], geo[at, :]
        act, slope = gelu_and_slope(dot(x, wi_ref[...]))
        act = act.astype(BF16)
        eo[at, :] += dot(act, wd_ref[...])
        gh = (dot(g, wd_ref[...], NT) * slope).astype(BF16)
        gi[at, :] += dot(gh, wi_ref[...], NT)
        dwd[...] += dot(act, g, TN)
        dwi[...] += dot(x, gh, TN)
        return 0
    lax.fori_loop(0, tiles, tile, 0)
    dwi_ref[...] = dwi[...].astype(BF16)
    dwd_ref[...] = dwd[...].astype(BF16)

    @pl.when(f == last)
    def _():
        def finish(i, _):
            at = rows_of(i)
            out = eo[at, :].astype(BF16).astype(F32)
            gg = jnp.sum(out * c_ref[at, :].astype(F32), axis=1, keepdims=True)
            parts = split3(gg)
            spread = jnp.zeros((MOE_ROWS, 128), BF16)
            for n in range(3):
                spread = jnp.where(lane == n, jnp.broadcast_to(parts[n], (MOE_ROWS, 128)), spread)
            gg_ref[at, :] = spread
            eo_ref[at, :] = (out * gate[at, :1]).astype(BF16)
            gi_ref[at, :] = gi[at, :].astype(BF16)
            return 0
        lax.fori_loop(0, tiles, finish, 0)


def expert_layer(info, expert, x, other, cot, router, w_in, w_down, sources):
    room, width = x.shape
    hidden = w_in.shape[1]
    whole = lambda a: pl.BlockSpec(a.shape, lambda f, *_: (0, 0))
    fixed = lambda cols: pl.BlockSpec((room, cols), lambda f, *_: (0, 0))
    return pl.pallas_call(
        functools.partial(expert_kernel, sources),
        grid_spec=pltpu.PrefetchScalarGridSpec(
            num_scalar_prefetch=2, grid=(hidden // FF_TILE,),
            in_specs=[whole(x), whole(other), whole(cot), whole(router),
                      pl.BlockSpec((width, FF_TILE), lambda f, *_: (0, f)),
                      pl.BlockSpec((FF_TILE, width), lambda f, *_: (f, 0))],
            out_specs=[fixed(width), fixed(width), fixed(128),
                       pl.BlockSpec((width, FF_TILE), lambda f, *_: (0, f)),
                       pl.BlockSpec((FF_TILE, width), lambda f, *_: (f, 0))],
            scratch_shapes=[pltpu.VMEM((room, width), BF16), pltpu.VMEM((room, 128), F32),
                            pltpu.VMEM((room, width), F32), pltpu.VMEM((room, width), F32),
                            pltpu.VMEM((width, FF_TILE), F32), pltpu.VMEM((FF_TILE, width), F32)]),
        out_shape=[jax.ShapeDtypeStruct((room, width), BF16), jax.ShapeDtypeStruct((room, width), BF16),
                   jax.ShapeDtypeStruct((room, 128), BF16),
                   jax.ShapeDtypeStruct(w_in.shape, BF16), jax.ShapeDtypeStruct(w_down.shape, BF16)],
        compiler_params=pltpu.CompilerParams(vmem_limit_bytes=63 << 20),
        name="expert_layer",
    )(info, expert, x, other, cot, router, w_in, w_down)


def exchange_pairs(normed_ffn, middle, cotangent, expert_ids, priority, router, w_in, w_down):
    rows, width = normed_ffn.shape
    logits = jnp.dot(normed_ffn, router, preferred_element_type=jnp.float32)
    experts_total = router.shape[1]
    picks = expert_ids[:, :, None] == jnp.arange(experts_total)[None, None, :]
    chosen = jnp.sum(jnp.where(picks, logits[:, None, :], 0.0), axis=2)
    gates = jax.nn.softmax(chosen, axis=-1)
    top = expert_ids.shape[1]
    levels = PRIO
    local_experts = w_in.shape[0]
    capacity = rows * top // local_experts
    send = max(2, 2 * rows * top // experts_total)
    flat_expert = expert_ids.reshape(-1)
    code = priority.reshape(-1) * experts_total + flat_expert
    onehot = (code[:, None] == jnp.arange(levels * experts_total)[None, :]).astype(jnp.int32)
    rank = jnp.sum((jnp.cumsum(onehot, axis=0) - onehot) * onehot, axis=1)
    counts = jnp.sum(onehot, axis=0)
    every = lax.all_gather(counts[None, :], "expert", axis=0, tiled=True).reshape(
        -1, levels, experts_total
    )
    expert_index = lax.axis_index("expert")
    totals = jnp.sum(every, axis=0)
    lower = jnp.cumsum(totals, axis=0) - totals
    earlier_sources = jnp.cumsum(every, axis=0) - every
    mine_prefix = lax.dynamic_index_in_dim(earlier_sources, expert_index, 0, keepdims=False)
    base = (lower + mine_prefix).reshape(-1)
    slot = rank + jnp.sum(onehot * base[None, :], axis=1)
    kept = slot < capacity
    own_counts = counts.reshape(levels, experts_total)
    own_lower = (jnp.cumsum(own_counts, axis=0) - own_counts).reshape(-1)
    place = rank + jnp.sum(onehot * own_lower[None, :], axis=1)
    target = flat_expert * send + place
    first_mine = expert_index * local_experts
    counts_mine = lax.dynamic_slice_in_dim(every, first_mine, local_experts, 2)
    base_mine = lax.dynamic_slice_in_dim(
        lower[None] + earlier_sources, first_mine, local_experts, 2
    )
    band_end = jnp.cumsum(counts_mine, axis=1)
    band_start = band_end - counts_mine
    place_index = jnp.arange(send, dtype=jnp.int32)
    level = jnp.sum(
        (place_index[None, None, None, :] >= band_end[:, :, :, None]).astype(jnp.int32), axis=1
    )
    level_hot = level[:, None, :, :] == jnp.arange(levels)[None, :, None, None]
    start_of = jnp.sum(jnp.where(level_hot, band_start[:, :, :, None], 0), axis=1)
    base_of = jnp.sum(jnp.where(level_hot, base_mine[:, :, :, None], 0), axis=1)
    arrived_slot = base_of + place_index[None, None, :] - start_of
    usable = (level < levels) & (arrived_slot < capacity)
    landing = jnp.where(
        usable,
        jnp.arange(local_experts)[None, :, None] * capacity + arrived_slot,
        local_experts * capacity,
    ).reshape(-1)
    live = landing < local_experts * capacity
    safe = jnp.minimum(landing, local_experts * capacity - 1)
    pair_inputs = jnp.repeat(normed_ffn, top, axis=0)
    outgoing = (
        jnp.zeros((experts_total * send, width), jnp.bfloat16)
        .at[target]
        .set(pair_inputs)
        .reshape(experts_total, send, width)
    )
    arrived = lax.all_to_all(outgoing, "expert", split_axis=0, concat_axis=0, tiled=True)
    expert_inputs = (
        jnp.zeros((local_experts * capacity, width), jnp.bfloat16)
        .at[landing]
        .set(arrived.reshape(-1, width), mode="drop")
        .reshape(local_experts, capacity, width)
    )
    hidden = jnp.einsum("ecd,edf->ecf", expert_inputs, w_in, preferred_element_type=jnp.float32)
    activated = jax.nn.gelu(hidden).astype(jnp.bfloat16)
    expert_out = jnp.einsum(
        "ecf,efd->ecd", activated, w_down, preferred_element_type=jnp.float32
    ).astype(jnp.bfloat16)
    returning = jnp.where(
        live[:, None],
        jnp.take(expert_out.reshape(-1, width), safe, axis=0),
        jnp.zeros((), jnp.bfloat16),
    ).reshape(experts_total, send, width)
    returned = lax.all_to_all(returning, "expert", split_axis=0, concat_axis=0, tiled=True)
    pair_out = jnp.where(
        kept[:, None],
        jnp.take(returned.reshape(-1, width), target, axis=0).astype(jnp.float32),
        0.0,
    ).reshape(rows, top, width)
    mixed = jnp.sum(gates[:, :, None] * pair_out, axis=1)
    grad_out = cotangent.astype(jnp.float32)
    grad_gates = jnp.sum(grad_out[:, None, :] * pair_out, axis=2)
    pair_grads = (gates[:, :, None] * grad_out[:, None, :]).astype(jnp.bfloat16).reshape(-1, width)
    outgoing_grads = (
        jnp.zeros((experts_total * send, width), jnp.bfloat16)
        .at[target]
        .set(pair_grads)
        .reshape(experts_total, send, width)
    )
    arrived_grads = lax.all_to_all(
        outgoing_grads, "expert", split_axis=0, concat_axis=0, tiled=True
    )
    grad_expert_out = (
        jnp.zeros((local_experts * capacity, width), jnp.bfloat16)
        .at[landing]
        .set(arrived_grads.reshape(-1, width), mode="drop")
        .reshape(local_experts, capacity, width)
    )
    hidden_again = jnp.einsum(
        "ecd,edf->ecf", expert_inputs, w_in, preferred_element_type=jnp.float32
    )
    activated_again, gelu_back = jax.vjp(jax.nn.gelu, hidden_again)
    grad_activated = jnp.einsum(
        "ecd,efd->ecf", grad_expert_out, w_down, preferred_element_type=jnp.float32
    )
    grad_hidden = gelu_back(grad_activated)[0].astype(jnp.bfloat16)
    grad_w_down = jnp.einsum(
        "ecf,ecd->efd",
        activated_again.astype(jnp.bfloat16),
        grad_expert_out,
        preferred_element_type=jnp.float32,
    )
    grad_w_in = jnp.einsum(
        "ecd,ecf->edf", expert_inputs, grad_hidden, preferred_element_type=jnp.float32
    )
    grad_inputs = jnp.einsum(
        "ecf,edf->ecd", grad_hidden, w_in, preferred_element_type=jnp.float32
    ).astype(jnp.bfloat16)
    back_rows = jnp.where(
        live[:, None],
        jnp.take(grad_inputs.reshape(-1, width), safe, axis=0),
        jnp.zeros((), jnp.bfloat16),
    ).reshape(experts_total, send, width)
    came_back = lax.all_to_all(back_rows, "expert", split_axis=0, concat_axis=0, tiled=True)
    pair_back = jnp.where(
        kept[:, None],
        jnp.take(came_back.reshape(-1, width), target, axis=0).astype(jnp.float32),
        0.0,
    )
    grad_normed_ffn = jnp.sum(pair_back.reshape(rows, top, width), axis=1)
    grad_chosen = gates * (grad_gates - jnp.sum(gates * grad_gates, axis=-1, keepdims=True))
    grad_logits = jnp.sum(jnp.where(picks, grad_chosen[:, :, None], 0.0), axis=1).astype(
        jnp.bfloat16
    )
    grad_normed_ffn = grad_normed_ffn + jnp.dot(
        grad_logits, router.T, preferred_element_type=jnp.float32
    )
    expert_parts = (
        lax.psum_scatter(grad_w_in.astype(jnp.bfloat16), "dp", scatter_dimension=1, tiled=True),
        lax.psum_scatter(grad_w_down.astype(jnp.bfloat16), "dp", scatter_dimension=1, tiled=True),
    )
    return mixed, grad_logits, grad_normed_ffn, expert_parts


def gather_codes(expert_ids, priority):
    return lax.all_gather(expert_ids * PRIO + priority, "expert", axis=0)


def plan_tokens(codes, rows, top):
    expert = lax.axis_index("expert").astype(jnp.int32)
    place, info, other = expert_slots(codes // PRIO, codes % PRIO, expert, rows * top)
    other_hot = (other.reshape(-1, 1) == jnp.arange(128)[None, :]).astype(jnp.bfloat16)
    own_place = lax.all_to_all(place, "expert", split_axis=0, concat_axis=0, tiled=True)
    return place, info, other_hot, own_place


def exchange_tokens(normed_ffn, all_cotangents, plan, expert_ids, router, w_in, w_down):
    rows, width = normed_ffn.shape
    experts_total = router.shape[1]
    top = expert_ids.shape[1]
    expert = lax.axis_index("expert").astype(jnp.int32)
    place, info, other_hot, own_place = plan
    sources = place.shape[0]
    room = (rows * top + 16 * sources + 2 * MOE_ROWS - 1) // MOE_ROWS * MOE_ROWS
    sent, all_cotangents = lax.optimization_barrier((normed_ffn, all_cotangents))
    all_tokens = lax.all_gather(sent, "expert", axis=0, tiled=True)
    packed_cot, packed_other = pack(info, place, [all_cotangents, other_hot], room)
    (packed,) = pack(info, place, [all_tokens], room)
    wide_router = jnp.pad(router, ((0, 0), (0, 128 - experts_total)))
    grad_rows, mixed_rows, grad_gate, grad_w_in, grad_w_down = expert_layer(
        info, expert[None], packed, packed_other, packed_cot, wide_router, w_in[0], w_down[0], sources
    )
    grad_all, gate_all = unpack(info, place, [grad_rows, grad_gate], [jnp.bfloat16, jnp.float32])
    gate_all = jnp.sum(gate_all[:, :3], axis=1).reshape(sources, rows)
    gate_own = lax.all_to_all(gate_all, "expert", split_axis=0, concat_axis=0, tiled=True)
    grad_own = lax.psum_scatter(grad_all, "expert", scatter_dimension=0, tiled=True)
    send = 2 * rows * top // experts_total
    windows = jnp.concatenate([lax.dynamic_slice_in_dim(mixed_rows, info[d], send, 0) for d in range(sources)], axis=0)
    windows, grad_w_in, grad_w_down, grad_own = lax.optimization_barrier(
        (windows, grad_w_in, grad_w_down, grad_own)
    )
    mixed = (lax.all_to_all(windows, "expert", split_axis=0, concat_axis=0, tiled=True), own_place)
    expert_parts = (
        lax.psum_scatter(grad_w_in[None], "dp", scatter_dimension=1, tiled=True),
        lax.psum_scatter(grad_w_down[None], "dp", scatter_dimension=1, tiled=True),
    )
    logits = jnp.dot(normed_ffn, router, preferred_element_type=jnp.float32)
    picks = expert_ids[:, :, None] == jnp.arange(experts_total)[None, None, :]
    chosen = jnp.sum(jnp.where(picks, logits[:, None, :], 0.0), axis=2)
    gates = jax.nn.softmax(chosen, axis=-1)
    grad_gates = jnp.sum(jnp.where(picks, gate_own.T[:, None, :], 0.0), axis=2)
    grad_chosen = gates * (grad_gates - jnp.sum(gates * grad_gates, axis=-1, keepdims=True))
    grad_logits = jnp.sum(jnp.where(picks, grad_chosen[:, :, None], 0.0), axis=1).astype(
        jnp.bfloat16
    )
    grad_normed_ffn = grad_own.astype(jnp.float32) + jnp.dot(
        grad_logits, router.T, preferred_element_type=jnp.float32
    )
    return mixed, grad_logits, grad_normed_ffn, expert_parts


def per_device(
    tokens_in,
    cont_ids,
    expert_ids,
    priority,
    gain_attn,
    w_qkv,
    rel_table,
    w_out,
    gain_ffn,
    w_router,
    w_in,
    w_down,
    cotangent,
):
    rows, width = tokens_in.shape
    heads = rel_table.shape[1]
    dp_count = lax.axis_size("dp")
    dp_index = lax.axis_index("dp")
    prompt_rows = PROMPT // dp_count
    few_experts = lax.axis_size("expert") <= 16 and w_in.shape[0] == 1
    local_ids = cont_ids[0]
    info = info_of(local_ids, dp_index)
    row_start = row_start_of(local_ids)
    rows_bias = bias_rows(rel_table)
    if few_experts:
        codes = gather_codes(expert_ids, priority)
    experts_total = w_router.shape[1]
    dense = jnp.concatenate(
        [pairs_together(w_qkv), w_out, jnp.pad(w_router, ((0, 0), (0, 128 - experts_total)))], axis=1
    )
    dense = lax.all_gather(dense, ("dp", "expert"), axis=0, tiled=True)
    part_heads = heads // PARTS
    tables = [bias_tables(info, rows_bias, row_start, g * part_heads, part_heads) for g in range(PARTS)]
    dense, tables[0] = lax.optimization_barrier((dense, tables[0]))
    if few_experts:
        plan = plan_tokens(codes, rows, expert_ids.shape[1])
        dense, plan = lax.optimization_barrier((dense, plan))
    whole_qkv, whole_out = dense[:, : 3 * width], dense[:, 3 * width : 4 * width]
    whole_router = dense[:, 4 * width : 4 * width + experts_total]
    inputs = tokens_in.astype(jnp.float32)
    normed_attn = normed(inputs, gain_attn).astype(jnp.bfloat16)
    projected = jnp.dot(normed_attn, whole_qkv, preferred_element_type=jnp.float32).astype(
        jnp.bfloat16
    )
    parts = PARTS
    columns = 2 * width // parts
    kept = [projected[:, width + columns * g : width + columns * (g + 1)] for g in range(parts)]
    gathered = [lax.all_gather(kv[:prompt_rows], "dp", axis=0, tiled=True) for kv in kept]
    if few_experts:
        late_cotangent, gathered[0] = lax.optimization_barrier((cotangent, gathered[0]))
        all_cotangents = lax.all_gather(late_cotangent, "expert", axis=0, tiled=True)
    gathered[0], tables = lax.optimization_barrier((gathered[0], tables))
    keys_values = []
    exact, log_total = [], []
    for g in range(parts):
        if g:
            gathered[g], exact[-1] = lax.optimization_barrier((gathered[g], exact[-1]))
        keys_values.append(jnp.concatenate([gathered[g], kept[g][prompt_rows:]], axis=0))
        out, total = attention_forward(info, projected, keys_values[g], tables[g], g)
        exact.append(out)
        log_total.append(total)
    attended = jnp.concatenate(exact, axis=1).astype(jnp.bfloat16)
    middle = inputs + jnp.dot(attended, whole_out, preferred_element_type=jnp.float32)
    normed_ffn = normed(middle, gain_ffn).astype(jnp.bfloat16)
    if few_experts:
        mixed, grad_logits, grad_normed_ffn, expert_parts = exchange_tokens(
            normed_ffn, all_cotangents, plan, expert_ids, whole_router, w_in, w_down
        )
    else:
        mixed, grad_logits, grad_normed_ffn, expert_parts = exchange_pairs(
            normed_ffn, middle, cotangent, expert_ids, priority, whole_router, w_in, w_down
        )
    grad_out = cotangent.astype(jnp.float32)
    grad_router = jnp.dot(normed_ffn.T, grad_logits, preferred_element_type=jnp.float32)
    _, ffn_norm_back = jax.vjp(normed, middle, gain_ffn)
    grad_middle_part, grad_gain_ffn = ffn_norm_back(grad_normed_ffn)
    grad_middle = grad_out + grad_middle_part
    grad_branch = grad_middle.astype(jnp.bfloat16)
    grad_out_weight = jnp.dot(attended.T, grad_branch, preferred_element_type=jnp.float32)
    grad_attended = jnp.dot(
        grad_branch, whole_out.T, preferred_element_type=jnp.float32
    ).astype(jnp.bfloat16)
    grad_queries, grad_prompts, grad_conts, grad_lines = [], [], [], []
    for g in range(parts):
        if g:
            grad_attended, expert_parts, grad_queries[-1] = lax.optimization_barrier(
                (grad_attended, expert_parts, grad_queries[-1])
            )
        grad_query, grad_kv, lines = attention_backward(
            info, projected, grad_attended, exact[g], log_total[g], keys_values[g], tables[g], g
        )
        grad_queries.append(grad_query)
        grad_prompts.append(lax.psum_scatter(grad_kv[:PROMPT], "dp", scatter_dimension=0, tiled=True))
        grad_conts.append(grad_kv[PROMPT:])
        grad_lines.append(lines)
    mixed, middle, grad_queries[-1] = lax.optimization_barrier((mixed, middle, grad_queries[-1]))
    if few_experts:
        returned, own_place = mixed
        mixed = collect(own_place, returned, returned.shape[0] // own_place.shape[0])
    output = (middle + mixed).astype(jnp.bfloat16)
    grad_table = table_grad(jnp.concatenate(grad_lines, axis=0), rel_table.shape[0])
    grad_projected = jnp.concatenate(
        grad_queries + [jnp.concatenate([a, b], axis=0) for a, b in zip(grad_prompts, grad_conts)], axis=1
    )
    grad_normed_attn = jnp.dot(grad_projected, whole_qkv.T, preferred_element_type=jnp.float32)
    grad_qkv = jnp.dot(normed_attn.T, grad_projected, preferred_element_type=jnp.float32)
    _, attn_norm_back = jax.vjp(normed, inputs, gain_attn)
    grad_inputs_part, grad_gain_attn = attn_norm_back(grad_normed_attn)
    grad_tokens = grad_middle + grad_inputs_part
    dense_grad = lax.psum_scatter(
        jnp.concatenate([grad_qkv, grad_out_weight], axis=1), ("dp", "expert"), scatter_dimension=0, tiled=True
    )
    own_router = lax.psum_scatter(grad_router, ("dp", "expert"), scatter_dimension=0, tiled=True)
    small_parts = lax.psum((grad_gain_attn, grad_gain_ffn, grad_table.T), ("dp", "expert"))
    return (
        output,
        grad_tokens,
        small_parts[0],
        pairs_apart(dense_grad[:, : 3 * width]),
        small_parts[2],
        dense_grad[:, 3 * width :],
        small_parts[1],
        own_router,
        expert_parts[0].astype(jnp.float32),
        expert_parts[1].astype(jnp.float32),
    )


def solution(mesh):
    return jax.shard_map(
        per_device,
        mesh=mesh,
        in_specs=(
            P(("dp", "expert"), None),
            P(("dp", "expert"), None),
            P(("dp", "expert"), None),
            P(("dp", "expert"), None),
            P(),
            P(("dp", "expert"), None),
            P(),
            P(("dp", "expert"), None),
            P(),
            P(("dp", "expert"), None),
            P("expert", None, None),
            P("expert", None, None),
            P(("dp", "expert"), None),
        ),
        out_specs=(
            P(("dp", "expert"), None),
            P(("dp", "expert"), None),
            P(),
            P(("dp", "expert"), None),
            P(),
            P(("dp", "expert"), None),
            P(),
            P(("dp", "expert"), None),
            P("expert", "dp", None),
            P("expert", "dp", None),
        ),
        check_vma=False,
    )
```

```python
import functools
import math
import jax
import jax.numpy as jnp
from jax import lax
from jax.experimental import pallas as pl
from jax.experimental.pallas import tpu as pltpu
from jax.sharding import PartitionSpec as P

PRIO = 4
PROMPT = 2048


BORDERS = (16, 24, 32, 48, 64, 96, 128, 192, 256, 384, 512, 768, 1024, 1536, 2048)
EPSILON = 1e-06
MASKED = -1e30


def bucket_of(distance):
    distance = jnp.maximum(distance, 0)
    counted = jnp.minimum(distance, 15)
    for border in BORDERS:
        counted = counted + (distance >= border).astype(jnp.int32)
    return counted


def normed(values, gain):
    return values * lax.rsqrt(jnp.mean(values * values, axis=-1, keepdims=True) + EPSILON) * gain


def pairs_together(w_qkv):
    width = w_qkv.shape[1] // 3
    rows = w_qkv.shape[0]
    keys_values = w_qkv[:, width:].reshape(rows, 2, width // 128, 128).swapaxes(1, 2)
    return jnp.concatenate([w_qkv[:, :width], keys_values.reshape(rows, 2 * width)], axis=1)


def pairs_apart(grad):
    width = grad.shape[1] // 3
    rows = grad.shape[0]
    keys_values = grad[:, width:].reshape(rows, width // 128, 2, 128).swapaxes(1, 2)
    return jnp.concatenate([grad[:, :width], keys_values.reshape(rows, 2 * width)], axis=1)


LOG2E = math.log2(math.e)
F32, BF16 = jnp.float32, jnp.bfloat16
QT = 256
KT = 512
RUN = 256
PARTS = 2
ROWS = 32
NT = (((1,), (1,)), ((), ()))
NN = (((1,), (0,)), ((), ()))

def dot(a, b, dims=NN):
    return lax.dot_general(a, b, dims, preferred_element_type=F32)

def bias_rows(rel_table):
    width = PROMPT + 512 + RUN
    distance = PROMPT + RUN - jnp.arange(width)[None, :] + jnp.arange(8)[:, None]
    bucket = bucket_of(distance)
    table = rel_table.T[:, None, None, :] * LOG2E
    hot = (bucket[..., None] == jnp.arange(rel_table.shape[0])).astype(F32)
    rows = jnp.sum(hot[None] * table, axis=-1)
    return jnp.where(distance[None] >= 0, rows, MASKED)

def bias_kernel(info, base_ref, row_start, t_ref, b_ref):
    base, t_scr, b_scr = base_ref[0], t_ref.at[0], b_ref.at[0]
    width = base.shape[-1]
    for a in range(16):
        t_scr[8 * a:8 * a + 8, :] = pltpu.roll(base, 8 * a, 1) if a else base
    lane = lax.broadcasted_iota(jnp.int32, (ROWS, 128), 1)
    sub = lax.broadcasted_iota(jnp.int32, (ROWS, 128), 0)
    for s in range(4):
        start, end = info[s], info[s + 1]
        turn = start % 128
        left = (128 - turn) % 128
        here = (lane < left) | (left == 0)
        def place(g, _):
            at = pl.ds(pl.multiple_of(ROWS * g, ROWS), ROWS)
            first = start - turn + RUN - 128 * (g // (128 // ROWS))
            of = pl.ds(pl.multiple_of(ROWS * (g % (128 // ROWS)), ROWS), ROWS)
            mine = sub + ROWS * g >= start
            turned = None
            for b in range(PROMPT // 128 + 1):
                after = pltpu.roll(t_scr[of, pl.ds(pl.multiple_of(first + 128 * b, 128), 128)], left, 1)
                if b:
                    cols = slice(128 * b - 128, 128 * b)
                    b_scr[at, cols] = jnp.where(mine, jnp.where(here, turned, after), b_scr[at, cols])
                turned = after
            return 0
        lax.fori_loop(start // ROWS, (end + ROWS - 1) // ROWS, place, 0)
    lane = lax.broadcasted_iota(jnp.int32, (128, 128), 1)
    for i in range(KT // 128):
        rows = slice(128 * i, 128 * i + 128)
        own = row_start[rows, :]
        for b in range(KT // 128):
            first = PROMPT + RUN - 128 * i + 128 * b
            b_scr[rows, PROMPT + 128 * b:PROMPT + 128 * b + 128] = jnp.where(
                lane + 128 * b >= own, t_scr[:, first:first + 128], MASKED)

def bias_tables(info, rows_bias, row_start, first, heads):
    wide = rows_bias.shape[2]
    block = lambda rows, cols: pl.BlockSpec((1, rows, cols), lambda h, *_: (h, 0, 0))
    return pl.pallas_call(
        bias_kernel,
        grid_spec=pltpu.PrefetchScalarGridSpec(
            num_scalar_prefetch=1, grid=(heads,),
            in_specs=[pl.BlockSpec((1, 8, wide), lambda h, *_: (first + h, 0, 0)),
                      pl.BlockSpec((KT, 128), lambda h, *_: (0, 0))],
            out_specs=[block(128, wide), block(KT, PROMPT + KT)]),
        out_shape=[jax.ShapeDtypeStruct((heads, 128, wide), F32),
                   jax.ShapeDtypeStruct((heads, KT, PROMPT + KT), F32)],
        compiler_params=pltpu.CompilerParams(vmem_limit_bytes=32 << 20),
        cost_estimate=pl.CostEstimate(flops=0, bytes_accessed=heads * KT * (PROMPT + KT) * 8, transcendentals=0),
        name="bias_tables",
    )(info, rows_bias, row_start)

def own_lanes(h, rows):
    lane = lax.broadcasted_iota(jnp.int32, (rows, 128), 1)
    return lane // 64 == h % 2

def fwd_kernel(scale2, info, q_ref, k_ref, v_ref, t_ref, b_ref, o_ref, lse_ref):
    h = pl.program_id(0)
    dp = info[5]
    t_scr, b_scr = t_ref.at[0], b_ref.at[0]
    own = own_lanes(h, QT)
    head_lane = lax.broadcasted_iota(jnp.int32, (QT, 128), 1) == h

    def tile(first, key_tiles, bias_of, block):
        rows = pl.ds(first, QT)
        q = jnp.where(own, q_ref[rows, :], jnp.zeros((), BF16))
        def step(t, carry):
            m, l, acc = carry
            cols = pl.ds(pl.multiple_of(block(t) * KT, KT), KT)
            s = dot(q, k_ref[cols, :], NT) * scale2 + bias_of(t)
            new = jnp.maximum(m, jnp.max(s, axis=1, keepdims=True))
            keep = jnp.exp2(m - new)
            p = jnp.exp2(s - jnp.concatenate([new] * (KT // 128), axis=1))
            part = p[:, :128]
            for c in range(1, KT // 128):
                part = part + p[:, 128 * c:128 * (c + 1)]
            return new, l * keep + part, acc * keep + dot(p.astype(BF16), v_ref[cols, :])
        zero = jnp.zeros((QT, 128), F32)
        m, l, acc = lax.fori_loop(0, key_tiles, step, (jnp.full((QT, 128), MASKED, F32), zero, zero))
        l = jnp.sum(l, axis=1, keepdims=True)
        o_ref[rows, :] = jnp.where(own, acc / l, o_ref[rows, :])
        lse_ref[rows, :] = jnp.where(head_lane, m + jnp.log2(l), lse_ref[rows, :])

    for j in range(2):
        shift = PROMPT - KT * dp - QT * j + RUN
        def bias(t, shift=shift):
            first = (dp - t) * KT + shift
            return jnp.concatenate([t_scr[:, pl.ds(pl.multiple_of(first - 128 * x, 128), KT)] for x in range(QT // 128)], axis=0)
        tile(QT * j, dp + 1, bias, lambda t: dp - t)
    for j in range(2):
        tile(KT + QT * j, PROMPT // KT + 1,
             lambda t: b_scr[pl.ds(QT * j, QT), pl.ds(pl.multiple_of(t * KT, KT), KT)], lambda t: t)

def attention_forward(info, projected, keys_values, tables, part):
    n = projected.shape[0]
    keys, columns = keys_values.shape
    heads = columns // 128
    head_size = 64
    scale2 = head_size ** -0.5 * LOG2E
    first = part * heads // 2
    return pl.pallas_call(
        functools.partial(fwd_kernel, scale2),
        grid_spec=pltpu.PrefetchScalarGridSpec(
            num_scalar_prefetch=1, grid=(heads,),
            in_specs=[pl.BlockSpec((n, 128), lambda h, *_: (0, first + h // 2)),
                      pl.BlockSpec((keys, 128), lambda h, *_: (0, h // 2 * 2)),
                      pl.BlockSpec((keys, 128), lambda h, *_: (0, h // 2 * 2 + 1)),
                      *[pl.BlockSpec((1,) + t.shape[1:], lambda h, *_: (h, 0, 0)) for t in tables]],
            out_specs=[pl.BlockSpec((n, 128), lambda h, *_: (0, h // 2)),
                       pl.BlockSpec((n, 128), lambda h, *_: (0, 0))]),
        out_shape=[jax.ShapeDtypeStruct((n, heads * 64), F32), jax.ShapeDtypeStruct((n, 128), F32)],
        compiler_params=pltpu.CompilerParams(vmem_limit_bytes=60 << 20),
        cost_estimate=pl.CostEstimate(flops=heads * n * keys * 128 * 4, bytes_accessed=n * keys * 4, transcendentals=heads * n * keys),
        name="attention_forward",
    )(info, projected, keys_values, keys_values, *tables)

def split3(x):
    hi = x.astype(BF16)
    rest = x - hi.astype(F32)
    mid = rest.astype(BF16)
    return hi, mid, (rest - mid.astype(F32)).astype(BF16)

def bwd_kernel(scale, info, q_ref, do_ref, o_ref, lse_ref, k_ref, v_ref, t_ref, b_ref,
               dq_ref, dkv_ref, dd_ref,
               e_scr, db_scr, qa, da, ka, va, qt, dot_t, dkt, dvt):
    h = pl.program_id(0)
    dp = info[5]
    n, keys = q_ref.shape[0], k_ref.shape[0]
    half = h % 2
    t_scr, b_scr = t_ref.at[0], b_ref.at[0]
    base = pl.multiple_of(64 * half, 64)
    other = 64 - 64 * half

    @pl.when(half == 0)
    def _():
        qt[...] = q_ref[...].T
        dot_t[...] = do_ref[...].T
        dq_ref[...] = jnp.zeros_like(dq_ref)

    lane_n = lax.broadcasted_iota(jnp.int32, (QT, 128), 1)
    own_n = lane_n // 64 == half
    def augment(i, _):
        rows = pl.ds(pl.multiple_of(i * QT, QT), QT)
        lse = jnp.sum(jnp.where(lane_n == h, lse_ref[rows, :], 0.0), axis=1, keepdims=True)
        parts = split3(-lse / (scale * LOG2E))
        aug = jnp.zeros((QT, 128), BF16)
        for x in range(3):
            aug = jnp.where(lane_n == other + x, jnp.broadcast_to(parts[x], (QT, 128)), aug)
        qa[rows, :] = jnp.where(own_n, q_ref[rows, :], aug)
        do = do_ref[rows, :]
        delta = jnp.sum(jnp.where(own_n, do.astype(F32) * o_ref[rows, :], 0.0), axis=1, keepdims=True)
        parts = split3(-delta)
        aug = jnp.zeros((QT, 128), BF16)
        for x in range(3):
            aug = jnp.where(lane_n == other + x, jnp.broadcast_to(parts[x], (QT, 128)), aug)
        da[rows, :] = jnp.where(own_n, do, aug)
        return 0
    lax.fori_loop(0, n // QT, augment, 0)
    lane_k = lax.broadcasted_iota(jnp.int32, (KT, 128), 1)
    ones = jnp.where((lane_k >= other) & (lane_k < other + 3), 1.0, 0.0).astype(BF16)
    own_k = lane_k // 64 == half
    def augment_keys(i, _):
        rows = pl.ds(pl.multiple_of(i * KT, KT), KT)
        ka[rows, :] = jnp.where(own_k, k_ref[rows, :], ones)
        va[rows, :] = jnp.where(own_k, v_ref[rows, :], ones)
        return 0
    lax.fori_loop(0, keys // KT, augment_keys, 0)
    head_rows = pl.ds(base, 64)
    dkt[head_rows, :] = jnp.zeros((64, keys), F32)
    dvt[head_rows, :] = jnp.zeros((64, keys), F32)
    e_scr[...] = jnp.zeros_like(e_scr)

    def tile(first, key_tiles, bias_of, grad_bias):
        rows = pl.ds(first, QT)
        q, do = qa[rows, :], da[rows, :]
        q_t, do_t = qt[head_rows, rows], dot_t[head_rows, rows]
        def step(t, dq):
            cols = pl.ds(pl.multiple_of(t * KT, KT), KT)
            kk = ka[cols, :]
            p = jnp.exp2(dot(q, kk, NT) * (scale * LOG2E) + bias_of(t))
            ds = p * dot(do, va[cols, :], NT)
            grad_bias(t, ds)
            low = ds.astype(BF16)
            dvt[head_rows, cols] += dot(do_t, p.astype(BF16))
            dkt[head_rows, cols] += dot(q_t, low)
            return dq + dot(low, kk)
        dq = lax.fori_loop(0, key_tiles, step, jnp.zeros((QT, 128), F32))
        dq_ref[rows, :] = jnp.where(own_n, dq * scale, dq_ref[rows, :].astype(F32)).astype(BF16)

    for j in range(2):
        shift = PROMPT - KT * dp - QT * j + RUN
        def part(t, x, shift=shift):
            return (slice(None), pl.ds(pl.multiple_of(t * KT + shift - 128 * x, 128), KT))
        def bias(t):
            return jnp.concatenate([t_scr[part(t, x)] for x in range(QT // 128)], axis=0)
        def add(t, ds):
            for x in range(QT // 128):
                e_scr[part(t, x)] += ds[128 * x:128 * x + 128, :]
        tile(QT * j, dp + 1, bias, add)
    for j in range(2):
        def where(t):
            return (pl.ds(QT * j, QT), pl.ds(pl.multiple_of(t * KT, KT), KT))
        def put(t, ds):
            db_scr[where(t)] = ds
        tile(KT + QT * j, PROMPT // KT + 1, lambda t: b_scr[where(t)], put)

    lane = lax.broadcasted_iota(jnp.int32, (ROWS, 128), 1)
    sub = lax.broadcasted_iota(jnp.int32, (ROWS, 128), 0)
    for s in range(4):
        start, end = info[s], info[s + 1]
        turn = start % 128
        def fold(g, _):
            at = pl.ds(pl.multiple_of(ROWS * g, ROWS), ROWS)
            first = start - turn + RUN - 128 * (g // (128 // ROWS))
            to = pl.ds(pl.multiple_of(ROWS * (g % (128 // ROWS)), ROWS), ROWS)
            mine = (sub + ROWS * g >= start) & (sub + ROWS * g < end)
            before = jnp.zeros((ROWS, 128), F32)
            for b in range(PROMPT // 128 + 1):
                if b < PROMPT // 128:
                    turned = pltpu.roll(jnp.where(mine, db_scr[at, 128 * b:128 * b + 128], 0.0), turn, 1)
                else:
                    turned = jnp.zeros((ROWS, 128), F32)
                e_scr[to, pl.ds(pl.multiple_of(first + 128 * b, 128), 128)] += jnp.where(lane >= turn, turned, before)
                before = turned
            return 0
        lax.fori_loop(start // ROWS, (end + ROWS - 1) // ROWS, fold, 0)
    for i in range(KT // 128):
        first = PROMPT + RUN - 128 * i
        e_scr[:, first:first + KT] += db_scr[128 * i:128 * i + 128, PROMPT:]
    width = t_ref.shape[2]
    acc = e_scr[0:8, :]
    for a in range(1, 16):
        acc = acc + pltpu.roll(e_scr[8 * a:8 * a + 8, :], width - 8 * a, 1)
    total = acc[0:1, :]
    for i in range(1, 8):
        total = total + pltpu.roll(acc, width - i, 1)[i:i + 1, :]
    dd_ref[0] = total

    @pl.when(half == 1)
    def _():
        dkv_ref[:, :128] = (dkt[...] * scale).T.astype(BF16)
        dkv_ref[:, 128:] = dvt[...].T.astype(BF16)

def attention_backward(info, projected, do, o32, lse, keys_values, tables, part):
    n = projected.shape[0]
    keys, columns = keys_values.shape
    heads = columns // 128
    wide = tables[0].shape[2]
    first = part * heads // 2
    own = pl.BlockSpec((n, 128), lambda h, *_: (0, h // 2))
    shifted = pl.BlockSpec((n, 128), lambda h, *_: (0, first + h // 2))
    cols = PROMPT + KT
    return pl.pallas_call(
        functools.partial(bwd_kernel, 64 ** -0.5),
        grid_spec=pltpu.PrefetchScalarGridSpec(
            num_scalar_prefetch=1, grid=(heads,),
            in_specs=[shifted, shifted, own, pl.BlockSpec((n, 128), lambda h, *_: (0, 0)),
                      pl.BlockSpec((keys, 128), lambda h, *_: (0, h // 2 * 2)),
                      pl.BlockSpec((keys, 128), lambda h, *_: (0, h // 2 * 2 + 1)),
                      *[pl.BlockSpec((1,) + t.shape[1:], lambda h, *_: (h, 0, 0)) for t in tables]],
            out_specs=[own, pl.BlockSpec((keys, 256), lambda h, *_: (0, h // 2)),
                       pl.BlockSpec((1, 1, wide), lambda h, *_: (h, 0, 0))],
            scratch_shapes=[pltpu.VMEM((128, wide), F32), pltpu.VMEM((KT, cols), F32),
                            pltpu.VMEM((n, 128), BF16), pltpu.VMEM((n, 128), BF16),
                            pltpu.VMEM((keys, 128), BF16), pltpu.VMEM((keys, 128), BF16),
                            pltpu.VMEM((128, n), BF16), pltpu.VMEM((128, n), BF16),
                            pltpu.VMEM((128, keys), F32), pltpu.VMEM((128, keys), F32)]),
        out_shape=[jax.ShapeDtypeStruct((n, heads * 64), BF16), jax.ShapeDtypeStruct((keys, columns), BF16),
                   jax.ShapeDtypeStruct((heads, 1, wide), F32)],
        compiler_params=pltpu.CompilerParams(vmem_limit_bytes=60 << 20),
        cost_estimate=pl.CostEstimate(flops=heads * n * keys * 128 * 10, bytes_accessed=n * keys * 4, transcendentals=heads * n * keys),
        name="attention_backward",
    )(info, projected, do, o32, lse, keys_values, keys_values, *tables)

def info_of(ids, dp):
    starts = jnp.sum((ids[None, :] < jnp.arange(5)[:, None]).astype(jnp.int32), axis=1)
    return jnp.concatenate([starts, jnp.reshape(dp, (1,)).astype(jnp.int32)])

def table_grad(dd, buckets):
    width = dd.shape[2]
    distance = PROMPT + RUN - jnp.arange(width)
    hot = ((bucket_of(distance)[:, None] == jnp.arange(buckets)[None, :]) & (distance >= 0)[:, None]).astype(F32)
    return jnp.dot(dd[:, 0, :], hot, precision=lax.Precision.HIGHEST)

def row_start_of(ids):
    starts = jnp.sum((ids[None, :] < ids[:, None]).astype(jnp.int32), axis=1)
    return jnp.broadcast_to(starts[:, None], (ids.shape[0], 128))


TN = (((0,), (0,)), ((), ()))
MOE_ROWS = 256
FF_TILE = 768


def expert_slots(ids, levels, expert, capacity):
    hits = ids == expert
    hit = jnp.any(hits, axis=2)
    level = jnp.sum(jnp.where(hits, levels, 0), axis=2)
    hot = hit[:, :, None] & (level[:, :, None] == jnp.arange(PRIO)[None, None, :])
    tokens = ids.shape[1]
    earlier = (jnp.arange(tokens)[:, None] > jnp.arange(tokens)[None, :]).astype(BF16)
    rank = jnp.einsum("ut,dtl->dul", earlier, hot.astype(BF16), preferred_element_type=F32).astype(jnp.int32)
    counts = jnp.sum(hot.astype(jnp.int32), axis=1)
    totals = jnp.sum(counts, axis=0)
    lower = jnp.cumsum(totals) - totals
    base = lower[None, :] + jnp.cumsum(counts, axis=0) - counts
    slot = jnp.sum(jnp.where(hot, base[:, None, :] + rank, 0), axis=2)
    kept = hit & (slot < capacity)
    rank = jnp.einsum("ut,dt->du", earlier, kept.astype(BF16), preferred_element_type=F32).astype(jnp.int32)
    place = jnp.where(kept, rank, -1)
    sizes = jnp.sum(kept.astype(jnp.int32), axis=1)
    padded = (sizes + 15) // 16 * 16
    ends = jnp.cumsum(padded)
    other = jnp.sum(jnp.where(hits, 0, ids), axis=2)
    return place, jnp.concatenate([ends - padded, sizes, ends[-1:]]).astype(jnp.int32), other


def pack_kernel(sources, info, place_ref, *refs):
    ins, outs = refs[:len(refs) // 2], refs[len(refs) // 2:]
    d = pl.program_id(0)

    @pl.when(d == 0)
    def _():
        for out in outs:
            out[...] = jnp.zeros_like(out)

    tokens = place_ref.shape[2]
    row = lax.broadcasted_iota(jnp.int32, (MOE_ROWS, tokens), 0)

    def chunk(j, _):
        pick = jnp.where(place_ref[0] == row + MOE_ROWS * j, 1.0, 0.0).astype(BF16)
        at = pl.ds(pl.multiple_of(info[d] + MOE_ROWS * j, 16), MOE_ROWS)
        for x, out in zip(ins, outs):
            out[at, :] = dot(pick, x[...]).astype(BF16)
        return 0
    lax.fori_loop(0, (info[sources + d] + MOE_ROWS - 1) // MOE_ROWS, chunk, 0)


def pack(info, place, arrays, room):
    sources, tokens = place.shape
    return pl.pallas_call(
        functools.partial(pack_kernel, sources),
        grid_spec=pltpu.PrefetchScalarGridSpec(
            num_scalar_prefetch=1, grid=(sources,),
            in_specs=[pl.BlockSpec((1, 1, tokens), lambda d, *_: (d, 0, 0))]
            + [pl.BlockSpec((tokens, x.shape[1]), lambda d, *_: (d, 0)) for x in arrays],
            out_specs=[pl.BlockSpec((room, x.shape[1]), lambda d, *_: (0, 0)) for x in arrays]),
        out_shape=[jax.ShapeDtypeStruct((room, x.shape[1]), BF16) for x in arrays],
        compiler_params=pltpu.CompilerParams(vmem_limit_bytes=40 << 20),
        name="pack_tokens",
    )(info, place[:, None, :], *arrays)


def unpack_kernel(send, info, place_ref, *refs):
    ins, outs = refs[:len(refs) // 2], refs[len(refs) // 2:]
    tokens = place_ref.shape[0]
    lane = lax.broadcasted_iota(jnp.int32, (tokens, 128), 1)
    put = jnp.concatenate(
        [jnp.where(place_ref[...] == lane + 128 * b, 1.0, 0.0).astype(BF16) for b in range(send // 128)], axis=1)
    at = pl.ds(pl.multiple_of(info[pl.program_id(0)], 16), send)
    for x, out in zip(ins, outs):
        out[...] = dot(put, x[at, :]).astype(out.dtype)


def unpack(info, place, arrays, dtypes, send):
    sources, tokens = place.shape
    spread = jnp.broadcast_to(place.reshape(-1, 1), (sources * tokens, 128))
    return pl.pallas_call(
        functools.partial(unpack_kernel, send),
        grid_spec=pltpu.PrefetchScalarGridSpec(
            num_scalar_prefetch=1, grid=(sources,),
            in_specs=[pl.BlockSpec((tokens, 128), lambda d, *_: (d, 0))]
            + [pl.BlockSpec(x.shape, lambda d, *_: (0, 0)) for x in arrays],
            out_specs=[pl.BlockSpec((tokens, x.shape[1]), lambda d, *_: (d, 0)) for x in arrays]),
        out_shape=[jax.ShapeDtypeStruct((sources * tokens, x.shape[1]), t) for x, t in zip(arrays, dtypes)],
        compiler_params=pltpu.CompilerParams(vmem_limit_bytes=40 << 20),
        name="unpack_tokens",
    )(info, spread, *arrays)


def collect_kernel(place_ref, x_ref, out_ref):
    tokens = place_ref.shape[0]
    lane = lax.broadcasted_iota(jnp.int32, (tokens, 128), 1)
    put = jnp.concatenate(
        [jnp.where(place_ref[...] == lane + 128 * b, 1.0, 0.0).astype(BF16) for b in range(x_ref.shape[0] // 128)],
        axis=1)
    total = dot(put, x_ref[...])

    @pl.when(pl.program_id(0) == 0)
    def _():
        out_ref[...] = total

    @pl.when(pl.program_id(0) > 0)
    def _():
        out_ref[...] += total


def collect(place, returned, send):
    experts, tokens = place.shape
    width = returned.shape[1]
    spread = jnp.broadcast_to(place.reshape(-1, 1), (experts * tokens, 128))
    return pl.pallas_call(
        collect_kernel,
        grid=(experts,),
        in_specs=[pl.BlockSpec((tokens, 128), lambda e: (e, 0)), pl.BlockSpec((send, width), lambda e: (e, 0))],
        out_specs=pl.BlockSpec((tokens, width), lambda e: (0, 0)),
        out_shape=jax.ShapeDtypeStruct((tokens, width), F32),
        compiler_params=pltpu.CompilerParams(vmem_limit_bytes=40 << 20),
        name="collect_rows",
    )(spread, returned)


def gelu_and_slope(v):
    c = math.sqrt(2.0 / math.pi)
    t = jnp.tanh(c * (v + 0.044715 * (v * v * v)))
    half = 0.5 * (1.0 + t)
    return v * half, half + 0.5 * v * (1.0 - t * t) * (c * (1.0 + 3 * 0.044715 * (v * v)))


def expert_kernel(sources, info, expert, x_ref, o_ref, c_ref, r_ref, wi_ref, wd_ref,
                  gi_ref, eo_ref, gg_ref, dwi_ref, dwd_ref, geo, gate, eo, gi, dwi, dwd):
    f = pl.program_id(0)
    last = pl.num_programs(0) - 1
    tiles = (info[2 * sources] + MOE_ROWS - 1) // MOE_ROWS
    lane = lax.broadcasted_iota(jnp.int32, (MOE_ROWS, 128), 1)

    def rows_of(i):
        return pl.ds(pl.multiple_of(i * MOE_ROWS, MOE_ROWS), MOE_ROWS)

    @pl.when(f == 0)
    def _():
        gi_ref[...] = jnp.zeros_like(gi_ref)
        eo_ref[...] = jnp.zeros_like(eo_ref)
        gg_ref[...] = jnp.zeros_like(gg_ref)

        def start(i, _):
            at = rows_of(i)
            logits = dot(x_ref[at, :], r_ref[...])
            mine = jnp.sum(jnp.where(lane == expert[0], logits, 0.0), axis=1, keepdims=True)
            other = jnp.sum(jnp.where(o_ref[at, :] > 0, logits, 0.0), axis=1, keepdims=True)
            top = jnp.maximum(mine, other)
            a, b = jnp.exp(mine - top), jnp.exp(other - top)
            g = a / (a + b)
            gate[at, :] = jnp.broadcast_to(g, (MOE_ROWS, 128))
            geo[at, :] = (c_ref[at, :].astype(F32) * g).astype(BF16)
            eo[at, :] = jnp.zeros((MOE_ROWS, eo.shape[1]), F32)
            gi[at, :] = jnp.zeros((MOE_ROWS, gi.shape[1]), F32)
            return 0
        lax.fori_loop(0, tiles, start, 0)

    dwi[...] = jnp.zeros_like(dwi)
    dwd[...] = jnp.zeros_like(dwd)

    def tile(i, _):
        at = rows_of(i)
        x, g = x_ref[at, :], geo[at, :]
        act, slope = gelu_and_slope(dot(x, wi_ref[...]))
        act = act.astype(BF16)
        eo[at, :] += dot(act, wd_ref[...])
        gh = (dot(g, wd_ref[...], NT) * slope).astype(BF16)
        gi[at, :] += dot(gh, wi_ref[...], NT)
        dwd[...] += dot(act, g, TN)
        dwi[...] += dot(x, gh, TN)
        return 0
    lax.fori_loop(0, tiles, tile, 0)
    dwi_ref[...] = dwi[...].astype(BF16)
    dwd_ref[...] = dwd[...].astype(BF16)

    @pl.when(f == last)
    def _():
        def finish(i, _):
            at = rows_of(i)
            out = eo[at, :].astype(BF16).astype(F32)
            gg = jnp.sum(out * c_ref[at, :].astype(F32), axis=1, keepdims=True)
            parts = split3(gg)
            spread = jnp.zeros((MOE_ROWS, 128), BF16)
            for n in range(3):
                spread = jnp.where(lane == n, jnp.broadcast_to(parts[n], (MOE_ROWS, 128)), spread)
            gg_ref[at, :] = spread
            eo_ref[at, :] = (out * gate[at, :1]).astype(BF16)
            gi_ref[at, :] = gi[at, :].astype(BF16)
            return 0
        lax.fori_loop(0, tiles, finish, 0)


def expert_layer(info, expert, x, other, cot, router, w_in, w_down, sources):
    room, width = x.shape
    hidden = w_in.shape[1]
    whole = lambda a: pl.BlockSpec(a.shape, lambda f, *_: (0, 0))
    fixed = lambda cols: pl.BlockSpec((room, cols), lambda f, *_: (0, 0))
    return pl.pallas_call(
        functools.partial(expert_kernel, sources),
        grid_spec=pltpu.PrefetchScalarGridSpec(
            num_scalar_prefetch=2, grid=(hidden // FF_TILE,),
            in_specs=[whole(x), whole(other), whole(cot), whole(router),
                      pl.BlockSpec((width, FF_TILE), lambda f, *_: (0, f)),
                      pl.BlockSpec((FF_TILE, width), lambda f, *_: (f, 0))],
            out_specs=[fixed(width), fixed(width), fixed(128),
                       pl.BlockSpec((width, FF_TILE), lambda f, *_: (0, f)),
                       pl.BlockSpec((FF_TILE, width), lambda f, *_: (f, 0))],
            scratch_shapes=[pltpu.VMEM((room, width), BF16), pltpu.VMEM((room, 128), F32),
                            pltpu.VMEM((room, width), F32), pltpu.VMEM((room, width), F32),
                            pltpu.VMEM((width, FF_TILE), F32), pltpu.VMEM((FF_TILE, width), F32)]),
        out_shape=[jax.ShapeDtypeStruct((room, width), BF16), jax.ShapeDtypeStruct((room, width), BF16),
                   jax.ShapeDtypeStruct((room, 128), BF16),
                   jax.ShapeDtypeStruct(w_in.shape, BF16), jax.ShapeDtypeStruct(w_down.shape, BF16)],
        compiler_params=pltpu.CompilerParams(vmem_limit_bytes=63 << 20),
        name="expert_layer",
    )(info, expert, x, other, cot, router, w_in, w_down)


MESH_ID = pl.DeviceIdType.MESH


def dense_kernel(q_ref, w_ref, s_ref, out_ref, small_ref, give, h, r0, ra1, rb1, ra2, rb2, rz, s_acc, s_got, s_all,
                 send, recv, s_send, s_recv):
    i, j = lax.axis_index("dp"), lax.axis_index("expert")
    y, x, z, c = i // 2, i % 2, j // 2, j % 2
    other_core = (i, z * 2 + 1 - c)
    other_x = (y * 2 + 1 - x, j)
    other_y = ((1 - y) * 2 + x, j)
    peers = [(i, (z + d) % 4 * 2 + c) for d in (1, 2, 3)]
    barrier = pltpu.get_barrier_semaphore()
    for device in [other_core, other_x, other_y] + peers:
        pl.semaphore_signal(barrier, inc=1, device_id=device, device_id_type=MESH_ID)
    pl.semaphore_wait(barrier, 6)

    def copy(n, src, dst, device):
        return pltpu.make_async_remote_copy(src_ref=src, dst_ref=dst, send_sem=send.at[n], recv_sem=recv.at[n],
                                            device_id=device, device_id_type=MESH_ID)

    def small_copy(n, src, dst, device):
        return pltpu.make_async_remote_copy(src_ref=src, dst_ref=dst, send_sem=s_send.at[n], recv_sem=s_recv.at[n],
                                            device_id=device, device_id_type=MESH_ID)

    def block(b, core):
        rows = jnp.concatenate([q_ref[b, core], w_ref[b, core]], axis=1)
        half = rows.shape[1] // 2
        return jnp.concatenate([rows[:, :half], rows[:, half:]], axis=0)

    small = small_copy(0, s_ref, s_got.at[0], other_core)
    small.start()
    copies = []
    for g in range(4):
        def convert(b, _):
            give[b] = block(b, 1 - c).astype(BF16)
            return 0
        lax.fori_loop(4 * g, 4 * g + 4, convert, 0)
        copies.append(copy(g, give.at[pl.ds(4 * g, 4)], r0.at[pl.ds(4 * g, 4)], other_core))
        copies[-1].start()
    small.wait()
    s_acc[0] = s_ref[...] + s_got[0]
    small = small_copy(1, s_acc.at[0], s_got.at[1], other_x)
    small.start()
    for g in range(4):
        copies[g].wait()
        def add(b, _):
            h[b // 8, b // 4 % 2, b % 4] = (block(b, c) + r0[b].astype(F32)).astype(BF16)
            return 0
        lax.fori_loop(4 * g, 4 * g + 4, add, 0)

    half = h.shape[4] // 2
    left, right = pl.ds(0, half), pl.ds(half, half)
    ca = copy(4, h.at[:, 1 - x, :, :, left], ra1, other_x)
    cb = copy(5, h.at[1 - y, :, :, :, right], rb1, other_y)
    ca.start()
    cb.start()
    small.wait()
    s_acc[1] = s_acc[0] + s_got[1]
    small = small_copy(2, s_acc.at[1], s_got.at[2], other_y)
    small.start()
    ca.wait()

    def add_x(b, _):
        u, v = b // 4, b % 4
        h[u, x, v, :, left] = (h[u, x, v, :, left].astype(F32) + ra1[u, v].astype(F32)).astype(BF16)
        return 0
    lax.fori_loop(0, 8, add_x, 0)
    ca = copy(6, h.at[1 - y, x, :, :, left], ra2, other_y)
    ca.start()
    cb.wait()

    def add_y(b, _):
        u, v = b // 4, b % 4
        h[y, u, v, :, right] = (h[y, u, v, :, right].astype(F32) + rb1[u, v].astype(F32)).astype(BF16)
        return 0
    lax.fori_loop(0, 8, add_y, 0)
    cb = copy(7, h.at[y, 1 - x, :, :, right], rb2, other_x)
    cb.start()
    small.wait()
    s_acc[2] = s_acc[1] + s_got[2]
    smalls = [small_copy(3 + n, s_acc.at[2], s_all.at[z], device) for n, device in enumerate(peers)]
    for one in smalls:
        one.start()
    ca.wait()
    cb.wait()

    def add_both(v, _):
        h[y, x, v, :, left] = (h[y, x, v, :, left].astype(F32) + ra2[v].astype(F32)).astype(BF16)
        h[y, x, v, :, right] = (h[y, x, v, :, right].astype(F32) + rb2[v].astype(F32)).astype(BF16)
        return 0
    lax.fori_loop(0, 4, add_both, 0)
    copies = [copy(8 + n, h.at[y, x, (z + 1 + n) % 4], rz.at[n], device) for n, device in enumerate(peers)]
    for one in copies:
        one.start()
    total = h[y, x, z].astype(F32)
    for one in smalls:
        one.wait()
    s_all[z] = s_acc[2]
    small_ref[...] = (s_all[0] + s_all[1]) + (s_all[2] + s_all[3])
    for n, one in enumerate(copies):
        one.wait()
        total = total + rz[n].astype(F32)
    rows = total.shape[0] // 2
    out_ref[:, :2 * half] = total[:rows]
    out_ref[:, 2 * half:] = total[rows:]


def dense_sum(grad_qkv, grad_out, small):
    rows, wide = grad_qkv.shape
    narrow = grad_out.shape[1]
    own = rows // 32
    width = wide + narrow
    half = width // 2
    pair = own * 2
    vmem = pl.BlockSpec(memory_space=pltpu.VMEM)
    return pl.pallas_call(
        dense_kernel,
        in_specs=[vmem] * 3, out_specs=[vmem] * 2,
        out_shape=[jax.ShapeDtypeStruct((own, width), F32), jax.ShapeDtypeStruct(small.shape, F32)],
        scratch_shapes=[
            pltpu.VMEM((16, pair, half), BF16), pltpu.VMEM((2, 2, 4, pair, half), BF16), pltpu.VMEM((16, pair, half), BF16),
            pltpu.VMEM((2, 4, pair, half // 2), BF16), pltpu.VMEM((2, 4, pair, half // 2), BF16),
            pltpu.VMEM((4, pair, half // 2), BF16), pltpu.VMEM((4, pair, half // 2), BF16), pltpu.VMEM((3, pair, half), BF16),
            pltpu.VMEM((3,) + small.shape, F32), pltpu.VMEM((3,) + small.shape, F32), pltpu.VMEM((4,) + small.shape, F32),
            pltpu.SemaphoreType.DMA((11,)), pltpu.SemaphoreType.DMA((11,)),
            pltpu.SemaphoreType.DMA((6,)), pltpu.SemaphoreType.DMA((6,))],
        compiler_params=pltpu.CompilerParams(collective_id=0, has_side_effects=True, vmem_limit_bytes=48 << 20),
        name="dense_sum",
    )(grad_qkv.reshape(16, 2, own, wide), grad_out.reshape(16, 2, own, narrow), small)


def exchange_pairs(normed_ffn, middle, cotangent, expert_ids, priority, router, w_in, w_down):
    rows, width = normed_ffn.shape
    logits = jnp.dot(normed_ffn, router, preferred_element_type=jnp.float32)
    experts_total = router.shape[1]
    picks = expert_ids[:, :, None] == jnp.arange(experts_total)[None, None, :]
    chosen = jnp.sum(jnp.where(picks, logits[:, None, :], 0.0), axis=2)
    gates = jax.nn.softmax(chosen, axis=-1)
    top = expert_ids.shape[1]
    levels = PRIO
    local_experts = w_in.shape[0]
    capacity = rows * top // local_experts
    send = max(2, 2 * rows * top // experts_total)
    flat_expert = expert_ids.reshape(-1)
    code = priority.reshape(-1) * experts_total + flat_expert
    onehot = (code[:, None] == jnp.arange(levels * experts_total)[None, :]).astype(jnp.int32)
    rank = jnp.sum((jnp.cumsum(onehot, axis=0) - onehot) * onehot, axis=1)
    counts = jnp.sum(onehot, axis=0)
    every = lax.all_gather(counts[None, :], "expert", axis=0, tiled=True).reshape(
        -1, levels, experts_total
    )
    expert_index = lax.axis_index("expert")
    totals = jnp.sum(every, axis=0)
    lower = jnp.cumsum(totals, axis=0) - totals
    earlier_sources = jnp.cumsum(every, axis=0) - every
    mine_prefix = lax.dynamic_index_in_dim(earlier_sources, expert_index, 0, keepdims=False)
    base = (lower + mine_prefix).reshape(-1)
    slot = rank + jnp.sum(onehot * base[None, :], axis=1)
    kept = slot < capacity
    own_counts = counts.reshape(levels, experts_total)
    own_lower = (jnp.cumsum(own_counts, axis=0) - own_counts).reshape(-1)
    place = rank + jnp.sum(onehot * own_lower[None, :], axis=1)
    target = flat_expert * send + place
    first_mine = expert_index * local_experts
    counts_mine = lax.dynamic_slice_in_dim(every, first_mine, local_experts, 2)
    base_mine = lax.dynamic_slice_in_dim(
        lower[None] + earlier_sources, first_mine, local_experts, 2
    )
    band_end = jnp.cumsum(counts_mine, axis=1)
    band_start = band_end - counts_mine
    place_index = jnp.arange(send, dtype=jnp.int32)
    level = jnp.sum(
        (place_index[None, None, None, :] >= band_end[:, :, :, None]).astype(jnp.int32), axis=1
    )
    level_hot = level[:, None, :, :] == jnp.arange(levels)[None, :, None, None]
    start_of = jnp.sum(jnp.where(level_hot, band_start[:, :, :, None], 0), axis=1)
    base_of = jnp.sum(jnp.where(level_hot, base_mine[:, :, :, None], 0), axis=1)
    arrived_slot = base_of + place_index[None, None, :] - start_of
    usable = (level < levels) & (arrived_slot < capacity)
    landing = jnp.where(
        usable,
        jnp.arange(local_experts)[None, :, None] * capacity + arrived_slot,
        local_experts * capacity,
    ).reshape(-1)
    live = landing < local_experts * capacity
    safe = jnp.minimum(landing, local_experts * capacity - 1)
    pair_inputs = jnp.repeat(normed_ffn, top, axis=0)
    outgoing = (
        jnp.zeros((experts_total * send, width), jnp.bfloat16)
        .at[target]
        .set(pair_inputs)
        .reshape(experts_total, send, width)
    )
    arrived = lax.all_to_all(outgoing, "expert", split_axis=0, concat_axis=0, tiled=True)
    expert_inputs = (
        jnp.zeros((local_experts * capacity, width), jnp.bfloat16)
        .at[landing]
        .set(arrived.reshape(-1, width), mode="drop")
        .reshape(local_experts, capacity, width)
    )
    hidden = jnp.einsum("ecd,edf->ecf", expert_inputs, w_in, preferred_element_type=jnp.float32)
    activated = jax.nn.gelu(hidden).astype(jnp.bfloat16)
    expert_out = jnp.einsum(
        "ecf,efd->ecd", activated, w_down, preferred_element_type=jnp.float32
    ).astype(jnp.bfloat16)
    returning = jnp.where(
        live[:, None],
        jnp.take(expert_out.reshape(-1, width), safe, axis=0),
        jnp.zeros((), jnp.bfloat16),
    ).reshape(experts_total, send, width)
    returned = lax.all_to_all(returning, "expert", split_axis=0, concat_axis=0, tiled=True)
    pair_out = jnp.where(
        kept[:, None],
        jnp.take(returned.reshape(-1, width), target, axis=0).astype(jnp.float32),
        0.0,
    ).reshape(rows, top, width)
    mixed = jnp.sum(gates[:, :, None] * pair_out, axis=1)
    grad_out = cotangent.astype(jnp.float32)
    grad_gates = jnp.sum(grad_out[:, None, :] * pair_out, axis=2)
    pair_grads = (gates[:, :, None] * grad_out[:, None, :]).astype(jnp.bfloat16).reshape(-1, width)
    outgoing_grads = (
        jnp.zeros((experts_total * send, width), jnp.bfloat16)
        .at[target]
        .set(pair_grads)
        .reshape(experts_total, send, width)
    )
    arrived_grads = lax.all_to_all(
        outgoing_grads, "expert", split_axis=0, concat_axis=0, tiled=True
    )
    grad_expert_out = (
        jnp.zeros((local_experts * capacity, width), jnp.bfloat16)
        .at[landing]
        .set(arrived_grads.reshape(-1, width), mode="drop")
        .reshape(local_experts, capacity, width)
    )
    hidden_again = jnp.einsum(
        "ecd,edf->ecf", expert_inputs, w_in, preferred_element_type=jnp.float32
    )
    activated_again, gelu_back = jax.vjp(jax.nn.gelu, hidden_again)
    grad_activated = jnp.einsum(
        "ecd,efd->ecf", grad_expert_out, w_down, preferred_element_type=jnp.float32
    )
    grad_hidden = gelu_back(grad_activated)[0].astype(jnp.bfloat16)
    grad_w_down = jnp.einsum(
        "ecf,ecd->efd",
        activated_again.astype(jnp.bfloat16),
        grad_expert_out,
        preferred_element_type=jnp.float32,
    )
    grad_w_in = jnp.einsum(
        "ecd,ecf->edf", expert_inputs, grad_hidden, preferred_element_type=jnp.float32
    )
    grad_inputs = jnp.einsum(
        "ecf,edf->ecd", grad_hidden, w_in, preferred_element_type=jnp.float32
    ).astype(jnp.bfloat16)
    back_rows = jnp.where(
        live[:, None],
        jnp.take(grad_inputs.reshape(-1, width), safe, axis=0),
        jnp.zeros((), jnp.bfloat16),
    ).reshape(experts_total, send, width)
    came_back = lax.all_to_all(back_rows, "expert", split_axis=0, concat_axis=0, tiled=True)
    pair_back = jnp.where(
        kept[:, None],
        jnp.take(came_back.reshape(-1, width), target, axis=0).astype(jnp.float32),
        0.0,
    )
    grad_normed_ffn = jnp.sum(pair_back.reshape(rows, top, width), axis=1)
    grad_chosen = gates * (grad_gates - jnp.sum(gates * grad_gates, axis=-1, keepdims=True))
    grad_logits = jnp.sum(jnp.where(picks, grad_chosen[:, :, None], 0.0), axis=1).astype(
        jnp.bfloat16
    )
    grad_normed_ffn = grad_normed_ffn + jnp.dot(
        grad_logits, router.T, preferred_element_type=jnp.float32
    )
    expert_parts = (
        lax.psum_scatter(grad_w_in.astype(jnp.bfloat16), "dp", scatter_dimension=1, tiled=True),
        lax.psum_scatter(grad_w_down.astype(jnp.bfloat16), "dp", scatter_dimension=1, tiled=True),
    )
    return mixed, grad_logits, grad_normed_ffn, expert_parts


def gather_codes(expert_ids, priority):
    return lax.all_gather(expert_ids * PRIO + priority, "expert", axis=0)


def plan_tokens(codes, rows, top):
    expert = lax.axis_index("expert").astype(jnp.int32)
    place, info, other = expert_slots(codes // PRIO, codes % PRIO, expert, rows * top)
    other_hot = (other.reshape(-1, 1) == jnp.arange(128)[None, :]).astype(jnp.bfloat16)
    own_place = lax.all_to_all(place, "expert", split_axis=0, concat_axis=0, tiled=True)
    return place, info, other_hot, own_place


def exchange_tokens(normed_ffn, all_cotangents, plan, expert_ids, router, w_in, w_down):
    rows, width = normed_ffn.shape
    experts_total = router.shape[1]
    top = expert_ids.shape[1]
    expert = lax.axis_index("expert").astype(jnp.int32)
    place, info, other_hot, own_place = plan
    sources = place.shape[0]
    send = 2 * rows * top // experts_total
    room = (rows * top + 16 * sources + send + MOE_ROWS - 1) // MOE_ROWS * MOE_ROWS
    sent, all_cotangents = lax.optimization_barrier((normed_ffn, all_cotangents))
    all_tokens = lax.all_gather(sent, "expert", axis=0, tiled=True)
    packed_cot, packed_other = pack(info, place, [all_cotangents, other_hot], room)
    (packed,) = pack(info, place, [all_tokens], room)
    wide_router = jnp.pad(router, ((0, 0), (0, 128 - experts_total)))
    grad_rows, mixed_rows, grad_gate, grad_w_in, grad_w_down = expert_layer(
        info, expert[None], packed, packed_other, packed_cot, wide_router, w_in[0], w_down[0], sources
    )
    grad_all, gate_all = unpack(info, place, [grad_rows, grad_gate], [jnp.bfloat16, jnp.float32], send)
    gate_all = jnp.sum(gate_all[:, :3], axis=1).reshape(sources, rows)
    gate_own = lax.all_to_all(gate_all, "expert", split_axis=0, concat_axis=0, tiled=True)
    grad_own = lax.psum_scatter(grad_all, "expert", scatter_dimension=0, tiled=True)
    windows = jnp.concatenate([lax.dynamic_slice_in_dim(mixed_rows, info[d], send, 0) for d in range(sources)], axis=0)
    windows, grad_w_in, grad_w_down, grad_own = lax.optimization_barrier(
        (windows, grad_w_in, grad_w_down, grad_own)
    )
    mixed = (lax.all_to_all(windows, "expert", split_axis=0, concat_axis=0, tiled=True), own_place)
    expert_parts = (
        lax.psum_scatter(grad_w_in[None], "dp", scatter_dimension=1, tiled=True),
        lax.psum_scatter(grad_w_down[None], "dp", scatter_dimension=1, tiled=True),
    )
    logits = jnp.dot(normed_ffn, router, preferred_element_type=jnp.float32)
    picks = expert_ids[:, :, None] == jnp.arange(experts_total)[None, None, :]
    chosen = jnp.sum(jnp.where(picks, logits[:, None, :], 0.0), axis=2)
    gates = jax.nn.softmax(chosen, axis=-1)
    grad_gates = jnp.sum(jnp.where(picks, gate_own.T[:, None, :], 0.0), axis=2)
    grad_chosen = gates * (grad_gates - jnp.sum(gates * grad_gates, axis=-1, keepdims=True))
    grad_logits = jnp.sum(jnp.where(picks, grad_chosen[:, :, None], 0.0), axis=1).astype(
        jnp.bfloat16
    )
    grad_normed_ffn = grad_own.astype(jnp.float32) + jnp.dot(
        grad_logits, router.T, preferred_element_type=jnp.float32
    )
    return mixed, grad_logits, grad_normed_ffn, expert_parts


def per_device(
    tokens_in,
    cont_ids,
    expert_ids,
    priority,
    gain_attn,
    w_qkv,
    rel_table,
    w_out,
    gain_ffn,
    w_router,
    w_in,
    w_down,
    cotangent,
):
    rows, width = tokens_in.shape
    heads = rel_table.shape[1]
    dp_count = lax.axis_size("dp")
    dp_index = lax.axis_index("dp")
    prompt_rows = PROMPT // dp_count
    few_experts = lax.axis_size("expert") <= 16 and w_in.shape[0] == 1
    local_ids = cont_ids[0]
    info = info_of(local_ids, dp_index)
    row_start = row_start_of(local_ids)
    rows_bias = bias_rows(rel_table)
    if few_experts:
        codes = gather_codes(expert_ids, priority)
    experts_total = w_router.shape[1]
    dense = jnp.concatenate(
        [pairs_together(w_qkv), w_out, jnp.pad(w_router, ((0, 0), (0, 128 - experts_total)))], axis=1
    )
    dense = lax.all_gather(dense, ("dp", "expert"), axis=0, tiled=True)
    part_heads = heads // PARTS
    tables = [bias_tables(info, rows_bias, row_start, g * part_heads, part_heads) for g in range(PARTS)]
    dense, tables[0] = lax.optimization_barrier((dense, tables[0]))
    if few_experts:
        plan = plan_tokens(codes, rows, expert_ids.shape[1])
        dense, plan = lax.optimization_barrier((dense, plan))
    whole_qkv, whole_out = dense[:, : 3 * width], dense[:, 3 * width : 4 * width]
    whole_router = dense[:, 4 * width : 4 * width + experts_total]
    inputs = tokens_in.astype(jnp.float32)
    normed_attn = normed(inputs, gain_attn).astype(jnp.bfloat16)
    projected = jnp.dot(normed_attn, whole_qkv, preferred_element_type=jnp.float32).astype(
        jnp.bfloat16
    )
    parts = PARTS
    columns = 2 * width // parts
    kept = [projected[:, width + columns * g : width + columns * (g + 1)] for g in range(parts)]
    gathered = [lax.all_gather(kv[:prompt_rows], "dp", axis=0, tiled=True) for kv in kept]
    if few_experts:
        late_cotangent, gathered[0], tables = lax.optimization_barrier((cotangent, gathered[0], tables))
        all_cotangents = lax.all_gather(late_cotangent, "expert", axis=0, tiled=True)
    gathered[0], tables = lax.optimization_barrier((gathered[0], tables))
    keys_values = []
    exact, log_total = [], []
    for g in range(parts):
        if g:
            gathered[g], exact[-1] = lax.optimization_barrier((gathered[g], exact[-1]))
        keys_values.append(jnp.concatenate([gathered[g], kept[g][prompt_rows:]], axis=0))
        out, total = attention_forward(info, projected, keys_values[g], tables[g], g)
        exact.append(out)
        log_total.append(total)
    attended = jnp.concatenate(exact, axis=1).astype(jnp.bfloat16)
    middle = inputs + jnp.dot(attended, whole_out, preferred_element_type=jnp.float32)
    normed_ffn = normed(middle, gain_ffn).astype(jnp.bfloat16)
    if few_experts:
        mixed, grad_logits, grad_normed_ffn, expert_parts = exchange_tokens(
            normed_ffn, all_cotangents, plan, expert_ids, whole_router, w_in, w_down
        )
    else:
        mixed, grad_logits, grad_normed_ffn, expert_parts = exchange_pairs(
            normed_ffn, middle, cotangent, expert_ids, priority, whole_router, w_in, w_down
        )
    grad_out = cotangent.astype(jnp.float32)
    grad_router = jnp.dot(normed_ffn.T, grad_logits, preferred_element_type=jnp.float32)
    _, ffn_norm_back = jax.vjp(normed, middle, gain_ffn)
    grad_middle_part, grad_gain_ffn = ffn_norm_back(grad_normed_ffn)
    grad_middle = grad_out + grad_middle_part
    grad_branch = grad_middle.astype(jnp.bfloat16)
    grad_out_weight = jnp.dot(attended.T, grad_branch, preferred_element_type=jnp.float32)
    grad_attended = jnp.dot(
        grad_branch, whole_out.T, preferred_element_type=jnp.float32
    ).astype(jnp.bfloat16)
    grad_queries, grad_prompts, grad_conts, grad_lines = [], [], [], []
    for g in range(parts):
        if g:
            grad_attended, expert_parts, grad_queries[-1] = lax.optimization_barrier(
                (grad_attended, expert_parts, grad_queries[-1])
            )
        grad_query, grad_kv, lines = attention_backward(
            info, projected, grad_attended, exact[g], log_total[g], keys_values[g], tables[g], g
        )
        grad_queries.append(grad_query)
        grad_prompts.append(lax.psum_scatter(grad_kv[:PROMPT], "dp", scatter_dimension=0, tiled=True))
        grad_conts.append(grad_kv[PROMPT:])
        grad_lines.append(lines)
    mixed, middle, grad_queries[-1] = lax.optimization_barrier((mixed, middle, grad_queries[-1]))
    if few_experts:
        returned, own_place = mixed
        mixed = collect(own_place, returned, returned.shape[0] // own_place.shape[0])
    output = (middle + mixed).astype(jnp.bfloat16)
    grad_table = table_grad(jnp.concatenate(grad_lines, axis=0), rel_table.shape[0])
    grad_projected = jnp.concatenate(
        grad_queries + [jnp.concatenate([a, b], axis=0) for a, b in zip(grad_prompts, grad_conts)], axis=1
    )
    grad_normed_attn = jnp.dot(grad_projected, whole_qkv.T, preferred_element_type=jnp.float32)
    grad_qkv = jnp.dot(normed_attn.T, grad_projected, preferred_element_type=jnp.float32)
    _, attn_norm_back = jax.vjp(normed, inputs, gain_attn)
    grad_inputs_part, grad_gain_attn = attn_norm_back(grad_normed_attn)
    grad_tokens = grad_middle + grad_inputs_part
    if (dp_count, lax.axis_size("expert")) == (4, 8):
        pieces = [grad_gain_attn, grad_gain_ffn, grad_table.reshape(-1), grad_router.reshape(-1)]
        sizes = [piece.shape[0] for piece in pieces]
        small = jnp.concatenate(pieces)
        small = jnp.pad(small, (0, -small.shape[0] % 1024)).reshape(-1, 128)
        dense_grad, small = dense_sum(grad_qkv, grad_out_weight, small)
        ends = [sum(sizes[: n + 1]) for n in range(4)]
        flat = small.reshape(-1)
        grad_gain_attn, grad_gain_ffn = flat[: ends[0]], flat[ends[0] : ends[1]]
        grad_table = flat[ends[1] : ends[2]].reshape(grad_table.shape)
        own_rows = w_router.shape[0]
        mine = (dp_index * lax.axis_size("expert") + lax.axis_index("expert")) * own_rows
        own_router = lax.dynamic_slice_in_dim(
            flat[ends[2] : ends[3]].reshape(grad_router.shape), mine, own_rows, 0
        )
        small_parts = (grad_gain_attn, grad_gain_ffn, grad_table.T)
    else:
        dense_grad = lax.psum_scatter(
            jnp.concatenate([grad_qkv, grad_out_weight], axis=1), ("dp", "expert"), scatter_dimension=0, tiled=True
        )
        own_router = lax.psum_scatter(grad_router, ("dp", "expert"), scatter_dimension=0, tiled=True)
        small_parts = lax.psum((grad_gain_attn, grad_gain_ffn, grad_table.T), ("dp", "expert"))
    return (
        output,
        grad_tokens,
        small_parts[0],
        pairs_apart(dense_grad[:, : 3 * width]),
        small_parts[2],
        dense_grad[:, 3 * width :],
        small_parts[1],
        own_router,
        expert_parts[0].astype(jnp.float32),
        expert_parts[1].astype(jnp.float32),
    )


def solution(mesh):
    return jax.shard_map(
        per_device,
        mesh=mesh,
        in_specs=(
            P(("dp", "expert"), None),
            P(("dp", "expert"), None),
            P(("dp", "expert"), None),
            P(("dp", "expert"), None),
            P(),
            P(("dp", "expert"), None),
            P(),
            P(("dp", "expert"), None),
            P(),
            P(("dp", "expert"), None),
            P("expert", None, None),
            P("expert", None, None),
            P(("dp", "expert"), None),
        ),
        out_specs=(
            P(("dp", "expert"), None),
            P(("dp", "expert"), None),
            P(),
            P(("dp", "expert"), None),
            P(),
            P(("dp", "expert"), None),
            P(),
            P(("dp", "expert"), None),
            P("expert", "dp", None),
            P("expert", "dp", None),
        ),
        check_vma=False,
    )
```

```python
import functools
import math
import jax
import jax.numpy as jnp
from jax import lax
from jax.experimental import pallas as pl
from jax.experimental.pallas import tpu as pltpu
from jax.sharding import PartitionSpec as P

PRIO = 4
PROMPT = 2048


BORDERS = (16, 24, 32, 48, 64, 96, 128, 192, 256, 384, 512, 768, 1024, 1536, 2048)
EPSILON = 1e-06
MASKED = -1e30


def bucket_of(distance):
    distance = jnp.maximum(distance, 0)
    counted = jnp.minimum(distance, 15)
    for border in BORDERS:
        counted = counted + (distance >= border).astype(jnp.int32)
    return counted


def normed(values, gain):
    return values * lax.rsqrt(jnp.mean(values * values, axis=-1, keepdims=True) + EPSILON) * gain


def pairs_together(w_qkv):
    width = w_qkv.shape[1] // 3
    rows = w_qkv.shape[0]
    keys_values = w_qkv[:, width:].reshape(rows, 2, width // 128, 128).swapaxes(1, 2)
    return jnp.concatenate([w_qkv[:, :width], keys_values.reshape(rows, 2 * width)], axis=1)


def pairs_apart(grad):
    width = grad.shape[1] // 3
    rows = grad.shape[0]
    keys_values = grad[:, width:].reshape(rows, width // 128, 2, 128).swapaxes(1, 2)
    return jnp.concatenate([grad[:, :width], keys_values.reshape(rows, 2 * width)], axis=1)


LOG2E = math.log2(math.e)
F32, BF16 = jnp.float32, jnp.bfloat16
QT = 256
KT = 512
RUN = 256
EARLY = pl.CostEstimate(flops=1 << 20, bytes_accessed=1 << 20, transcendentals=0)
PARTS = 2
ROWS = 32
NT = (((1,), (1,)), ((), ()))
NN = (((1,), (0,)), ((), ()))

def dot(a, b, dims=NN):
    return lax.dot_general(a, b, dims, preferred_element_type=F32)

def bias_rows(rel_table):
    width = PROMPT + 512 + RUN
    distance = PROMPT + RUN - jnp.arange(width)[None, :] + jnp.arange(8)[:, None]
    bucket = bucket_of(distance)
    table = rel_table.T[:, None, None, :] * LOG2E
    hot = (bucket[..., None] == jnp.arange(rel_table.shape[0])).astype(F32)
    rows = jnp.sum(hot[None] * table, axis=-1)
    return jnp.where(distance[None] >= 0, rows, MASKED)

def bias_kernel(info, base_ref, row_start, t_ref, b_ref):
    base, t_scr, b_scr = base_ref[0], t_ref.at[0], b_ref.at[0]
    width = base.shape[-1]
    for a in range(16):
        t_scr[8 * a:8 * a + 8, :] = pltpu.roll(base, 8 * a, 1) if a else base
    lane = lax.broadcasted_iota(jnp.int32, (ROWS, 128), 1)
    sub = lax.broadcasted_iota(jnp.int32, (ROWS, 128), 0)
    for s in range(4):
        start, end = info[s], info[s + 1]
        turn = start % 128
        left = (128 - turn) % 128
        here = (lane < left) | (left == 0)
        def place(g, _):
            at = pl.ds(pl.multiple_of(ROWS * g, ROWS), ROWS)
            first = start - turn + RUN - 128 * (g // (128 // ROWS))
            of = pl.ds(pl.multiple_of(ROWS * (g % (128 // ROWS)), ROWS), ROWS)
            mine = sub + ROWS * g >= start
            turned = None
            for b in range(PROMPT // 128 + 1):
                after = pltpu.roll(t_scr[of, pl.ds(pl.multiple_of(first + 128 * b, 128), 128)], left, 1)
                if b:
                    cols = slice(128 * b - 128, 128 * b)
                    b_scr[at, cols] = jnp.where(mine, jnp.where(here, turned, after), b_scr[at, cols])
                turned = after
            return 0
        lax.fori_loop(start // ROWS, (end + ROWS - 1) // ROWS, place, 0)
    lane = lax.broadcasted_iota(jnp.int32, (128, 128), 1)
    for i in range(KT // 128):
        rows = slice(128 * i, 128 * i + 128)
        own = row_start[rows, :]
        for b in range(KT // 128):
            first = PROMPT + RUN - 128 * i + 128 * b
            b_scr[rows, PROMPT + 128 * b:PROMPT + 128 * b + 128] = jnp.where(
                lane + 128 * b >= own, t_scr[:, first:first + 128], MASKED)

def bias_tables(info, rows_bias, row_start, first, heads):
    wide = rows_bias.shape[2]
    block = lambda rows, cols: pl.BlockSpec((1, rows, cols), lambda h, *_: (h, 0, 0))
    return pl.pallas_call(
        bias_kernel,
        grid_spec=pltpu.PrefetchScalarGridSpec(
            num_scalar_prefetch=1, grid=(heads,),
            in_specs=[pl.BlockSpec((1, 8, wide), lambda h, *_: (first + h, 0, 0)),
                      pl.BlockSpec((KT, 128), lambda h, *_: (0, 0))],
            out_specs=[block(128, wide), block(KT, PROMPT + KT)]),
        out_shape=[jax.ShapeDtypeStruct((heads, 128, wide), F32),
                   jax.ShapeDtypeStruct((heads, KT, PROMPT + KT), F32)],
        compiler_params=pltpu.CompilerParams(vmem_limit_bytes=32 << 20),
        cost_estimate=EARLY,
        name="bias_tables",
    )(info, rows_bias, row_start)

def own_lanes(h, rows):
    lane = lax.broadcasted_iota(jnp.int32, (rows, 128), 1)
    return lane // 64 == h % 2

def fwd_kernel(scale2, cont, info, q_ref, k_ref, v_ref, table_ref, o_ref, lse_ref):
    h = pl.program_id(0)
    dp = info[5]
    table = table_ref.at[0]
    own = own_lanes(h, QT)
    head_lane = lax.broadcasted_iota(jnp.int32, (QT, 128), 1) == h

    def tile(first, key_tiles, bias_of, block):
        rows = pl.ds(first, QT)
        q = jnp.where(own, q_ref[rows, :], jnp.zeros((), BF16))
        def step(t, carry):
            m, l, acc = carry
            cols = pl.ds(pl.multiple_of(block(t) * KT, KT), KT)
            s = dot(q, k_ref[cols, :], NT) * scale2 + bias_of(t)
            new = jnp.maximum(m, jnp.max(s, axis=1, keepdims=True))
            keep = jnp.exp2(m - new)
            p = jnp.exp2(s - jnp.concatenate([new] * (KT // 128), axis=1))
            part = p[:, :128]
            for c in range(1, KT // 128):
                part = part + p[:, 128 * c:128 * (c + 1)]
            return new, l * keep + part, acc * keep + dot(p.astype(BF16), v_ref[cols, :])
        zero = jnp.zeros((QT, 128), F32)
        m, l, acc = lax.fori_loop(0, key_tiles, step, (jnp.full((QT, 128), MASKED, F32), zero, zero))
        l = jnp.sum(l, axis=1, keepdims=True)
        o_ref[rows, :] = jnp.where(own, acc / l, o_ref[rows, :])
        lse_ref[rows, :] = jnp.where(head_lane, m + jnp.log2(l), lse_ref[rows, :])

    for j in range(KT // QT):
        if cont:
            tile(QT * j, PROMPT // KT + 1,
                 lambda t: table[pl.ds(QT * j, QT), pl.ds(pl.multiple_of(t * KT, KT), KT)], lambda t: t)
            continue
        shift = PROMPT - KT * dp - QT * j + RUN
        def bias(t, shift=shift):
            first = (dp - t) * KT + shift
            return jnp.concatenate([table[:, pl.ds(pl.multiple_of(first - 128 * x, 128), KT)] for x in range(QT // 128)], axis=0)
        tile(QT * j, dp + 1, bias, lambda t: dp - t)

def attention_forward(info, projected, keys_values, tables, part, cont):
    keys, columns = keys_values.shape
    heads = columns // 128
    scale2 = 64 ** -0.5 * LOG2E
    first = part * heads // 2
    table = tables[int(cont)]
    return pl.pallas_call(
        functools.partial(fwd_kernel, scale2, cont),
        grid_spec=pltpu.PrefetchScalarGridSpec(
            num_scalar_prefetch=1, grid=(heads,),
            in_specs=[pl.BlockSpec((KT, 128), lambda h, *_: (int(cont), first + h // 2)),
                      pl.BlockSpec((keys, 128), lambda h, *_: (0, h // 2 * 2)),
                      pl.BlockSpec((keys, 128), lambda h, *_: (0, h // 2 * 2 + 1)),
                      pl.BlockSpec((1,) + table.shape[1:], lambda h, *_: (h, 0, 0))],
            out_specs=[pl.BlockSpec((KT, 128), lambda h, *_: (0, h // 2)),
                       pl.BlockSpec((KT, 128), lambda h, *_: (0, 0))]),
        out_shape=[jax.ShapeDtypeStruct((KT, heads * 64), F32), jax.ShapeDtypeStruct((KT, 128), F32)],
        compiler_params=pltpu.CompilerParams(vmem_limit_bytes=60 << 20),
        cost_estimate=EARLY,
        name="attention_forward",
    )(info, projected, keys_values, keys_values, table)

def split3(x):
    hi = x.astype(BF16)
    rest = x - hi.astype(F32)
    mid = rest.astype(BF16)
    return hi, mid, (rest - mid.astype(F32)).astype(BF16)

def bwd_kernel(scale, info, q_ref, do_ref, o_ref, lse_ref, k_ref, v_ref, t_ref, b_ref,
               dq_ref, dkv_ref, dd_ref,
               e_scr, db_scr, qa, da, ka, va, qt, dot_t, dkt, dvt):
    h = pl.program_id(0)
    dp = info[5]
    n, keys = q_ref.shape[0], k_ref.shape[0]
    half = h % 2
    t_scr, b_scr = t_ref.at[0], b_ref.at[0]
    base = pl.multiple_of(64 * half, 64)
    other = 64 - 64 * half

    @pl.when(half == 0)
    def _():
        qt[...] = q_ref[...].T
        dot_t[...] = do_ref[...].T
        dq_ref[...] = jnp.zeros_like(dq_ref)

    lane_n = lax.broadcasted_iota(jnp.int32, (QT, 128), 1)
    own_n = lane_n // 64 == half
    def augment(i, _):
        rows = pl.ds(pl.multiple_of(i * QT, QT), QT)
        lse = jnp.sum(jnp.where(lane_n == h, lse_ref[rows, :], 0.0), axis=1, keepdims=True)
        parts = split3(-lse / (scale * LOG2E))
        aug = jnp.zeros((QT, 128), BF16)
        for x in range(3):
            aug = jnp.where(lane_n == other + x, jnp.broadcast_to(parts[x], (QT, 128)), aug)
        qa[rows, :] = jnp.where(own_n, q_ref[rows, :], aug)
        do = do_ref[rows, :]
        delta = jnp.sum(jnp.where(own_n, do.astype(F32) * o_ref[rows, :], 0.0), axis=1, keepdims=True)
        parts = split3(-delta)
        aug = jnp.zeros((QT, 128), BF16)
        for x in range(3):
            aug = jnp.where(lane_n == other + x, jnp.broadcast_to(parts[x], (QT, 128)), aug)
        da[rows, :] = jnp.where(own_n, do, aug)
        return 0
    lax.fori_loop(0, n // QT, augment, 0)
    lane_k = lax.broadcasted_iota(jnp.int32, (KT, 128), 1)
    ones = jnp.where((lane_k >= other) & (lane_k < other + 3), 1.0, 0.0).astype(BF16)
    own_k = lane_k // 64 == half
    def augment_keys(i, _):
        rows = pl.ds(pl.multiple_of(i * KT, KT), KT)
        ka[rows, :] = jnp.where(own_k, k_ref[rows, :], ones)
        va[rows, :] = jnp.where(own_k, v_ref[rows, :], ones)
        return 0
    lax.fori_loop(0, keys // KT, augment_keys, 0)
    head_rows = pl.ds(base, 64)
    dkt[head_rows, :] = jnp.zeros((64, keys), F32)
    dvt[head_rows, :] = jnp.zeros((64, keys), F32)
    e_scr[...] = jnp.zeros_like(e_scr)

    def tile(first, key_tiles, bias_of, grad_bias):
        rows = pl.ds(first, QT)
        q, do = qa[rows, :], da[rows, :]
        q_t, do_t = qt[head_rows, rows], dot_t[head_rows, rows]
        def step(t, dq):
            cols = pl.ds(pl.multiple_of(t * KT, KT), KT)
            kk = ka[cols, :]
            p = jnp.exp2(dot(q, kk, NT) * (scale * LOG2E) + bias_of(t))
            ds = p * dot(do, va[cols, :], NT)
            grad_bias(t, ds)
            low = ds.astype(BF16)
            dvt[head_rows, cols] += dot(do_t, p.astype(BF16))
            dkt[head_rows, cols] += dot(q_t, low)
            return dq + dot(low, kk)
        dq = lax.fori_loop(0, key_tiles, step, jnp.zeros((QT, 128), F32))
        dq_ref[rows, :] = jnp.where(own_n, dq * scale, dq_ref[rows, :].astype(F32)).astype(BF16)

    for j in range(2):
        shift = PROMPT - KT * dp - QT * j + RUN
        def part(t, x, shift=shift):
            return (slice(None), pl.ds(pl.multiple_of(t * KT + shift - 128 * x, 128), KT))
        def bias(t):
            return jnp.concatenate([t_scr[part(t, x)] for x in range(QT // 128)], axis=0)
        def add(t, ds):
            for x in range(QT // 128):
                e_scr[part(t, x)] += ds[128 * x:128 * x + 128, :]
        tile(QT * j, dp + 1, bias, add)
    for j in range(2):
        def where(t):
            return (pl.ds(QT * j, QT), pl.ds(pl.multiple_of(t * KT, KT), KT))
        def put(t, ds):
            db_scr[where(t)] = ds
        tile(KT + QT * j, PROMPT // KT + 1, lambda t: b_scr[where(t)], put)

    lane = lax.broadcasted_iota(jnp.int32, (ROWS, 128), 1)
    sub = lax.broadcasted_iota(jnp.int32, (ROWS, 128), 0)
    for s in range(4):
        start, end = info[s], info[s + 1]
        turn = start % 128
        def fold(g, _):
            at = pl.ds(pl.multiple_of(ROWS * g, ROWS), ROWS)
            first = start - turn + RUN - 128 * (g // (128 // ROWS))
            to = pl.ds(pl.multiple_of(ROWS * (g % (128 // ROWS)), ROWS), ROWS)
            mine = (sub + ROWS * g >= start) & (sub + ROWS * g < end)
            before = jnp.zeros((ROWS, 128), F32)
            for b in range(PROMPT // 128 + 1):
                if b < PROMPT // 128:
                    turned = pltpu.roll(jnp.where(mine, db_scr[at, 128 * b:128 * b + 128], 0.0), turn, 1)
                else:
                    turned = jnp.zeros((ROWS, 128), F32)
                e_scr[to, pl.ds(pl.multiple_of(first + 128 * b, 128), 128)] += jnp.where(lane >= turn, turned, before)
                before = turned
            return 0
        lax.fori_loop(start // ROWS, (end + ROWS - 1) // ROWS, fold, 0)
    for i in range(KT // 128):
        first = PROMPT + RUN - 128 * i
        e_scr[:, first:first + KT] += db_scr[128 * i:128 * i + 128, PROMPT:]
    width = t_ref.shape[2]
    acc = e_scr[0:8, :]
    for a in range(1, 16):
        acc = acc + pltpu.roll(e_scr[8 * a:8 * a + 8, :], width - 8 * a, 1)
    total = acc[0:1, :]
    for i in range(1, 8):
        total = total + pltpu.roll(acc, width - i, 1)[i:i + 1, :]
    dd_ref[0] = total

    @pl.when(half == 1)
    def _():
        dkv_ref[:, :128] = (dkt[...] * scale).T.astype(BF16)
        dkv_ref[:, 128:] = dvt[...].T.astype(BF16)

def attention_backward(info, projected, do, o32, lse, keys_values, tables, part):
    n = projected.shape[0]
    keys, columns = keys_values.shape
    heads = columns // 128
    wide = tables[0].shape[2]
    first = part * heads // 2
    own = pl.BlockSpec((n, 128), lambda h, *_: (0, h // 2))
    shifted = pl.BlockSpec((n, 128), lambda h, *_: (0, first + h // 2))
    cols = PROMPT + KT
    return pl.pallas_call(
        functools.partial(bwd_kernel, 64 ** -0.5),
        grid_spec=pltpu.PrefetchScalarGridSpec(
            num_scalar_prefetch=1, grid=(heads,),
            in_specs=[shifted, shifted, own, pl.BlockSpec((n, 128), lambda h, *_: (0, 0)),
                      pl.BlockSpec((keys, 128), lambda h, *_: (0, h // 2 * 2)),
                      pl.BlockSpec((keys, 128), lambda h, *_: (0, h // 2 * 2 + 1)),
                      *[pl.BlockSpec((1,) + t.shape[1:], lambda h, *_: (h, 0, 0)) for t in tables]],
            out_specs=[own, pl.BlockSpec((keys, 256), lambda h, *_: (0, h // 2)),
                       pl.BlockSpec((1, 1, wide), lambda h, *_: (h, 0, 0))],
            scratch_shapes=[pltpu.VMEM((128, wide), F32), pltpu.VMEM((KT, cols), F32),
                            pltpu.VMEM((n, 128), BF16), pltpu.VMEM((n, 128), BF16),
                            pltpu.VMEM((keys, 128), BF16), pltpu.VMEM((keys, 128), BF16),
                            pltpu.VMEM((128, n), BF16), pltpu.VMEM((128, n), BF16),
                            pltpu.VMEM((128, keys), F32), pltpu.VMEM((128, keys), F32)]),
        out_shape=[jax.ShapeDtypeStruct((n, heads * 64), BF16), jax.ShapeDtypeStruct((keys, columns), BF16),
                   jax.ShapeDtypeStruct((heads, 1, wide), F32)],
        compiler_params=pltpu.CompilerParams(vmem_limit_bytes=60 << 20),
        cost_estimate=EARLY,
        name="attention_backward",
    )(info, projected, do, o32, lse, keys_values, keys_values, *tables)

def info_of(ids, dp):
    starts = jnp.sum((ids[None, :] < jnp.arange(5)[:, None]).astype(jnp.int32), axis=1)
    return jnp.concatenate([starts, jnp.reshape(dp, (1,)).astype(jnp.int32)])

def table_grad(dd, buckets):
    width = dd.shape[2]
    distance = PROMPT + RUN - jnp.arange(width)
    hot = ((bucket_of(distance)[:, None] == jnp.arange(buckets)[None, :]) & (distance >= 0)[:, None]).astype(F32)
    return jnp.dot(dd[:, 0, :], hot, precision=lax.Precision.HIGHEST)

def row_start_of(ids):
    starts = jnp.sum((ids[None, :] < ids[:, None]).astype(jnp.int32), axis=1)
    return jnp.broadcast_to(starts[:, None], (ids.shape[0], 128))


TN = (((0,), (0,)), ((), ()))
MOE_ROWS = 256
FF_TILE = 768


def expert_slots(ids, levels, expert, capacity):
    hits = ids == expert
    hit = jnp.any(hits, axis=2)
    level = jnp.sum(jnp.where(hits, levels, 0), axis=2)
    hot = hit[:, :, None] & (level[:, :, None] == jnp.arange(PRIO)[None, None, :])
    tokens = ids.shape[1]
    earlier = (jnp.arange(tokens)[:, None] > jnp.arange(tokens)[None, :]).astype(BF16)
    rank = jnp.einsum("ut,dtl->dul", earlier, hot.astype(BF16), preferred_element_type=F32).astype(jnp.int32)
    counts = jnp.sum(hot.astype(jnp.int32), axis=1)
    totals = jnp.sum(counts, axis=0)
    lower = jnp.cumsum(totals) - totals
    base = lower[None, :] + jnp.cumsum(counts, axis=0) - counts
    slot = jnp.sum(jnp.where(hot, base[:, None, :] + rank, 0), axis=2)
    kept = hit & (slot < capacity)
    rank = jnp.einsum("ut,dt->du", earlier, kept.astype(BF16), preferred_element_type=F32).astype(jnp.int32)
    place = jnp.where(kept, rank, -1)
    other = jnp.sum(jnp.where(hits, 0, ids), axis=2)
    return place, other


def half_plan(place, other, half):
    tokens = place.shape[1] // 2
    before = jnp.sum((place[:, : half * tokens] >= 0).astype(jnp.int32), axis=1)
    part = place[:, half * tokens : (half + 1) * tokens]
    kept = part >= 0
    sizes = jnp.sum(kept.astype(jnp.int32), axis=1)
    part = jnp.where(kept, part - before[:, None], -1)
    padded = (sizes + 15) // 16 * 16
    ends = jnp.cumsum(padded)
    info = jnp.concatenate([ends - padded, sizes, ends[-1:]]).astype(jnp.int32)
    hot = other[:, half * tokens : (half + 1) * tokens].reshape(-1, 1) == jnp.arange(128)[None, :]
    return info, part, hot.astype(jnp.bfloat16)


def pack_kernel(sources, info, place_ref, *refs):
    ins, outs = refs[:len(refs) // 2], refs[len(refs) // 2:]
    d = pl.program_id(0)

    @pl.when(d == 0)
    def _():
        for out in outs:
            out[...] = jnp.zeros_like(out)

    tokens = place_ref.shape[2]
    row = lax.broadcasted_iota(jnp.int32, (MOE_ROWS, tokens), 0)

    def chunk(j, _):
        pick = jnp.where(place_ref[0] == row + MOE_ROWS * j, 1.0, 0.0).astype(BF16)
        at = pl.ds(pl.multiple_of(info[d] + MOE_ROWS * j, 16), MOE_ROWS)
        for x, out in zip(ins, outs):
            out[at, :] = dot(pick, x[...]).astype(BF16)
        return 0
    lax.fori_loop(0, (info[sources + d] + MOE_ROWS - 1) // MOE_ROWS, chunk, 0)


def pack(info, place, arrays, room, halves=1, half=0):
    sources, tokens = place.shape
    return pl.pallas_call(
        functools.partial(pack_kernel, sources),
        grid_spec=pltpu.PrefetchScalarGridSpec(
            num_scalar_prefetch=1, grid=(sources,),
            in_specs=[pl.BlockSpec((1, 1, tokens), lambda d, *_: (d, 0, 0))]
            + [pl.BlockSpec((tokens, x.shape[1]), lambda d, *_: (halves * d + half, 0)) for x in arrays],
            out_specs=[pl.BlockSpec((room, x.shape[1]), lambda d, *_: (0, 0)) for x in arrays]),
        out_shape=[jax.ShapeDtypeStruct((room, x.shape[1]), BF16) for x in arrays],
        compiler_params=pltpu.CompilerParams(vmem_limit_bytes=40 << 20),
        cost_estimate=EARLY,
        name="pack_tokens",
    )(info, place[:, None, :], *arrays)


def unpack_kernel(send, info, place_ref, *refs):
    ins, outs = refs[:len(refs) // 2], refs[len(refs) // 2:]
    tokens = place_ref.shape[0]
    lane = lax.broadcasted_iota(jnp.int32, (tokens, 128), 1)
    put = jnp.concatenate(
        [jnp.where(place_ref[...] == lane + 128 * b, 1.0, 0.0).astype(BF16) for b in range(send // 128)], axis=1)
    at = pl.ds(pl.multiple_of(info[pl.program_id(0)], 16), send)
    for x, out in zip(ins, outs):
        out[...] = dot(put, x[at, :]).astype(out.dtype)


def unpack(info, place, arrays, dtypes, send):
    sources, tokens = place.shape
    spread = jnp.broadcast_to(place.reshape(-1, 1), (sources * tokens, 128))
    return pl.pallas_call(
        functools.partial(unpack_kernel, send),
        grid_spec=pltpu.PrefetchScalarGridSpec(
            num_scalar_prefetch=1, grid=(sources,),
            in_specs=[pl.BlockSpec((tokens, 128), lambda d, *_: (d, 0))]
            + [pl.BlockSpec(x.shape, lambda d, *_: (0, 0)) for x in arrays],
            out_specs=[pl.BlockSpec((tokens, x.shape[1]), lambda d, *_: (d, 0)) for x in arrays]),
        out_shape=[jax.ShapeDtypeStruct((sources * tokens, x.shape[1]), t) for x, t in zip(arrays, dtypes)],
        compiler_params=pltpu.CompilerParams(vmem_limit_bytes=40 << 20),
        cost_estimate=EARLY,
        name="unpack_tokens",
    )(info, spread, *arrays)


def collect_kernel(place_ref, x_ref, out_ref):
    tokens = place_ref.shape[0]
    lane = lax.broadcasted_iota(jnp.int32, (tokens, 128), 1)
    put = jnp.concatenate(
        [jnp.where(place_ref[...] == lane + 128 * b, 1.0, 0.0).astype(BF16) for b in range(x_ref.shape[0] // 128)],
        axis=1)
    total = dot(put, x_ref[...])

    @pl.when(pl.program_id(0) == 0)
    def _():
        out_ref[...] = total

    @pl.when(pl.program_id(0) > 0)
    def _():
        out_ref[...] += total


def collect(place, returned, send):
    experts, tokens = place.shape
    width = returned.shape[1]
    spread = jnp.broadcast_to(place.reshape(-1, 1), (experts * tokens, 128))
    return pl.pallas_call(
        collect_kernel,
        grid=(experts,),
        in_specs=[pl.BlockSpec((tokens, 128), lambda e: (e, 0)), pl.BlockSpec((send, width), lambda e: (e, 0))],
        out_specs=pl.BlockSpec((tokens, width), lambda e: (0, 0)),
        out_shape=jax.ShapeDtypeStruct((tokens, width), F32),
        compiler_params=pltpu.CompilerParams(vmem_limit_bytes=40 << 20),
        cost_estimate=EARLY,
        name="collect_rows",
    )(spread, returned)


def gelu_and_slope(v):
    c = math.sqrt(2.0 / math.pi)
    t = jnp.tanh(c * (v + 0.044715 * (v * v * v)))
    half = 0.5 * (1.0 + t)
    return v * half, half + 0.5 * v * (1.0 - t * t) * (c * (1.0 + 3 * 0.044715 * (v * v)))


def expert_kernel(sources, info, expert, x_ref, o_ref, c_ref, r_ref, wi_ref, wd_ref,
                  gi_ref, eo_ref, gg_ref, dwi_ref, dwd_ref, geo, gate, eo, gi, dwi, dwd):
    f = pl.program_id(0)
    last = pl.num_programs(0) - 1
    tiles = (info[2 * sources] + MOE_ROWS - 1) // MOE_ROWS
    lane = lax.broadcasted_iota(jnp.int32, (MOE_ROWS, 128), 1)

    def rows_of(i):
        return pl.ds(pl.multiple_of(i * MOE_ROWS, MOE_ROWS), MOE_ROWS)

    @pl.when(f == 0)
    def _():
        gi_ref[...] = jnp.zeros_like(gi_ref)
        eo_ref[...] = jnp.zeros_like(eo_ref)
        gg_ref[...] = jnp.zeros_like(gg_ref)

        def start(i, _):
            at = rows_of(i)
            logits = dot(x_ref[at, :], r_ref[...])
            mine = jnp.sum(jnp.where(lane == expert[0], logits, 0.0), axis=1, keepdims=True)
            other = jnp.sum(jnp.where(o_ref[at, :] > 0, logits, 0.0), axis=1, keepdims=True)
            top = jnp.maximum(mine, other)
            a, b = jnp.exp(mine - top), jnp.exp(other - top)
            g = a / (a + b)
            gate[at, :] = jnp.broadcast_to(g, (MOE_ROWS, 128))
            geo[at, :] = (c_ref[at, :].astype(F32) * g).astype(BF16)
            eo[at, :] = jnp.zeros((MOE_ROWS, eo.shape[1]), F32)
            gi[at, :] = jnp.zeros((MOE_ROWS, gi.shape[1]), F32)
            return 0
        lax.fori_loop(0, tiles, start, 0)

    dwi[...] = jnp.zeros_like(dwi)
    dwd[...] = jnp.zeros_like(dwd)

    def tile(i, _):
        at = rows_of(i)
        x, g = x_ref[at, :], geo[at, :]
        act, slope = gelu_and_slope(dot(x, wi_ref[...]))
        act = act.astype(BF16)
        eo[at, :] += dot(act, wd_ref[...])
        gh = (dot(g, wd_ref[...], NT) * slope).astype(BF16)
        gi[at, :] += dot(gh, wi_ref[...], NT)
        dwd[...] += dot(act, g, TN)
        dwi[...] += dot(x, gh, TN)
        return 0
    lax.fori_loop(0, tiles, tile, 0)
    dwi_ref[...] = dwi[...].astype(BF16)
    dwd_ref[...] = dwd[...].astype(BF16)

    @pl.when(f == last)
    def _():
        def finish(i, _):
            at = rows_of(i)
            out = eo[at, :].astype(BF16).astype(F32)
            gg = jnp.sum(out * c_ref[at, :].astype(F32), axis=1, keepdims=True)
            parts = split3(gg)
            spread = jnp.zeros((MOE_ROWS, 128), BF16)
            for n in range(3):
                spread = jnp.where(lane == n, jnp.broadcast_to(parts[n], (MOE_ROWS, 128)), spread)
            gg_ref[at, :] = spread
            eo_ref[at, :] = (out * gate[at, :1]).astype(BF16)
            gi_ref[at, :] = gi[at, :].astype(BF16)
            return 0
        lax.fori_loop(0, tiles, finish, 0)


def expert_layer(info, expert, x, other, cot, router, w_in, w_down, sources):
    room, width = x.shape
    hidden = w_in.shape[1]
    whole = lambda a: pl.BlockSpec(a.shape, lambda f, *_: (0, 0))
    fixed = lambda cols: pl.BlockSpec((room, cols), lambda f, *_: (0, 0))
    return pl.pallas_call(
        functools.partial(expert_kernel, sources),
        grid_spec=pltpu.PrefetchScalarGridSpec(
            num_scalar_prefetch=2, grid=(hidden // FF_TILE,),
            in_specs=[whole(x), whole(other), whole(cot), whole(router),
                      pl.BlockSpec((width, FF_TILE), lambda f, *_: (0, f)),
                      pl.BlockSpec((FF_TILE, width), lambda f, *_: (f, 0))],
            out_specs=[fixed(width), fixed(width), fixed(128),
                       pl.BlockSpec((width, FF_TILE), lambda f, *_: (0, f)),
                       pl.BlockSpec((FF_TILE, width), lambda f, *_: (f, 0))],
            scratch_shapes=[pltpu.VMEM((room, width), BF16), pltpu.VMEM((room, 128), F32),
                            pltpu.VMEM((room, width), F32), pltpu.VMEM((room, width), F32),
                            pltpu.VMEM((width, FF_TILE), F32), pltpu.VMEM((FF_TILE, width), F32)]),
        out_shape=[jax.ShapeDtypeStruct((room, width), BF16), jax.ShapeDtypeStruct((room, width), BF16),
                   jax.ShapeDtypeStruct((room, 128), BF16),
                   jax.ShapeDtypeStruct(w_in.shape, BF16), jax.ShapeDtypeStruct(w_down.shape, BF16)],
        compiler_params=pltpu.CompilerParams(vmem_limit_bytes=63 << 20),
        cost_estimate=EARLY,
        name="expert_layer",
    )(info, expert, x, other, cot, router, w_in, w_down)


MESH_ID = pl.DeviceIdType.MESH


def dense_kernel(q_ref, w_ref, s_ref, out_ref, small_ref, give, h, r0, ra1, rb1, ra2, rb2, rz, s_acc, s_got, s_all,
                 send, recv, s_send, s_recv):
    i, j = lax.axis_index("dp"), lax.axis_index("expert")
    y, x, z, c = i // 2, i % 2, j // 2, j % 2
    other_core = (i, z * 2 + 1 - c)
    other_x = (y * 2 + 1 - x, j)
    other_y = ((1 - y) * 2 + x, j)
    peers = [(i, (z + d) % 4 * 2 + c) for d in (1, 2, 3)]
    barrier = pltpu.get_barrier_semaphore()
    for device in [other_core, other_x, other_y] + peers:
        pl.semaphore_signal(barrier, inc=1, device_id=device, device_id_type=MESH_ID)
    pl.semaphore_wait(barrier, 6)

    def copy(n, src, dst, device):
        return pltpu.make_async_remote_copy(src_ref=src, dst_ref=dst, send_sem=send.at[n], recv_sem=recv.at[n],
                                            device_id=device, device_id_type=MESH_ID)

    def small_copy(n, src, dst, device):
        return pltpu.make_async_remote_copy(src_ref=src, dst_ref=dst, send_sem=s_send.at[n], recv_sem=s_recv.at[n],
                                            device_id=device, device_id_type=MESH_ID)

    def block(b, core):
        rows = jnp.concatenate([q_ref[b, core], w_ref[b, core]], axis=1)
        half = rows.shape[1] // 2
        return jnp.concatenate([rows[:, :half], rows[:, half:]], axis=0)

    small = small_copy(0, s_ref, s_got.at[0], other_core)
    small.start()
    copies = []
    for g in range(4):
        def convert(b, _):
            give[b] = block(b, 1 - c).astype(BF16)
            return 0
        lax.fori_loop(4 * g, 4 * g + 4, convert, 0)
        copies.append(copy(g, give.at[pl.ds(4 * g, 4)], r0.at[pl.ds(4 * g, 4)], other_core))
        copies[-1].start()
    small.wait()
    s_acc[0] = s_ref[...] + s_got[0]
    small = small_copy(1, s_acc.at[0], s_got.at[1], other_x)
    small.start()
    for g in range(4):
        copies[g].wait()
        def add(b, _):
            h[b // 8, b // 4 % 2, b % 4] = (block(b, c) + r0[b].astype(F32)).astype(BF16)
            return 0
        lax.fori_loop(4 * g, 4 * g + 4, add, 0)

    half = h.shape[4] // 2
    left, right = pl.ds(0, half), pl.ds(half, half)
    ca = copy(4, h.at[:, 1 - x, :, :, left], ra1, other_x)
    cb = copy(5, h.at[1 - y, :, :, :, right], rb1, other_y)
    ca.start()
    cb.start()
    small.wait()
    s_acc[1] = s_acc[0] + s_got[1]
    small = small_copy(2, s_acc.at[1], s_got.at[2], other_y)
    small.start()
    ca.wait()

    def add_x(b, _):
        u, v = b // 4, b % 4
        h[u, x, v, :, left] = (h[u, x, v, :, left].astype(F32) + ra1[u, v].astype(F32)).astype(BF16)
        return 0
    lax.fori_loop(0, 8, add_x, 0)
    ca = copy(6, h.at[1 - y, x, :, :, left], ra2, other_y)
    ca.start()
    cb.wait()

    def add_y(b, _):
        u, v = b // 4, b % 4
        h[y, u, v, :, right] = (h[y, u, v, :, right].astype(F32) + rb1[u, v].astype(F32)).astype(BF16)
        return 0
    lax.fori_loop(0, 8, add_y, 0)
    cb = copy(7, h.at[y, 1 - x, :, :, right], rb2, other_x)
    cb.start()
    small.wait()
    s_acc[2] = s_acc[1] + s_got[2]
    smalls = [small_copy(3 + n, s_acc.at[2], s_all.at[z], device) for n, device in enumerate(peers)]
    for one in smalls:
        one.start()
    ca.wait()
    cb.wait()

    def add_both(v, _):
        h[y, x, v, :, left] = (h[y, x, v, :, left].astype(F32) + ra2[v].astype(F32)).astype(BF16)
        h[y, x, v, :, right] = (h[y, x, v, :, right].astype(F32) + rb2[v].astype(F32)).astype(BF16)
        return 0
    lax.fori_loop(0, 4, add_both, 0)
    copies = [copy(8 + n, h.at[y, x, (z + 1 + n) % 4], rz.at[n], device) for n, device in enumerate(peers)]
    for one in copies:
        one.start()
    total = h[y, x, z].astype(F32)
    for one in smalls:
        one.wait()
    s_all[z] = s_acc[2]
    small_ref[...] = (s_all[0] + s_all[1]) + (s_all[2] + s_all[3])
    for n, one in enumerate(copies):
        one.wait()
        total = total + rz[n].astype(F32)
    rows = total.shape[0] // 2
    out_ref[:, :2 * half] = total[:rows]
    out_ref[:, 2 * half:] = total[rows:]


def dense_sum(grad_qkv, grad_out, small):
    rows, wide = grad_qkv.shape
    narrow = grad_out.shape[1]
    own = rows // 32
    width = wide + narrow
    half = width // 2
    pair = own * 2
    vmem = pl.BlockSpec(memory_space=pltpu.VMEM)
    return pl.pallas_call(
        dense_kernel,
        in_specs=[vmem] * 3, out_specs=[vmem] * 2,
        out_shape=[jax.ShapeDtypeStruct((own, width), F32), jax.ShapeDtypeStruct(small.shape, F32)],
        scratch_shapes=[
            pltpu.VMEM((16, pair, half), BF16), pltpu.VMEM((2, 2, 4, pair, half), BF16), pltpu.VMEM((16, pair, half), BF16),
            pltpu.VMEM((2, 4, pair, half // 2), BF16), pltpu.VMEM((2, 4, pair, half // 2), BF16),
            pltpu.VMEM((4, pair, half // 2), BF16), pltpu.VMEM((4, pair, half // 2), BF16), pltpu.VMEM((3, pair, half), BF16),
            pltpu.VMEM((3,) + small.shape, F32), pltpu.VMEM((3,) + small.shape, F32), pltpu.VMEM((4,) + small.shape, F32),
            pltpu.SemaphoreType.DMA((11,)), pltpu.SemaphoreType.DMA((11,)),
            pltpu.SemaphoreType.DMA((6,)), pltpu.SemaphoreType.DMA((6,))],
        compiler_params=pltpu.CompilerParams(collective_id=0, has_side_effects=True, vmem_limit_bytes=48 << 20),
        name="dense_sum",
    )(grad_qkv.reshape(16, 2, own, wide), grad_out.reshape(16, 2, own, narrow), small)


def exchange_pairs(normed_ffn, middle, cotangent, expert_ids, priority, router, w_in, w_down):
    rows, width = normed_ffn.shape
    logits = jnp.dot(normed_ffn, router, preferred_element_type=jnp.float32)
    experts_total = router.shape[1]
    picks = expert_ids[:, :, None] == jnp.arange(experts_total)[None, None, :]
    chosen = jnp.sum(jnp.where(picks, logits[:, None, :], 0.0), axis=2)
    gates = jax.nn.softmax(chosen, axis=-1)
    top = expert_ids.shape[1]
    levels = PRIO
    local_experts = w_in.shape[0]
    capacity = rows * top // local_experts
    send = max(2, 2 * rows * top // experts_total)
    flat_expert = expert_ids.reshape(-1)
    code = priority.reshape(-1) * experts_total + flat_expert
    onehot = (code[:, None] == jnp.arange(levels * experts_total)[None, :]).astype(jnp.int32)
    rank = jnp.sum((jnp.cumsum(onehot, axis=0) - onehot) * onehot, axis=1)
    counts = jnp.sum(onehot, axis=0)
    every = lax.all_gather(counts[None, :], "expert", axis=0, tiled=True).reshape(
        -1, levels, experts_total
    )
    expert_index = lax.axis_index("expert")
    totals = jnp.sum(every, axis=0)
    lower = jnp.cumsum(totals, axis=0) - totals
    earlier_sources = jnp.cumsum(every, axis=0) - every
    mine_prefix = lax.dynamic_index_in_dim(earlier_sources, expert_index, 0, keepdims=False)
    base = (lower + mine_prefix).reshape(-1)
    slot = rank + jnp.sum(onehot * base[None, :], axis=1)
    kept = slot < capacity
    own_counts = counts.reshape(levels, experts_total)
    own_lower = (jnp.cumsum(own_counts, axis=0) - own_counts).reshape(-1)
    place = rank + jnp.sum(onehot * own_lower[None, :], axis=1)
    target = flat_expert * send + place
    first_mine = expert_index * local_experts
    counts_mine = lax.dynamic_slice_in_dim(every, first_mine, local_experts, 2)
    base_mine = lax.dynamic_slice_in_dim(
        lower[None] + earlier_sources, first_mine, local_experts, 2
    )
    band_end = jnp.cumsum(counts_mine, axis=1)
    band_start = band_end - counts_mine
    place_index = jnp.arange(send, dtype=jnp.int32)
    level = jnp.sum(
        (place_index[None, None, None, :] >= band_end[:, :, :, None]).astype(jnp.int32), axis=1
    )
    level_hot = level[:, None, :, :] == jnp.arange(levels)[None, :, None, None]
    start_of = jnp.sum(jnp.where(level_hot, band_start[:, :, :, None], 0), axis=1)
    base_of = jnp.sum(jnp.where(level_hot, base_mine[:, :, :, None], 0), axis=1)
    arrived_slot = base_of + place_index[None, None, :] - start_of
    usable = (level < levels) & (arrived_slot < capacity)
    landing = jnp.where(
        usable,
        jnp.arange(local_experts)[None, :, None] * capacity + arrived_slot,
        local_experts * capacity,
    ).reshape(-1)
    live = landing < local_experts * capacity
    safe = jnp.minimum(landing, local_experts * capacity - 1)
    pair_inputs = jnp.repeat(normed_ffn, top, axis=0)
    outgoing = (
        jnp.zeros((experts_total * send, width), jnp.bfloat16)
        .at[target]
        .set(pair_inputs)
        .reshape(experts_total, send, width)
    )
    arrived = lax.all_to_all(outgoing, "expert", split_axis=0, concat_axis=0, tiled=True)
    expert_inputs = (
        jnp.zeros((local_experts * capacity, width), jnp.bfloat16)
        .at[landing]
        .set(arrived.reshape(-1, width), mode="drop")
        .reshape(local_experts, capacity, width)
    )
    hidden = jnp.einsum("ecd,edf->ecf", expert_inputs, w_in, preferred_element_type=jnp.float32)
    activated = jax.nn.gelu(hidden).astype(jnp.bfloat16)
    expert_out = jnp.einsum(
        "ecf,efd->ecd", activated, w_down, preferred_element_type=jnp.float32
    ).astype(jnp.bfloat16)
    returning = jnp.where(
        live[:, None],
        jnp.take(expert_out.reshape(-1, width), safe, axis=0),
        jnp.zeros((), jnp.bfloat16),
    ).reshape(experts_total, send, width)
    returned = lax.all_to_all(returning, "expert", split_axis=0, concat_axis=0, tiled=True)
    pair_out = jnp.where(
        kept[:, None],
        jnp.take(returned.reshape(-1, width), target, axis=0).astype(jnp.float32),
        0.0,
    ).reshape(rows, top, width)
    mixed = jnp.sum(gates[:, :, None] * pair_out, axis=1)
    grad_out = cotangent.astype(jnp.float32)
    grad_gates = jnp.sum(grad_out[:, None, :] * pair_out, axis=2)
    pair_grads = (gates[:, :, None] * grad_out[:, None, :]).astype(jnp.bfloat16).reshape(-1, width)
    outgoing_grads = (
        jnp.zeros((experts_total * send, width), jnp.bfloat16)
        .at[target]
        .set(pair_grads)
        .reshape(experts_total, send, width)
    )
    arrived_grads = lax.all_to_all(
        outgoing_grads, "expert", split_axis=0, concat_axis=0, tiled=True
    )
    grad_expert_out = (
        jnp.zeros((local_experts * capacity, width), jnp.bfloat16)
        .at[landing]
        .set(arrived_grads.reshape(-1, width), mode="drop")
        .reshape(local_experts, capacity, width)
    )
    hidden_again = jnp.einsum(
        "ecd,edf->ecf", expert_inputs, w_in, preferred_element_type=jnp.float32
    )
    activated_again, gelu_back = jax.vjp(jax.nn.gelu, hidden_again)
    grad_activated = jnp.einsum(
        "ecd,efd->ecf", grad_expert_out, w_down, preferred_element_type=jnp.float32
    )
    grad_hidden = gelu_back(grad_activated)[0].astype(jnp.bfloat16)
    grad_w_down = jnp.einsum(
        "ecf,ecd->efd",
        activated_again.astype(jnp.bfloat16),
        grad_expert_out,
        preferred_element_type=jnp.float32,
    )
    grad_w_in = jnp.einsum(
        "ecd,ecf->edf", expert_inputs, grad_hidden, preferred_element_type=jnp.float32
    )
    grad_inputs = jnp.einsum(
        "ecf,edf->ecd", grad_hidden, w_in, preferred_element_type=jnp.float32
    ).astype(jnp.bfloat16)
    back_rows = jnp.where(
        live[:, None],
        jnp.take(grad_inputs.reshape(-1, width), safe, axis=0),
        jnp.zeros((), jnp.bfloat16),
    ).reshape(experts_total, send, width)
    came_back = lax.all_to_all(back_rows, "expert", split_axis=0, concat_axis=0, tiled=True)
    pair_back = jnp.where(
        kept[:, None],
        jnp.take(came_back.reshape(-1, width), target, axis=0).astype(jnp.float32),
        0.0,
    )
    grad_normed_ffn = jnp.sum(pair_back.reshape(rows, top, width), axis=1)
    grad_chosen = gates * (grad_gates - jnp.sum(gates * grad_gates, axis=-1, keepdims=True))
    grad_logits = jnp.sum(jnp.where(picks, grad_chosen[:, :, None], 0.0), axis=1).astype(
        jnp.bfloat16
    )
    grad_normed_ffn = grad_normed_ffn + jnp.dot(
        grad_logits, router.T, preferred_element_type=jnp.float32
    )
    expert_parts = (
        lax.psum_scatter(grad_w_in.astype(jnp.bfloat16), "dp", scatter_dimension=1, tiled=True),
        lax.psum_scatter(grad_w_down.astype(jnp.bfloat16), "dp", scatter_dimension=1, tiled=True),
    )
    return mixed, grad_logits, grad_normed_ffn, expert_parts


def gather_codes(expert_ids, priority):
    return lax.all_gather(expert_ids * PRIO + priority, "expert", axis=0)


def plan_tokens(codes, rows, top):
    expert = lax.axis_index("expert").astype(jnp.int32)
    place, other = expert_slots(codes // PRIO, codes % PRIO, expert, rows * top)
    own_place = lax.all_to_all(place, "expert", split_axis=0, concat_axis=0, tiled=True)
    return own_place, half_plan(place, other, 0), half_plan(place, other, 1)


def expert_half(all_tokens, all_cotangents, number, half, router, w_in, w_down, send):
    info, place, other_hot = half
    sources, tokens = place.shape
    room = (4 * tokens + 16 * sources + send + MOE_ROWS - 1) // MOE_ROWS * MOE_ROWS
    expert = lax.axis_index("expert").astype(jnp.int32)
    (packed_cot,) = pack(info, place, [all_cotangents], room, 2, number)
    packed, packed_other = pack(info, place, [all_tokens, other_hot], room)
    grad_rows, mixed_rows, grad_gate, grad_w_in, grad_w_down = expert_layer(
        info, expert[None], packed, packed_other, packed_cot, router, w_in[0], w_down[0], sources
    )
    grad_all, gate_all = unpack(info, place, [grad_rows, grad_gate], [jnp.bfloat16, jnp.float32], send)
    gate_all = jnp.sum(gate_all[:, :3], axis=1).reshape(sources, tokens)
    return grad_all, gate_all, mixed_rows, grad_w_in, grad_w_down


def exchange_tokens(normed_halves, all_cotangents, plan, expert_ids, router, w_in, w_down):
    rows = expert_ids.shape[0]
    experts_total = router.shape[1]
    top = expert_ids.shape[1]
    own_place, *halves = plan
    send = 2 * rows * top // experts_total
    wide_router = jnp.pad(router, ((0, 0), (0, 128 - experts_total)))
    tokens = [lax.all_gather(x, "expert", axis=0, tiled=True) for x in normed_halves]
    first = expert_half(tokens[0], all_cotangents, 0, halves[0], wide_router, w_in, w_down, send)
    grad_own = [lax.psum_scatter(first[0], "expert", scatter_dimension=0, tiled=True)]
    tokens[1], all_cotangents, _ = lax.optimization_barrier((tokens[1], all_cotangents, first))
    second = expert_half(tokens[1], all_cotangents, 1, halves[1], wide_router, w_in, w_down, send)
    grad_later, grad_own[0] = lax.optimization_barrier((second[0], grad_own[0]))
    grad_own.append(lax.psum_scatter(grad_later, "expert", scatter_dimension=0, tiled=True))
    gate_all = jnp.concatenate([first[1], second[1]], axis=1)
    gate_own = lax.all_to_all(gate_all, "expert", split_axis=0, concat_axis=0, tiled=True)
    info, later = halves[0][0], halves[1][0]
    sources = halves[0][1].shape[0]
    shifted = jnp.pad(second[2], ((send, 0), (0, 0)))
    row = jnp.arange(send)[:, None]
    windows = jnp.concatenate([
        jnp.where(
            row < info[sources + d],
            lax.dynamic_slice_in_dim(first[2], info[d], send, 0),
            lax.dynamic_slice_in_dim(shifted, later[d] + send - info[sources + d], send, 0),
        )
        for d in range(sources)
    ], axis=0)
    grad_w_in, grad_w_down = first[3] + second[3], first[4] + second[4]
    grad_own = jnp.concatenate(grad_own, axis=0)
    normed_ffn = jnp.concatenate(normed_halves, axis=0)
    windows, grad_w_in, grad_w_down, grad_own = lax.optimization_barrier(
        (windows, grad_w_in, grad_w_down, grad_own)
    )
    mixed = (lax.all_to_all(windows, "expert", split_axis=0, concat_axis=0, tiled=True), own_place)
    expert_parts = (
        lax.psum_scatter(grad_w_in[None], "dp", scatter_dimension=1, tiled=True),
        lax.psum_scatter(grad_w_down[None], "dp", scatter_dimension=1, tiled=True),
    )
    logits = jnp.dot(normed_ffn, router, preferred_element_type=jnp.float32)
    picks = expert_ids[:, :, None] == jnp.arange(experts_total)[None, None, :]
    chosen = jnp.sum(jnp.where(picks, logits[:, None, :], 0.0), axis=2)
    gates = jax.nn.softmax(chosen, axis=-1)
    grad_gates = jnp.sum(jnp.where(picks, gate_own.T[:, None, :], 0.0), axis=2)
    grad_chosen = gates * (grad_gates - jnp.sum(gates * grad_gates, axis=-1, keepdims=True))
    grad_logits = jnp.sum(jnp.where(picks, grad_chosen[:, :, None], 0.0), axis=1).astype(
        jnp.bfloat16
    )
    grad_normed_ffn = grad_own.astype(jnp.float32) + jnp.dot(
        grad_logits, router.T, preferred_element_type=jnp.float32
    )
    return mixed, grad_logits, grad_normed_ffn, expert_parts


def per_device(
    tokens_in,
    cont_ids,
    expert_ids,
    priority,
    gain_attn,
    w_qkv,
    rel_table,
    w_out,
    gain_ffn,
    w_router,
    w_in,
    w_down,
    cotangent,
):
    rows, width = tokens_in.shape
    heads = rel_table.shape[1]
    dp_count = lax.axis_size("dp")
    dp_index = lax.axis_index("dp")
    prompt_rows = PROMPT // dp_count
    few_experts = lax.axis_size("expert") <= 16 and w_in.shape[0] == 1 and prompt_rows == KT
    local_ids = cont_ids[0]
    info = info_of(local_ids, dp_index)
    row_start = row_start_of(local_ids)
    rows_bias = bias_rows(rel_table)
    if few_experts:
        codes = gather_codes(expert_ids, priority)
    experts_total = w_router.shape[1]
    dense = jnp.concatenate(
        [pairs_together(w_qkv), w_out, jnp.pad(w_router, ((0, 0), (0, 128 - experts_total)))], axis=1
    )
    dense = lax.all_gather(dense, ("dp", "expert"), axis=0, tiled=True)
    part_heads = heads // PARTS
    tables = [bias_tables(info, rows_bias, row_start, g * part_heads, part_heads) for g in range(PARTS)]
    dense, tables[0] = lax.optimization_barrier((dense, tables[0]))
    if few_experts:
        plan = plan_tokens(codes, rows, expert_ids.shape[1])
        dense, plan = lax.optimization_barrier((dense, plan))
    whole_qkv, whole_out = dense[:, : 3 * width], dense[:, 3 * width : 4 * width]
    whole_router = dense[:, 4 * width : 4 * width + experts_total]
    inputs = tokens_in.astype(jnp.float32)
    normed_attn = normed(inputs, gain_attn).astype(jnp.bfloat16)
    projected = jnp.dot(normed_attn, whole_qkv, preferred_element_type=jnp.float32).astype(
        jnp.bfloat16
    )
    parts = PARTS
    columns = 2 * width // parts
    kept = [projected[:, width + columns * g : width + columns * (g + 1)] for g in range(parts)]
    gathered = [lax.all_gather(kept[0][:prompt_rows], "dp", axis=0, tiled=True)]
    for kv in kept[1:]:
        copies = jnp.broadcast_to(kv[None, :prompt_rows], (dp_count, prompt_rows, columns))
        gathered.append(
            lax.all_to_all(copies, "dp", split_axis=0, concat_axis=0, tiled=True).reshape(PROMPT, columns)
        )
    if few_experts:
        late_cotangent, gathered[0], tables = lax.optimization_barrier((cotangent, gathered[0], tables))
        all_cotangents = lax.all_gather(late_cotangent, "expert", axis=0, tiled=True)
    gathered[0], tables = lax.optimization_barrier((gathered[0], tables))
    results = {}
    keys_values = []
    middles, normed_halves, attended_halves = [], [], []
    order = [(g, c) for g in range(parts) for c in (0, 1)]

    def after_attention(c):
        attended = jnp.concatenate([results[g, c][0] for g in range(parts)], axis=1).astype(jnp.bfloat16)
        middle = inputs[c * KT : (c + 1) * KT] + jnp.dot(attended, whole_out, preferred_element_type=jnp.float32)
        attended_halves.append(attended)
        middles.append(middle)
        normed_halves.append(normed(middle, gain_ffn).astype(jnp.bfloat16))

    last = None
    for g, c in order:
        if last is not None:
            gathered[g], results[last] = lax.optimization_barrier((gathered[g], results[last]))
        if c == 0:
            source = gathered[g]
        else:
            source = jnp.concatenate([gathered[g], kept[g][prompt_rows:]], axis=0)
            keys_values.append(source)
        results[g, c] = attention_forward(info, projected, source, tables[g], g, bool(c))
        last = (g, c)
        if (g, c) == (parts - 1, 0):
            after_attention(0)
            if few_experts:
                normed_halves[0], all_cotangents = lax.optimization_barrier((normed_halves[0], all_cotangents))
            gathered[g], normed_halves[0] = lax.optimization_barrier((gathered[g], normed_halves[0]))
    after_attention(1)
    exact = [jnp.concatenate([results[g, 0][0], results[g, 1][0]], axis=0) for g in range(parts)]
    log_total = [jnp.concatenate([results[g, 0][1], results[g, 1][1]], axis=0) for g in range(parts)]
    attended = jnp.concatenate(attended_halves, axis=0)
    middle = jnp.concatenate(middles, axis=0)
    normed_ffn = jnp.concatenate(normed_halves, axis=0)
    if few_experts:
        mixed, grad_logits, grad_normed_ffn, expert_parts = exchange_tokens(
            normed_halves, all_cotangents, plan, expert_ids, whole_router, w_in, w_down
        )
    else:
        mixed, grad_logits, grad_normed_ffn, expert_parts = exchange_pairs(
            normed_ffn, middle, cotangent, expert_ids, priority, whole_router, w_in, w_down
        )
    grad_out = cotangent.astype(jnp.float32)
    grad_router = jnp.dot(normed_ffn.T, grad_logits, preferred_element_type=jnp.float32)
    _, ffn_norm_back = jax.vjp(normed, middle, gain_ffn)
    grad_middle_part, grad_gain_ffn = ffn_norm_back(grad_normed_ffn)
    grad_middle = grad_out + grad_middle_part
    grad_branch = grad_middle.astype(jnp.bfloat16)
    grad_out_weight = jnp.dot(attended.T, grad_branch, preferred_element_type=jnp.float32)
    grad_attended = jnp.dot(
        grad_branch, whole_out.T, preferred_element_type=jnp.float32
    ).astype(jnp.bfloat16)
    grad_queries, grad_prompts, grad_conts, grad_lines = [], [], [], []
    for g in range(parts):
        if g:
            grad_attended, expert_parts, grad_queries[-1] = lax.optimization_barrier(
                (grad_attended, expert_parts, grad_queries[-1])
            )
        grad_query, grad_kv, lines = attention_backward(
            info, projected, grad_attended, exact[g], log_total[g], keys_values[g], tables[g], g
        )
        grad_queries.append(grad_query)
        grad_prompts.append(lax.psum_scatter(grad_kv[:PROMPT], "dp", scatter_dimension=0, tiled=True))
        grad_conts.append(grad_kv[PROMPT:])
        grad_lines.append(lines)
    mixed, middle, grad_queries[-1] = lax.optimization_barrier((mixed, middle, grad_queries[-1]))
    if few_experts:
        returned, own_place = mixed
        mixed = collect(own_place, returned, returned.shape[0] // own_place.shape[0])
    output = (middle + mixed).astype(jnp.bfloat16)
    grad_table = table_grad(jnp.concatenate(grad_lines, axis=0), rel_table.shape[0])
    grad_projected = jnp.concatenate(
        grad_queries + [jnp.concatenate([a, b], axis=0) for a, b in zip(grad_prompts, grad_conts)], axis=1
    )
    grad_normed_attn = jnp.dot(grad_projected, whole_qkv.T, preferred_element_type=jnp.float32)
    grad_qkv = jnp.dot(normed_attn.T, grad_projected, preferred_element_type=jnp.float32)
    _, attn_norm_back = jax.vjp(normed, inputs, gain_attn)
    grad_inputs_part, grad_gain_attn = attn_norm_back(grad_normed_attn)
    grad_tokens = grad_middle + grad_inputs_part
    if (dp_count, lax.axis_size("expert")) == (4, 8):
        pieces = [grad_gain_attn, grad_gain_ffn, grad_table.reshape(-1), grad_router.reshape(-1)]
        sizes = [piece.shape[0] for piece in pieces]
        small = jnp.concatenate(pieces)
        small = jnp.pad(small, (0, -small.shape[0] % 1024)).reshape(-1, 128)
        dense_grad, small = dense_sum(grad_qkv, grad_out_weight, small)
        ends = [sum(sizes[: n + 1]) for n in range(4)]
        flat = small.reshape(-1)
        grad_gain_attn, grad_gain_ffn = flat[: ends[0]], flat[ends[0] : ends[1]]
        grad_table = flat[ends[1] : ends[2]].reshape(grad_table.shape)
        own_rows = w_router.shape[0]
        mine = (dp_index * lax.axis_size("expert") + lax.axis_index("expert")) * own_rows
        own_router = lax.dynamic_slice_in_dim(
            flat[ends[2] : ends[3]].reshape(grad_router.shape), mine, own_rows, 0
        )
        small_parts = (grad_gain_attn, grad_gain_ffn, grad_table.T)
    else:
        dense_grad = lax.psum_scatter(
            jnp.concatenate([grad_qkv, grad_out_weight], axis=1), ("dp", "expert"), scatter_dimension=0, tiled=True
        )
        own_router = lax.psum_scatter(grad_router, ("dp", "expert"), scatter_dimension=0, tiled=True)
        small_parts = lax.psum((grad_gain_attn, grad_gain_ffn, grad_table.T), ("dp", "expert"))
    return (
        output,
        grad_tokens,
        small_parts[0],
        pairs_apart(dense_grad[:, : 3 * width]),
        small_parts[2],
        dense_grad[:, 3 * width :],
        small_parts[1],
        own_router,
        expert_parts[0].astype(jnp.float32),
        expert_parts[1].astype(jnp.float32),
    )


def solution(mesh):
    return jax.shard_map(
        per_device,
        mesh=mesh,
        in_specs=(
            P(("dp", "expert"), None),
            P(("dp", "expert"), None),
            P(("dp", "expert"), None),
            P(("dp", "expert"), None),
            P(),
            P(("dp", "expert"), None),
            P(),
            P(("dp", "expert"), None),
            P(),
            P(("dp", "expert"), None),
            P("expert", None, None),
            P("expert", None, None),
            P(("dp", "expert"), None),
        ),
        out_specs=(
            P(("dp", "expert"), None),
            P(("dp", "expert"), None),
            P(),
            P(("dp", "expert"), None),
            P(),
            P(("dp", "expert"), None),
            P(),
            P(("dp", "expert"), None),
            P("expert", "dp", None),
            P("expert", "dp", None),
        ),
        check_vma=False,
    )
```

```python
import functools
import math
import jax
import jax.numpy as jnp
from jax import lax
from jax.experimental import pallas as pl
from jax.experimental.pallas import tpu as pltpu
from jax.sharding import PartitionSpec as P

PRIO = 4
PROMPT = 2048


BORDERS = (16, 24, 32, 48, 64, 96, 128, 192, 256, 384, 512, 768, 1024, 1536, 2048)
EPSILON = 1e-06
MASKED = -1e30


def bucket_of(distance):
    distance = jnp.maximum(distance, 0)
    counted = jnp.minimum(distance, 15)
    for border in BORDERS:
        counted = counted + (distance >= border).astype(jnp.int32)
    return counted


def normed(values, gain):
    return values * lax.rsqrt(jnp.mean(values * values, axis=-1, keepdims=True) + EPSILON) * gain


def pairs_together(w_qkv):
    width = w_qkv.shape[1] // 3
    rows = w_qkv.shape[0]
    keys_values = w_qkv[:, width:].reshape(rows, 2, width // 128, 128).swapaxes(1, 2)
    return jnp.concatenate([w_qkv[:, :width], keys_values.reshape(rows, 2 * width)], axis=1)


def pairs_apart(grad):
    width = grad.shape[1] // 3
    rows = grad.shape[0]
    keys_values = grad[:, width:].reshape(rows, width // 128, 2, 128).swapaxes(1, 2)
    return jnp.concatenate([grad[:, :width], keys_values.reshape(rows, 2 * width)], axis=1)


LOG2E = math.log2(math.e)
F32, BF16 = jnp.float32, jnp.bfloat16
QT = 256
KT = 512
RUN = 256
EARLY = pl.CostEstimate(flops=1 << 20, bytes_accessed=1 << 20, transcendentals=0)
PARTS = 2
ROWS = 32
NT = (((1,), (1,)), ((), ()))
NN = (((1,), (0,)), ((), ()))

def dot(a, b, dims=NN):
    return lax.dot_general(a, b, dims, preferred_element_type=F32)

def bias_rows(rel_table):
    width = PROMPT + 512 + RUN
    distance = PROMPT + RUN - jnp.arange(width)[None, :] + jnp.arange(8)[:, None]
    bucket = bucket_of(distance)
    table = rel_table.T[:, None, None, :] * LOG2E
    hot = (bucket[..., None] == jnp.arange(rel_table.shape[0])).astype(F32)
    rows = jnp.sum(hot[None] * table, axis=-1)
    return jnp.where(distance[None] >= 0, rows, MASKED)

def bias_kernel(info, base_ref, row_start, t_ref, b_ref):
    base, t_scr, b_scr = base_ref[0], t_ref.at[0], b_ref.at[0]
    width = base.shape[-1]
    for a in range(16):
        t_scr[8 * a:8 * a + 8, :] = pltpu.roll(base, 8 * a, 1) if a else base
    lane = lax.broadcasted_iota(jnp.int32, (ROWS, 128), 1)
    sub = lax.broadcasted_iota(jnp.int32, (ROWS, 128), 0)
    for s in range(4):
        start, end = info[s], info[s + 1]
        turn = start % 128
        left = (128 - turn) % 128
        here = (lane < left) | (left == 0)
        def place(g, _):
            at = pl.ds(pl.multiple_of(ROWS * g, ROWS), ROWS)
            first = start - turn + RUN - 128 * (g // (128 // ROWS))
            of = pl.ds(pl.multiple_of(ROWS * (g % (128 // ROWS)), ROWS), ROWS)
            mine = sub + ROWS * g >= start
            turned = None
            for b in range(PROMPT // 128 + 1):
                after = pltpu.roll(t_scr[of, pl.ds(pl.multiple_of(first + 128 * b, 128), 128)], left, 1)
                if b:
                    cols = slice(128 * b - 128, 128 * b)
                    b_scr[at, cols] = jnp.where(mine, jnp.where(here, turned, after), b_scr[at, cols])
                turned = after
            return 0
        lax.fori_loop(start // ROWS, (end + ROWS - 1) // ROWS, place, 0)
    lane = lax.broadcasted_iota(jnp.int32, (128, 128), 1)
    for i in range(KT // 128):
        rows = slice(128 * i, 128 * i + 128)
        own = row_start[rows, :]
        for b in range(KT // 128):
            first = PROMPT + RUN - 128 * i + 128 * b
            b_scr[rows, PROMPT + 128 * b:PROMPT + 128 * b + 128] = jnp.where(
                lane + 128 * b >= own, t_scr[:, first:first + 128], MASKED)

def bias_tables(info, rows_bias, row_start, first, heads):
    wide = rows_bias.shape[2]
    block = lambda rows, cols: pl.BlockSpec((1, rows, cols), lambda h, *_: (h, 0, 0))
    return pl.pallas_call(
        bias_kernel,
        grid_spec=pltpu.PrefetchScalarGridSpec(
            num_scalar_prefetch=1, grid=(heads,),
            in_specs=[pl.BlockSpec((1, 8, wide), lambda h, *_: (first + h, 0, 0)),
                      pl.BlockSpec((KT, 128), lambda h, *_: (0, 0))],
            out_specs=[block(128, wide), block(KT, PROMPT + KT)]),
        out_shape=[jax.ShapeDtypeStruct((heads, 128, wide), F32),
                   jax.ShapeDtypeStruct((heads, KT, PROMPT + KT), F32)],
        compiler_params=pltpu.CompilerParams(vmem_limit_bytes=32 << 20),
        cost_estimate=EARLY,
        name="bias_tables",
    )(info, rows_bias, row_start)

def own_lanes(h, rows):
    lane = lax.broadcasted_iota(jnp.int32, (rows, 128), 1)
    return lane // 64 == h % 2

def fwd_kernel(scale2, cont, info, q_ref, k_ref, v_ref, table_ref, o_ref, lse_ref):
    h = pl.program_id(0)
    dp = info[5]
    table = table_ref.at[0]
    own = own_lanes(h, QT)
    head_lane = lax.broadcasted_iota(jnp.int32, (QT, 128), 1) == h

    def tile(first, key_tiles, bias_of, block):
        rows = pl.ds(first, QT)
        q = jnp.where(own, q_ref[rows, :], jnp.zeros((), BF16))
        def step(t, carry):
            m, l, acc = carry
            cols = pl.ds(pl.multiple_of(block(t) * KT, KT), KT)
            s = dot(q, k_ref[cols, :], NT) * scale2 + bias_of(t)
            new = jnp.maximum(m, jnp.max(s, axis=1, keepdims=True))
            keep = jnp.exp2(m - new)
            p = jnp.exp2(s - jnp.concatenate([new] * (KT // 128), axis=1))
            part = p[:, :128]
            for c in range(1, KT // 128):
                part = part + p[:, 128 * c:128 * (c + 1)]
            return new, l * keep + part, acc * keep + dot(p.astype(BF16), v_ref[cols, :])
        zero = jnp.zeros((QT, 128), F32)
        m, l, acc = lax.fori_loop(0, key_tiles, step, (jnp.full((QT, 128), MASKED, F32), zero, zero))
        l = jnp.sum(l, axis=1, keepdims=True)
        o_ref[rows, :] = jnp.where(own, acc / l, o_ref[rows, :])
        lse_ref[rows, :] = jnp.where(head_lane, m + jnp.log2(l), lse_ref[rows, :])

    for j in range(KT // QT):
        if cont:
            tile(QT * j, PROMPT // KT + 1,
                 lambda t: table[pl.ds(QT * j, QT), pl.ds(pl.multiple_of(t * KT, KT), KT)], lambda t: t)
            continue
        shift = PROMPT - KT * dp - QT * j + RUN
        def bias(t, shift=shift):
            first = (dp - t) * KT + shift
            return jnp.concatenate([table[:, pl.ds(pl.multiple_of(first - 128 * x, 128), KT)] for x in range(QT // 128)], axis=0)
        tile(QT * j, dp + 1, bias, lambda t: dp - t)

def attention_forward(info, projected, keys_values, tables, part, cont):
    keys, columns = keys_values.shape
    heads = columns // 128
    scale2 = 64 ** -0.5 * LOG2E
    first = part * heads // 2
    table = tables[int(cont)]
    return pl.pallas_call(
        functools.partial(fwd_kernel, scale2, cont),
        grid_spec=pltpu.PrefetchScalarGridSpec(
            num_scalar_prefetch=1, grid=(heads,),
            in_specs=[pl.BlockSpec((KT, 128), lambda h, *_: (int(cont), first + h // 2)),
                      pl.BlockSpec((keys, 128), lambda h, *_: (0, h // 2 * 2)),
                      pl.BlockSpec((keys, 128), lambda h, *_: (0, h // 2 * 2 + 1)),
                      pl.BlockSpec((1,) + table.shape[1:], lambda h, *_: (h, 0, 0))],
            out_specs=[pl.BlockSpec((KT, 128), lambda h, *_: (0, h // 2)),
                       pl.BlockSpec((KT, 128), lambda h, *_: (0, 0))]),
        out_shape=[jax.ShapeDtypeStruct((KT, heads * 64), F32), jax.ShapeDtypeStruct((KT, 128), F32)],
        compiler_params=pltpu.CompilerParams(vmem_limit_bytes=60 << 20),
        cost_estimate=EARLY,
        name="attention_forward",
    )(info, projected, keys_values, keys_values, table)

def split3(x):
    hi = x.astype(BF16)
    rest = x - hi.astype(F32)
    mid = rest.astype(BF16)
    return hi, mid, (rest - mid.astype(F32)).astype(BF16)

def bwd_kernel(scale, cont, info, q_ref, do_ref, o_ref, lse_ref, k_ref, v_ref, table_ref, *refs):
    if cont:
        prev_ref, dq_ref, dkv_ref, dd_ref, e_scr, qa, da, ka, va, qt, dot_t, dkt, dvt, db_scr = refs
    else:
        dq_ref, dkv_ref, dd_ref, e_scr, qa, da, ka, va, qt, dot_t, dkt, dvt = refs
    table = table_ref.at[0]
    h = pl.program_id(0)
    dp = info[5]
    n, keys = q_ref.shape[0], k_ref.shape[0]
    half = h % 2
    base = pl.multiple_of(64 * half, 64)
    other = 64 - 64 * half

    @pl.when(half == 0)
    def _():
        qt[...] = q_ref[...].T
        dot_t[...] = do_ref[...].T
        dq_ref[...] = jnp.zeros_like(dq_ref)

    lane_n = lax.broadcasted_iota(jnp.int32, (QT, 128), 1)
    own_n = lane_n // 64 == half
    def augment(i, _):
        rows = pl.ds(pl.multiple_of(i * QT, QT), QT)
        lse = jnp.sum(jnp.where(lane_n == h, lse_ref[rows, :], 0.0), axis=1, keepdims=True)
        parts = split3(-lse / (scale * LOG2E))
        aug = jnp.zeros((QT, 128), BF16)
        for x in range(3):
            aug = jnp.where(lane_n == other + x, jnp.broadcast_to(parts[x], (QT, 128)), aug)
        qa[rows, :] = jnp.where(own_n, q_ref[rows, :], aug)
        do = do_ref[rows, :]
        delta = jnp.sum(jnp.where(own_n, do.astype(F32) * o_ref[rows, :], 0.0), axis=1, keepdims=True)
        parts = split3(-delta)
        aug = jnp.zeros((QT, 128), BF16)
        for x in range(3):
            aug = jnp.where(lane_n == other + x, jnp.broadcast_to(parts[x], (QT, 128)), aug)
        da[rows, :] = jnp.where(own_n, do, aug)
        return 0
    lax.fori_loop(0, n // QT, augment, 0)
    lane_k = lax.broadcasted_iota(jnp.int32, (KT, 128), 1)
    ones = jnp.where((lane_k >= other) & (lane_k < other + 3), 1.0, 0.0).astype(BF16)
    own_k = lane_k // 64 == half
    def augment_keys(i, _):
        rows = pl.ds(pl.multiple_of(i * KT, KT), KT)
        ka[rows, :] = jnp.where(own_k, k_ref[rows, :], ones)
        va[rows, :] = jnp.where(own_k, v_ref[rows, :], ones)
        return 0
    lax.fori_loop(0, keys // KT, augment_keys, 0)
    head_rows = pl.ds(base, 64)
    dkt[head_rows, :] = jnp.zeros((64, keys), F32)
    dvt[head_rows, :] = jnp.zeros((64, keys), F32)
    e_scr[...] = jnp.zeros_like(e_scr)

    def tile(first, key_tiles, bias_of, grad_bias):
        rows = pl.ds(first, QT)
        q, do = qa[rows, :], da[rows, :]
        q_t, do_t = qt[head_rows, rows], dot_t[head_rows, rows]
        def step(t, dq):
            cols = pl.ds(pl.multiple_of(t * KT, KT), KT)
            kk = ka[cols, :]
            p = jnp.exp2(dot(q, kk, NT) * (scale * LOG2E) + bias_of(t))
            ds = p * dot(do, va[cols, :], NT)
            grad_bias(t, ds)
            low = ds.astype(BF16)
            dvt[head_rows, cols] += dot(do_t, p.astype(BF16))
            dkt[head_rows, cols] += dot(q_t, low)
            return dq + dot(low, kk)
        dq = lax.fori_loop(0, key_tiles, step, jnp.zeros((QT, 128), F32))
        dq_ref[rows, :] = jnp.where(own_n, dq * scale, dq_ref[rows, :].astype(F32)).astype(BF16)

    for j in range(KT // QT):
        if cont:
            def where(t):
                return (pl.ds(QT * j, QT), pl.ds(pl.multiple_of(t * KT, KT), KT))
            def put(t, ds):
                db_scr[where(t)] = ds
            tile(QT * j, PROMPT // KT + 1, lambda t: table[where(t)], put)
            continue
        shift = PROMPT - KT * dp - QT * j + RUN
        def part(t, x, shift=shift):
            return (slice(None), pl.ds(pl.multiple_of(t * KT + shift - 128 * x, 128), KT))
        def bias(t):
            return jnp.concatenate([table[part(t, x)] for x in range(QT // 128)], axis=0)
        def add(t, ds):
            for x in range(QT // 128):
                e_scr[part(t, x)] += ds[128 * x:128 * x + 128, :]
        tile(QT * j, dp + 1, bias, add)

    if cont:
        lane = lax.broadcasted_iota(jnp.int32, (ROWS, 128), 1)
        sub = lax.broadcasted_iota(jnp.int32, (ROWS, 128), 0)
        for s in range(4):
            start, end = info[s], info[s + 1]
            turn = start % 128
            def fold(g, _):
                at = pl.ds(pl.multiple_of(ROWS * g, ROWS), ROWS)
                first = start - turn + RUN - 128 * (g // (128 // ROWS))
                to = pl.ds(pl.multiple_of(ROWS * (g % (128 // ROWS)), ROWS), ROWS)
                mine = (sub + ROWS * g >= start) & (sub + ROWS * g < end)
                before = jnp.zeros((ROWS, 128), F32)
                for b in range(PROMPT // 128 + 1):
                    if b < PROMPT // 128:
                        turned = pltpu.roll(jnp.where(mine, db_scr[at, 128 * b:128 * b + 128], 0.0), turn, 1)
                    else:
                        turned = jnp.zeros((ROWS, 128), F32)
                    e_scr[to, pl.ds(pl.multiple_of(first + 128 * b, 128), 128)] += jnp.where(lane >= turn, turned, before)
                    before = turned
                return 0
            lax.fori_loop(start // ROWS, (end + ROWS - 1) // ROWS, fold, 0)
        for i in range(KT // 128):
            first = PROMPT + RUN - 128 * i
            e_scr[:, first:first + KT] += db_scr[128 * i:128 * i + 128, PROMPT:]
    width = e_scr.shape[1]
    acc = e_scr[0:8, :]
    for a in range(1, 16):
        acc = acc + pltpu.roll(e_scr[8 * a:8 * a + 8, :], width - 8 * a, 1)
    total = acc[0:1, :]
    for i in range(1, 8):
        total = total + pltpu.roll(acc, width - i, 1)[i:i + 1, :]
    dd_ref[0] = total

    @pl.when(half == 1)
    def _():
        for at, total in ((0, dkt[...] * scale), (128, dvt[...])):
            total = total.T
            if cont:
                dkv_ref[:PROMPT, at:at + 128] = (total[:PROMPT] + prev_ref[:, at:at + 128].astype(F32)).astype(BF16)
                dkv_ref[PROMPT:, at:at + 128] = total[PROMPT:].astype(BF16)
            else:
                dkv_ref[:, at:at + 128] = total.astype(BF16)

def attention_backward(info, projected, do, o32, lse, keys_values, tables, part, cont, prev):
    keys, columns = keys_values.shape
    heads = columns // 128
    wide = tables[0].shape[2]
    first = part * heads // 2
    own = pl.BlockSpec((KT, 128), lambda h, *_: (0, h // 2))
    table = tables[int(cont)]
    before = [pl.BlockSpec((PROMPT, 256), lambda h, *_: (0, h // 2))] if cont else []
    scores = [pltpu.VMEM((KT, PROMPT + KT), F32)] if cont else []
    return pl.pallas_call(
        functools.partial(bwd_kernel, 64 ** -0.5, cont),
        grid_spec=pltpu.PrefetchScalarGridSpec(
            num_scalar_prefetch=1, grid=(heads,),
            in_specs=[pl.BlockSpec((KT, 128), lambda h, *_: (int(cont), first + h // 2)),
                      pl.BlockSpec((KT, 128), lambda h, *_: (0, first + h // 2)),
                      own, pl.BlockSpec((KT, 128), lambda h, *_: (0, 0)),
                      pl.BlockSpec((keys, 128), lambda h, *_: (0, h // 2 * 2)),
                      pl.BlockSpec((keys, 128), lambda h, *_: (0, h // 2 * 2 + 1)),
                      pl.BlockSpec((1,) + table.shape[1:], lambda h, *_: (h, 0, 0))] + before,
            out_specs=[own, pl.BlockSpec((keys, 256), lambda h, *_: (0, h // 2)),
                       pl.BlockSpec((1, 1, wide), lambda h, *_: (h, 0, 0))],
            scratch_shapes=[pltpu.VMEM((128, wide), F32),
                            pltpu.VMEM((KT, 128), BF16), pltpu.VMEM((KT, 128), BF16),
                            pltpu.VMEM((keys, 128), BF16), pltpu.VMEM((keys, 128), BF16),
                            pltpu.VMEM((128, KT), BF16), pltpu.VMEM((128, KT), BF16),
                            pltpu.VMEM((128, keys), F32), pltpu.VMEM((128, keys), F32)] + scores),
        out_shape=[jax.ShapeDtypeStruct((KT, heads * 64), BF16), jax.ShapeDtypeStruct((keys, columns), BF16),
                   jax.ShapeDtypeStruct((heads, 1, wide), F32)],
        compiler_params=pltpu.CompilerParams(vmem_limit_bytes=60 << 20),
        cost_estimate=EARLY,
        name="attention_backward",
    )(info, projected, do, o32, lse, keys_values, keys_values, table, *([prev] if cont else []))

def info_of(ids, dp):
    starts = jnp.sum((ids[None, :] < jnp.arange(5)[:, None]).astype(jnp.int32), axis=1)
    return jnp.concatenate([starts, jnp.reshape(dp, (1,)).astype(jnp.int32)])

def table_grad(dd, buckets):
    width = dd.shape[2]
    distance = PROMPT + RUN - jnp.arange(width)
    hot = ((bucket_of(distance)[:, None] == jnp.arange(buckets)[None, :]) & (distance >= 0)[:, None]).astype(F32)
    return jnp.dot(dd[:, 0, :], hot, precision=lax.Precision.HIGHEST)

def row_start_of(ids):
    starts = jnp.sum((ids[None, :] < ids[:, None]).astype(jnp.int32), axis=1)
    return jnp.broadcast_to(starts[:, None], (ids.shape[0], 128))


TN = (((0,), (0,)), ((), ()))
MOE_ROWS = 256
FF_TILE = 768


def expert_slots(ids, levels, expert, capacity):
    hits = ids == expert
    hit = jnp.any(hits, axis=2)
    level = jnp.sum(jnp.where(hits, levels, 0), axis=2)
    hot = hit[:, :, None] & (level[:, :, None] == jnp.arange(PRIO)[None, None, :])
    tokens = ids.shape[1]
    earlier = (jnp.arange(tokens)[:, None] > jnp.arange(tokens)[None, :]).astype(BF16)
    rank = jnp.einsum("ut,dtl->dul", earlier, hot.astype(BF16), preferred_element_type=F32).astype(jnp.int32)
    counts = jnp.sum(hot.astype(jnp.int32), axis=1)
    totals = jnp.sum(counts, axis=0)
    lower = jnp.cumsum(totals) - totals
    base = lower[None, :] + jnp.cumsum(counts, axis=0) - counts
    slot = jnp.sum(jnp.where(hot, base[:, None, :] + rank, 0), axis=2)
    kept = hit & (slot < capacity)
    rank = jnp.einsum("ut,dt->du", earlier, kept.astype(BF16), preferred_element_type=F32).astype(jnp.int32)
    place = jnp.where(kept, rank, -1)
    other = jnp.sum(jnp.where(hits, 0, ids), axis=2)
    return place, other


def half_plan(place, other, half):
    tokens = place.shape[1] // 2
    before = jnp.sum((place[:, : half * tokens] >= 0).astype(jnp.int32), axis=1)
    part = place[:, half * tokens : (half + 1) * tokens]
    kept = part >= 0
    sizes = jnp.sum(kept.astype(jnp.int32), axis=1)
    part = jnp.where(kept, part - before[:, None], -1)
    padded = (sizes + 15) // 16 * 16
    ends = jnp.cumsum(padded)
    info = jnp.concatenate([ends - padded, sizes, ends[-1:]]).astype(jnp.int32)
    hot = other[:, half * tokens : (half + 1) * tokens].reshape(-1, 1) == jnp.arange(128)[None, :]
    return info, part, hot.astype(jnp.bfloat16)


def pack_kernel(sources, info, place_ref, *refs):
    ins, outs = refs[:len(refs) // 2], refs[len(refs) // 2:]
    d = pl.program_id(0)

    @pl.when(d == 0)
    def _():
        for out in outs:
            out[...] = jnp.zeros_like(out)

    tokens = place_ref.shape[2]
    row = lax.broadcasted_iota(jnp.int32, (MOE_ROWS, tokens), 0)

    def chunk(j, _):
        pick = jnp.where(place_ref[0] == row + MOE_ROWS * j, 1.0, 0.0).astype(BF16)
        at = pl.ds(pl.multiple_of(info[d] + MOE_ROWS * j, 16), MOE_ROWS)
        for x, out in zip(ins, outs):
            out[at, :] = dot(pick, x[...]).astype(BF16)
        return 0
    lax.fori_loop(0, (info[sources + d] + MOE_ROWS - 1) // MOE_ROWS, chunk, 0)


def pack(info, place, arrays, room, halves=1, half=0):
    sources, tokens = place.shape
    return pl.pallas_call(
        functools.partial(pack_kernel, sources),
        grid_spec=pltpu.PrefetchScalarGridSpec(
            num_scalar_prefetch=1, grid=(sources,),
            in_specs=[pl.BlockSpec((1, 1, tokens), lambda d, *_: (d, 0, 0))]
            + [pl.BlockSpec((tokens, x.shape[1]), lambda d, *_: (halves * d + half, 0)) for x in arrays],
            out_specs=[pl.BlockSpec((room, x.shape[1]), lambda d, *_: (0, 0)) for x in arrays]),
        out_shape=[jax.ShapeDtypeStruct((room, x.shape[1]), BF16) for x in arrays],
        compiler_params=pltpu.CompilerParams(vmem_limit_bytes=40 << 20),
        cost_estimate=EARLY,
        name="pack_tokens",
    )(info, place[:, None, :], *arrays)


def unpack_kernel(send, info, place_ref, *refs):
    ins, outs = refs[:len(refs) // 2], refs[len(refs) // 2:]
    tokens = place_ref.shape[0]
    lane = lax.broadcasted_iota(jnp.int32, (tokens, 128), 1)
    put = jnp.concatenate(
        [jnp.where(place_ref[...] == lane + 128 * b, 1.0, 0.0).astype(BF16) for b in range(send // 128)], axis=1)
    at = pl.ds(pl.multiple_of(info[pl.program_id(0)], 16), send)
    for x, out in zip(ins, outs):
        out[...] = dot(put, x[at, :]).astype(out.dtype)


def unpack(info, place, arrays, dtypes, send):
    sources, tokens = place.shape
    spread = jnp.broadcast_to(place.reshape(-1, 1), (sources * tokens, 128))
    return pl.pallas_call(
        functools.partial(unpack_kernel, send),
        grid_spec=pltpu.PrefetchScalarGridSpec(
            num_scalar_prefetch=1, grid=(sources,),
            in_specs=[pl.BlockSpec((tokens, 128), lambda d, *_: (d, 0))]
            + [pl.BlockSpec(x.shape, lambda d, *_: (0, 0)) for x in arrays],
            out_specs=[pl.BlockSpec((tokens, x.shape[1]), lambda d, *_: (d, 0)) for x in arrays]),
        out_shape=[jax.ShapeDtypeStruct((sources * tokens, x.shape[1]), t) for x, t in zip(arrays, dtypes)],
        compiler_params=pltpu.CompilerParams(vmem_limit_bytes=40 << 20),
        cost_estimate=EARLY,
        name="unpack_tokens",
    )(info, spread, *arrays)


def window_kernel(sources, info, later, x_ref, y_ref, *out_refs):
    d = pl.program_id(0)
    send = out_refs[0].shape[0]
    count = info[sources + d]
    row = lax.broadcasted_iota(jnp.int32, (send, send), 0)
    column = lax.broadcasted_iota(jnp.int32, (send, send), 1)
    pick = jnp.where(column == row - count, 1.0, 0.0).astype(BF16)
    moved = dot(pick, y_ref[pl.ds(pl.multiple_of(later[d], 16), send), :]).astype(BF16)
    rows = x_ref[pl.ds(pl.multiple_of(info[d], 16), send), :]
    first = lax.broadcasted_iota(jnp.int32, rows.shape, 0) < count
    both = jnp.where(first, rows, moved)
    at = 0
    for out_ref in out_refs:
        out_ref[...] = both[:, at:at + out_ref.shape[1]]
        at += out_ref.shape[1]


def windows_of(info, later, x, y, sources, send, columns):
    whole = pl.BlockSpec(x.shape, lambda d, *_: (0, 0))
    return pl.pallas_call(
        functools.partial(window_kernel, sources),
        grid_spec=pltpu.PrefetchScalarGridSpec(
            num_scalar_prefetch=2, grid=(sources,), in_specs=[whole, whole],
            out_specs=[pl.BlockSpec((send, n), lambda d, *_: (d, 0)) for n in columns]),
        out_shape=[jax.ShapeDtypeStruct((sources * send, n), BF16) for n in columns],
        compiler_params=pltpu.CompilerParams(vmem_limit_bytes=40 << 20),
        cost_estimate=EARLY,
        name="window_rows",
    )(info, later, x, y)


def collect_kernel(place_ref, *refs):
    x_refs, out_ref = refs[:-1], refs[-1]
    tokens = place_ref.shape[0]
    lane = lax.broadcasted_iota(jnp.int32, (tokens, 128), 1)
    put = jnp.concatenate(
        [jnp.where(place_ref[...] == lane + 128 * b, 1.0, 0.0).astype(BF16) for b in range(x_refs[0].shape[0] // 128)],
        axis=1)
    total = jnp.concatenate([dot(put, x_ref[...]) for x_ref in x_refs], axis=1)

    @pl.when(pl.program_id(0) == 0)
    def _():
        out_ref[...] = total

    @pl.when(pl.program_id(0) > 0)
    def _():
        out_ref[...] += total


def collect(place, returned, send):
    experts, tokens = place.shape
    width = sum(x.shape[1] for x in returned)
    spread = jnp.broadcast_to(place.reshape(-1, 1), (experts * tokens, 128))
    return pl.pallas_call(
        collect_kernel,
        grid=(experts,),
        in_specs=[pl.BlockSpec((tokens, 128), lambda e: (e, 0)), *[pl.BlockSpec((send, x.shape[1]), lambda e: (e, 0)) for x in returned]],
        out_specs=pl.BlockSpec((tokens, width), lambda e: (0, 0)),
        out_shape=jax.ShapeDtypeStruct((tokens, width), F32),
        compiler_params=pltpu.CompilerParams(vmem_limit_bytes=40 << 20),
        cost_estimate=EARLY,
        name="collect_rows",
    )(spread, *returned)


def gelu_and_slope(v):
    c = math.sqrt(2.0 / math.pi)
    t = jnp.tanh(c * (v + 0.044715 * (v * v * v)))
    half = 0.5 * (1.0 + t)
    return v * half, half + 0.5 * v * (1.0 - t * t) * (c * (1.0 + 3 * 0.044715 * (v * v)))


def expert_kernel(sources, more, info, expert, x_ref, o_ref, c_ref, r_ref, wi_ref, wd_ref, *refs):
    if more:
        dwi_before, dwd_before, *refs = refs
    gi_ref, eo_ref, gg_ref, dwi_ref, dwd_ref, geo, gate, eo, gi, dwi, dwd = refs
    f = pl.program_id(0)
    last = pl.num_programs(0) - 1
    tiles = (info[2 * sources] + MOE_ROWS - 1) // MOE_ROWS
    lane = lax.broadcasted_iota(jnp.int32, (MOE_ROWS, 128), 1)

    def rows_of(i):
        return pl.ds(pl.multiple_of(i * MOE_ROWS, MOE_ROWS), MOE_ROWS)

    @pl.when(f == 0)
    def _():
        gi_ref[...] = jnp.zeros_like(gi_ref)
        eo_ref[...] = jnp.zeros_like(eo_ref)
        gg_ref[...] = jnp.zeros_like(gg_ref)

        def start(i, _):
            at = rows_of(i)
            logits = dot(x_ref[at, :], r_ref[...])
            mine = jnp.sum(jnp.where(lane == expert[0], logits, 0.0), axis=1, keepdims=True)
            other = jnp.sum(jnp.where(o_ref[at, :] > 0, logits, 0.0), axis=1, keepdims=True)
            top = jnp.maximum(mine, other)
            a, b = jnp.exp(mine - top), jnp.exp(other - top)
            g = a / (a + b)
            gate[at, :] = jnp.broadcast_to(g, (MOE_ROWS, 128))
            geo[at, :] = (c_ref[at, :].astype(F32) * g).astype(BF16)
            eo[at, :] = jnp.zeros((MOE_ROWS, eo.shape[1]), F32)
            gi[at, :] = jnp.zeros((MOE_ROWS, gi.shape[1]), F32)
            return 0
        lax.fori_loop(0, tiles, start, 0)

    dwi[...] = dwi_before[...].astype(F32) if more else jnp.zeros_like(dwi)
    dwd[...] = dwd_before[...].astype(F32) if more else jnp.zeros_like(dwd)

    def tile(i, _):
        at = rows_of(i)
        x, g = x_ref[at, :], geo[at, :]
        act, slope = gelu_and_slope(dot(x, wi_ref[...]))
        act = act.astype(BF16)
        eo[at, :] += dot(act, wd_ref[...])
        gh = (dot(g, wd_ref[...], NT) * slope).astype(BF16)
        gi[at, :] += dot(gh, wi_ref[...], NT)
        dwd[...] += dot(act, g, TN)
        dwi[...] += dot(x, gh, TN)
        return 0
    lax.fori_loop(0, tiles, tile, 0)
    dwi_ref[...] = dwi[...].astype(BF16)
    dwd_ref[...] = dwd[...].astype(BF16)

    @pl.when(f == last)
    def _():
        def finish(i, _):
            at = rows_of(i)
            out = eo[at, :].astype(BF16).astype(F32)
            gg = jnp.sum(out * c_ref[at, :].astype(F32), axis=1, keepdims=True)
            parts = split3(gg)
            spread = jnp.zeros((MOE_ROWS, 128), BF16)
            for n in range(3):
                spread = jnp.where(lane == n, jnp.broadcast_to(parts[n], (MOE_ROWS, 128)), spread)
            gg_ref[at, :] = spread
            eo_ref[at, :] = (out * gate[at, :1]).astype(BF16)
            gi_ref[at, :] = gi[at, :].astype(BF16)
            return 0
        lax.fori_loop(0, tiles, finish, 0)


def expert_layer(info, expert, x, other, cot, router, w_in, w_down, sources, before):
    room, width = x.shape
    hidden = w_in.shape[1]
    whole = lambda a: pl.BlockSpec(a.shape, lambda f, *_: (0, 0))
    fixed = lambda cols: pl.BlockSpec((room, cols), lambda f, *_: (0, 0))
    return pl.pallas_call(
        functools.partial(expert_kernel, sources, bool(before)),
        grid_spec=pltpu.PrefetchScalarGridSpec(
            num_scalar_prefetch=2, grid=(hidden // FF_TILE,),
            in_specs=[whole(x), whole(other), whole(cot), whole(router),
                      *([pl.BlockSpec((width, FF_TILE), lambda f, *_: (0, f)),
                         pl.BlockSpec((FF_TILE, width), lambda f, *_: (f, 0))] * (2 if before else 1))],
            out_specs=[fixed(width), fixed(width), fixed(128),
                       pl.BlockSpec((width, FF_TILE), lambda f, *_: (0, f)),
                       pl.BlockSpec((FF_TILE, width), lambda f, *_: (f, 0))],
            scratch_shapes=[pltpu.VMEM((room, width), BF16), pltpu.VMEM((room, 128), F32),
                            pltpu.VMEM((room, width), F32), pltpu.VMEM((room, width), F32),
                            pltpu.VMEM((width, FF_TILE), F32), pltpu.VMEM((FF_TILE, width), F32)]),
        out_shape=[jax.ShapeDtypeStruct((room, width), BF16), jax.ShapeDtypeStruct((room, width), BF16),
                   jax.ShapeDtypeStruct((room, 128), BF16),
                   jax.ShapeDtypeStruct(w_in.shape, BF16), jax.ShapeDtypeStruct(w_down.shape, BF16)],
        compiler_params=pltpu.CompilerParams(vmem_limit_bytes=63 << 20),
        cost_estimate=EARLY,
        name="expert_layer",
    )(info, expert, x, other, cot, router, w_in, w_down, *before)


MESH_ID = pl.DeviceIdType.MESH


def dense_kernel(q_ref, w_ref, s_ref, out_ref, small_ref, give, h, r0, ra1, rb1, ra2, rb2, rz, s_acc, s_got, s_all,
                 send, recv, s_send, s_recv):
    i, j = lax.axis_index("dp"), lax.axis_index("expert")
    y, x, z, c = i // 2, i % 2, j // 2, j % 2
    other_core = (i, z * 2 + 1 - c)
    other_x = (y * 2 + 1 - x, j)
    other_y = ((1 - y) * 2 + x, j)
    peers = [(i, (z + d) % 4 * 2 + c) for d in (1, 2, 3)]
    barrier = pltpu.get_barrier_semaphore()
    for device in [other_core, other_x, other_y] + peers:
        pl.semaphore_signal(barrier, inc=1, device_id=device, device_id_type=MESH_ID)
    pl.semaphore_wait(barrier, 6)

    def copy(n, src, dst, device):
        return pltpu.make_async_remote_copy(src_ref=src, dst_ref=dst, send_sem=send.at[n], recv_sem=recv.at[n],
                                            device_id=device, device_id_type=MESH_ID)

    def small_copy(n, src, dst, device):
        return pltpu.make_async_remote_copy(src_ref=src, dst_ref=dst, send_sem=s_send.at[n], recv_sem=s_recv.at[n],
                                            device_id=device, device_id_type=MESH_ID)

    def block(b, core):
        rows = jnp.concatenate([q_ref[b, core], w_ref[b, core]], axis=1)
        half = rows.shape[1] // 2
        return jnp.concatenate([rows[:, :half], rows[:, half:]], axis=0)

    small = small_copy(0, s_ref, s_got.at[0], other_core)
    small.start()
    copies = []
    for g in range(4):
        def convert(b, _):
            give[b] = block(b, 1 - c).astype(BF16)
            return 0
        lax.fori_loop(4 * g, 4 * g + 4, convert, 0)
        copies.append(copy(g, give.at[pl.ds(4 * g, 4)], r0.at[pl.ds(4 * g, 4)], other_core))
        copies[-1].start()
    small.wait()
    s_acc[0] = s_ref[...] + s_got[0]
    small = small_copy(1, s_acc.at[0], s_got.at[1], other_x)
    small.start()
    for g in range(4):
        copies[g].wait()
        def add(b, _):
            h[b // 8, b // 4 % 2, b % 4] = (block(b, c) + r0[b].astype(F32)).astype(BF16)
            return 0
        lax.fori_loop(4 * g, 4 * g + 4, add, 0)

    half = h.shape[4] // 2
    left, right = pl.ds(0, half), pl.ds(half, half)
    ca = copy(4, h.at[:, 1 - x, :, :, left], ra1, other_x)
    cb = copy(5, h.at[1 - y, :, :, :, right], rb1, other_y)
    ca.start()
    cb.start()
    small.wait()
    s_acc[1] = s_acc[0] + s_got[1]
    small = small_copy(2, s_acc.at[1], s_got.at[2], other_y)
    small.start()
    ca.wait()

    def add_x(b, _):
        u, v = b // 4, b % 4
        h[u, x, v, :, left] = (h[u, x, v, :, left].astype(F32) + ra1[u, v].astype(F32)).astype(BF16)
        return 0
    lax.fori_loop(0, 8, add_x, 0)
    ca = copy(6, h.at[1 - y, x, :, :, left], ra2, other_y)
    ca.start()
    cb.wait()

    def add_y(b, _):
        u, v = b // 4, b % 4
        h[y, u, v, :, right] = (h[y, u, v, :, right].astype(F32) + rb1[u, v].astype(F32)).astype(BF16)
        return 0
    lax.fori_loop(0, 8, add_y, 0)
    cb = copy(7, h.at[y, 1 - x, :, :, right], rb2, other_x)
    cb.start()
    small.wait()
    s_acc[2] = s_acc[1] + s_got[2]
    smalls = [small_copy(3 + n, s_acc.at[2], s_all.at[z], device) for n, device in enumerate(peers)]
    for one in smalls:
        one.start()
    ca.wait()
    cb.wait()

    def add_both(v, _):
        h[y, x, v, :, left] = (h[y, x, v, :, left].astype(F32) + ra2[v].astype(F32)).astype(BF16)
        h[y, x, v, :, right] = (h[y, x, v, :, right].astype(F32) + rb2[v].astype(F32)).astype(BF16)
        return 0
    lax.fori_loop(0, 4, add_both, 0)
    copies = [copy(8 + n, h.at[y, x, (z + 1 + n) % 4], rz.at[n], device) for n, device in enumerate(peers)]
    for one in copies:
        one.start()
    total = h[y, x, z].astype(F32)
    for one in smalls:
        one.wait()
    s_all[z] = s_acc[2]
    small_ref[...] = (s_all[0] + s_all[1]) + (s_all[2] + s_all[3])
    for n, one in enumerate(copies):
        one.wait()
        total = total + rz[n].astype(F32)
    rows = total.shape[0] // 2
    out_ref[:, :2 * half] = total[:rows]
    out_ref[:, 2 * half:] = total[rows:]


def dense_sum(grad_qkv, grad_out, small):
    rows, wide = grad_qkv.shape
    narrow = grad_out.shape[1]
    own = rows // 32
    width = wide + narrow
    half = width // 2
    pair = own * 2
    vmem = pl.BlockSpec(memory_space=pltpu.VMEM)
    return pl.pallas_call(
        dense_kernel,
        in_specs=[vmem] * 3, out_specs=[vmem] * 2,
        out_shape=[jax.ShapeDtypeStruct((own, width), F32), jax.ShapeDtypeStruct(small.shape, F32)],
        scratch_shapes=[
            pltpu.VMEM((16, pair, half), BF16), pltpu.VMEM((2, 2, 4, pair, half), BF16), pltpu.VMEM((16, pair, half), BF16),
            pltpu.VMEM((2, 4, pair, half // 2), BF16), pltpu.VMEM((2, 4, pair, half // 2), BF16),
            pltpu.VMEM((4, pair, half // 2), BF16), pltpu.VMEM((4, pair, half // 2), BF16), pltpu.VMEM((3, pair, half), BF16),
            pltpu.VMEM((3,) + small.shape, F32), pltpu.VMEM((3,) + small.shape, F32), pltpu.VMEM((4,) + small.shape, F32),
            pltpu.SemaphoreType.DMA((11,)), pltpu.SemaphoreType.DMA((11,)),
            pltpu.SemaphoreType.DMA((6,)), pltpu.SemaphoreType.DMA((6,))],
        compiler_params=pltpu.CompilerParams(collective_id=0, has_side_effects=True, vmem_limit_bytes=48 << 20),
        name="dense_sum",
    )(grad_qkv.reshape(16, 2, own, wide), grad_out.reshape(16, 2, own, narrow), small)


def exchange_pairs(normed_ffn, middle, cotangent, expert_ids, priority, router, w_in, w_down):
    rows, width = normed_ffn.shape
    logits = jnp.dot(normed_ffn, router, preferred_element_type=jnp.float32)
    experts_total = router.shape[1]
    picks = expert_ids[:, :, None] == jnp.arange(experts_total)[None, None, :]
    chosen = jnp.sum(jnp.where(picks, logits[:, None, :], 0.0), axis=2)
    gates = jax.nn.softmax(chosen, axis=-1)
    top = expert_ids.shape[1]
    levels = PRIO
    local_experts = w_in.shape[0]
    capacity = rows * top // local_experts
    send = max(2, 2 * rows * top // experts_total)
    flat_expert = expert_ids.reshape(-1)
    code = priority.reshape(-1) * experts_total + flat_expert
    onehot = (code[:, None] == jnp.arange(levels * experts_total)[None, :]).astype(jnp.int32)
    rank = jnp.sum((jnp.cumsum(onehot, axis=0) - onehot) * onehot, axis=1)
    counts = jnp.sum(onehot, axis=0)
    every = lax.all_gather(counts[None, :], "expert", axis=0, tiled=True).reshape(
        -1, levels, experts_total
    )
    expert_index = lax.axis_index("expert")
    totals = jnp.sum(every, axis=0)
    lower = jnp.cumsum(totals, axis=0) - totals
    earlier_sources = jnp.cumsum(every, axis=0) - every
    mine_prefix = lax.dynamic_index_in_dim(earlier_sources, expert_index, 0, keepdims=False)
    base = (lower + mine_prefix).reshape(-1)
    slot = rank + jnp.sum(onehot * base[None, :], axis=1)
    kept = slot < capacity
    own_counts = counts.reshape(levels, experts_total)
    own_lower = (jnp.cumsum(own_counts, axis=0) - own_counts).reshape(-1)
    place = rank + jnp.sum(onehot * own_lower[None, :], axis=1)
    target = flat_expert * send + place
    first_mine = expert_index * local_experts
    counts_mine = lax.dynamic_slice_in_dim(every, first_mine, local_experts, 2)
    base_mine = lax.dynamic_slice_in_dim(
        lower[None] + earlier_sources, first_mine, local_experts, 2
    )
    band_end = jnp.cumsum(counts_mine, axis=1)
    band_start = band_end - counts_mine
    place_index = jnp.arange(send, dtype=jnp.int32)
    level = jnp.sum(
        (place_index[None, None, None, :] >= band_end[:, :, :, None]).astype(jnp.int32), axis=1
    )
    level_hot = level[:, None, :, :] == jnp.arange(levels)[None, :, None, None]
    start_of = jnp.sum(jnp.where(level_hot, band_start[:, :, :, None], 0), axis=1)
    base_of = jnp.sum(jnp.where(level_hot, base_mine[:, :, :, None], 0), axis=1)
    arrived_slot = base_of + place_index[None, None, :] - start_of
    usable = (level < levels) & (arrived_slot < capacity)
    landing = jnp.where(
        usable,
        jnp.arange(local_experts)[None, :, None] * capacity + arrived_slot,
        local_experts * capacity,
    ).reshape(-1)
    live = landing < local_experts * capacity
    safe = jnp.minimum(landing, local_experts * capacity - 1)
    pair_inputs = jnp.repeat(normed_ffn, top, axis=0)
    outgoing = (
        jnp.zeros((experts_total * send, width), jnp.bfloat16)
        .at[target]
        .set(pair_inputs)
        .reshape(experts_total, send, width)
    )
    arrived = lax.all_to_all(outgoing, "expert", split_axis=0, concat_axis=0, tiled=True)
    expert_inputs = (
        jnp.zeros((local_experts * capacity, width), jnp.bfloat16)
        .at[landing]
        .set(arrived.reshape(-1, width), mode="drop")
        .reshape(local_experts, capacity, width)
    )
    hidden = jnp.einsum("ecd,edf->ecf", expert_inputs, w_in, preferred_element_type=jnp.float32)
    activated = jax.nn.gelu(hidden).astype(jnp.bfloat16)
    expert_out = jnp.einsum(
        "ecf,efd->ecd", activated, w_down, preferred_element_type=jnp.float32
    ).astype(jnp.bfloat16)
    returning = jnp.where(
        live[:, None],
        jnp.take(expert_out.reshape(-1, width), safe, axis=0),
        jnp.zeros((), jnp.bfloat16),
    ).reshape(experts_total, send, width)
    returned = lax.all_to_all(returning, "expert", split_axis=0, concat_axis=0, tiled=True)
    pair_out = jnp.where(
        kept[:, None],
        jnp.take(returned.reshape(-1, width), target, axis=0).astype(jnp.float32),
        0.0,
    ).reshape(rows, top, width)
    mixed = jnp.sum(gates[:, :, None] * pair_out, axis=1)
    grad_out = cotangent.astype(jnp.float32)
    grad_gates = jnp.sum(grad_out[:, None, :] * pair_out, axis=2)
    pair_grads = (gates[:, :, None] * grad_out[:, None, :]).astype(jnp.bfloat16).reshape(-1, width)
    outgoing_grads = (
        jnp.zeros((experts_total * send, width), jnp.bfloat16)
        .at[target]
        .set(pair_grads)
        .reshape(experts_total, send, width)
    )
    arrived_grads = lax.all_to_all(
        outgoing_grads, "expert", split_axis=0, concat_axis=0, tiled=True
    )
    grad_expert_out = (
        jnp.zeros((local_experts * capacity, width), jnp.bfloat16)
        .at[landing]
        .set(arrived_grads.reshape(-1, width), mode="drop")
        .reshape(local_experts, capacity, width)
    )
    hidden_again = jnp.einsum(
        "ecd,edf->ecf", expert_inputs, w_in, preferred_element_type=jnp.float32
    )
    activated_again, gelu_back = jax.vjp(jax.nn.gelu, hidden_again)
    grad_activated = jnp.einsum(
        "ecd,efd->ecf", grad_expert_out, w_down, preferred_element_type=jnp.float32
    )
    grad_hidden = gelu_back(grad_activated)[0].astype(jnp.bfloat16)
    grad_w_down = jnp.einsum(
        "ecf,ecd->efd",
        activated_again.astype(jnp.bfloat16),
        grad_expert_out,
        preferred_element_type=jnp.float32,
    )
    grad_w_in = jnp.einsum(
        "ecd,ecf->edf", expert_inputs, grad_hidden, preferred_element_type=jnp.float32
    )
    grad_inputs = jnp.einsum(
        "ecf,edf->ecd", grad_hidden, w_in, preferred_element_type=jnp.float32
    ).astype(jnp.bfloat16)
    back_rows = jnp.where(
        live[:, None],
        jnp.take(grad_inputs.reshape(-1, width), safe, axis=0),
        jnp.zeros((), jnp.bfloat16),
    ).reshape(experts_total, send, width)
    came_back = lax.all_to_all(back_rows, "expert", split_axis=0, concat_axis=0, tiled=True)
    pair_back = jnp.where(
        kept[:, None],
        jnp.take(came_back.reshape(-1, width), target, axis=0).astype(jnp.float32),
        0.0,
    )
    grad_normed_ffn = jnp.sum(pair_back.reshape(rows, top, width), axis=1)
    grad_chosen = gates * (grad_gates - jnp.sum(gates * grad_gates, axis=-1, keepdims=True))
    grad_logits = jnp.sum(jnp.where(picks, grad_chosen[:, :, None], 0.0), axis=1).astype(
        jnp.bfloat16
    )
    grad_normed_ffn = grad_normed_ffn + jnp.dot(
        grad_logits, router.T, preferred_element_type=jnp.float32
    )
    expert_parts = (
        lax.psum_scatter(grad_w_in.astype(jnp.bfloat16), "dp", scatter_dimension=1, tiled=True),
        lax.psum_scatter(grad_w_down.astype(jnp.bfloat16), "dp", scatter_dimension=1, tiled=True),
    )
    return mixed, grad_logits, grad_normed_ffn, expert_parts


def gather_codes(expert_ids, priority):
    return lax.all_gather(expert_ids * PRIO + priority, "expert", axis=0)


def plan_tokens(codes, rows, top):
    expert = lax.axis_index("expert").astype(jnp.int32)
    place, other = expert_slots(codes // PRIO, codes % PRIO, expert, rows * top)
    own_place = lax.all_to_all(place, "expert", split_axis=0, concat_axis=0, tiled=True)
    return own_place, half_plan(place, other, 0), half_plan(place, other, 1)


def expert_half(all_tokens, all_cotangents, number, half, router, w_in, w_down, send, before):
    info, place, other_hot = half
    sources, tokens = place.shape
    room = (4 * tokens + 16 * sources + send + MOE_ROWS - 1) // MOE_ROWS * MOE_ROWS
    expert = lax.axis_index("expert").astype(jnp.int32)
    (packed_cot,) = pack(info, place, [all_cotangents], room, 2, number)
    packed, packed_other = pack(info, place, [all_tokens, other_hot], room)
    grad_rows, mixed_rows, grad_gate, grad_w_in, grad_w_down = expert_layer(
        info, expert[None], packed, packed_other, packed_cot, router, w_in[0], w_down[0], sources, before
    )
    grad_all, gate_all = unpack(info, place, [grad_rows, grad_gate], [jnp.bfloat16, jnp.float32], send)
    gate_all = jnp.sum(gate_all[:, :3], axis=1).reshape(sources, tokens)
    return grad_all, gate_all, mixed_rows, grad_w_in, grad_w_down


def exchange_tokens(normed_halves, all_cotangents, plan, expert_ids, router, w_in, w_down):
    rows = expert_ids.shape[0]
    experts_total = router.shape[1]
    top = expert_ids.shape[1]
    own_place, *halves = plan
    send = 2 * rows * top // experts_total
    wide_router = jnp.pad(router, ((0, 0), (0, 128 - experts_total)))
    tokens = [lax.all_gather(x, "expert", axis=0, tiled=True) for x in normed_halves]
    first = expert_half(tokens[0], all_cotangents, 0, halves[0], wide_router, w_in, w_down, send, ())
    grad_own = [lax.psum_scatter(first[0], "expert", scatter_dimension=0, tiled=True)]
    tokens[1], all_cotangents, _ = lax.optimization_barrier((tokens[1], all_cotangents, first))
    second = expert_half(tokens[1], all_cotangents, 1, halves[1], wide_router, w_in, w_down, send, first[3:])
    grad_later, grad_own[0] = lax.optimization_barrier((second[0], grad_own[0]))
    grad_own.append(lax.psum_scatter(grad_later, "expert", scatter_dimension=0, tiled=True))
    gate_own = [lax.all_to_all(x[1], "expert", split_axis=0, concat_axis=0, tiled=True) for x in (first, second)]
    windows = windows_of(halves[0][0], halves[1][0], first[2], second[2], own_place.shape[0], send, (256, first[2].shape[1] - 256))
    return grad_own, gate_own, windows, second[3], second[4]


def router_back(normed_ffn, expert_ids, router, gate_own):
    logits = jnp.dot(normed_ffn, router, preferred_element_type=jnp.float32)
    picks = expert_ids[:, :, None] == jnp.arange(router.shape[1])[None, None, :]
    chosen = jnp.sum(jnp.where(picks, logits[:, None, :], 0.0), axis=2)
    gates = jax.nn.softmax(chosen, axis=-1)
    grad_gates = jnp.sum(jnp.where(picks, gate_own.T[:, None, :], 0.0), axis=2)
    grad_chosen = gates * (grad_gates - jnp.sum(gates * grad_gates, axis=-1, keepdims=True))
    return jnp.sum(jnp.where(picks, grad_chosen[:, :, None], 0.0), axis=1).astype(jnp.bfloat16)


def per_device(
    tokens_in,
    cont_ids,
    expert_ids,
    priority,
    gain_attn,
    w_qkv,
    rel_table,
    w_out,
    gain_ffn,
    w_router,
    w_in,
    w_down,
    cotangent,
):
    rows, width = tokens_in.shape
    heads = rel_table.shape[1]
    dp_count = lax.axis_size("dp")
    dp_index = lax.axis_index("dp")
    prompt_rows = PROMPT // dp_count
    few_experts = lax.axis_size("expert") <= 16 and w_in.shape[0] == 1 and prompt_rows == KT
    local_ids = cont_ids[0]
    info = info_of(local_ids, dp_index)
    row_start = row_start_of(local_ids)
    rows_bias = bias_rows(rel_table)
    if few_experts:
        codes = gather_codes(expert_ids, priority)
    experts_total = w_router.shape[1]
    dense = jnp.concatenate(
        [pairs_together(w_qkv), w_out, jnp.pad(w_router, ((0, 0), (0, 128 - experts_total)))], axis=1
    )
    dense = lax.all_gather(dense, ("dp", "expert"), axis=0, tiled=True)
    part_heads = heads // PARTS
    tables = [bias_tables(info, rows_bias, row_start, g * part_heads, part_heads) for g in range(PARTS)]
    dense, tables[0] = lax.optimization_barrier((dense, tables[0]))
    if few_experts:
        plan = plan_tokens(codes, rows, expert_ids.shape[1])
        dense, plan = lax.optimization_barrier((dense, plan))
    whole_qkv, whole_out = dense[:, : 3 * width], dense[:, 3 * width : 4 * width]
    whole_router = dense[:, 4 * width : 4 * width + experts_total]
    inputs = tokens_in.astype(jnp.float32)
    normed_attn = normed(inputs, gain_attn).astype(jnp.bfloat16)
    projected = jnp.dot(normed_attn, whole_qkv, preferred_element_type=jnp.float32).astype(
        jnp.bfloat16
    )
    parts = PARTS
    columns = 2 * width // parts
    kept = [projected[:, width + columns * g : width + columns * (g + 1)] for g in range(parts)]
    gathered = [lax.all_gather(kept[0][:prompt_rows], "dp", axis=0, tiled=True)]
    for kv in kept[1:]:
        copies = jnp.broadcast_to(kv[None, :prompt_rows], (dp_count, prompt_rows, columns))
        gathered.append(
            lax.all_to_all(copies, "dp", split_axis=0, concat_axis=0, tiled=True).reshape(PROMPT, columns)
        )
    if few_experts:
        late_cotangent, gathered[0], tables = lax.optimization_barrier((cotangent, gathered[0], tables))
        all_cotangents = lax.all_gather(late_cotangent, "expert", axis=0, tiled=True)
    gathered[0], tables = lax.optimization_barrier((gathered[0], tables))
    results = {}
    keys_values = []
    middles, normed_halves, attended_halves = [], [], []
    order = [(g, c) for g in range(parts) for c in (0, 1)]

    def after_attention(c):
        attended = jnp.concatenate([results[g, c][0] for g in range(parts)], axis=1).astype(jnp.bfloat16)
        middle = inputs[c * KT : (c + 1) * KT] + jnp.dot(attended, whole_out, preferred_element_type=jnp.float32)
        attended_halves.append(attended)
        middles.append(middle)
        normed_halves.append(normed(middle, gain_ffn).astype(jnp.bfloat16))

    last = None
    for g, c in order:
        if last is not None:
            gathered[g], results[last] = lax.optimization_barrier((gathered[g], results[last]))
        if c == 0:
            source = gathered[g]
        else:
            source = jnp.concatenate([gathered[g], kept[g][prompt_rows:]], axis=0)
            keys_values.append(source)
        results[g, c] = attention_forward(info, projected, source, tables[g], g, bool(c))
        last = (g, c)
        if (g, c) == (parts - 1, 0):
            after_attention(0)
            if few_experts:
                normed_halves[0], all_cotangents = lax.optimization_barrier((normed_halves[0], all_cotangents))
            gathered[g], normed_halves[0] = lax.optimization_barrier((gathered[g], normed_halves[0]))
    after_attention(1)
    attended = jnp.concatenate(attended_halves, axis=0)
    middle = jnp.concatenate(middles, axis=0)
    normed_ffn = jnp.concatenate(normed_halves, axis=0)
    cut = [slice(0, KT), slice(KT, rows)]
    if few_experts:
        grad_own, gate_own, windows, *grad_w = exchange_tokens(
            normed_halves, all_cotangents, plan, expert_ids, whole_router, w_in, w_down
        )
    else:
        mixed, grad_logits, grad_normed_ffn, expert_parts = exchange_pairs(
            normed_ffn, middle, cotangent, expert_ids, priority, whole_router, w_in, w_down
        )
        grad_logits = [grad_logits[at] for at in cut]
        grad_normed_halves = [grad_normed_ffn[at] for at in cut]
    if few_experts:
        grad_logits, grad_normed_halves = [None, None], [None, None]
    grad_out = cotangent.astype(jnp.float32)
    grad_middles, grad_branches, grad_gain_ffn = [], [], 0.0
    grad_queries, grad_kv, grad_lines = {}, [None] * parts, 0.0
    grad_prompts, grad_conts = [], []
    for c in (0, 1):
        if few_experts:
            if c:
                grad_own[1], gate_own[1], grad_kv = lax.optimization_barrier((grad_own[1], gate_own[1], grad_kv))
                grad_own[1], windows, grad_w = lax.optimization_barrier((grad_own[1], windows, grad_w))
                mixed = [lax.all_to_all(x, "expert", split_axis=0, concat_axis=0, tiled=True) for x in windows]
                expert_in = lax.psum_scatter(grad_w[0][None], "dp", scatter_dimension=1, tiled=True)
            grad_logits[c] = router_back(normed_halves[c], expert_ids[cut[c]], whole_router, gate_own[c])
            grad_normed_halves[c] = grad_own[c].astype(jnp.float32) + jnp.dot(
                grad_logits[c], whole_router.T, preferred_element_type=jnp.float32
            )
        _, ffn_norm_back = jax.vjp(normed, middles[c], gain_ffn)
        grad_middle_part, grad_gain = ffn_norm_back(grad_normed_halves[c])
        grad_gain_ffn = grad_gain_ffn + grad_gain
        grad_middles.append(grad_out[cut[c]] + grad_middle_part)
        grad_branches.append(grad_middles[c].astype(jnp.bfloat16))
        grad_attended = jnp.dot(
            grad_branches[c], whole_out.T, preferred_element_type=jnp.float32
        ).astype(jnp.bfloat16)
        lines = []
        for g in range(parts):
            if c and g and few_experts:
                grad_attended, expert_in, grad_queries[g - 1, c] = lax.optimization_barrier(
                    (grad_attended, expert_in, grad_queries[g - 1, c])
                )
            out, total = results[g, c]
            grad_queries[g, c], grad_kv[g], line = attention_backward(
                info, projected, grad_attended, out, total, keys_values[g] if c else gathered[g], tables[g], g, bool(c),
                grad_kv[g],
            )
            lines.append(line)
            if c:
                if g:
                    grad_kv[g], grad_prompts[-1] = lax.optimization_barrier((grad_kv[g], grad_prompts[-1]))
                    if few_experts:
                        grad_kv[g], mixed[0] = lax.optimization_barrier((grad_kv[g], mixed[0]))
                grad_prompts.append(lax.psum_scatter(grad_kv[g][:PROMPT], "dp", scatter_dimension=0, tiled=True))
                grad_conts.append(grad_kv[g][PROMPT:])
        grad_lines = grad_lines + jnp.concatenate(lines, axis=0)
    if few_experts:
        grad_prompts[-1], grad_down = lax.optimization_barrier((grad_prompts[-1], grad_w[1]))
        expert_parts = (expert_in, lax.psum_scatter(grad_down[None], "dp", scatter_dimension=1, tiled=True))
    grad_middle = jnp.concatenate(grad_middles, axis=0)
    grad_branch = jnp.concatenate(grad_branches, axis=0)
    grad_router = jnp.dot(
        normed_ffn.T, jnp.concatenate(grad_logits, axis=0), preferred_element_type=jnp.float32
    )
    grad_out_weight = jnp.dot(attended.T, grad_branch, preferred_element_type=jnp.float32)
    mixed, middle, grad_prompts[-1] = lax.optimization_barrier((mixed, middle, grad_prompts[-1]))
    if few_experts:
        mixed = collect(plan[0], mixed, mixed[0].shape[0] // plan[0].shape[0])
    output = (middle + mixed).astype(jnp.bfloat16)
    grad_table = table_grad(grad_lines, rel_table.shape[0])
    grad_projected = jnp.concatenate(
        [jnp.concatenate([grad_queries[g, 0], grad_queries[g, 1]], axis=0) for g in range(parts)]
        + [jnp.concatenate([a, b], axis=0) for a, b in zip(grad_prompts, grad_conts)], axis=1
    )
    grad_normed_attn = jnp.dot(grad_projected, whole_qkv.T, preferred_element_type=jnp.float32)
    grad_qkv = jnp.dot(normed_attn.T, grad_projected, preferred_element_type=jnp.float32)
    _, attn_norm_back = jax.vjp(normed, inputs, gain_attn)
    grad_inputs_part, grad_gain_attn = attn_norm_back(grad_normed_attn)
    grad_tokens = grad_middle + grad_inputs_part
    if (dp_count, lax.axis_size("expert")) == (4, 8):
        pieces = [grad_gain_attn, grad_gain_ffn, grad_table.reshape(-1), grad_router.reshape(-1)]
        sizes = [piece.shape[0] for piece in pieces]
        small = jnp.concatenate(pieces)
        small = jnp.pad(small, (0, -small.shape[0] % 1024)).reshape(-1, 128)
        dense_grad, small = dense_sum(grad_qkv, grad_out_weight, small)
        ends = [sum(sizes[: n + 1]) for n in range(4)]
        flat = small.reshape(-1)
        grad_gain_attn, grad_gain_ffn = flat[: ends[0]], flat[ends[0] : ends[1]]
        grad_table = flat[ends[1] : ends[2]].reshape(grad_table.shape)
        own_rows = w_router.shape[0]
        mine = (dp_index * lax.axis_size("expert") + lax.axis_index("expert")) * own_rows
        own_router = lax.dynamic_slice_in_dim(
            flat[ends[2] : ends[3]].reshape(grad_router.shape), mine, own_rows, 0
        )
        small_parts = (grad_gain_attn, grad_gain_ffn, grad_table.T)
    else:
        dense_grad = lax.psum_scatter(
            jnp.concatenate([grad_qkv, grad_out_weight], axis=1), ("dp", "expert"), scatter_dimension=0, tiled=True
        )
        own_router = lax.psum_scatter(grad_router, ("dp", "expert"), scatter_dimension=0, tiled=True)
        small_parts = lax.psum((grad_gain_attn, grad_gain_ffn, grad_table.T), ("dp", "expert"))
    return (
        output,
        grad_tokens,
        small_parts[0],
        pairs_apart(dense_grad[:, : 3 * width]),
        small_parts[2],
        dense_grad[:, 3 * width :],
        small_parts[1],
        own_router,
        expert_parts[0].astype(jnp.float32),
        expert_parts[1].astype(jnp.float32),
    )


def solution(mesh):
    return jax.shard_map(
        per_device,
        mesh=mesh,
        in_specs=(
            P(("dp", "expert"), None),
            P(("dp", "expert"), None),
            P(("dp", "expert"), None),
            P(("dp", "expert"), None),
            P(),
            P(("dp", "expert"), None),
            P(),
            P(("dp", "expert"), None),
            P(),
            P(("dp", "expert"), None),
            P("expert", None, None),
            P("expert", None, None),
            P(("dp", "expert"), None),
        ),
        out_specs=(
            P(("dp", "expert"), None),
            P(("dp", "expert"), None),
            P(),
            P(("dp", "expert"), None),
            P(),
            P(("dp", "expert"), None),
            P(),
            P(("dp", "expert"), None),
            P("expert", "dp", None),
            P("expert", "dp", None),
        ),
        check_vma=False,
    )
```

```python
import functools
import math
import jax
import jax.numpy as jnp
from jax import lax
from jax.experimental import pallas as pl
from jax.experimental.pallas import tpu as pltpu
from jax.sharding import PartitionSpec as P

PRIO = 4
PROMPT = 2048


BORDERS = (16, 24, 32, 48, 64, 96, 128, 192, 256, 384, 512, 768, 1024, 1536, 2048)
EPSILON = 1e-06
MASKED = -1e30


def bucket_of(distance):
    distance = jnp.maximum(distance, 0)
    counted = jnp.minimum(distance, 15)
    for border in BORDERS:
        counted = counted + (distance >= border).astype(jnp.int32)
    return counted


def normed(values, gain):
    return values * lax.rsqrt(jnp.mean(values * values, axis=-1, keepdims=True) + EPSILON) * gain


def pairs_together(w_qkv):
    width = w_qkv.shape[1] // 3
    rows = w_qkv.shape[0]
    keys_values = w_qkv[:, width:].reshape(rows, 2, width // 128, 128).swapaxes(1, 2)
    return jnp.concatenate([w_qkv[:, :width], keys_values.reshape(rows, 2 * width)], axis=1)


def pairs_apart(grad):
    width = grad.shape[1] // 3
    rows = grad.shape[0]
    keys_values = grad[:, width:].reshape(rows, width // 128, 2, 128).swapaxes(1, 2)
    return jnp.concatenate([grad[:, :width], keys_values.reshape(rows, 2 * width)], axis=1)


LOG2E = math.log2(math.e)
F32, BF16 = jnp.float32, jnp.bfloat16
QT = 256
KT = 512
RUN = 256
EARLY = pl.CostEstimate(flops=1 << 20, bytes_accessed=1 << 20, transcendentals=0)
PARTS = 2
ROWS = 64
NT = (((1,), (1,)), ((), ()))
NN = (((1,), (0,)), ((), ()))

def dot(a, b, dims=NN):
    return lax.dot_general(a, b, dims, preferred_element_type=F32)

def bias_rows(rel_table):
    width = PROMPT + 512 + RUN
    distance = PROMPT + RUN - jnp.arange(width)[None, :] + jnp.arange(8)[:, None]
    bucket = bucket_of(distance)
    table = rel_table.T[:, None, None, :] * LOG2E
    hot = (bucket[..., None] == jnp.arange(rel_table.shape[0])).astype(F32)
    rows = jnp.sum(hot[None] * table, axis=-1)
    return jnp.where(distance[None] >= 0, rows, MASKED)

def bias_kernel(info, base_ref, row_start, t_ref, b_ref):
    base, t_scr, b_scr = base_ref[0], t_ref.at[0], b_ref.at[0]
    width = base.shape[-1]
    for a in range(16):
        t_scr[8 * a:8 * a + 8, :] = pltpu.roll(base, 8 * a, 1) if a else base
    lane = lax.broadcasted_iota(jnp.int32, (ROWS, 128), 1)
    sub = lax.broadcasted_iota(jnp.int32, (ROWS, 128), 0)
    for s in range(4):
        start, end = info[s], info[s + 1]
        turn = start % 128
        left = (128 - turn) % 128
        here = (lane < left) | (left == 0)
        def place(g, _):
            at = pl.ds(pl.multiple_of(ROWS * g, ROWS), ROWS)
            first = start - turn + RUN - 128 * (g // (128 // ROWS))
            of = pl.ds(pl.multiple_of(ROWS * (g % (128 // ROWS)), ROWS), ROWS)
            mine = sub + ROWS * g >= start
            turned = None
            for b in range(PROMPT // 128 + 1):
                after = pltpu.roll(t_scr[of, pl.ds(pl.multiple_of(first + 128 * b, 128), 128)], left, 1)
                if b:
                    cols = slice(128 * b - 128, 128 * b)
                    b_scr[at, cols] = jnp.where(mine, jnp.where(here, turned, after), b_scr[at, cols])
                turned = after
            return 0
        lax.fori_loop(start // ROWS, (end + ROWS - 1) // ROWS, place, 0)
    lane = lax.broadcasted_iota(jnp.int32, (128, 128), 1)
    for i in range(KT // 128):
        rows = slice(128 * i, 128 * i + 128)
        own = row_start[rows, :]
        for b in range(KT // 128):
            first = PROMPT + RUN - 128 * i + 128 * b
            b_scr[rows, PROMPT + 128 * b:PROMPT + 128 * b + 128] = jnp.where(
                lane + 128 * b >= own, t_scr[:, first:first + 128], MASKED)

def bias_tables(info, rows_bias, row_start, first, heads):
    wide = rows_bias.shape[2]
    block = lambda rows, cols: pl.BlockSpec((1, rows, cols), lambda h, *_: (h, 0, 0))
    return pl.pallas_call(
        bias_kernel,
        grid_spec=pltpu.PrefetchScalarGridSpec(
            num_scalar_prefetch=1, grid=(heads,),
            in_specs=[pl.BlockSpec((1, 8, wide), lambda h, *_: (first + h, 0, 0)),
                      pl.BlockSpec((KT, 128), lambda h, *_: (0, 0))],
            out_specs=[block(128, wide), block(KT, PROMPT + KT)]),
        out_shape=[jax.ShapeDtypeStruct((heads, 128, wide), F32),
                   jax.ShapeDtypeStruct((heads, KT, PROMPT + KT), F32)],
        compiler_params=pltpu.CompilerParams(vmem_limit_bytes=32 << 20),
        cost_estimate=EARLY,
        name="bias_tables",
    )(info, rows_bias, row_start)

def own_lanes(h, rows):
    lane = lax.broadcasted_iota(jnp.int32, (rows, 128), 1)
    return lane // 64 == h % 2

def fwd_kernel(scale2, cont, info, q_ref, k_ref, v_ref, table_ref, o_ref, lse_ref):
    h = pl.program_id(0)
    dp = info[5]
    table = table_ref.at[0]
    own = own_lanes(h, QT)
    head_lane = lax.broadcasted_iota(jnp.int32, (QT, 128), 1) == h

    def tile(first, key_tiles, bias_of, block):
        rows = pl.ds(first, QT)
        q = jnp.where(own, q_ref[rows, :], jnp.zeros((), BF16))
        def step(t, carry):
            m, l, acc = carry
            cols = pl.ds(pl.multiple_of(block(t) * KT, KT), KT)
            s = dot(q, k_ref[cols, :], NT) * scale2 + bias_of(t)
            new = jnp.maximum(m, jnp.max(s, axis=1, keepdims=True))
            keep = jnp.exp2(m - new)
            p = jnp.exp2(s - jnp.concatenate([new] * (KT // 128), axis=1))
            part = p[:, :128]
            for c in range(1, KT // 128):
                part = part + p[:, 128 * c:128 * (c + 1)]
            return new, l * keep + part, acc * keep + dot(p.astype(BF16), v_ref[cols, :])
        zero = jnp.zeros((QT, 128), F32)
        m, l, acc = lax.fori_loop(0, key_tiles, step, (jnp.full((QT, 128), MASKED, F32), zero, zero))
        l = jnp.sum(l, axis=1, keepdims=True)
        o_ref[rows, :] = jnp.where(own, acc / l, o_ref[rows, :])
        lse_ref[rows, :] = jnp.where(head_lane, m + jnp.log2(l), lse_ref[rows, :])

    for j in range(KT // QT):
        if cont:
            tile(QT * j, PROMPT // KT + 1,
                 lambda t: table[pl.ds(QT * j, QT), pl.ds(pl.multiple_of(t * KT, KT), KT)], lambda t: t)
            continue
        shift = PROMPT - KT * dp - QT * j + RUN
        def bias(t, shift=shift):
            first = (dp - t) * KT + shift
            return jnp.concatenate([table[:, pl.ds(pl.multiple_of(first - 128 * x, 128), KT)] for x in range(QT // 128)], axis=0)
        tile(QT * j, dp + 1, bias, lambda t: dp - t)

def attention_forward(info, projected, keys_values, tables, part, cont):
    keys, columns = keys_values.shape
    heads = columns // 128
    scale2 = 64 ** -0.5 * LOG2E
    first = part * heads // 2
    table = tables[int(cont)]
    return pl.pallas_call(
        functools.partial(fwd_kernel, scale2, cont),
        grid_spec=pltpu.PrefetchScalarGridSpec(
            num_scalar_prefetch=1, grid=(heads,),
            in_specs=[pl.BlockSpec((KT, 128), lambda h, *_: (int(cont), first + h // 2)),
                      pl.BlockSpec((keys, 128), lambda h, *_: (0, h // 2 * 2)),
                      pl.BlockSpec((keys, 128), lambda h, *_: (0, h // 2 * 2 + 1)),
                      pl.BlockSpec((1,) + table.shape[1:], lambda h, *_: (h, 0, 0))],
            out_specs=[pl.BlockSpec((KT, 128), lambda h, *_: (0, h // 2)),
                       pl.BlockSpec((KT, 128), lambda h, *_: (0, 0))]),
        out_shape=[jax.ShapeDtypeStruct((KT, heads * 64), F32), jax.ShapeDtypeStruct((KT, 128), F32)],
        compiler_params=pltpu.CompilerParams(vmem_limit_bytes=60 << 20),
        cost_estimate=EARLY,
        name="attention_forward",
    )(info, projected, keys_values, keys_values, table)

def split3(x):
    hi = x.astype(BF16)
    rest = x - hi.astype(F32)
    mid = rest.astype(BF16)
    return hi, mid, (rest - mid.astype(F32)).astype(BF16)

def bwd_kernel(scale, cont, info, q_ref, do_ref, o_ref, lse_ref, k_ref, v_ref, table_ref, *refs):
    if cont:
        prev_ref, dq_ref, dkv_ref, dd_ref, e_scr, qa, da, ka, va, qt, dot_t, dkt, dvt, db_scr = refs
    else:
        dq_ref, dkv_ref, dd_ref, e_scr, qa, da, ka, va, qt, dot_t, dkt, dvt = refs
    table = table_ref.at[0]
    h = pl.program_id(0)
    dp = info[5]
    n, keys = q_ref.shape[0], k_ref.shape[0]
    half = h % 2
    base = pl.multiple_of(64 * half, 64)
    other = 64 - 64 * half

    @pl.when(half == 0)
    def _():
        qt[...] = q_ref[...].T
        dot_t[...] = do_ref[...].T
        dq_ref[...] = jnp.zeros_like(dq_ref)

    lane_n = lax.broadcasted_iota(jnp.int32, (QT, 128), 1)
    own_n = lane_n // 64 == half
    def augment(i, _):
        rows = pl.ds(pl.multiple_of(i * QT, QT), QT)
        lse = jnp.sum(jnp.where(lane_n == h, lse_ref[rows, :], 0.0), axis=1, keepdims=True)
        parts = split3(-lse / (scale * LOG2E))
        aug = jnp.zeros((QT, 128), BF16)
        for x in range(3):
            aug = jnp.where(lane_n == other + x, jnp.broadcast_to(parts[x], (QT, 128)), aug)
        qa[rows, :] = jnp.where(own_n, q_ref[rows, :], aug)
        do = do_ref[rows, :]
        delta = jnp.sum(jnp.where(own_n, do.astype(F32) * o_ref[rows, :], 0.0), axis=1, keepdims=True)
        parts = split3(-delta)
        aug = jnp.zeros((QT, 128), BF16)
        for x in range(3):
            aug = jnp.where(lane_n == other + x, jnp.broadcast_to(parts[x], (QT, 128)), aug)
        da[rows, :] = jnp.where(own_n, do, aug)
        return 0
    lax.fori_loop(0, n // QT, augment, 0)
    lane_k = lax.broadcasted_iota(jnp.int32, (KT, 128), 1)
    ones = jnp.where((lane_k >= other) & (lane_k < other + 3), 1.0, 0.0).astype(BF16)
    own_k = lane_k // 64 == half
    def augment_keys(i, _):
        rows = pl.ds(pl.multiple_of(i * KT, KT), KT)
        ka[rows, :] = jnp.where(own_k, k_ref[rows, :], ones)
        va[rows, :] = jnp.where(own_k, v_ref[rows, :], ones)
        return 0
    lax.fori_loop(0, keys // KT, augment_keys, 0)
    head_rows = pl.ds(base, 64)
    dkt[head_rows, :] = jnp.zeros((64, keys), F32)
    dvt[head_rows, :] = jnp.zeros((64, keys), F32)
    e_scr[...] = jnp.zeros_like(e_scr)

    def tile(first, key_tiles, bias_of, grad_bias):
        rows = pl.ds(first, QT)
        q, do = qa[rows, :], da[rows, :]
        q_t, do_t = qt[head_rows, rows], dot_t[head_rows, rows]
        def step(t, dq):
            cols = pl.ds(pl.multiple_of(t * KT, KT), KT)
            kk = ka[cols, :]
            p = jnp.exp2(dot(q, kk, NT) * (scale * LOG2E) + bias_of(t))
            ds = p * dot(do, va[cols, :], NT)
            grad_bias(t, ds)
            low = ds.astype(BF16)
            dvt[head_rows, cols] += dot(do_t, p.astype(BF16))
            dkt[head_rows, cols] += dot(q_t, low)
            return dq + dot(low, kk)
        dq = lax.fori_loop(0, key_tiles, step, jnp.zeros((QT, 128), F32))
        dq_ref[rows, :] = jnp.where(own_n, dq * scale, dq_ref[rows, :].astype(F32)).astype(BF16)

    for j in range(KT // QT):
        if cont:
            def where(t):
                return (pl.ds(QT * j, QT), pl.ds(pl.multiple_of(t * KT, KT), KT))
            def put(t, ds):
                db_scr[where(t)] = ds
            tile(QT * j, PROMPT // KT + 1, lambda t: table[where(t)], put)
            continue
        shift = PROMPT - KT * dp - QT * j + RUN
        def part(t, x, shift=shift):
            return (slice(None), pl.ds(pl.multiple_of(t * KT + shift - 128 * x, 128), KT))
        def bias(t):
            return jnp.concatenate([table[part(t, x)] for x in range(QT // 128)], axis=0)
        def add(t, ds):
            for x in range(QT // 128):
                e_scr[part(t, x)] += ds[128 * x:128 * x + 128, :]
        tile(QT * j, dp + 1, bias, add)

    if cont:
        lane = lax.broadcasted_iota(jnp.int32, (ROWS, 128), 1)
        sub = lax.broadcasted_iota(jnp.int32, (ROWS, 128), 0)
        for s in range(4):
            start, end = info[s], info[s + 1]
            turn = start % 128
            def fold(g, _):
                at = pl.ds(pl.multiple_of(ROWS * g, ROWS), ROWS)
                first = start - turn + RUN - 128 * (g // (128 // ROWS))
                to = pl.ds(pl.multiple_of(ROWS * (g % (128 // ROWS)), ROWS), ROWS)
                mine = (sub + ROWS * g >= start) & (sub + ROWS * g < end)
                window = (to, pl.ds(pl.multiple_of(first, 128), PROMPT + 128))
                before = jnp.zeros((ROWS, 128), F32)
                moved = []
                for b in range(PROMPT // 128 + 1):
                    turned = jnp.zeros((ROWS, 128), F32)
                    if b < PROMPT // 128:
                        turned = pltpu.roll(jnp.where(mine, db_scr[at, 128 * b:128 * b + 128], 0.0), turn, 1)
                    moved.append(jnp.where(lane >= turn, turned, before))
                    before = turned
                e_scr[window] += jnp.concatenate(moved, axis=1)
                return 0
            lax.fori_loop(start // ROWS, (end + ROWS - 1) // ROWS, fold, 0)
        for i in range(KT // 128):
            first = PROMPT + RUN - 128 * i
            e_scr[:, first:first + KT] += db_scr[128 * i:128 * i + 128, PROMPT:]
    width = e_scr.shape[1]
    acc = e_scr[0:8, :]
    for a in range(1, 16):
        acc = acc + pltpu.roll(e_scr[8 * a:8 * a + 8, :], width - 8 * a, 1)
    total = acc[0:1, :]
    for i in range(1, 8):
        total = total + pltpu.roll(acc, width - i, 1)[i:i + 1, :]
    dd_ref[0] = total

    @pl.when(half == 1)
    def _():
        for at, total in ((0, dkt[...] * scale), (128, dvt[...])):
            total = total.T
            if cont:
                dkv_ref[:PROMPT, at:at + 128] = (total[:PROMPT] + prev_ref[:, at:at + 128].astype(F32)).astype(BF16)
                dkv_ref[PROMPT:, at:at + 128] = total[PROMPT:].astype(BF16)
            else:
                dkv_ref[:, at:at + 128] = total.astype(BF16)

def attention_backward(info, projected, do, o32, lse, keys_values, tables, part, cont, prev):
    keys, columns = keys_values.shape
    heads = columns // 128
    wide = tables[0].shape[2]
    first = part * heads // 2
    own = pl.BlockSpec((KT, 128), lambda h, *_: (0, h // 2))
    table = tables[int(cont)]
    before = [pl.BlockSpec((PROMPT, 256), lambda h, *_: (0, h // 2))] if cont else []
    scores = [pltpu.VMEM((KT, PROMPT + KT), F32)] if cont else []
    return pl.pallas_call(
        functools.partial(bwd_kernel, 64 ** -0.5, cont),
        grid_spec=pltpu.PrefetchScalarGridSpec(
            num_scalar_prefetch=1, grid=(heads,),
            in_specs=[pl.BlockSpec((KT, 128), lambda h, *_: (int(cont), first + h // 2)),
                      pl.BlockSpec((KT, 128), lambda h, *_: (0, first + h // 2)),
                      own, pl.BlockSpec((KT, 128), lambda h, *_: (0, 0)),
                      pl.BlockSpec((keys, 128), lambda h, *_: (0, h // 2 * 2)),
                      pl.BlockSpec((keys, 128), lambda h, *_: (0, h // 2 * 2 + 1)),
                      pl.BlockSpec((1,) + table.shape[1:], lambda h, *_: (h, 0, 0))] + before,
            out_specs=[own, pl.BlockSpec((keys, 256), lambda h, *_: (0, h // 2)),
                       pl.BlockSpec((1, 1, wide), lambda h, *_: (h, 0, 0))],
            scratch_shapes=[pltpu.VMEM((128, wide), F32),
                            pltpu.VMEM((KT, 128), BF16), pltpu.VMEM((KT, 128), BF16),
                            pltpu.VMEM((keys, 128), BF16), pltpu.VMEM((keys, 128), BF16),
                            pltpu.VMEM((128, KT), BF16), pltpu.VMEM((128, KT), BF16),
                            pltpu.VMEM((128, keys), F32), pltpu.VMEM((128, keys), F32)] + scores),
        out_shape=[jax.ShapeDtypeStruct((KT, heads * 64), BF16), jax.ShapeDtypeStruct((keys, columns), BF16),
                   jax.ShapeDtypeStruct((heads, 1, wide), F32)],
        compiler_params=pltpu.CompilerParams(vmem_limit_bytes=60 << 20),
        cost_estimate=EARLY,
        name="attention_backward",
    )(info, projected, do, o32, lse, keys_values, keys_values, table, *([prev] if cont else []))

def info_of(ids, dp):
    starts = jnp.sum((ids[None, :] < jnp.arange(5)[:, None]).astype(jnp.int32), axis=1)
    return jnp.concatenate([starts, jnp.reshape(dp, (1,)).astype(jnp.int32)])

def table_grad(dd, buckets):
    width = dd.shape[2]
    distance = PROMPT + RUN - jnp.arange(width)
    hot = ((bucket_of(distance)[:, None] == jnp.arange(buckets)[None, :]) & (distance >= 0)[:, None]).astype(F32)
    return jnp.dot(dd[:, 0, :], hot, precision=lax.Precision.HIGHEST)

def row_start_of(ids):
    starts = jnp.sum((ids[None, :] < ids[:, None]).astype(jnp.int32), axis=1)
    return jnp.broadcast_to(starts[:, None], (ids.shape[0], 128))


TN = (((0,), (0,)), ((), ()))
MOE_ROWS = 256
FF_TILE = 768


def expert_slots(ids, levels, expert, capacity):
    hits = ids == expert
    hit = jnp.any(hits, axis=2)
    level = jnp.sum(jnp.where(hits, levels, 0), axis=2)
    hot = hit[:, :, None] & (level[:, :, None] == jnp.arange(PRIO)[None, None, :])
    tokens = ids.shape[1]
    earlier = (jnp.arange(tokens)[:, None] > jnp.arange(tokens)[None, :]).astype(BF16)
    rank = jnp.einsum("ut,dtl->dul", earlier, hot.astype(BF16), preferred_element_type=F32).astype(jnp.int32)
    counts = jnp.sum(hot.astype(jnp.int32), axis=1)
    totals = jnp.sum(counts, axis=0)
    lower = jnp.cumsum(totals) - totals
    base = lower[None, :] + jnp.cumsum(counts, axis=0) - counts
    slot = jnp.sum(jnp.where(hot, base[:, None, :] + rank, 0), axis=2)
    kept = hit & (slot < capacity)
    rank = jnp.einsum("ut,dt->du", earlier, kept.astype(BF16), preferred_element_type=F32).astype(jnp.int32)
    place = jnp.where(kept, rank, -1)
    other = jnp.sum(jnp.where(hits, 0, ids), axis=2)
    return place, other


def half_plan(place, other, half):
    tokens = place.shape[1] // 2
    before = jnp.sum((place[:, : half * tokens] >= 0).astype(jnp.int32), axis=1)
    part = place[:, half * tokens : (half + 1) * tokens]
    kept = part >= 0
    sizes = jnp.sum(kept.astype(jnp.int32), axis=1)
    part = jnp.where(kept, part - before[:, None], -1)
    padded = (sizes + 15) // 16 * 16
    ends = jnp.cumsum(padded)
    info = jnp.concatenate([ends - padded, sizes, ends[-1:]]).astype(jnp.int32)
    hot = other[:, half * tokens : (half + 1) * tokens].reshape(-1, 1) == jnp.arange(128)[None, :]
    return info, part, hot.astype(jnp.bfloat16)


def pack_kernel(sources, info, place_ref, *refs):
    ins, outs = refs[:len(refs) // 2], refs[len(refs) // 2:]
    d = pl.program_id(0)

    @pl.when(d == 0)
    def _():
        for out in outs:
            out[...] = jnp.zeros_like(out)

    tokens = place_ref.shape[2]
    row = lax.broadcasted_iota(jnp.int32, (MOE_ROWS, tokens), 0)

    def chunk(j, _):
        pick = jnp.where(place_ref[0] == row + MOE_ROWS * j, 1.0, 0.0).astype(BF16)
        at = pl.ds(pl.multiple_of(info[d] + MOE_ROWS * j, 16), MOE_ROWS)
        for x, out in zip(ins, outs):
            out[at, :] = dot(pick, x[...]).astype(BF16)
        return 0
    lax.fori_loop(0, (info[sources + d] + MOE_ROWS - 1) // MOE_ROWS, chunk, 0)


def pack(info, place, arrays, room, halves=1, half=0):
    sources, tokens = place.shape
    return pl.pallas_call(
        functools.partial(pack_kernel, sources),
        grid_spec=pltpu.PrefetchScalarGridSpec(
            num_scalar_prefetch=1, grid=(sources,),
            in_specs=[pl.BlockSpec((1, 1, tokens), lambda d, *_: (d, 0, 0))]
            + [pl.BlockSpec((tokens, x.shape[1]), lambda d, *_: (halves * d + half, 0)) for x in arrays],
            out_specs=[pl.BlockSpec((room, x.shape[1]), lambda d, *_: (0, 0)) for x in arrays]),
        out_shape=[jax.ShapeDtypeStruct((room, x.shape[1]), BF16) for x in arrays],
        compiler_params=pltpu.CompilerParams(vmem_limit_bytes=40 << 20),
        cost_estimate=EARLY,
        name="pack_tokens",
    )(info, place[:, None, :], *arrays)


def unpack_kernel(send, info, place_ref, *refs):
    ins, outs = refs[:len(refs) // 2], refs[len(refs) // 2:]
    tokens = place_ref.shape[0]
    lane = lax.broadcasted_iota(jnp.int32, (tokens, 128), 1)
    put = jnp.concatenate(
        [jnp.where(place_ref[...] == lane + 128 * b, 1.0, 0.0).astype(BF16) for b in range(send // 128)], axis=1)
    at = pl.ds(pl.multiple_of(info[pl.program_id(0)], 16), send)
    for x, out in zip(ins, outs):
        out[...] = dot(put, x[at, :]).astype(out.dtype)


def unpack(info, place, arrays, dtypes, send):
    sources, tokens = place.shape
    spread = jnp.broadcast_to(place.reshape(-1, 1), (sources * tokens, 128))
    return pl.pallas_call(
        functools.partial(unpack_kernel, send),
        grid_spec=pltpu.PrefetchScalarGridSpec(
            num_scalar_prefetch=1, grid=(sources,),
            in_specs=[pl.BlockSpec((tokens, 128), lambda d, *_: (d, 0))]
            + [pl.BlockSpec(x.shape, lambda d, *_: (0, 0)) for x in arrays],
            out_specs=[pl.BlockSpec((tokens, x.shape[1]), lambda d, *_: (d, 0)) for x in arrays]),
        out_shape=[jax.ShapeDtypeStruct((sources * tokens, x.shape[1]), t) for x, t in zip(arrays, dtypes)],
        compiler_params=pltpu.CompilerParams(vmem_limit_bytes=40 << 20),
        cost_estimate=EARLY,
        name="unpack_tokens",
    )(info, spread, *arrays)


def window_kernel(sources, info, later, x_ref, y_ref, *out_refs):
    d = pl.program_id(0)
    send = out_refs[0].shape[0]
    count = info[sources + d]
    row = lax.broadcasted_iota(jnp.int32, (send, send), 0)
    column = lax.broadcasted_iota(jnp.int32, (send, send), 1)
    pick = jnp.where(column == row - count, 1.0, 0.0).astype(BF16)
    moved = dot(pick, y_ref[pl.ds(pl.multiple_of(later[d], 16), send), :]).astype(BF16)
    rows = x_ref[pl.ds(pl.multiple_of(info[d], 16), send), :]
    first = lax.broadcasted_iota(jnp.int32, rows.shape, 0) < count
    both = jnp.where(first, rows, moved)
    at = 0
    for out_ref in out_refs:
        out_ref[...] = both[:, at:at + out_ref.shape[1]]
        at += out_ref.shape[1]


def windows_of(info, later, x, y, sources, send, columns):
    whole = pl.BlockSpec(x.shape, lambda d, *_: (0, 0))
    return pl.pallas_call(
        functools.partial(window_kernel, sources),
        grid_spec=pltpu.PrefetchScalarGridSpec(
            num_scalar_prefetch=2, grid=(sources,), in_specs=[whole, whole],
            out_specs=[pl.BlockSpec((send, n), lambda d, *_: (d, 0)) for n in columns]),
        out_shape=[jax.ShapeDtypeStruct((sources * send, n), BF16) for n in columns],
        compiler_params=pltpu.CompilerParams(vmem_limit_bytes=40 << 20),
        cost_estimate=EARLY,
        name="window_rows",
    )(info, later, x, y)


def collect_kernel(place_ref, *refs):
    x_refs, out_ref = refs[:-1], refs[-1]
    tokens = place_ref.shape[0]
    lane = lax.broadcasted_iota(jnp.int32, (tokens, 128), 1)
    put = jnp.concatenate(
        [jnp.where(place_ref[...] == lane + 128 * b, 1.0, 0.0).astype(BF16) for b in range(x_refs[0].shape[0] // 128)],
        axis=1)
    total = jnp.concatenate([dot(put, x_ref[...]) for x_ref in x_refs], axis=1)

    @pl.when(pl.program_id(0) == 0)
    def _():
        out_ref[...] = total

    @pl.when(pl.program_id(0) > 0)
    def _():
        out_ref[...] += total


def collect(place, returned, send):
    experts, tokens = place.shape
    width = sum(x.shape[1] for x in returned)
    spread = jnp.broadcast_to(place.reshape(-1, 1), (experts * tokens, 128))
    return pl.pallas_call(
        collect_kernel,
        grid=(experts,),
        in_specs=[pl.BlockSpec((tokens, 128), lambda e: (e, 0)), *[pl.BlockSpec((send, x.shape[1]), lambda e: (e, 0)) for x in returned]],
        out_specs=pl.BlockSpec((tokens, width), lambda e: (0, 0)),
        out_shape=jax.ShapeDtypeStruct((tokens, width), F32),
        compiler_params=pltpu.CompilerParams(vmem_limit_bytes=40 << 20),
        cost_estimate=EARLY,
        name="collect_rows",
    )(spread, *returned)


def gelu_and_slope(v):
    c = math.sqrt(2.0 / math.pi)
    t = jnp.tanh(c * (v + 0.044715 * (v * v * v)))
    half = 0.5 * (1.0 + t)
    return v * half, half + 0.5 * v * (1.0 - t * t) * (c * (1.0 + 3 * 0.044715 * (v * v)))


def expert_kernel(sources, more, info, expert, x_ref, o_ref, c_ref, r_ref, wi_ref, wd_ref, *refs):
    if more:
        dwi_before, dwd_before, *refs = refs
    gi_ref, eo_ref, gg_ref, dwi_ref, dwd_ref, geo, gate, eo, gi, dwi, dwd = refs
    f = pl.program_id(0)
    last = pl.num_programs(0) - 1
    tiles = (info[2 * sources] + MOE_ROWS - 1) // MOE_ROWS
    lane = lax.broadcasted_iota(jnp.int32, (MOE_ROWS, 128), 1)

    def rows_of(i):
        return pl.ds(pl.multiple_of(i * MOE_ROWS, MOE_ROWS), MOE_ROWS)

    @pl.when(f == 0)
    def _():
        gi_ref[...] = jnp.zeros_like(gi_ref)
        eo_ref[...] = jnp.zeros_like(eo_ref)
        gg_ref[...] = jnp.zeros_like(gg_ref)

        def start(i, _):
            at = rows_of(i)
            logits = dot(x_ref[at, :], r_ref[...])
            mine = jnp.sum(jnp.where(lane == expert[0], logits, 0.0), axis=1, keepdims=True)
            other = jnp.sum(jnp.where(o_ref[at, :] > 0, logits, 0.0), axis=1, keepdims=True)
            top = jnp.maximum(mine, other)
            a, b = jnp.exp(mine - top), jnp.exp(other - top)
            g = a / (a + b)
            gate[at, :] = jnp.broadcast_to(g, (MOE_ROWS, 128))
            geo[at, :] = (c_ref[at, :].astype(F32) * g).astype(BF16)
            eo[at, :] = jnp.zeros((MOE_ROWS, eo.shape[1]), F32)
            gi[at, :] = jnp.zeros((MOE_ROWS, gi.shape[1]), F32)
            return 0
        lax.fori_loop(0, tiles, start, 0)

    dwi[...] = dwi_before[...].astype(F32) if more else jnp.zeros_like(dwi)
    dwd[...] = dwd_before[...].astype(F32) if more else jnp.zeros_like(dwd)

    def tile(i, _):
        at = rows_of(i)
        x, g = x_ref[at, :], geo[at, :]
        act, slope = gelu_and_slope(dot(x, wi_ref[...]))
        act = act.astype(BF16)
        eo[at, :] += dot(act, wd_ref[...])
        gh = (dot(g, wd_ref[...], NT) * slope).astype(BF16)
        gi[at, :] += dot(gh, wi_ref[...], NT)
        dwd[...] += dot(act, g, TN)
        dwi[...] += dot(x, gh, TN)
        return 0
    lax.fori_loop(0, tiles, tile, 0)
    dwi_ref[...] = dwi[...].astype(BF16)
    dwd_ref[...] = dwd[...].astype(BF16)

    @pl.when(f == last)
    def _():
        def finish(i, _):
            at = rows_of(i)
            out = eo[at, :].astype(BF16).astype(F32)
            gg = jnp.sum(out * c_ref[at, :].astype(F32), axis=1, keepdims=True)
            parts = split3(gg)
            spread = jnp.zeros((MOE_ROWS, 128), BF16)
            for n in range(3):
                spread = jnp.where(lane == n, jnp.broadcast_to(parts[n], (MOE_ROWS, 128)), spread)
            gg_ref[at, :] = spread
            eo_ref[at, :] = (out * gate[at, :1]).astype(BF16)
            gi_ref[at, :] = gi[at, :].astype(BF16)
            return 0
        lax.fori_loop(0, tiles, finish, 0)


def expert_layer(info, expert, x, other, cot, router, w_in, w_down, sources, before):
    room, width = x.shape
    hidden = w_in.shape[1]
    whole = lambda a: pl.BlockSpec(a.shape, lambda f, *_: (0, 0))
    fixed = lambda cols: pl.BlockSpec((room, cols), lambda f, *_: (0, 0))
    return pl.pallas_call(
        functools.partial(expert_kernel, sources, bool(before)),
        grid_spec=pltpu.PrefetchScalarGridSpec(
            num_scalar_prefetch=2, grid=(hidden // FF_TILE,),
            in_specs=[whole(x), whole(other), whole(cot), whole(router),
                      *([pl.BlockSpec((width, FF_TILE), lambda f, *_: (0, f)),
                         pl.BlockSpec((FF_TILE, width), lambda f, *_: (f, 0))] * (2 if before else 1))],
            out_specs=[fixed(width), fixed(width), fixed(128),
                       pl.BlockSpec((width, FF_TILE), lambda f, *_: (0, f)),
                       pl.BlockSpec((FF_TILE, width), lambda f, *_: (f, 0))],
            scratch_shapes=[pltpu.VMEM((room, width), BF16), pltpu.VMEM((room, 128), F32),
                            pltpu.VMEM((room, width), F32), pltpu.VMEM((room, width), F32),
                            pltpu.VMEM((width, FF_TILE), F32), pltpu.VMEM((FF_TILE, width), F32)]),
        out_shape=[jax.ShapeDtypeStruct((room, width), BF16), jax.ShapeDtypeStruct((room, width), BF16),
                   jax.ShapeDtypeStruct((room, 128), BF16),
                   jax.ShapeDtypeStruct(w_in.shape, BF16), jax.ShapeDtypeStruct(w_down.shape, BF16)],
        compiler_params=pltpu.CompilerParams(vmem_limit_bytes=63 << 20),
        cost_estimate=EARLY,
        name="expert_layer",
    )(info, expert, x, other, cot, router, w_in, w_down, *before)


MESH_ID = pl.DeviceIdType.MESH


def dense_kernel(q_ref, w_ref, s_ref, out_ref, small_ref, give, h, r0, ra1, rb1, ra2, rb2, rz, s_acc, s_got, s_all,
                 send, recv, s_send, s_recv):
    i, j = lax.axis_index("dp"), lax.axis_index("expert")
    y, x, z, c = i // 2, i % 2, j // 2, j % 2
    other_core = (i, z * 2 + 1 - c)
    other_x = (y * 2 + 1 - x, j)
    other_y = ((1 - y) * 2 + x, j)
    peers = [(i, (z + d) % 4 * 2 + c) for d in (1, 2, 3)]
    barrier = pltpu.get_barrier_semaphore()
    for device in [other_core, other_x, other_y] + peers:
        pl.semaphore_signal(barrier, inc=1, device_id=device, device_id_type=MESH_ID)
    pl.semaphore_wait(barrier, 6)

    def copy(n, src, dst, device):
        return pltpu.make_async_remote_copy(src_ref=src, dst_ref=dst, send_sem=send.at[n], recv_sem=recv.at[n],
                                            device_id=device, device_id_type=MESH_ID)

    def small_copy(n, src, dst, device):
        return pltpu.make_async_remote_copy(src_ref=src, dst_ref=dst, send_sem=s_send.at[n], recv_sem=s_recv.at[n],
                                            device_id=device, device_id_type=MESH_ID)

    def block(b, core):
        rows = jnp.concatenate([q_ref[b, core], w_ref[b, core]], axis=1)
        half = rows.shape[1] // 2
        return jnp.concatenate([rows[:, :half], rows[:, half:]], axis=0)

    small = small_copy(0, s_ref, s_got.at[0], other_core)
    small.start()
    copies = []
    for g in range(4):
        def convert(b, _):
            give[b] = block(b, 1 - c).astype(BF16)
            return 0
        lax.fori_loop(4 * g, 4 * g + 4, convert, 0)
        copies.append(copy(g, give.at[pl.ds(4 * g, 4)], r0.at[pl.ds(4 * g, 4)], other_core))
        copies[-1].start()
    small.wait()
    s_acc[0] = s_ref[...] + s_got[0]
    small = small_copy(1, s_acc.at[0], s_got.at[1], other_x)
    small.start()
    for g in range(4):
        copies[g].wait()
        def add(b, _):
            h[b // 8, b // 4 % 2, b % 4] = (block(b, c) + r0[b].astype(F32)).astype(BF16)
            return 0
        lax.fori_loop(4 * g, 4 * g + 4, add, 0)

    half = h.shape[4] // 2
    left, right = pl.ds(0, half), pl.ds(half, half)
    ca = copy(4, h.at[:, 1 - x, :, :, left], ra1, other_x)
    cb = copy(5, h.at[1 - y, :, :, :, right], rb1, other_y)
    ca.start()
    cb.start()
    small.wait()
    s_acc[1] = s_acc[0] + s_got[1]
    small = small_copy(2, s_acc.at[1], s_got.at[2], other_y)
    small.start()
    ca.wait()

    def add_x(b, _):
        u, v = b // 4, b % 4
        h[u, x, v, :, left] = (h[u, x, v, :, left].astype(F32) + ra1[u, v].astype(F32)).astype(BF16)
        return 0
    lax.fori_loop(0, 8, add_x, 0)
    ca = copy(6, h.at[1 - y, x, :, :, left], ra2, other_y)
    ca.start()
    cb.wait()

    def add_y(b, _):
        u, v = b // 4, b % 4
        h[y, u, v, :, right] = (h[y, u, v, :, right].astype(F32) + rb1[u, v].astype(F32)).astype(BF16)
        return 0
    lax.fori_loop(0, 8, add_y, 0)
    cb = copy(7, h.at[y, 1 - x, :, :, right], rb2, other_x)
    cb.start()
    small.wait()
    s_acc[2] = s_acc[1] + s_got[2]
    smalls = [small_copy(3 + n, s_acc.at[2], s_all.at[z], device) for n, device in enumerate(peers)]
    for one in smalls:
        one.start()
    ca.wait()
    cb.wait()

    def add_both(v, _):
        h[y, x, v, :, left] = (h[y, x, v, :, left].astype(F32) + ra2[v].astype(F32)).astype(BF16)
        h[y, x, v, :, right] = (h[y, x, v, :, right].astype(F32) + rb2[v].astype(F32)).astype(BF16)
        return 0
    lax.fori_loop(0, 4, add_both, 0)
    copies = [copy(8 + n, h.at[y, x, (z + 1 + n) % 4], rz.at[n], device) for n, device in enumerate(peers)]
    for one in copies:
        one.start()
    total = h[y, x, z].astype(F32)
    for one in smalls:
        one.wait()
    s_all[z] = s_acc[2]
    small_ref[...] = (s_all[0] + s_all[1]) + (s_all[2] + s_all[3])
    for n, one in enumerate(copies):
        one.wait()
        total = total + rz[n].astype(F32)
    rows = total.shape[0] // 2
    out_ref[:, :2 * half] = total[:rows]
    out_ref[:, 2 * half:] = total[rows:]


def dense_sum(grad_qkv, grad_out, small):
    rows, wide = grad_qkv.shape
    narrow = grad_out.shape[1]
    own = rows // 32
    width = wide + narrow
    half = width // 2
    pair = own * 2
    vmem = pl.BlockSpec(memory_space=pltpu.VMEM)
    return pl.pallas_call(
        dense_kernel,
        in_specs=[vmem] * 3, out_specs=[vmem] * 2,
        out_shape=[jax.ShapeDtypeStruct((own, width), F32), jax.ShapeDtypeStruct(small.shape, F32)],
        scratch_shapes=[
            pltpu.VMEM((16, pair, half), BF16), pltpu.VMEM((2, 2, 4, pair, half), BF16), pltpu.VMEM((16, pair, half), BF16),
            pltpu.VMEM((2, 4, pair, half // 2), BF16), pltpu.VMEM((2, 4, pair, half // 2), BF16),
            pltpu.VMEM((4, pair, half // 2), BF16), pltpu.VMEM((4, pair, half // 2), BF16), pltpu.VMEM((3, pair, half), BF16),
            pltpu.VMEM((3,) + small.shape, F32), pltpu.VMEM((3,) + small.shape, F32), pltpu.VMEM((4,) + small.shape, F32),
            pltpu.SemaphoreType.DMA((11,)), pltpu.SemaphoreType.DMA((11,)),
            pltpu.SemaphoreType.DMA((6,)), pltpu.SemaphoreType.DMA((6,))],
        compiler_params=pltpu.CompilerParams(collective_id=0, has_side_effects=True, vmem_limit_bytes=48 << 20),
        name="dense_sum",
    )(grad_qkv.reshape(16, 2, own, wide), grad_out.reshape(16, 2, own, narrow), small)


def exchange_pairs(normed_ffn, middle, cotangent, expert_ids, priority, router, w_in, w_down):
    rows, width = normed_ffn.shape
    logits = jnp.dot(normed_ffn, router, preferred_element_type=jnp.float32)
    experts_total = router.shape[1]
    picks = expert_ids[:, :, None] == jnp.arange(experts_total)[None, None, :]
    chosen = jnp.sum(jnp.where(picks, logits[:, None, :], 0.0), axis=2)
    gates = jax.nn.softmax(chosen, axis=-1)
    top = expert_ids.shape[1]
    levels = PRIO
    local_experts = w_in.shape[0]
    capacity = rows * top // local_experts
    send = max(2, 2 * rows * top // experts_total)
    flat_expert = expert_ids.reshape(-1)
    code = priority.reshape(-1) * experts_total + flat_expert
    onehot = (code[:, None] == jnp.arange(levels * experts_total)[None, :]).astype(jnp.int32)
    rank = jnp.sum((jnp.cumsum(onehot, axis=0) - onehot) * onehot, axis=1)
    counts = jnp.sum(onehot, axis=0)
    every = lax.all_gather(counts[None, :], "expert", axis=0, tiled=True).reshape(
        -1, levels, experts_total
    )
    expert_index = lax.axis_index("expert")
    totals = jnp.sum(every, axis=0)
    lower = jnp.cumsum(totals, axis=0) - totals
    earlier_sources = jnp.cumsum(every, axis=0) - every
    mine_prefix = lax.dynamic_index_in_dim(earlier_sources, expert_index, 0, keepdims=False)
    base = (lower + mine_prefix).reshape(-1)
    slot = rank + jnp.sum(onehot * base[None, :], axis=1)
    kept = slot < capacity
    own_counts = counts.reshape(levels, experts_total)
    own_lower = (jnp.cumsum(own_counts, axis=0) - own_counts).reshape(-1)
    place = rank + jnp.sum(onehot * own_lower[None, :], axis=1)
    target = flat_expert * send + place
    first_mine = expert_index * local_experts
    counts_mine = lax.dynamic_slice_in_dim(every, first_mine, local_experts, 2)
    base_mine = lax.dynamic_slice_in_dim(
        lower[None] + earlier_sources, first_mine, local_experts, 2
    )
    band_end = jnp.cumsum(counts_mine, axis=1)
    band_start = band_end - counts_mine
    place_index = jnp.arange(send, dtype=jnp.int32)
    level = jnp.sum(
        (place_index[None, None, None, :] >= band_end[:, :, :, None]).astype(jnp.int32), axis=1
    )
    level_hot = level[:, None, :, :] == jnp.arange(levels)[None, :, None, None]
    start_of = jnp.sum(jnp.where(level_hot, band_start[:, :, :, None], 0), axis=1)
    base_of = jnp.sum(jnp.where(level_hot, base_mine[:, :, :, None], 0), axis=1)
    arrived_slot = base_of + place_index[None, None, :] - start_of
    usable = (level < levels) & (arrived_slot < capacity)
    landing = jnp.where(
        usable,
        jnp.arange(local_experts)[None, :, None] * capacity + arrived_slot,
        local_experts * capacity,
    ).reshape(-1)
    live = landing < local_experts * capacity
    safe = jnp.minimum(landing, local_experts * capacity - 1)
    pair_inputs = jnp.repeat(normed_ffn, top, axis=0)
    outgoing = (
        jnp.zeros((experts_total * send, width), jnp.bfloat16)
        .at[target]
        .set(pair_inputs)
        .reshape(experts_total, send, width)
    )
    arrived = lax.all_to_all(outgoing, "expert", split_axis=0, concat_axis=0, tiled=True)
    expert_inputs = (
        jnp.zeros((local_experts * capacity, width), jnp.bfloat16)
        .at[landing]
        .set(arrived.reshape(-1, width), mode="drop")
        .reshape(local_experts, capacity, width)
    )
    hidden = jnp.einsum("ecd,edf->ecf", expert_inputs, w_in, preferred_element_type=jnp.float32)
    activated = jax.nn.gelu(hidden).astype(jnp.bfloat16)
    expert_out = jnp.einsum(
        "ecf,efd->ecd", activated, w_down, preferred_element_type=jnp.float32
    ).astype(jnp.bfloat16)
    returning = jnp.where(
        live[:, None],
        jnp.take(expert_out.reshape(-1, width), safe, axis=0),
        jnp.zeros((), jnp.bfloat16),
    ).reshape(experts_total, send, width)
    returned = lax.all_to_all(returning, "expert", split_axis=0, concat_axis=0, tiled=True)
    pair_out = jnp.where(
        kept[:, None],
        jnp.take(returned.reshape(-1, width), target, axis=0).astype(jnp.float32),
        0.0,
    ).reshape(rows, top, width)
    mixed = jnp.sum(gates[:, :, None] * pair_out, axis=1)
    grad_out = cotangent.astype(jnp.float32)
    grad_gates = jnp.sum(grad_out[:, None, :] * pair_out, axis=2)
    pair_grads = (gates[:, :, None] * grad_out[:, None, :]).astype(jnp.bfloat16).reshape(-1, width)
    outgoing_grads = (
        jnp.zeros((experts_total * send, width), jnp.bfloat16)
        .at[target]
        .set(pair_grads)
        .reshape(experts_total, send, width)
    )
    arrived_grads = lax.all_to_all(
        outgoing_grads, "expert", split_axis=0, concat_axis=0, tiled=True
    )
    grad_expert_out = (
        jnp.zeros((local_experts * capacity, width), jnp.bfloat16)
        .at[landing]
        .set(arrived_grads.reshape(-1, width), mode="drop")
        .reshape(local_experts, capacity, width)
    )
    hidden_again = jnp.einsum(
        "ecd,edf->ecf", expert_inputs, w_in, preferred_element_type=jnp.float32
    )
    activated_again, gelu_back = jax.vjp(jax.nn.gelu, hidden_again)
    grad_activated = jnp.einsum(
        "ecd,efd->ecf", grad_expert_out, w_down, preferred_element_type=jnp.float32
    )
    grad_hidden = gelu_back(grad_activated)[0].astype(jnp.bfloat16)
    grad_w_down = jnp.einsum(
        "ecf,ecd->efd",
        activated_again.astype(jnp.bfloat16),
        grad_expert_out,
        preferred_element_type=jnp.float32,
    )
    grad_w_in = jnp.einsum(
        "ecd,ecf->edf", expert_inputs, grad_hidden, preferred_element_type=jnp.float32
    )
    grad_inputs = jnp.einsum(
        "ecf,edf->ecd", grad_hidden, w_in, preferred_element_type=jnp.float32
    ).astype(jnp.bfloat16)
    back_rows = jnp.where(
        live[:, None],
        jnp.take(grad_inputs.reshape(-1, width), safe, axis=0),
        jnp.zeros((), jnp.bfloat16),
    ).reshape(experts_total, send, width)
    came_back = lax.all_to_all(back_rows, "expert", split_axis=0, concat_axis=0, tiled=True)
    pair_back = jnp.where(
        kept[:, None],
        jnp.take(came_back.reshape(-1, width), target, axis=0).astype(jnp.float32),
        0.0,
    )
    grad_normed_ffn = jnp.sum(pair_back.reshape(rows, top, width), axis=1)
    grad_chosen = gates * (grad_gates - jnp.sum(gates * grad_gates, axis=-1, keepdims=True))
    grad_logits = jnp.sum(jnp.where(picks, grad_chosen[:, :, None], 0.0), axis=1).astype(
        jnp.bfloat16
    )
    grad_normed_ffn = grad_normed_ffn + jnp.dot(
        grad_logits, router.T, preferred_element_type=jnp.float32
    )
    expert_parts = (
        lax.psum_scatter(grad_w_in.astype(jnp.bfloat16), "dp", scatter_dimension=1, tiled=True),
        lax.psum_scatter(grad_w_down.astype(jnp.bfloat16), "dp", scatter_dimension=1, tiled=True),
    )
    return mixed, grad_logits, grad_normed_ffn, expert_parts


def gather_codes(expert_ids, priority):
    return lax.all_gather(expert_ids * PRIO + priority, "expert", axis=0)


def plan_tokens(codes, rows, top):
    expert = lax.axis_index("expert").astype(jnp.int32)
    place, other = expert_slots(codes // PRIO, codes % PRIO, expert, rows * top)
    own_place = lax.all_to_all(place, "expert", split_axis=0, concat_axis=0, tiled=True)
    return own_place, half_plan(place, other, 0), half_plan(place, other, 1)


def expert_half(all_tokens, all_cotangents, number, half, router, w_in, w_down, send, before):
    info, place, other_hot = half
    sources, tokens = place.shape
    room = (4 * tokens + 16 * sources + send + MOE_ROWS - 1) // MOE_ROWS * MOE_ROWS
    expert = lax.axis_index("expert").astype(jnp.int32)
    (packed_cot,) = pack(info, place, [all_cotangents], room, 2, number)
    packed, packed_other = pack(info, place, [all_tokens, other_hot], room)
    grad_rows, mixed_rows, grad_gate, grad_w_in, grad_w_down = expert_layer(
        info, expert[None], packed, packed_other, packed_cot, router, w_in[0], w_down[0], sources, before
    )
    grad_all, gate_all = unpack(info, place, [grad_rows, grad_gate], [jnp.bfloat16, jnp.float32], send)
    gate_all = jnp.sum(gate_all[:, :3], axis=1).reshape(sources, tokens)
    return grad_all, gate_all, mixed_rows, grad_w_in, grad_w_down


def exchange_tokens(normed_halves, all_cotangents, plan, expert_ids, router, w_in, w_down):
    rows = expert_ids.shape[0]
    experts_total = router.shape[1]
    top = expert_ids.shape[1]
    own_place, *halves = plan
    send = 2 * rows * top // experts_total
    wide_router = jnp.pad(router, ((0, 0), (0, 128 - experts_total)))
    tokens = [lax.all_gather(x, "expert", axis=0, tiled=True) for x in normed_halves]
    first = expert_half(tokens[0], all_cotangents, 0, halves[0], wide_router, w_in, w_down, send, ())
    grad_own = [lax.psum_scatter(first[0], "expert", scatter_dimension=0, tiled=True)]
    tokens[1], all_cotangents, _ = lax.optimization_barrier((tokens[1], all_cotangents, first))
    second = expert_half(tokens[1], all_cotangents, 1, halves[1], wide_router, w_in, w_down, send, first[3:])
    grad_later, grad_own[0] = lax.optimization_barrier((second[0], grad_own[0]))
    grad_own.append(lax.psum_scatter(grad_later, "expert", scatter_dimension=0, tiled=True))
    gate_own = [lax.all_to_all(x[1], "expert", split_axis=0, concat_axis=0, tiled=True) for x in (first, second)]
    windows = windows_of(halves[0][0], halves[1][0], first[2], second[2], own_place.shape[0], send, (first[2].shape[1],))
    return grad_own, gate_own, windows, second[3], second[4]


def router_back(normed_ffn, expert_ids, router, gate_own):
    logits = jnp.dot(normed_ffn, router, preferred_element_type=jnp.float32)
    picks = expert_ids[:, :, None] == jnp.arange(router.shape[1])[None, None, :]
    chosen = jnp.sum(jnp.where(picks, logits[:, None, :], 0.0), axis=2)
    gates = jax.nn.softmax(chosen, axis=-1)
    grad_gates = jnp.sum(jnp.where(picks, gate_own.T[:, None, :], 0.0), axis=2)
    grad_chosen = gates * (grad_gates - jnp.sum(gates * grad_gates, axis=-1, keepdims=True))
    return jnp.sum(jnp.where(picks, grad_chosen[:, :, None], 0.0), axis=1).astype(jnp.bfloat16)


def per_device(
    tokens_in,
    cont_ids,
    expert_ids,
    priority,
    gain_attn,
    w_qkv,
    rel_table,
    w_out,
    gain_ffn,
    w_router,
    w_in,
    w_down,
    cotangent,
):
    rows, width = tokens_in.shape
    heads = rel_table.shape[1]
    dp_count = lax.axis_size("dp")
    dp_index = lax.axis_index("dp")
    prompt_rows = PROMPT // dp_count
    few_experts = lax.axis_size("expert") <= 16 and w_in.shape[0] == 1 and prompt_rows == KT
    local_ids = cont_ids[0]
    info = info_of(local_ids, dp_index)
    row_start = row_start_of(local_ids)
    rows_bias = bias_rows(rel_table)
    if few_experts:
        codes = gather_codes(expert_ids, priority)
    experts_total = w_router.shape[1]
    dense = jnp.concatenate(
        [pairs_together(w_qkv), w_out, jnp.pad(w_router, ((0, 0), (0, 128 - experts_total)))], axis=1
    )
    dense = lax.all_gather(dense, ("dp", "expert"), axis=0, tiled=True)
    part_heads = heads // PARTS
    tables = [bias_tables(info, rows_bias, row_start, g * part_heads, part_heads) for g in range(PARTS)]
    dense, tables[0] = lax.optimization_barrier((dense, tables[0]))
    if few_experts:
        plan = plan_tokens(codes, rows, expert_ids.shape[1])
        dense, plan = lax.optimization_barrier((dense, plan))
    whole_qkv, whole_out = dense[:, : 3 * width], dense[:, 3 * width : 4 * width]
    whole_router = dense[:, 4 * width : 4 * width + experts_total]
    inputs = tokens_in.astype(jnp.float32)
    normed_attn = normed(inputs, gain_attn).astype(jnp.bfloat16)
    projected = jnp.dot(normed_attn, whole_qkv, preferred_element_type=jnp.float32).astype(
        jnp.bfloat16
    )
    parts = PARTS
    columns = 2 * width // parts
    kept = [projected[:, width + columns * g : width + columns * (g + 1)] for g in range(parts)]
    gathered = [lax.all_gather(kept[0][:prompt_rows], "dp", axis=0, tiled=True)]
    for kv in kept[1:]:
        copies = jnp.broadcast_to(kv[None, :prompt_rows], (dp_count, prompt_rows, columns))
        gathered.append(
            lax.all_to_all(copies, "dp", split_axis=0, concat_axis=0, tiled=True).reshape(PROMPT, columns)
        )
    if few_experts:
        late_cotangent, gathered[0], tables = lax.optimization_barrier((cotangent, gathered[0], tables))
        all_cotangents = lax.all_gather(late_cotangent, "expert", axis=0, tiled=True)
    gathered[0], tables = lax.optimization_barrier((gathered[0], tables))
    results = {}
    keys_values = []
    middles, normed_halves, attended_halves = [], [], []
    order = [(g, c) for g in range(parts) for c in (0, 1)]

    def after_attention(c):
        attended = jnp.concatenate([results[g, c][0] for g in range(parts)], axis=1).astype(jnp.bfloat16)
        middle = inputs[c * KT : (c + 1) * KT] + jnp.dot(attended, whole_out, preferred_element_type=jnp.float32)
        attended_halves.append(attended)
        middles.append(middle)
        normed_halves.append(normed(middle, gain_ffn).astype(jnp.bfloat16))

    last = None
    for g, c in order:
        if last is not None:
            gathered[g], results[last] = lax.optimization_barrier((gathered[g], results[last]))
        if c == 0:
            source = gathered[g]
        else:
            source = jnp.concatenate([gathered[g], kept[g][prompt_rows:]], axis=0)
            keys_values.append(source)
        results[g, c] = attention_forward(info, projected, source, tables[g], g, bool(c))
        last = (g, c)
        if (g, c) == (parts - 1, 0):
            after_attention(0)
            if few_experts:
                normed_halves[0], all_cotangents = lax.optimization_barrier((normed_halves[0], all_cotangents))
            gathered[g], normed_halves[0] = lax.optimization_barrier((gathered[g], normed_halves[0]))
    after_attention(1)
    attended = jnp.concatenate(attended_halves, axis=0)
    middle = jnp.concatenate(middles, axis=0)
    normed_ffn = jnp.concatenate(normed_halves, axis=0)
    cut = [slice(0, KT), slice(KT, rows)]
    if few_experts:
        grad_own, gate_own, windows, *grad_w = exchange_tokens(
            normed_halves, all_cotangents, plan, expert_ids, whole_router, w_in, w_down
        )
    else:
        mixed, grad_logits, grad_normed_ffn, expert_parts = exchange_pairs(
            normed_ffn, middle, cotangent, expert_ids, priority, whole_router, w_in, w_down
        )
        grad_logits = [grad_logits[at] for at in cut]
        grad_normed_halves = [grad_normed_ffn[at] for at in cut]
    if few_experts:
        grad_logits, grad_normed_halves = [None, None], [None, None]
    grad_out = cotangent.astype(jnp.float32)
    grad_middles, grad_branches, grad_gain_ffn = [], [], 0.0
    grad_queries, grad_kv, grad_lines = {}, [None] * parts, 0.0
    grad_prompts, grad_conts = [], []
    for c in (0, 1):
        if few_experts:
            if c:
                grad_own[1], gate_own[1], grad_kv = lax.optimization_barrier((grad_own[1], gate_own[1], grad_kv))
                grad_own[1], windows, grad_w = lax.optimization_barrier((grad_own[1], windows, grad_w))
                mixed = [lax.all_to_all(x, "expert", split_axis=0, concat_axis=0, tiled=True) for x in windows]
                expert_in = lax.psum_scatter(grad_w[0][None], "dp", scatter_dimension=1, tiled=True)
            grad_logits[c] = router_back(normed_halves[c], expert_ids[cut[c]], whole_router, gate_own[c])
            grad_normed_halves[c] = grad_own[c].astype(jnp.float32) + jnp.dot(
                grad_logits[c], whole_router.T, preferred_element_type=jnp.float32
            )
        _, ffn_norm_back = jax.vjp(normed, middles[c], gain_ffn)
        grad_middle_part, grad_gain = ffn_norm_back(grad_normed_halves[c])
        grad_gain_ffn = grad_gain_ffn + grad_gain
        grad_middles.append(grad_out[cut[c]] + grad_middle_part)
        grad_branches.append(grad_middles[c].astype(jnp.bfloat16))
        grad_attended = jnp.dot(
            grad_branches[c], whole_out.T, preferred_element_type=jnp.float32
        ).astype(jnp.bfloat16)
        lines = []
        for g in range(parts):
            if c and g and few_experts:
                grad_attended, expert_in, grad_queries[g - 1, c] = lax.optimization_barrier(
                    (grad_attended, expert_in, grad_queries[g - 1, c])
                )
            out, total = results[g, c]
            grad_queries[g, c], grad_kv[g], line = attention_backward(
                info, projected, grad_attended, out, total, keys_values[g] if c else gathered[g], tables[g], g, bool(c),
                grad_kv[g],
            )
            lines.append(line)
            if c:
                if g:
                    grad_kv[g], grad_prompts[-1] = lax.optimization_barrier((grad_kv[g], grad_prompts[-1]))
                grad_prompts.append(lax.psum_scatter(grad_kv[g][:PROMPT], "dp", scatter_dimension=0, tiled=True))
                grad_conts.append(grad_kv[g][PROMPT:])
        grad_lines = grad_lines + jnp.concatenate(lines, axis=0)
    if few_experts:
        grad_prompts[-1], grad_down = lax.optimization_barrier((grad_prompts[-1], grad_w[1]))
        expert_parts = (expert_in, lax.psum_scatter(grad_down[None], "dp", scatter_dimension=1, tiled=True))
    grad_middle = jnp.concatenate(grad_middles, axis=0)
    grad_branch = jnp.concatenate(grad_branches, axis=0)
    grad_router = jnp.dot(
        normed_ffn.T, jnp.concatenate(grad_logits, axis=0), preferred_element_type=jnp.float32
    )
    grad_out_weight = jnp.dot(attended.T, grad_branch, preferred_element_type=jnp.float32)
    last = (parts - 1, 1)
    mixed, middle, grad_queries[last] = lax.optimization_barrier((mixed, middle, grad_queries[last]))
    if few_experts:
        mixed = collect(plan[0], mixed, mixed[0].shape[0] // plan[0].shape[0])
    output = (middle + mixed).astype(jnp.bfloat16)
    grad_table = table_grad(grad_lines, rel_table.shape[0])
    grad_projected = jnp.concatenate(
        [jnp.concatenate([grad_queries[g, 0], grad_queries[g, 1]], axis=0) for g in range(parts)]
        + [jnp.concatenate([a, b], axis=0) for a, b in zip(grad_prompts, grad_conts)], axis=1
    )
    grad_normed_attn = jnp.dot(grad_projected, whole_qkv.T, preferred_element_type=jnp.float32)
    grad_qkv = jnp.dot(normed_attn.T, grad_projected, preferred_element_type=jnp.float32)
    _, attn_norm_back = jax.vjp(normed, inputs, gain_attn)
    grad_inputs_part, grad_gain_attn = attn_norm_back(grad_normed_attn)
    grad_tokens = grad_middle + grad_inputs_part
    if (dp_count, lax.axis_size("expert")) == (4, 8):
        pieces = [grad_gain_attn, grad_gain_ffn, grad_table.reshape(-1), grad_router.reshape(-1)]
        sizes = [piece.shape[0] for piece in pieces]
        small = jnp.concatenate(pieces)
        small = jnp.pad(small, (0, -small.shape[0] % 1024)).reshape(-1, 128)
        dense_grad, small = dense_sum(grad_qkv, grad_out_weight, small)
        ends = [sum(sizes[: n + 1]) for n in range(4)]
        flat = small.reshape(-1)
        grad_gain_attn, grad_gain_ffn = flat[: ends[0]], flat[ends[0] : ends[1]]
        grad_table = flat[ends[1] : ends[2]].reshape(grad_table.shape)
        own_rows = w_router.shape[0]
        mine = (dp_index * lax.axis_size("expert") + lax.axis_index("expert")) * own_rows
        own_router = lax.dynamic_slice_in_dim(
            flat[ends[2] : ends[3]].reshape(grad_router.shape), mine, own_rows, 0
        )
        small_parts = (grad_gain_attn, grad_gain_ffn, grad_table.T)
    else:
        dense_grad = lax.psum_scatter(
            jnp.concatenate([grad_qkv, grad_out_weight], axis=1), ("dp", "expert"), scatter_dimension=0, tiled=True
        )
        own_router = lax.psum_scatter(grad_router, ("dp", "expert"), scatter_dimension=0, tiled=True)
        small_parts = lax.psum((grad_gain_attn, grad_gain_ffn, grad_table.T), ("dp", "expert"))
    return (
        output,
        grad_tokens,
        small_parts[0],
        pairs_apart(dense_grad[:, : 3 * width]),
        small_parts[2],
        dense_grad[:, 3 * width :],
        small_parts[1],
        own_router,
        expert_parts[0].astype(jnp.float32),
        expert_parts[1].astype(jnp.float32),
    )


def solution(mesh):
    return jax.shard_map(
        per_device,
        mesh=mesh,
        in_specs=(
            P(("dp", "expert"), None),
            P(("dp", "expert"), None),
            P(("dp", "expert"), None),
            P(("dp", "expert"), None),
            P(),
            P(("dp", "expert"), None),
            P(),
            P(("dp", "expert"), None),
            P(),
            P(("dp", "expert"), None),
            P("expert", None, None),
            P("expert", None, None),
            P(("dp", "expert"), None),
        ),
        out_specs=(
            P(("dp", "expert"), None),
            P(("dp", "expert"), None),
            P(),
            P(("dp", "expert"), None),
            P(),
            P(("dp", "expert"), None),
            P(),
            P(("dp", "expert"), None),
            P("expert", "dp", None),
            P("expert", "dp", None),
        ),
        check_vma=False,
    )
```
